32 devices in a mesh: dp: 4 (over y, x), row: 2 (over core), col: 4 (over z).
Axes of the slice: x: 2, y: 2, z: 4, core: 2. Of those that a mesh axis runs over, the one named last changes fastest.
Arguments:
- states: bfloat16 [25088, 1024], P(('dp', 'row', 'col')), may hold values from -6 to 6
- ln1_gain: bfloat16 [1024], P('row'), may hold values from 0.5 to 1.5
- ln1_bias: bfloat16 [1024], P('row'), may hold values from -0.59765625 to 0.59765625
- w_qkv: bfloat16 [1024, 3, 1024], P('row', None, 'col'), may hold values from -0.1875 to 0.1875
- q_bias: bfloat16 [1024], P('col'), may hold values from -1.796875 to 1.796875
- v_bias: bfloat16 [1024], P('col'), may hold values from -0.29882812 to 0.29882812
- w_proj: bfloat16 [1024, 1024], P('col', 'row'), may hold values from -0.75 to 0.75
- proj_bias: bfloat16 [1024], P('row'), may hold values from -0.59765625 to 0.59765625
- ln2_gain: bfloat16 [1024], P('row'), may hold values from 0.5 to 1.5
- ln2_bias: bfloat16 [1024], P('row'), may hold values from -0.59765625 to 0.59765625
- w_fc1: bfloat16 [1024, 4096], P('row', 'col'), may hold values from -0.1875 to 0.1875
- fc1_bias: bfloat16 [4096], P('col'), may hold values from -0.59765625 to 0.59765625
- w_fc2: bfloat16 [4096, 1024], P('col', 'row'), may hold values from -0.09375 to 0.09375
- fc2_bias: bfloat16 [1024], P('row'), may hold values from -0.59765625 to 0.59765625
- teacher: bfloat16 [25088, 1024], P(('dp', 'row', 'col')), may hold values from -6 to 6
- loss_mask: int32 [25088], replicated, may hold values 0 or 1
- lengths: int32 [16], replicated, may hold values from 784 to 1568, as said below
Outputs:
- states_out: bfloat16 [25088, 1024], P(('dp', 'row', 'col'))
- loss: float32 [], replicated
- grad_states: bfloat16 [25088, 1024], P(('dp', 'row', 'col'))
- grad_ln1_gain: float32 [1024], P('row')
- grad_ln1_bias: float32 [1024], P('row')
- grad_w_qkv: float32 [1024, 3, 1024], P('row', None, 'col')
- grad_q_bias: float32 [1024], P('col')
- grad_v_bias: float32 [1024], P('col')
- grad_w_proj: float32 [1024, 1024], P('col', 'row')
- grad_proj_bias: float32 [1024], P('row')
- grad_ln2_gain: float32 [1024], P('row')
- grad_ln2_bias: float32 [1024], P('row')
- grad_w_fc1: float32 [1024, 4096], P('row', 'col')
- grad_fc1_bias: float32 [4096], P('col')
- grad_w_fc2: float32 [4096, 1024], P('col', 'row')
- grad_fc2_bias: float32 [1024], P('row')
The draws below stay inside these ranges and needn't reach their ends.
Inputs may be any that keep to these rules, and one draw needn't show every extreme that they name: `lengths`: each entry is the number of real tube tokens of one clip, from 784 to 1568; some clip has all 1568. Positions at or beyond it are padding.
All inputs are finite; a program needn't handle non-finite values.
Results may differ from the reference program's by a relative error of at most 0.012.
The reference program's roundings to bfloat16 on the way count: a program that leaves them out, or rounds other values in their place, can miss the bound.
Values may be sent and summed in bfloat16 or wider, within the bound.
No kernel may reach another device: no remote copies, remote signals or barrier semaphores. Data moves between devices by JAX's collectives and lax.ppermute only.
A program may use at most 320 MiB of HBM per device.

```python
import jax
import jax.numpy as jnp
from jax import lax

D = 1024
HEADS = 16
HD = 64
FF = 4096
L = 1568
CLIPS = 2
CLIPS_ALL = 16
TOKENS = 25088


def draw_lengths(key, part):
    first_key, second_key = jax.random.split(key)
    base = jax.random.randint(first_key, (CLIPS_ALL,), L // 2, L + 1)
    chosen = jax.random.randint(second_key, (), 0, CLIPS_ALL)
    return jnp.where(jnp.arange(CLIPS_ALL) == chosen, L, base).astype(jnp.int32)


def touch_ends(values, rng, smallest, largest):
    shape = values.shape
    place = [jax.random.randint(jax.random.fold_in(rng, axis), (), 0, shape[axis]) for axis in range(len(shape))]
    values = values.at[tuple(place)].set(smallest)
    longest = shape.index(max(shape))
    place[longest] = (place[longest] + 1) % shape[longest]
    return values.at[tuple(place)].set(largest)


def level_of(rng, dims, shards, smallest, largest):
    loudness = 1.0
    for dim, parts in shards:
        steps = jax.random.uniform(jax.random.fold_in(jax.random.fold_in(rng, 6), dim), (parts,), jnp.float32, smallest / len(shards), largest / len(shards))
        loudness = loudness * jnp.repeat(jnp.exp(steps), dims[dim] // parts).reshape((-1,) + (1,) * (len(dims) - 1 - dim))
    return loudness


def bell_draw(stream_key, dims, scale, bound, cuts=(), dtype=jnp.bfloat16):
    values = scale * jax.random.normal(stream_key, dims, jnp.float32)
    if cuts:
        values = values * level_of(stream_key, dims, cuts, -0.22, 0.18)
    return jnp.clip(values, -bound, bound).astype(dtype)


def setup_inputs(seed: int = 0) -> dict:
    key_of = jax.random.split(jax.random.key(seed), 18)
    return {
        "states": bell_draw(key_of[0], (TOKENS, D), 1.0, 6.0, ((0, 32),)),
        "ln1_gain": jnp.clip(1.0 + 0.1 * jax.random.normal(key_of[1], (D,), jnp.float32), 0.5, 1.5).astype(jnp.bfloat16),
        "ln1_bias": bell_draw(key_of[2], (D,), 0.1, 0.59765625, ((0, 2),)),
        "w_qkv": bell_draw(key_of[3], (D, 3, D), D ** -0.5, 0.1875, ((0, 2), (2, 4))),
        "q_bias": bell_draw(key_of[4], (D,), 0.3, 1.796875, ((0, 4),)),
        "v_bias": bell_draw(key_of[5], (D,), 0.05, 0.29882812, ((0, 4),)),
        "w_proj": bell_draw(key_of[6], (D, D), (D // 16) ** -0.5, 0.75, ((0, 4), (1, 2))),
        "proj_bias": bell_draw(key_of[7], (D,), 0.1, 0.59765625, ((0, 2),)),
        "ln2_gain": jnp.clip(1.0 + 0.1 * jax.random.normal(key_of[8], (D,), jnp.float32), 0.5, 1.5).astype(jnp.bfloat16),
        "ln2_bias": bell_draw(key_of[9], (D,), 0.1, 0.59765625, ((0, 2),)),
        "w_fc1": bell_draw(key_of[10], (D, FF), D ** -0.5, 0.1875, ((0, 2), (1, 4))),
        "fc1_bias": bell_draw(key_of[11], (FF,), 0.1, 0.59765625, ((0, 4),)),
        "w_fc2": bell_draw(key_of[12], (FF, D), FF ** -0.5, 0.09375, ((0, 4), (1, 2))),
        "fc2_bias": bell_draw(key_of[13], (D,), 0.1, 0.59765625, ((0, 2),)),
        "teacher": bell_draw(key_of[14], (TOKENS, D), 1.0, 6.0, ((0, 32),)),
        "loss_mask": touch_ends((jax.random.randint(key_of[15], (TOKENS,), 0, 4) < 3).astype(jnp.int32), jax.random.fold_in(key_of[15], 1), 0, 1),
        "lengths": draw_lengths(jax.random.fold_in(key_of[17], 71), 0),
    }


HIGHEST = lax.Precision.HIGHEST
EPSILON = 1e-06

@jax.custom_vjp
def low(v):
    return lax.optimization_barrier(v.astype(jnp.bfloat16)).astype(jnp.float32)

@jax.custom_vjp
def low_back(v):
    return v

def low_keep(v):
    return (low(v), None)

def low_pass(kept, grad):
    return (grad,)

def back_keep(v):
    return (v, None)

def back_low(kept, grad):
    return (low(grad),)
low.defvjp(low_keep, low_pass)
low_back.defvjp(back_keep, back_low)

def layer_norm(values, factor, offset):
    centered = values - lax.optimization_barrier(jnp.mean(values, axis=-1, keepdims=True))
    spread = lax.rsqrt(lax.optimization_barrier(jnp.mean(jnp.square(centered), axis=-1, keepdims=True)) + EPSILON)
    return centered * spread * factor + offset

def attention_clip(element):
    queries, key_rows, value_rows, length = element
    logits = jnp.einsum('ihd,jhd->hij', queries, key_rows, precision=HIGHEST) * HD ** (-0.5)
    logits = low_back(logits)
    keep = jnp.arange(key_rows.shape[0]) < length
    logits = jnp.where(keep[None, None, :], logits, -1e+30)
    totals = jax.nn.logsumexp(logits, axis=-1, keepdims=True)
    weights = low(jnp.exp(logits - totals))
    return jnp.einsum('hij,jhd->ihd', weights, value_rows, precision=HIGHEST)

def to_heads(values, clip_total):
    return values.reshape(clip_total, L, HEADS, HD)

def group_forward(params, inputs, targets, valid, clip_lengths, valid_total):
    ln1_gain, ln1_bias, w_qkv, q_bias, v_bias, w_proj, proj_bias, ln2_gain, ln2_bias, w_fc1, fc1_bias, w_fc2, fc2_bias = params
    row_total = inputs.shape[0]
    clip_total = row_total // L
    norm_one = low(layer_norm(inputs, ln1_gain, ln1_bias))
    projected = jnp.dot(norm_one, w_qkv.reshape(D, 3 * D), precision=HIGHEST).reshape(row_total, 3, D)
    queries = low(low_back(projected[:, 0] + q_bias))
    key_rows = low(low_back(projected[:, 1]))
    value_rows = low(low_back(projected[:, 2] + v_bias))
    attended = lax.map(jax.checkpoint(attention_clip), (to_heads(queries, clip_total), to_heads(key_rows, clip_total), to_heads(value_rows, clip_total), clip_lengths))
    attended = low(low_back(attended.reshape(row_total, D)))
    middle = inputs + low_back(jnp.dot(attended, w_proj, precision=HIGHEST) + proj_bias)
    norm_two = low(layer_norm(middle, ln2_gain, ln2_bias))
    hidden_pre = low_back(jnp.dot(norm_two, w_fc1, precision=HIGHEST) + fc1_bias)
    hidden = low(jax.nn.gelu(hidden_pre, approximate=False))
    outputs = middle + low_back(jnp.dot(hidden, w_fc2, precision=HIGHEST) + fc2_bias)
    differ = outputs - targets
    return (jnp.sum(valid[:, None] * differ * differ) / (valid_total * D), outputs)

def reference(states, ln1_gain, ln1_bias, w_qkv, q_bias, v_bias, w_proj, proj_bias, ln2_gain, ln2_bias, w_fc1, fc1_bias, w_fc2, fc2_bias, teacher, loss_mask, lengths):
    params = (ln1_gain.astype(jnp.float32), ln1_bias.astype(jnp.float32), w_qkv.astype(jnp.float32), q_bias.astype(jnp.float32), v_bias.astype(jnp.float32), w_proj.astype(jnp.float32), proj_bias.astype(jnp.float32), ln2_gain.astype(jnp.float32), ln2_bias.astype(jnp.float32), w_fc1.astype(jnp.float32), fc1_bias.astype(jnp.float32), w_fc2.astype(jnp.float32), fc2_bias.astype(jnp.float32))
    all_clips = lengths.shape[0]
    valid = (loss_mask.reshape(all_clips, L) * (jnp.arange(L)[None, :] < lengths[:, None])).astype(jnp.float32)
    valid_total = jnp.maximum(jnp.sum(valid), 1.0)
    groups = all_clips // CLIPS
    per_group = CLIPS * L
    inputs = states.astype(jnp.float32).reshape(groups, per_group, D)
    targets = teacher.astype(jnp.float32).reshape(groups, per_group, D)
    valid_groups = valid.reshape(groups, per_group)
    length_groups = lengths.reshape(groups, CLIPS)
    loss_scale = TOKENS * D / 2.0

    def step(carry, element):
        grad_sums, loss_sum = carry
        block_inputs, block_targets, block_valid, block_lengths = element

        def loss_of(params_now, inputs_now):
            return group_forward(params_now, inputs_now, block_targets, block_valid, block_lengths, valid_total)
        part, backward, outputs = jax.vjp(loss_of, params, block_inputs, has_aux=True)
        grad_params, grad_inputs = backward(loss_scale * jnp.ones_like(part))
        grad_sums = jax.tree.map(jnp.add, grad_sums, grad_params)
        return ((grad_sums, loss_sum + part), (outputs.astype(jnp.bfloat16), grad_inputs.astype(jnp.bfloat16)))
    zeros = jax.tree.map(jnp.zeros_like, params)
    (grads, loss_value), (outputs, grad_inputs) = lax.scan(step, (zeros, jnp.zeros((), jnp.float32)), (inputs, targets, valid_groups, length_groups))
    return (outputs.reshape(TOKENS, D), loss_value, grad_inputs.reshape(TOKENS, D), grads[0], grads[1], grads[2], grads[3], grads[4], grads[5], grads[6], grads[7], grads[8], grads[9], grads[10], grads[11], grads[12])
```

```python
import jax
import jax.numpy as jnp
from jax import lax
from jax.experimental import pallas as pl
from jax.experimental.pallas import tpu as pltpu
from jax.sharding import PartitionSpec as P

HD = 64
L = 1568


EPSILON = 1e-06
MASKED = -1e30
ROOT_HALF = 0.7071067811865476
DENSITY_FACTOR = 0.3989422804014327


def normalize(values, factor, offset):
    centered = values - jnp.mean(values, axis=-1, keepdims=True)
    spread = lax.rsqrt(jnp.mean(centered * centered, axis=-1, keepdims=True) + EPSILON)
    normal = centered * spread
    return (normal * factor + offset, normal, spread)


def norm_back(upstream, normal, spread, factor):
    inner = upstream * factor
    center_term = jnp.mean(inner, axis=-1, keepdims=True)
    slope_term = jnp.mean(inner * normal, axis=-1, keepdims=True)
    back = spread * (inner - center_term - normal * slope_term)
    return (back, jnp.sum(upstream * normal, axis=0), jnp.sum(upstream, axis=0))


def gelu_value(values):
    return values * (0.5 * (1.0 + lax.erf(values * ROOT_HALF)))


def gelu_slope(values):
    normal_cdf = 0.5 * (1.0 + lax.erf(values * ROOT_HALF))
    return normal_cdf + values * jnp.exp(-0.5 * values * values) * DENSITY_FACTOR


def masked_scores(queries, key_rows, length, score_scale):
    logits = (
        jnp.einsum("ihd,jhd->hij", queries, key_rows, preferred_element_type=jnp.float32)
        * score_scale
    )
    keep = jnp.arange(key_rows.shape[0]) < length
    return jnp.where(keep[None, None, :], logits, MASKED)


def attend_clip(packed, length, score_scale):
    half_span = packed.shape[0] // 2
    key_rows = packed[:, 1]
    value_rows = packed[:, 2]
    pieces = []
    totals = []
    for block_index in range(2):
        queries = packed[block_index * half_span : (block_index + 1) * half_span, 0]
        logits = masked_scores(queries, key_rows, length, score_scale)
        peak = jnp.max(logits, axis=-1, keepdims=True)
        total = peak + jnp.log(jnp.sum(jnp.exp(logits - peak), axis=-1, keepdims=True))
        weights = jnp.exp(logits - total).astype(jnp.bfloat16)
        pieces.append(
            jnp.einsum("hij,jhd->ihd", weights, value_rows, preferred_element_type=jnp.float32)
        )
        totals.append(total[..., 0])
    return (jnp.concatenate(pieces, 0), jnp.concatenate(totals, 1))


def attend_clip_back(packed, length, totals, upstream, score_scale):
    half_span = packed.shape[0] // 2
    key_rows = packed[:, 1]
    value_rows = packed[:, 2]
    grad_keys = jnp.zeros(key_rows.shape, jnp.float32)
    grad_values = jnp.zeros(value_rows.shape, jnp.float32)
    grad_queries = []
    for block_index in range(2):
        first = block_index * half_span
        queries = packed[first : first + half_span, 0]
        logits = masked_scores(queries, key_rows, length, score_scale)
        probs = jnp.exp(logits - totals[:, first : first + half_span][..., None])
        incoming = upstream[first : first + half_span]
        grad_values = grad_values + jnp.einsum(
            "hij,ihd->jhd", probs.astype(jnp.bfloat16), incoming, preferred_element_type=jnp.float32
        )
        grad_probs = jnp.einsum(
            "ihd,jhd->hij", incoming, value_rows, preferred_element_type=jnp.float32
        )
        grad_logits = (
            probs * (grad_probs - jnp.sum(probs * grad_probs, axis=-1, keepdims=True))
        ).astype(jnp.bfloat16)
        grad_queries.append(
            jnp.einsum("hij,jhd->ihd", grad_logits, key_rows, preferred_element_type=jnp.float32)
            * score_scale
        )
        grad_keys = (
            grad_keys
            + jnp.einsum("hij,ihd->jhd", grad_logits, queries, preferred_element_type=jnp.float32)
            * score_scale
        )
    return jnp.stack([jnp.concatenate(grad_queries, 0), grad_keys, grad_values], axis=1)


def local_general(
    states,
    ln1_gain,
    ln1_bias,
    w_qkv,
    q_bias,
    v_bias,
    w_proj,
    proj_bias,
    ln2_gain,
    ln2_bias,
    w_fc1,
    fc1_bias,
    w_fc2,
    fc2_bias,
    teacher,
    loss_mask,
    lengths,
):
    row_count = lax.axis_size("row")
    col_count = lax.axis_size("col")
    col_index = lax.axis_index("col")
    group_index = lax.axis_index("dp") * row_count + lax.axis_index("row")
    local_rows = states.shape[0]
    width = states.shape[1]
    group_rows = local_rows * col_count
    clip_count = group_rows // L
    head_width = w_qkv.shape[2]
    heads_here = head_width // HD
    hidden_width = w_fc1.shape[1]
    score_scale = HD ** (-0.5)
    vectors = jnp.stack([ln1_gain, ln1_bias, proj_bias, ln2_gain, ln2_bias, fc2_bias])
    qkv_full, proj_full, fc1_full, fc2_full, vector_full = (
        lax.all_gather(w_qkv, "row", axis=0, tiled=True),
        lax.all_gather(w_proj, "row", axis=1, tiled=True),
        lax.all_gather(w_fc1, "row", axis=0, tiled=True),
        lax.all_gather(w_fc2, "row", axis=1, tiled=True),
        lax.all_gather(vectors, "row", axis=1, tiled=True),
    )
    vector_full = vector_full.astype(jnp.float32)
    gain_one = vector_full[0]
    shift_one = vector_full[1]
    bias_proj = vector_full[2]
    gain_two = vector_full[3]
    shift_two = vector_full[4]
    bias_two = vector_full[5]
    all_clips = lengths.shape[0]
    valid_all = (
        loss_mask.reshape(all_clips, L) * (jnp.arange(L)[None, :] < lengths[:, None])
    ).astype(jnp.float32)
    valid_total = jnp.maximum(jnp.sum(valid_all), 1.0)
    first_row = (group_index * col_count + col_index) * local_rows
    valid = lax.dynamic_slice_in_dim(valid_all.reshape(all_clips * L), first_row, local_rows)
    my_lengths = lax.dynamic_slice_in_dim(lengths, group_index * clip_count, clip_count)
    inputs = states.astype(jnp.float32)
    norm_one, unit_one, spread_one = normalize(inputs, gain_one, shift_one)
    norm_one = norm_one.astype(jnp.bfloat16)
    tokens_one = lax.all_gather(norm_one, "col", axis=0, tiled=True)
    qkv_matrix = qkv_full.reshape(width, 3 * head_width)
    projected = jnp.dot(tokens_one, qkv_matrix, preferred_element_type=jnp.float32).reshape(
        group_rows, 3, head_width
    )
    bias_rows = jnp.stack(
        [
            q_bias.astype(jnp.float32),
            jnp.zeros((head_width,), jnp.float32),
            v_bias.astype(jnp.float32),
        ]
    )
    packed = (projected + bias_rows[None]).astype(jnp.bfloat16)
    clips_packed = packed.reshape(clip_count, L, 3, heads_here, HD)
    attended, totals = lax.map(
        lambda element: attend_clip(element[0], element[1], score_scale), (clips_packed, my_lengths)
    )
    attended = attended.reshape(group_rows, head_width).astype(jnp.bfloat16)
    proj_whole, qkv_whole = (
        lax.all_gather(proj_full, "col", axis=0, tiled=True),
        lax.all_gather(qkv_full, "col", axis=2, tiled=True),
    )
    attended_rows = lax.all_to_all(attended, "col", split_axis=0, concat_axis=1, tiled=True)
    middle = inputs + (
        jnp.dot(attended_rows, proj_whole, preferred_element_type=jnp.float32) + bias_proj
    )
    norm_two, unit_two, spread_two = normalize(middle, gain_two, shift_two)
    norm_two = norm_two.astype(jnp.bfloat16)
    fc1_whole, fc2_whole, fc1_bias_whole = (
        lax.all_gather(fc1_full, "col", axis=1, tiled=True),
        lax.all_gather(fc2_full, "col", axis=0, tiled=True),
        lax.all_gather(fc1_bias, "col", axis=0, tiled=True),
    )
    hidden_pre = jnp.dot(
        norm_two, fc1_whole, preferred_element_type=jnp.float32
    ) + fc1_bias_whole.astype(jnp.float32)
    hidden = gelu_value(hidden_pre).astype(jnp.bfloat16)
    outputs = middle + (jnp.dot(hidden, fc2_whole, preferred_element_type=jnp.float32) + bias_two)
    differ = outputs - teacher.astype(jnp.float32)
    numerator = jnp.sum(valid[:, None] * differ * differ)
    loss_scale = all_clips * L * width / 2.0
    grad_out = loss_scale * 2.0 / (valid_total * width) * valid[:, None] * differ
    grad_low = grad_out.astype(jnp.bfloat16)
    grad_hidden = jnp.dot(grad_low, fc2_whole.T, preferred_element_type=jnp.float32)
    grad_pre = (grad_hidden * gelu_slope(hidden_pre)).astype(jnp.bfloat16)
    wide_fc2 = jnp.dot(hidden.T, grad_low, preferred_element_type=jnp.float32)
    wide_fc1 = jnp.dot(norm_two.T, grad_pre, preferred_element_type=jnp.float32)
    fc1_grad_part, fc2_grad_part = (
        lax.psum_scatter(
            wide_fc1.astype(jnp.bfloat16), "col", scatter_dimension=1, tiled=True
        ).astype(jnp.float32),
        lax.psum_scatter(
            wide_fc2.astype(jnp.bfloat16), "col", scatter_dimension=0, tiled=True
        ).astype(jnp.float32),
    )
    fc1_bias_sum = jnp.sum(grad_pre, axis=0, dtype=jnp.float32)
    grad_norm_two = jnp.dot(grad_pre, fc1_whole.T, preferred_element_type=jnp.float32)
    back_two, gain_two_grad, shift_two_grad = norm_back(
        grad_norm_two, unit_two, spread_two, gain_two
    )
    grad_mid = grad_out + back_two
    mid_low = grad_mid.astype(jnp.bfloat16)
    wide_proj = jnp.dot(attended_rows.T, mid_low, preferred_element_type=jnp.float32)
    proj_grad_part = lax.psum_scatter(
        wide_proj.astype(jnp.bfloat16), "col", scatter_dimension=0, tiled=True
    )
    grad_attended_rows = jnp.dot(mid_low, proj_whole.T, preferred_element_type=jnp.float32).astype(
        jnp.bfloat16
    )
    grad_attended = lax.all_to_all(
        grad_attended_rows, "col", split_axis=1, concat_axis=0, tiled=True
    )
    grads_packed = lax.map(
        lambda element: attend_clip_back(
            element[0], element[1], element[2], element[3], score_scale
        ),
        (clips_packed, my_lengths, totals, grad_attended.reshape(clip_count, L, heads_here, HD)),
    )
    grads_packed = grads_packed.reshape(group_rows, 3 * head_width).astype(jnp.bfloat16)
    qkv_grad_part = jnp.dot(tokens_one.T, grads_packed, preferred_element_type=jnp.float32).reshape(
        width, 3, head_width
    )
    bias_sums = jnp.sum(grads_packed.reshape(group_rows, 3, head_width), axis=0, dtype=jnp.float32)
    grads_rows = lax.all_to_all(
        grads_packed.reshape(group_rows, 3, head_width),
        "col",
        split_axis=0,
        concat_axis=2,
        tiled=True,
    )
    grad_norm_one = jnp.dot(
        grads_rows.reshape(local_rows, 3 * width),
        qkv_whole.reshape(width, 3 * width).T,
        preferred_element_type=jnp.float32,
    )
    back_one, gain_one_grad, shift_one_grad = norm_back(
        grad_norm_one, unit_one, spread_one, gain_one
    )
    grad_states = (grad_mid + back_one).astype(jnp.bfloat16)
    proj_bias_grad = jnp.sum(mid_low, axis=0, dtype=jnp.float32)
    fc2_bias_grad = jnp.sum(grad_low, axis=0, dtype=jnp.float32)
    token_vectors = jnp.stack(
        [
            gain_one_grad,
            shift_one_grad,
            proj_bias_grad,
            gain_two_grad,
            shift_two_grad,
            fc2_bias_grad,
        ]
    )
    head_vectors = lax.dynamic_update_slice(
        jnp.zeros((2, width), jnp.float32),
        jnp.stack([bias_sums[0], bias_sums[2]]),
        (0, col_index * head_width),
    )
    token_sums, head_sums, fc1_sums, loss_sum = lax.psum(
        (token_vectors, head_vectors, fc1_bias_sum, numerator), ("dp", "row", "col")
    )
    qkv_rows, proj_cols, fc1_rows, fc2_cols = (
        lax.psum_scatter(
            qkv_grad_part.astype(jnp.bfloat16), "row", scatter_dimension=0, tiled=True
        ).astype(jnp.float32),
        lax.psum_scatter(proj_grad_part, "row", scatter_dimension=1, tiled=True).astype(
            jnp.float32
        ),
        lax.psum_scatter(
            fc1_grad_part.astype(jnp.bfloat16), "row", scatter_dimension=0, tiled=True
        ).astype(jnp.float32),
        lax.psum_scatter(
            fc2_grad_part.astype(jnp.bfloat16), "row", scatter_dimension=1, tiled=True
        ).astype(jnp.float32),
    )
    qkv_grad, proj_grad, fc1_grad, fc2_grad = (
        lax.psum(qkv_rows.astype(jnp.bfloat16), "dp").astype(jnp.float32),
        lax.psum(proj_cols.astype(jnp.bfloat16), "dp").astype(jnp.float32),
        lax.psum(fc1_rows.astype(jnp.bfloat16), "dp").astype(jnp.float32),
        lax.psum(fc2_cols.astype(jnp.bfloat16), "dp").astype(jnp.float32),
    )
    half_width = width // row_count
    token_part = lax.dynamic_slice_in_dim(
        token_sums, lax.axis_index("row") * half_width, half_width, 1
    )
    head_part = lax.dynamic_slice_in_dim(head_sums, col_index * head_width, head_width, 1)
    fc1_part = lax.dynamic_slice_in_dim(fc1_sums, col_index * hidden_width, hidden_width, 0)
    loss_value = loss_sum / (valid_total * width)
    return (
        outputs.astype(jnp.bfloat16),
        loss_value,
        grad_states,
        token_part[0],
        token_part[1],
        qkv_grad,
        head_part[0],
        head_part[1],
        proj_grad,
        token_part[2],
        token_part[3],
        token_part[4],
        fc1_grad,
        fc1_part,
        fc2_grad,
        token_part[5],
    )


PAIRED_MESH = (4, 2, 4)
GROUP = 4
QT = 128


def dot_nn(a, b):
    return lax.dot_general(a, b, (((1,), (0,)), ((), ())), preferred_element_type=jnp.float32)


def dot_nt(a, b):
    return lax.dot_general(a, b, (((1,), (1,)), ((), ())), preferred_element_type=jnp.float32)


def dot_tn(a, b):
    return lax.dot_general(a, b, (((0,), (0,)), ((), ())), preferred_element_type=jnp.float32)


def head_stack(values, zero):
    lane_head = lax.broadcasted_iota(jnp.int32, values.shape, 1) // HD
    return jnp.concatenate([jnp.where(lane_head == h, values, zero) for h in range(GROUP)], axis=0)


def head_unstack(wide, count):
    return jnp.concatenate(
        [wide[h * HD : (h + 1) * HD, h * count : (h + 1) * count] for h in range(GROUP)], axis=0
    ).T


def attend_kernel(packed_ref, bias_ref, out_ref, lse_ref, vt_ref):
    width = GROUP * HD
    tokens = packed_ref.shape[0]
    vt_ref[...] = packed_ref[:, 2 * width : 3 * width].T

    def tile(start, count, index):
        stacked = head_stack(packed_ref[pl.ds(start, count), 0:width], jnp.zeros((), jnp.bfloat16))
        keys = packed_ref[:, width : 2 * width]
        bias = bias_ref[...]
        scores = dot_nt(keys, stacked) + jnp.concatenate([bias] * (GROUP * count // 128), axis=1)
        peak = jnp.max(scores, axis=0, keepdims=True)
        weights = jnp.exp(scores - peak)
        total = jnp.sum(weights, axis=0, keepdims=True)
        wide = dot_nn(vt_ref[...], weights.astype(jnp.bfloat16)) * (1.0 / total)
        out_ref[pl.ds(start, count), :] = head_unstack(wide, count).astype(jnp.bfloat16)
        lse_ref[index, :, 0 : GROUP * count] = jnp.broadcast_to(
            peak + jnp.log(total), (8, GROUP * count)
        )

    full = tokens // QT
    rest = tokens - full * QT

    @pl.loop(0, full)
    def _(index):
        tile(pl.multiple_of(index * QT, QT), QT, index)

    if rest:
        tile(full * QT, rest, full)


def attend_back_kernel(
    packed_ref, bias_ref, lse_ref, att_ref, up_ref, out_ref, kt_ref, dk_ref, dv_ref
):
    width = GROUP * HD
    tokens = packed_ref.shape[0]
    kt_ref[...] = packed_ref[:, width : 2 * width].T
    dk_ref[...] = jnp.zeros_like(dk_ref)
    dv_ref[...] = jnp.zeros_like(dv_ref)

    def tile(start, count, index):
        cols = GROUP * count
        zero = jnp.zeros((), jnp.bfloat16)
        up = up_ref[pl.ds(start, count), :]
        stacked = head_stack(packed_ref[pl.ds(start, count), 0:width], zero)
        up_stacked = head_stack(up, zero)
        product = head_stack(
            up.astype(jnp.float32) * att_ref[pl.ds(start, count), :].astype(jnp.float32),
            jnp.zeros((), jnp.float32),
        )
        high = product.astype(jnp.bfloat16)
        low = (product - high.astype(jnp.float32)).astype(jnp.bfloat16)
        ones = jnp.ones((8, width), jnp.bfloat16)
        delta = (dot_nt(ones, high) + dot_nt(ones, low))[0:1]
        keys = packed_ref[:, width : 2 * width]
        values = packed_ref[:, 2 * width : 3 * width]
        bias = bias_ref[...]
        scores = dot_nt(keys, stacked) + jnp.concatenate([bias] * (cols // 128), axis=1)
        weights = jnp.exp(scores - lse_ref[index, 0:1, 0:cols])
        dv_ref[...] += dot_nn(weights.astype(jnp.bfloat16), up_stacked)
        grad = (weights * (dot_nt(values, up_stacked) - delta)).astype(jnp.bfloat16)
        dk_ref[...] += dot_nn(grad, stacked)
        wide = dot_nn(kt_ref[...], grad) * (HD**-0.5)
        out_ref[pl.ds(start, count), 0:width] = head_unstack(wide, count).astype(jnp.bfloat16)

    full = tokens // QT
    rest = tokens - full * QT

    @pl.loop(0, full)
    def _(index):
        tile(pl.multiple_of(index * QT, QT), QT, index)

    if rest:
        tile(full * QT, rest, full)
    out_ref[:, width : 2 * width] = dk_ref[...].astype(jnp.bfloat16)
    out_ref[:, 2 * width : 3 * width] = dv_ref[...].astype(jnp.bfloat16)


def attend(packed, bias):
    tokens, width = packed.shape[0], GROUP * HD
    tiles = -(-tokens // QT)
    return pl.pallas_call(
        attend_kernel,
        out_shape=(
            jax.ShapeDtypeStruct((tokens, width), jnp.bfloat16),
            jax.ShapeDtypeStruct((tiles, 8, GROUP * QT), jnp.float32),
        ),
        in_specs=[pl.BlockSpec(memory_space=pltpu.VMEM)] * 2,
        out_specs=[pl.BlockSpec(memory_space=pltpu.VMEM)] * 2,
        scratch_shapes=[pltpu.VMEM((width, tokens), jnp.bfloat16)],
        compiler_params=pltpu.CompilerParams(vmem_limit_bytes=48 << 20),
        cost_estimate=pl.CostEstimate(
            flops=4 * tokens * tokens * width * 4, bytes_accessed=8 << 20, transcendentals=0
        ),
        name="attend",
    )(packed, bias)


def attend_back(packed, bias, lse, att, upstream):
    tokens, width = packed.shape[0], GROUP * HD
    return pl.pallas_call(
        attend_back_kernel,
        out_shape=jax.ShapeDtypeStruct((tokens, 3 * width), jnp.bfloat16),
        in_specs=[pl.BlockSpec(memory_space=pltpu.VMEM)] * 5,
        out_specs=pl.BlockSpec(memory_space=pltpu.VMEM),
        scratch_shapes=[
            pltpu.VMEM((width, tokens), jnp.bfloat16),
            pltpu.VMEM((tokens, width), jnp.float32),
            pltpu.VMEM((tokens, width), jnp.float32),
        ],
        compiler_params=pltpu.CompilerParams(vmem_limit_bytes=56 << 20),
        cost_estimate=pl.CostEstimate(
            flops=10 * tokens * tokens * width * 4, bytes_accessed=10 << 20, transcendentals=0
        ),
        name="attend_back",
    )(packed, bias, lse, att, upstream)


def swap(values, axis, mask, size):
    return lax.ppermute(values, axis, [(i, i ^ mask) for i in range(size)])


def over_row(values):
    return swap(values, "row", 1, 2)


def over_dp(values, mask):
    return swap(values, "dp", mask, 4)


def over_col(values, mask):
    return swap(values, "col", mask, 4)


def cut(values, index, size, axis=0):
    return lax.dynamic_slice_in_dim(values, index * size, size, axis)


def place(pieces, index_of, axis):
    size = pieces[0].shape[axis]
    shape = list(pieces[0].shape)
    shape[axis] = size * len(pieces)
    whole = jnp.zeros(shape, pieces[0].dtype)
    for s, piece in enumerate(pieces):
        whole = lax.dynamic_update_slice_in_dim(whole, piece, index_of(s) * size, axis)
    return whole


SUB_ORDER = (0, 2, 1, 3)


def local_paired(
    states,
    ln1_gain,
    ln1_bias,
    w_qkv,
    q_bias,
    v_bias,
    w_proj,
    proj_bias,
    ln2_gain,
    ln2_bias,
    w_fc1,
    fc1_bias,
    w_fc2,
    fc2_bias,
    teacher,
    loss_mask,
    lengths,
):
    f32, bf16 = jnp.float32, jnp.bfloat16
    dp = lax.axis_index("dp")
    row = lax.axis_index("row")
    col = lax.axis_index("col")
    local_rows, width = states.shape
    half = width // 2
    head_width = w_qkv.shape[2]
    hidden_width = w_fc1.shape[1]
    sub = hidden_width // 4
    group_index = dp * 2 + row
    clip = group_index * 2 + col // 2
    second = col % 2

    def quarter(s):
        return dp ^ s

    def frame(values):
        return jnp.where(
            row == 0, values, jnp.concatenate([values[:, half:], values[:, :half]], axis=1)
        )

    w_qkv2 = w_qkv.reshape(half, 3 * head_width)
    vectors = jnp.stack([ln1_gain, ln1_bias, proj_bias, ln2_gain, ln2_bias, fc2_bias])
    vectors_other = over_row(vectors)
    vector_full = jnp.concatenate([vectors, vectors_other], axis=1).astype(f32)
    gain_one, shift_one, bias_proj, gain_two, shift_two, bias_two = (vector_full[i] for i in range(6))

    inputs = frame(states).astype(f32)
    norm_one, unit_one, spread_one = normalize(inputs, gain_one, shift_one)
    norm_one = norm_one.astype(bf16)
    norm_other = over_col(norm_one, 1)

    qkv_other = over_row(w_qkv2)
    qkv_quarter = over_col(cut(w_qkv2, dp, half // 4), 2)
    qkv_pieces = [qkv_quarter] + [over_dp(qkv_quarter, s) for s in (1, 2, 3)]
    qkv_far = place(qkv_pieces, quarter, 0)
    qkv_far_other = over_row(qkv_far)
    qkv_near = jnp.concatenate([w_qkv2, qkv_other], axis=0)
    qkv_far = jnp.concatenate([qkv_far, qkv_far_other], axis=0)

    fc1_own = [cut(w_fc1, quarter(s), sub, 1) for s in range(4)]
    fc2_own = [cut(w_fc2, quarter(s), sub, 0) for s in range(4)]
    proj_cut = cut(w_proj, dp, head_width // 4, 0)
    slab = jnp.concatenate(
        [
            fc1_own[0],
            fc2_own[0][:, :sub],
            fc2_own[0][:, sub:],
            proj_cut[:, :sub],
            proj_cut[:, sub:],
        ],
        axis=0,
    )
    slab_rows = slab.shape[0]
    own = jnp.concatenate(
        [
            jnp.concatenate(fc1_own, axis=0),
            jnp.concatenate([f[:, i * sub : (i + 1) * sub] for f in fc2_own for i in range(2)], axis=0),
            w_proj[:, :sub],
            w_proj[:, sub:],
        ],
        axis=0,
    )
    own_other = over_row(own)
    near, far = [None], [None]
    for j in (1, 2, 3):
        first = over_col(slab, j)
        pieces = jnp.concatenate([first] + [over_dp(first, s) for s in (1, 2, 3)], axis=0)
        near.append(pieces)
        far.append(over_row(pieces))

    quarter_rows = head_width // 4

    def own_parts(block):
        fc1 = [block[s * half : (s + 1) * half] for s in range(4)]
        at = 4 * half
        fc2 = [
            jnp.concatenate(
                [block[at + (2 * s + i) * sub : at + (2 * s + i + 1) * sub] for i in range(2)], axis=1
            )
            for s in range(4)
        ]
        at += 8 * sub
        proj = jnp.concatenate([block[at : at + head_width], block[at + head_width :]], axis=1)
        return fc1, fc2, proj

    def far_parts(block):
        fc1, fc2, proj = [], [], []
        for s in range(4):
            at = s * slab_rows
            fc1.append(block[at : at + half])
            at += half
            fc2.append(jnp.concatenate([block[at : at + sub], block[at + sub : at + 2 * sub]], axis=1))
            at += 2 * sub
            proj.append(
                jnp.concatenate(
                    [block[at : at + quarter_rows], block[at + quarter_rows : at + 2 * quarter_rows]],
                    axis=1,
                )
            )
        return fc1, fc2, place(proj, quarter, 0)

    mine = [own_parts(own)] + [far_parts(near[j]) for j in (1, 2, 3)]
    theirs = [own_parts(own_other)] + [far_parts(far[j]) for j in (1, 2, 3)]
    order = [(s, j) for s in SUB_ORDER for j in range(4)]
    fc1_whole = jnp.concatenate(
        [
            jnp.concatenate([mine[j][0][s] for s, j in order], axis=1),
            jnp.concatenate([theirs[j][0][s] for s, j in order], axis=1),
        ],
        axis=0,
    )
    fc2_whole = jnp.concatenate(
        [
            jnp.concatenate([mine[j][1][s] for s, j in order], axis=0),
            jnp.concatenate([theirs[j][1][s] for s, j in order], axis=0),
        ],
        axis=1,
    )
    proj_whole = jnp.concatenate(
        [
            jnp.concatenate([mine[j][2] for j in range(4)], axis=0),
            jnp.concatenate([theirs[j][2] for j in range(4)], axis=0),
        ],
        axis=1,
    )
    fc1_biases = [fc1_bias] + [over_col(fc1_bias, j) for j in (1, 2, 3)]
    fc1_bias_whole = jnp.concatenate([cut(fc1_biases[j], quarter(s), sub) for s, j in order]).astype(f32)

    all_clips = lengths.shape[0]
    valid_all = (
        loss_mask.reshape(all_clips, L) * (jnp.arange(L)[None, :] < lengths[:, None])
    ).astype(f32)
    valid_total = jnp.maximum(jnp.sum(valid_all), 1.0)
    first_row = (group_index * 4 + col) * local_rows
    valid = lax.dynamic_slice_in_dim(valid_all.reshape(all_clips * L), first_row, local_rows)
    my_length = lax.dynamic_slice_in_dim(lengths, clip, 1)
    spot = jnp.arange(L)
    position = jnp.where(
        spot < local_rows, second * local_rows + spot, (1 - second) * local_rows + spot - local_rows
    )
    key_bias = jnp.where(position < my_length, 0.0, MASKED).astype(f32)
    key_bias = jnp.broadcast_to(key_bias[:, None], (L, 128))

    tokens_one = jnp.concatenate([norm_one, norm_other], axis=0)
    zero_bias = jnp.zeros((head_width,), f32)
    score_scale = HD**-0.5
    packs, atts, lses, att_others = [], [], [], []
    biases = [(q_bias, v_bias), tuple(over_col(jnp.stack([q_bias, v_bias]), 2))]
    for matrix, (q_add, v_add) in zip((qkv_near, qkv_far), biases, strict=True):
        projected = jnp.dot(tokens_one, matrix, preferred_element_type=f32)
        packed = (
            projected + jnp.concatenate([q_add.astype(f32), zero_bias, v_add.astype(f32)])[None]
        ).astype(bf16)
        scale = jnp.where(jnp.arange(3 * head_width) < head_width, score_scale, 1.0).astype(bf16)
        packed = packed * scale[None]
        att, lse = attend(packed, key_bias)
        packs.append(packed)
        atts.append(att)
        lses.append(lse)
        att_others.append(over_col(att[local_rows:], 1))
    attended_rows = jnp.concatenate(
        [atts[0][:local_rows], att_others[0], atts[1][:local_rows], att_others[1]], axis=1
    )
    middle = inputs + (jnp.dot(attended_rows, proj_whole, preferred_element_type=f32) + bias_proj)
    norm_two, unit_two, spread_two = normalize(middle, gain_two, shift_two)
    norm_two = norm_two.astype(bf16)
    hidden_pre = jnp.dot(norm_two, fc1_whole, preferred_element_type=f32) + fc1_bias_whole
    hidden = gelu_value(hidden_pre).astype(bf16)
    outputs = middle + (jnp.dot(hidden, fc2_whole, preferred_element_type=f32) + bias_two)
    differ = outputs - frame(teacher).astype(f32)
    numerator = jnp.sum(valid[:, None] * differ * differ)
    loss_scale = all_clips * L * width / 2.0
    grad_out = loss_scale * 2.0 / (valid_total * width) * valid[:, None] * differ
    grad_low = grad_out.astype(bf16)

    def both_halves(left, right, split_left):
        if split_left:
            given = dot_tn(left[:, half:], right)
            kept = dot_tn(left[:, :half], right)
        else:
            given = dot_tn(left, right[:, half:])
            kept = dot_tn(left, right[:, :half])
        taken = over_row(given.astype(bf16))
        return (kept + taken.astype(f32)).astype(bf16)

    wide_fc2 = both_halves(hidden, grad_low, False)
    grad_hidden = jnp.dot(grad_low, fc2_whole.T, preferred_element_type=f32)
    grad_pre = (grad_hidden * gelu_slope(hidden_pre)).astype(bf16)
    fc1_bias_sum = jnp.sum(grad_pre, axis=0, dtype=f32)
    grad_norm_two = jnp.dot(grad_pre, fc1_whole.T, preferred_element_type=f32)
    back_two, gain_two_grad, shift_two_grad = norm_back(grad_norm_two, unit_two, spread_two, gain_two)
    grad_mid = grad_out + back_two
    mid_low = grad_mid.astype(bf16)
    grad_att_rows = jnp.dot(mid_low, proj_whole.T, preferred_element_type=f32).astype(bf16)
    ups = []
    for b in range(2):
        at = 2 * b * head_width
        ups.append(
            jnp.concatenate(
                [
                    grad_att_rows[:, at : at + head_width],
                    over_col(grad_att_rows[:, at + head_width : at + 2 * head_width], 1),
                ],
                axis=0,
            )
        )
    wide_fc1 = both_halves(norm_two, grad_pre, True)
    wide_proj = both_halves(attended_rows, mid_low, False)

    span = 4 * sub

    def fc1_part(s):
        at = SUB_ORDER.index(s) * span
        return wide_fc1[:, at : at + span]

    def fc2_part(s):
        at = SUB_ORDER.index(s) * span
        return wide_fc2[at : at + span]

    def proj_part(s):
        return jnp.concatenate(
            [
                cut(wide_proj[j * head_width : (j + 1) * head_width], quarter(s), quarter_rows)
                for j in range(4)
            ],
            axis=0,
        )

    def gather_sum(own_part, taken):
        total = own_part.astype(f32)
        for piece in taken:
            total = total + piece.astype(f32)
        return total.astype(bf16)

    def reduce_parts(part, block, axis):
        plane = gather_sum(part(0), [over_dp(part(s), s) for s in (1, 2, 3)])
        cuts = [lax.slice_in_dim(plane, j * block, (j + 1) * block, axis=axis) for j in range(4)]
        mine_sum = gather_sum(cuts[0], [over_col(cuts[j], j) for j in (1, 2, 3)])
        pieces = [mine_sum] + [over_dp(mine_sum, s) for s in (1, 2, 3)]
        return place(pieces, quarter, axis).astype(f32)

    fc2_grad = reduce_parts(fc2_part, sub, 0)
    fc1_grad = reduce_parts(fc1_part, sub, 1)
    proj_grad = reduce_parts(proj_part, quarter_rows, 0)

    grads, wide_qkv, grad_norm_one = [], [], None
    for b, matrix in enumerate((qkv_near, qkv_far)):
        grad = attend_back(packs[b], key_bias, lses[b], atts[b], ups[b])
        grads.append(grad)
        wide_qkv.append(both_halves(tokens_one, grad, True))
        part = dot_nt(grad, matrix)
        grad_norm_one = part if grad_norm_one is None else grad_norm_one + part
    norm_taken = over_col(grad_norm_one[local_rows:].astype(bf16), 1)
    grad_norm_one = grad_norm_one[:local_rows] + norm_taken.astype(f32)
    back_one, gain_one_grad, shift_one_grad = norm_back(grad_norm_one, unit_one, spread_one, gain_one)
    grad_states = frame((grad_mid + back_one).astype(bf16))

    qkv_sum = gather_sum(wide_qkv[0], [over_col(wide_qkv[1], 2)])
    quarter_deep = half // 4
    qkv_parts = gather_sum(
        cut(qkv_sum, dp, quarter_deep),
        [over_dp(cut(qkv_sum, quarter(s), quarter_deep), s) for s in (1, 2, 3)],
    )
    qkv_grad = place([qkv_parts] + [over_dp(qkv_parts, s) for s in (1, 2, 3)], quarter, 0)
    qkv_grad = qkv_grad.astype(f32).reshape(half, 3, head_width)

    def row_half(stacked):
        return stacked[:, :half] + over_row(stacked[:, half:])

    early = jnp.stack(
        [
            gain_two_grad,
            shift_two_grad,
            jnp.sum(mid_low, axis=0, dtype=f32),
            jnp.sum(grad_low, axis=0, dtype=f32),
        ]
    )
    early = jnp.concatenate([row_half(early).reshape(-1), jnp.zeros((128,), f32).at[0].set(0.0)])
    tail_mask = jnp.arange(early.shape[0]) == early.shape[0] - 128
    numerator = numerator + over_row(numerator.reshape(1))[0]
    early = jnp.where(tail_mask, numerator, early)
    bias_sum = fc1_bias_sum + over_row(fc1_bias_sum)
    bias_parts = [bias_sum[SUB_ORDER.index(s) * span : (SUB_ORDER.index(s) + 1) * span] for s in range(4)]
    joined = jnp.concatenate([early, bias_parts[0]])
    for s in (1, 2, 3):
        joined = joined + over_dp(jnp.concatenate([early, bias_parts[s]]), s)
    early, bias_sum = joined[: early.shape[0]], joined[early.shape[0] :]
    joined = jnp.concatenate([early, bias_sum[:sub]])
    for j in (1, 2, 3):
        joined = joined + over_col(jnp.concatenate([early, bias_sum[j * sub : (j + 1) * sub]]), j)
    early, bias_sum = joined[: early.shape[0]], joined[early.shape[0] :]
    fc1_bias_grad = place([bias_sum] + [over_dp(bias_sum, s) for s in (1, 2, 3)], quarter, 0)
    loss_sum = early[early.shape[0] - 128]
    early = early[: early.shape[0] - 128].reshape(4, half)

    late = row_half(jnp.stack([gain_one_grad, shift_one_grad])).reshape(-1)
    head_sums = [
        jnp.concatenate([jnp.sum(g[:, i : i + head_width], axis=0, dtype=f32) for i in (0, 2 * head_width)])
        for g in grads
    ]
    heads = jnp.concatenate(head_sums)
    heads = heads + over_row(heads)
    late = jnp.concatenate([late, heads])
    late = late + over_dp(late, 1)
    late = late + over_dp(late, 2)
    cut_at = 2 * half
    late_heads = late[cut_at : cut_at + 2 * head_width] + over_col(late[cut_at + 2 * head_width :], 2)
    late = late[:cut_at]
    late = late + over_col(late, 1)
    late = late + over_col(late, 2)
    late = late.reshape(2, half)

    loss_value = loss_sum / (valid_total * width)
    return (
        frame(outputs.astype(bf16)),
        loss_value,
        grad_states,
        late[0],
        late[1],
        qkv_grad,
        late_heads[:head_width],
        late_heads[head_width:],
        proj_grad,
        early[2],
        early[0],
        early[1],
        fc1_grad,
        fc1_bias_grad,
        fc2_grad,
        early[3],
    )


def solution(mesh):
    sizes = (mesh.shape["dp"], mesh.shape["row"], mesh.shape["col"])
    body = local_paired if sizes == PAIRED_MESH else local_general
    in_specs = (
        P(("dp", "row", "col"), None),
        P("row"),
        P("row"),
        P("row", None, "col"),
        P("col"),
        P("col"),
        P("col", "row"),
        P("row"),
        P("row"),
        P("row"),
        P("row", "col"),
        P("col"),
        P("col", "row"),
        P("row"),
        P(("dp", "row", "col"), None),
        P(),
        P(),
    )
    out_specs = (
        P(("dp", "row", "col"), None),
        P(),
        P(("dp", "row", "col"), None),
        P("row"),
        P("row"),
        P("row", None, "col"),
        P("col"),
        P("col"),
        P("col", "row"),
        P("row"),
        P("row"),
        P("row"),
        P("row", "col"),
        P("col"),
        P("col", "row"),
        P("row"),
    )
    return jax.shard_map(body, mesh=mesh, in_specs=in_specs, out_specs=out_specs, check_vma=False)
```

```python
import functools

import jax
import jax.numpy as jnp
from jax import lax
from jax.experimental import pallas as pl
from jax.experimental.pallas import tpu as pltpu
from jax.sharding import PartitionSpec as P

HD = 64
L = 1568


EPSILON = 1e-06
MASKED = -1e30
ROOT_HALF = 0.7071067811865476
DENSITY_FACTOR = 0.3989422804014327


def normalize(values, factor, offset):
    centered = values - jnp.mean(values, axis=-1, keepdims=True)
    spread = lax.rsqrt(jnp.mean(centered * centered, axis=-1, keepdims=True) + EPSILON)
    normal = centered * spread
    return (normal * factor + offset, normal, spread)


def norm_back(upstream, normal, spread, factor):
    inner = upstream * factor
    center_term = jnp.mean(inner, axis=-1, keepdims=True)
    slope_term = jnp.mean(inner * normal, axis=-1, keepdims=True)
    back = spread * (inner - center_term - normal * slope_term)
    return (back, jnp.sum(upstream * normal, axis=0), jnp.sum(upstream, axis=0))


def gelu_value(values):
    return values * (0.5 * (1.0 + lax.erf(values * ROOT_HALF)))


def gelu_slope(values):
    normal_cdf = 0.5 * (1.0 + lax.erf(values * ROOT_HALF))
    return normal_cdf + values * jnp.exp(-0.5 * values * values) * DENSITY_FACTOR


def masked_scores(queries, key_rows, length, score_scale):
    logits = (
        jnp.einsum("ihd,jhd->hij", queries, key_rows, preferred_element_type=jnp.float32)
        * score_scale
    )
    keep = jnp.arange(key_rows.shape[0]) < length
    return jnp.where(keep[None, None, :], logits, MASKED)


def attend_clip(packed, length, score_scale):
    half_span = packed.shape[0] // 2
    key_rows = packed[:, 1]
    value_rows = packed[:, 2]
    pieces = []
    totals = []
    for block_index in range(2):
        queries = packed[block_index * half_span : (block_index + 1) * half_span, 0]
        logits = masked_scores(queries, key_rows, length, score_scale)
        peak = jnp.max(logits, axis=-1, keepdims=True)
        total = peak + jnp.log(jnp.sum(jnp.exp(logits - peak), axis=-1, keepdims=True))
        weights = jnp.exp(logits - total).astype(jnp.bfloat16)
        pieces.append(
            jnp.einsum("hij,jhd->ihd", weights, value_rows, preferred_element_type=jnp.float32)
        )
        totals.append(total[..., 0])
    return (jnp.concatenate(pieces, 0), jnp.concatenate(totals, 1))


def attend_clip_back(packed, length, totals, upstream, score_scale):
    half_span = packed.shape[0] // 2
    key_rows = packed[:, 1]
    value_rows = packed[:, 2]
    grad_keys = jnp.zeros(key_rows.shape, jnp.float32)
    grad_values = jnp.zeros(value_rows.shape, jnp.float32)
    grad_queries = []
    for block_index in range(2):
        first = block_index * half_span
        queries = packed[first : first + half_span, 0]
        logits = masked_scores(queries, key_rows, length, score_scale)
        probs = jnp.exp(logits - totals[:, first : first + half_span][..., None])
        incoming = upstream[first : first + half_span]
        grad_values = grad_values + jnp.einsum(
            "hij,ihd->jhd", probs.astype(jnp.bfloat16), incoming, preferred_element_type=jnp.float32
        )
        grad_probs = jnp.einsum(
            "ihd,jhd->hij", incoming, value_rows, preferred_element_type=jnp.float32
        )
        grad_logits = (
            probs * (grad_probs - jnp.sum(probs * grad_probs, axis=-1, keepdims=True))
        ).astype(jnp.bfloat16)
        grad_queries.append(
            jnp.einsum("hij,jhd->ihd", grad_logits, key_rows, preferred_element_type=jnp.float32)
            * score_scale
        )
        grad_keys = (
            grad_keys
            + jnp.einsum("hij,ihd->jhd", grad_logits, queries, preferred_element_type=jnp.float32)
            * score_scale
        )
    return jnp.stack([jnp.concatenate(grad_queries, 0), grad_keys, grad_values], axis=1)


def local_general(
    states,
    ln1_gain,
    ln1_bias,
    w_qkv,
    q_bias,
    v_bias,
    w_proj,
    proj_bias,
    ln2_gain,
    ln2_bias,
    w_fc1,
    fc1_bias,
    w_fc2,
    fc2_bias,
    teacher,
    loss_mask,
    lengths,
):
    row_count = lax.axis_size("row")
    col_count = lax.axis_size("col")
    col_index = lax.axis_index("col")
    group_index = lax.axis_index("dp") * row_count + lax.axis_index("row")
    local_rows = states.shape[0]
    width = states.shape[1]
    group_rows = local_rows * col_count
    clip_count = group_rows // L
    head_width = w_qkv.shape[2]
    heads_here = head_width // HD
    hidden_width = w_fc1.shape[1]
    score_scale = HD ** (-0.5)
    vectors = jnp.stack([ln1_gain, ln1_bias, proj_bias, ln2_gain, ln2_bias, fc2_bias])
    qkv_full, proj_full, fc1_full, fc2_full, vector_full = (
        lax.all_gather(w_qkv, "row", axis=0, tiled=True),
        lax.all_gather(w_proj, "row", axis=1, tiled=True),
        lax.all_gather(w_fc1, "row", axis=0, tiled=True),
        lax.all_gather(w_fc2, "row", axis=1, tiled=True),
        lax.all_gather(vectors, "row", axis=1, tiled=True),
    )
    vector_full = vector_full.astype(jnp.float32)
    gain_one = vector_full[0]
    shift_one = vector_full[1]
    bias_proj = vector_full[2]
    gain_two = vector_full[3]
    shift_two = vector_full[4]
    bias_two = vector_full[5]
    all_clips = lengths.shape[0]
    valid_all = (
        loss_mask.reshape(all_clips, L) * (jnp.arange(L)[None, :] < lengths[:, None])
    ).astype(jnp.float32)
    valid_total = jnp.maximum(jnp.sum(valid_all), 1.0)
    first_row = (group_index * col_count + col_index) * local_rows
    valid = lax.dynamic_slice_in_dim(valid_all.reshape(all_clips * L), first_row, local_rows)
    my_lengths = lax.dynamic_slice_in_dim(lengths, group_index * clip_count, clip_count)
    inputs = states.astype(jnp.float32)
    norm_one, unit_one, spread_one = normalize(inputs, gain_one, shift_one)
    norm_one = norm_one.astype(jnp.bfloat16)
    tokens_one = lax.all_gather(norm_one, "col", axis=0, tiled=True)
    qkv_matrix = qkv_full.reshape(width, 3 * head_width)
    projected = jnp.dot(tokens_one, qkv_matrix, preferred_element_type=jnp.float32).reshape(
        group_rows, 3, head_width
    )
    bias_rows = jnp.stack(
        [
            q_bias.astype(jnp.float32),
            jnp.zeros((head_width,), jnp.float32),
            v_bias.astype(jnp.float32),
        ]
    )
    packed = (projected + bias_rows[None]).astype(jnp.bfloat16)
    clips_packed = packed.reshape(clip_count, L, 3, heads_here, HD)
    attended, totals = lax.map(
        lambda element: attend_clip(element[0], element[1], score_scale), (clips_packed, my_lengths)
    )
    attended = attended.reshape(group_rows, head_width).astype(jnp.bfloat16)
    proj_whole, qkv_whole = (
        lax.all_gather(proj_full, "col", axis=0, tiled=True),
        lax.all_gather(qkv_full, "col", axis=2, tiled=True),
    )
    attended_rows = lax.all_to_all(attended, "col", split_axis=0, concat_axis=1, tiled=True)
    middle = inputs + (
        jnp.dot(attended_rows, proj_whole, preferred_element_type=jnp.float32) + bias_proj
    )
    norm_two, unit_two, spread_two = normalize(middle, gain_two, shift_two)
    norm_two = norm_two.astype(jnp.bfloat16)
    fc1_whole, fc2_whole, fc1_bias_whole = (
        lax.all_gather(fc1_full, "col", axis=1, tiled=True),
        lax.all_gather(fc2_full, "col", axis=0, tiled=True),
        lax.all_gather(fc1_bias, "col", axis=0, tiled=True),
    )
    hidden_pre = jnp.dot(
        norm_two, fc1_whole, preferred_element_type=jnp.float32
    ) + fc1_bias_whole.astype(jnp.float32)
    hidden = gelu_value(hidden_pre).astype(jnp.bfloat16)
    outputs = middle + (jnp.dot(hidden, fc2_whole, preferred_element_type=jnp.float32) + bias_two)
    differ = outputs - teacher.astype(jnp.float32)
    numerator = jnp.sum(valid[:, None] * differ * differ)
    loss_scale = all_clips * L * width / 2.0
    grad_out = loss_scale * 2.0 / (valid_total * width) * valid[:, None] * differ
    grad_low = grad_out.astype(jnp.bfloat16)
    grad_hidden = jnp.dot(grad_low, fc2_whole.T, preferred_element_type=jnp.float32)
    grad_pre = (grad_hidden * gelu_slope(hidden_pre)).astype(jnp.bfloat16)
    wide_fc2 = jnp.dot(hidden.T, grad_low, preferred_element_type=jnp.float32)
    wide_fc1 = jnp.dot(norm_two.T, grad_pre, preferred_element_type=jnp.float32)
    fc1_grad_part, fc2_grad_part = (
        lax.psum_scatter(
            wide_fc1.astype(jnp.bfloat16), "col", scatter_dimension=1, tiled=True
        ).astype(jnp.float32),
        lax.psum_scatter(
            wide_fc2.astype(jnp.bfloat16), "col", scatter_dimension=0, tiled=True
        ).astype(jnp.float32),
    )
    fc1_bias_sum = jnp.sum(grad_pre, axis=0, dtype=jnp.float32)
    grad_norm_two = jnp.dot(grad_pre, fc1_whole.T, preferred_element_type=jnp.float32)
    back_two, gain_two_grad, shift_two_grad = norm_back(
        grad_norm_two, unit_two, spread_two, gain_two
    )
    grad_mid = grad_out + back_two
    mid_low = grad_mid.astype(jnp.bfloat16)
    wide_proj = jnp.dot(attended_rows.T, mid_low, preferred_element_type=jnp.float32)
    proj_grad_part = lax.psum_scatter(
        wide_proj.astype(jnp.bfloat16), "col", scatter_dimension=0, tiled=True
    )
    grad_attended_rows = jnp.dot(mid_low, proj_whole.T, preferred_element_type=jnp.float32).astype(
        jnp.bfloat16
    )
    grad_attended = lax.all_to_all(
        grad_attended_rows, "col", split_axis=1, concat_axis=0, tiled=True
    )
    grads_packed = lax.map(
        lambda element: attend_clip_back(
            element[0], element[1], element[2], element[3], score_scale
        ),
        (clips_packed, my_lengths, totals, grad_attended.reshape(clip_count, L, heads_here, HD)),
    )
    grads_packed = grads_packed.reshape(group_rows, 3 * head_width).astype(jnp.bfloat16)
    qkv_grad_part = jnp.dot(tokens_one.T, grads_packed, preferred_element_type=jnp.float32).reshape(
        width, 3, head_width
    )
    bias_sums = jnp.sum(grads_packed.reshape(group_rows, 3, head_width), axis=0, dtype=jnp.float32)
    grads_rows = lax.all_to_all(
        grads_packed.reshape(group_rows, 3, head_width),
        "col",
        split_axis=0,
        concat_axis=2,
        tiled=True,
    )
    grad_norm_one = jnp.dot(
        grads_rows.reshape(local_rows, 3 * width),
        qkv_whole.reshape(width, 3 * width).T,
        preferred_element_type=jnp.float32,
    )
    back_one, gain_one_grad, shift_one_grad = norm_back(
        grad_norm_one, unit_one, spread_one, gain_one
    )
    grad_states = (grad_mid + back_one).astype(jnp.bfloat16)
    proj_bias_grad = jnp.sum(mid_low, axis=0, dtype=jnp.float32)
    fc2_bias_grad = jnp.sum(grad_low, axis=0, dtype=jnp.float32)
    token_vectors = jnp.stack(
        [
            gain_one_grad,
            shift_one_grad,
            proj_bias_grad,
            gain_two_grad,
            shift_two_grad,
            fc2_bias_grad,
        ]
    )
    head_vectors = lax.dynamic_update_slice(
        jnp.zeros((2, width), jnp.float32),
        jnp.stack([bias_sums[0], bias_sums[2]]),
        (0, col_index * head_width),
    )
    token_sums, head_sums, fc1_sums, loss_sum = lax.psum(
        (token_vectors, head_vectors, fc1_bias_sum, numerator), ("dp", "row", "col")
    )
    qkv_rows, proj_cols, fc1_rows, fc2_cols = (
        lax.psum_scatter(
            qkv_grad_part.astype(jnp.bfloat16), "row", scatter_dimension=0, tiled=True
        ).astype(jnp.float32),
        lax.psum_scatter(proj_grad_part, "row", scatter_dimension=1, tiled=True).astype(
            jnp.float32
        ),
        lax.psum_scatter(
            fc1_grad_part.astype(jnp.bfloat16), "row", scatter_dimension=0, tiled=True
        ).astype(jnp.float32),
        lax.psum_scatter(
            fc2_grad_part.astype(jnp.bfloat16), "row", scatter_dimension=1, tiled=True
        ).astype(jnp.float32),
    )
    qkv_grad, proj_grad, fc1_grad, fc2_grad = (
        lax.psum(qkv_rows.astype(jnp.bfloat16), "dp").astype(jnp.float32),
        lax.psum(proj_cols.astype(jnp.bfloat16), "dp").astype(jnp.float32),
        lax.psum(fc1_rows.astype(jnp.bfloat16), "dp").astype(jnp.float32),
        lax.psum(fc2_cols.astype(jnp.bfloat16), "dp").astype(jnp.float32),
    )
    half_width = width // row_count
    token_part = lax.dynamic_slice_in_dim(
        token_sums, lax.axis_index("row") * half_width, half_width, 1
    )
    head_part = lax.dynamic_slice_in_dim(head_sums, col_index * head_width, head_width, 1)
    fc1_part = lax.dynamic_slice_in_dim(fc1_sums, col_index * hidden_width, hidden_width, 0)
    loss_value = loss_sum / (valid_total * width)
    return (
        outputs.astype(jnp.bfloat16),
        loss_value,
        grad_states,
        token_part[0],
        token_part[1],
        qkv_grad,
        head_part[0],
        head_part[1],
        proj_grad,
        token_part[2],
        token_part[3],
        token_part[4],
        fc1_grad,
        fc1_part,
        fc2_grad,
        token_part[5],
    )


PAIRED_MESH = (4, 2, 4)
GROUP = 4
QT = 128


def dot_nn(a, b):
    return lax.dot_general(a, b, (((1,), (0,)), ((), ())), preferred_element_type=jnp.float32)


def dot_nt(a, b):
    return lax.dot_general(a, b, (((1,), (1,)), ((), ())), preferred_element_type=jnp.float32)


def dot_tn(a, b):
    return lax.dot_general(a, b, (((0,), (0,)), ((), ())), preferred_element_type=jnp.float32)


def head_stack(values, zero):
    lane_head = lax.broadcasted_iota(jnp.int32, values.shape, 1) // HD
    return jnp.concatenate([jnp.where(lane_head == h, values, zero) for h in range(GROUP)], axis=0)


def head_unstack(wide, count):
    return jnp.concatenate(
        [wide[h * HD : (h + 1) * HD, h * count : (h + 1) * count] for h in range(GROUP)], axis=0
    ).T


def tiles_of(rows, tile):
    full = rows // QT

    @pl.loop(0, full)
    def _(index):
        tile(pl.multiple_of(index * QT, QT), QT, index)

    if rows > full * QT:
        tile(full * QT, rows - full * QT, full)


def attend_kernel(first, packed_ref, bias_ref, out_ref, lse_ref, vt_ref):
    width = GROUP * HD
    vt_ref[...] = packed_ref[:, 2 * width : 3 * width].T

    def tile(start, count, index):
        cols = GROUP * count
        stacked = head_stack(
            packed_ref[pl.ds(first + start, count), 0:width], jnp.zeros((), jnp.bfloat16)
        )
        keys = packed_ref[:, width : 2 * width]
        bias = bias_ref[...]
        scores = dot_nt(keys, stacked) + jnp.concatenate([bias] * (cols // 128), axis=1)
        peak = jnp.max(scores, axis=0, keepdims=True)
        weights = jnp.exp(scores - peak)
        total = jnp.sum(weights, axis=0, keepdims=True)
        wide = dot_nn(vt_ref[...], weights.astype(jnp.bfloat16)) * (1.0 / total)
        out_ref[pl.ds(start, count), :] = head_unstack(wide, count).astype(jnp.bfloat16)
        lse_ref[index, :, 0:cols] = jnp.broadcast_to(peak + jnp.log(total), (8, cols))

    tiles_of(out_ref.shape[0], tile)


def attend_back_kernel(first, last, packed_ref, bias_ref, lse_ref, att_ref, up_ref, *refs):
    width = GROUP * HD
    if last:
        dq_in, dk_in, dv_in, out_ref, kt_ref, dk_ref, dv_ref = refs
        dk_ref[...] = dk_in[...]
        dv_ref[...] = dv_in[...]
        out_ref[0:first, 0:width] = dq_in[...]
        rows = out_ref.shape[0] - first
    else:
        out_ref, dk_ref, dv_ref, kt_ref = refs
        dk_ref[...] = jnp.zeros_like(dk_ref)
        dv_ref[...] = jnp.zeros_like(dv_ref)
        rows = out_ref.shape[0]
    kt_ref[...] = packed_ref[:, width : 2 * width].T

    def tile(start, count, index):
        cols = GROUP * count
        zero = jnp.zeros((), jnp.bfloat16)
        up = up_ref[pl.ds(start, count), :]
        stacked = head_stack(packed_ref[pl.ds(first + start, count), 0:width], zero)
        up_stacked = head_stack(up, zero)
        product = head_stack(
            up.astype(jnp.float32) * att_ref[pl.ds(start, count), :].astype(jnp.float32),
            jnp.zeros((), jnp.float32),
        )
        high = product.astype(jnp.bfloat16)
        low = (product - high.astype(jnp.float32)).astype(jnp.bfloat16)
        ones = jnp.ones((8, width), jnp.bfloat16)
        delta = (dot_nt(ones, high) + dot_nt(ones, low))[0:1]
        keys = packed_ref[:, width : 2 * width]
        values = packed_ref[:, 2 * width : 3 * width]
        bias = bias_ref[...]
        scores = dot_nt(keys, stacked) + jnp.concatenate([bias] * (cols // 128), axis=1)
        weights = jnp.exp(scores - lse_ref[index, 0:1, 0:cols])
        dv_ref[...] += dot_nn(weights.astype(jnp.bfloat16), up_stacked)
        grad = (weights * (dot_nt(values, up_stacked) - delta)).astype(jnp.bfloat16)
        dk_ref[...] += dot_nn(grad, stacked)
        wide = dot_nn(kt_ref[...], grad) * (HD**-0.5)
        at = pl.ds(first + start if last else start, count)
        out_ref[at, 0:width] = head_unstack(wide, count).astype(jnp.bfloat16)

    tiles_of(rows, tile)
    if last:
        out_ref[:, width : 2 * width] = dk_ref[...].astype(jnp.bfloat16)
        out_ref[:, 2 * width : 3 * width] = dv_ref[...].astype(jnp.bfloat16)


def attend(packed, bias, first, rows):
    tokens, width = packed.shape[0], GROUP * HD
    tiles = -(-rows // QT)
    return pl.pallas_call(
        functools.partial(attend_kernel, first),
        out_shape=(
            jax.ShapeDtypeStruct((rows, width), jnp.bfloat16),
            jax.ShapeDtypeStruct((tiles, 8, GROUP * QT), jnp.float32),
        ),
        in_specs=[pl.BlockSpec(memory_space=pltpu.VMEM)] * 2,
        out_specs=[pl.BlockSpec(memory_space=pltpu.VMEM)] * 2,
        scratch_shapes=[pltpu.VMEM((width, tokens), jnp.bfloat16)],
        compiler_params=pltpu.CompilerParams(vmem_limit_bytes=32 << 20),
        cost_estimate=pl.CostEstimate(
            flops=10 * rows * tokens * width * 4, bytes_accessed=6 << 20, transcendentals=0
        ),
        name="attend",
    )(packed, bias)


def attend_back(packed, bias, lse, att, upstream, first, before=None):
    tokens, width = packed.shape[0], GROUP * HD
    rows = att.shape[0]
    total = jax.ShapeDtypeStruct((tokens, width), jnp.float32)
    vmem = pl.BlockSpec(memory_space=pltpu.VMEM)
    turned = pltpu.VMEM((width, tokens), jnp.bfloat16)
    if before is None:
        extra = ()
        out_shape = (jax.ShapeDtypeStruct((rows, width), jnp.bfloat16), total, total)
        scratch = [turned]
        out_specs = (vmem,) * 3
    else:
        extra = before
        out_shape = jax.ShapeDtypeStruct((tokens, 3 * width), jnp.bfloat16)
        scratch = [turned] + [pltpu.VMEM((tokens, width), jnp.float32)] * 2
        out_specs = vmem
    return pl.pallas_call(
        functools.partial(attend_back_kernel, first, before is not None),
        out_shape=out_shape,
        in_specs=[vmem] * (5 + len(extra)),
        out_specs=out_specs,
        scratch_shapes=scratch,
        compiler_params=pltpu.CompilerParams(vmem_limit_bytes=48 << 20),
        cost_estimate=pl.CostEstimate(
            flops=20 * rows * tokens * width * 4, bytes_accessed=10 << 20, transcendentals=0
        ),
        name="attend_back",
    )(packed, bias, lse, att, upstream, *extra)


FF_CHUNK = 512


def ffn_kernel(
    table_ref,
    factor_ref,
    norm_ref,
    middle_ref,
    target_ref,
    valid_ref,
    bias_one_ref,
    bias_two_ref,
    fc1_own,
    fc1_other,
    fc2_own,
    fc2_other,
    two_mine,
    two_theirs,
    one_mine,
    one_theirs,
    out_ref,
    hidden_ref,
    pre_ref,
    grad_out_ref,
    grad_low_ref,
    grad_norm_ref,
    hidden_sum_ref,
    sums_ref,
    fc1_v,
    fc2_v,
    sem_one,
    sem_two,
):
    half = fc1_own.shape[0]
    sub = fc1_own.shape[1] // 4
    hidden_total = hidden_ref.shape[1]
    step = one_mine.shape[0] // 4

    def fc1_place(side, at):
        return fc1_v.at[side * half : (side + 1) * half, pl.ds(pl.multiple_of(at * sub, sub), sub)]

    def fc2_place(side, i, at):
        lane = side * half + i * sub
        return fc2_v.at[pl.ds(pl.multiple_of(at * sub, sub), sub), lane : lane + sub]

    def pieces():
        for a in range(4):
            at = table_ref[16 + a]
            rows = slice(a * sub, (a + 1) * sub)
            for side, (one, two) in enumerate(((fc1_own, fc2_own), (fc1_other, fc2_other))):
                yield side, at, one.at[:, rows], [two.at[rows, i * sub : (i + 1) * sub] for i in range(2)]
        for s in range(4):
            for j in (1, 2, 3):
                at = table_ref[4 * s + j]
                for side in range(2):
                    ref = (one_mine, one_theirs)[side] if j == 3 else (two_mine, two_theirs)[side]
                    base = s * step if j == 3 else (2 * s + j - 1) * step
                    low = base + half
                    yield (
                        side,
                        at,
                        ref.at[base : base + half, :],
                        [ref.at[low + i * sub : low + (i + 1) * sub, :] for i in range(2)],
                    )

    listed = list(pieces())
    for side, at, one, _ in listed:
        pltpu.make_async_copy(one, fc1_place(side, at), sem_one.at[side, at]).start()
    for side, at, _, two in listed:
        for i in range(2):
            pltpu.make_async_copy(two[i], fc2_place(side, i, at), sem_two.at[side, i, at]).start()
    grad_norm_ref[...] = jnp.zeros_like(grad_norm_ref)

    @pl.loop(0, hidden_total // FF_CHUNK)
    def _(k):
        for i in range(FF_CHUNK // sub):
            for side in range(2):
                at = k * (FF_CHUNK // sub) + i
                pltpu.make_async_copy(
                    fc1_own.at[:, 0:sub], fc1_place(side, at), sem_one.at[side, at]
                ).wait()
        span = pl.ds(pl.multiple_of(k * FF_CHUNK, FF_CHUNK), FF_CHUNK)
        pre = dot_nn(norm_ref[...], fc1_v[:, span]) + bias_one_ref[0:1, span]
        cdf = 0.5 * (1.0 + lax.erf(pre * ROOT_HALF))
        hidden_ref[:, span] = (pre * cdf).astype(jnp.bfloat16)
        slope = cdf + pre * jnp.exp(-0.5 * pre * pre) * DENSITY_FACTOR
        pre_ref[:, span] = slope.astype(jnp.bfloat16)

    @pl.loop(0, hidden_total // sub)
    def _(at):
        for side in range(2):
            for i in range(2):
                pltpu.make_async_copy(
                    fc2_own.at[0:sub, 0:sub], fc2_place(side, i, at), sem_two.at[side, i, at]
                ).wait()

    for i in range(2):
        cols = slice(i * half, (i + 1) * half)
        total = dot_nn(hidden_ref[...], fc2_v[:, cols]) + (middle_ref[:, cols] + bias_two_ref[0:1, cols])
        out_ref[:, cols] = total.astype(jnp.bfloat16)
        differ = total - target_ref[:, cols].astype(jnp.float32)
        weighted = valid_ref[...] * differ
        sums_ref[0:1, cols] = jnp.sum(weighted * differ, axis=0, keepdims=True)
        grad = factor_ref[0] * weighted
        grad_out_ref[:, cols] = grad
        low = grad.astype(jnp.bfloat16)
        grad_low_ref[:, cols] = low
        sums_ref[1:2, cols] = jnp.sum(low.astype(jnp.float32), axis=0, keepdims=True)

    @pl.loop(0, hidden_total // FF_CHUNK)
    def _(k):
        span = pl.ds(pl.multiple_of(k * FF_CHUNK, FF_CHUNK), FF_CHUNK)
        back = dot_nt(grad_low_ref[...], fc2_v[span, :])
        back = (back * pre_ref[:, span].astype(jnp.float32)).astype(jnp.bfloat16)
        pre_ref[:, span] = back
        hidden_sum_ref[0:1, span] = jnp.sum(back.astype(jnp.float32), axis=0, keepdims=True)
        grad_norm_ref[...] += dot_nt(back, fc1_v[:, span])


def feed_forward(table, factor, norm, middle, target, valid, bias_one, bias_two, pieces):
    rows, width = norm.shape
    hidden = bias_one.shape[1]
    vmem = pl.BlockSpec(memory_space=pltpu.VMEM)
    smem = pl.BlockSpec(memory_space=pltpu.SMEM)
    anywhere = pl.BlockSpec(memory_space=pl.ANY)
    f32, bf16 = jnp.float32, jnp.bfloat16
    return pl.pallas_call(
        ffn_kernel,
        out_shape=(
            jax.ShapeDtypeStruct((rows, width), bf16),
            jax.ShapeDtypeStruct((rows, hidden), bf16),
            jax.ShapeDtypeStruct((rows, hidden), bf16),
            jax.ShapeDtypeStruct((rows, width), f32),
            jax.ShapeDtypeStruct((rows, width), bf16),
            jax.ShapeDtypeStruct((rows, width), f32),
            jax.ShapeDtypeStruct((1, hidden), f32),
            jax.ShapeDtypeStruct((2, width), f32),
        ),
        in_specs=[smem] * 2 + [vmem] * 6 + [anywhere] * 8,
        out_specs=[vmem] * 8,
        scratch_shapes=[
            pltpu.VMEM((width, hidden), bf16),
            pltpu.VMEM((hidden, width), bf16),
            pltpu.SemaphoreType.DMA((2, 16)),
            pltpu.SemaphoreType.DMA((2, 2, 16)),
        ],
        compiler_params=pltpu.CompilerParams(vmem_limit_bytes=62 << 20),
        cost_estimate=pl.CostEstimate(
            flops=8 * rows * width * hidden, bytes_accessed=44 << 20, transcendentals=0
        ),
        name="feed_forward",
    )(table, factor, norm, middle, target, valid, bias_one, bias_two, *pieces)


def swap(values, axis, mask, size):
    return lax.ppermute(values, axis, [(i, i ^ mask) for i in range(size)])


def over_row(values):
    return swap(values, "row", 1, 2)


def over_dp(values, mask):
    return swap(values, "dp", mask, 4)


def over_col(values, mask):
    return swap(values, "col", mask, 4)


def cut(values, index, size, axis=0):
    return lax.dynamic_slice_in_dim(values, index * size, size, axis)


def place(pieces, index_of, axis):
    size = pieces[0].shape[axis]
    shape = list(pieces[0].shape)
    shape[axis] = size * len(pieces)
    whole = jnp.zeros(shape, pieces[0].dtype)
    for s, piece in enumerate(pieces):
        whole = lax.dynamic_update_slice_in_dim(whole, piece, index_of(s) * size, axis)
    return whole


def finish_kernel(part_rows, places_ref, *refs):
    pieces, (fc2_ref, fc1_ref, proj_ref) = refs[:4], refs[4:]
    sub = fc2_ref.shape[0] // 4
    for s, piece in enumerate(pieces):
        at = places_ref[s]
        rows = pl.ds(pl.multiple_of(at * sub, sub), sub)
        fc2_ref[rows, :] = piece[0:sub, :].astype(jnp.float32)
        fc1_ref[:, rows] = piece[sub : 2 * sub, :].astype(jnp.float32).T
        rows = pl.ds(pl.multiple_of(at * part_rows, part_rows), part_rows)
        proj_ref[rows, :] = piece[2 * sub :, :].astype(jnp.float32)


def finish_qkv_kernel(places_ref, *refs):
    out_ref = refs[4]
    deep, width = refs[0].shape[0], out_ref.shape[2]
    for s in range(4):
        rows = pl.ds(pl.multiple_of(places_ref[s] * deep, deep), deep)
        for k in range(3):
            out_ref[k, rows, :] = refs[s][:, k * width : (k + 1) * width].astype(jnp.float32)


def finish(places, pieces, part_rows):
    rows, half = pieces[0].shape
    sub = (rows - part_rows) // 2
    vmem = pl.BlockSpec(memory_space=pltpu.VMEM)
    return pl.pallas_call(
        functools.partial(finish_kernel, part_rows),
        out_shape=(
            jax.ShapeDtypeStruct((4 * sub, half), jnp.float32),
            jax.ShapeDtypeStruct((half, 4 * sub), jnp.float32),
            jax.ShapeDtypeStruct((4 * part_rows, half), jnp.float32),
        ),
        in_specs=[pl.BlockSpec(memory_space=pltpu.SMEM)] + [vmem] * 4,
        out_specs=[vmem] * 3,
        name="finish",
    )(places, *pieces)


def finish_qkv(places, pieces):
    deep, width = pieces[0].shape
    vmem = pl.BlockSpec(memory_space=pltpu.VMEM)
    return pl.pallas_call(
        finish_qkv_kernel,
        out_shape=jax.ShapeDtypeStruct((3, 4 * deep, width // 3), jnp.float32),
        in_specs=[pl.BlockSpec(memory_space=pltpu.SMEM)] + [vmem] * 4,
        out_specs=vmem,
        name="finish_qkv",
    )(places, *pieces)


def tie(value, *others):
    return lax.optimization_barrier((value, *others))[0]


def add_up(own, taken):
    total = own.astype(jnp.float32)
    for piece in taken:
        total = total + piece.astype(jnp.float32)
    return total


def local_paired(
    states,
    ln1_gain,
    ln1_bias,
    w_qkv,
    q_bias,
    v_bias,
    w_proj,
    proj_bias,
    ln2_gain,
    ln2_bias,
    w_fc1,
    fc1_bias,
    w_fc2,
    fc2_bias,
    teacher,
    loss_mask,
    lengths,
):
    f32, bf16 = jnp.float32, jnp.bfloat16
    dp = lax.axis_index("dp")
    row = lax.axis_index("row")
    col = lax.axis_index("col")
    local_rows, width = states.shape
    half = width // 2
    head_width = w_qkv.shape[2]
    hidden_width = w_fc1.shape[1]
    sub = hidden_width // 4
    span = 4 * sub
    part_rows = head_width // 4
    clip = (dp * 2 + row) * 2 + col // 2
    second = col % 2

    def quarter(s):
        return dp ^ s

    def frame(values):
        return jnp.where(
            row == 0, values, jnp.concatenate([values[:, half:], values[:, :half]], axis=1)
        )

    states_other = over_col(states, 1)
    proj_cut = cut(w_proj, dp, part_rows, 0)
    fc2_cut = cut(w_fc2, dp, sub, 0)
    slab = jnp.concatenate(
        [
            cut(w_fc1, dp, sub, 1),
            fc2_cut[:, :sub],
            fc2_cut[:, sub:],
            proj_cut[:, :sub],
            proj_cut[:, sub:],
        ],
        axis=0,
    )
    slab_rows = slab.shape[0]
    w_qkv2 = w_qkv.reshape(half, 3 * head_width)
    qkv_cut = cut(w_qkv2, dp, half // 4)
    qkv_quarter = over_col(qkv_cut, 2)
    two = jnp.concatenate([over_col(slab, 1), over_col(slab, 2)], axis=0)
    two_x, two_y = over_dp(two, 1), over_dp(two, 2)
    states_other = tie(states_other, two)

    vectors = jnp.stack([ln1_gain, ln1_bias, proj_bias, ln2_gain, ln2_bias, fc2_bias])
    vectors, fc1_bias, states, teacher, loss_mask = lax.optimization_barrier(
        (vectors, fc1_bias, states, teacher, loss_mask, slab, qkv_cut)
    )[:5]
    vector_full = jnp.concatenate([vectors, over_row(vectors)], axis=1).astype(f32)
    gain_one, shift_one, bias_proj, gain_two, shift_two, bias_two = (vector_full[i] for i in range(6))

    qkv_near = jnp.concatenate([w_qkv2, over_row(w_qkv2)], axis=0)
    qkv_pieces = [qkv_quarter] + [over_dp(qkv_quarter, s) for s in (1, 2, 3)]
    qkv_far = place(qkv_pieces, quarter, 0)
    qkv_far = jnp.concatenate([qkv_far, over_row(qkv_far)], axis=0)
    small = jnp.concatenate([fc1_bias, q_bias, v_bias])
    smalls = [small] + [over_col(small, j) for j in (1, 2, 3)]
    fc1_other = over_row(w_fc1)
    fc2_other = over_row(w_fc2)
    proj_other = over_row(w_proj)

    one = over_col(tie(slab, states_other), 3)

    all_clips = lengths.shape[0]
    valid_all = (
        loss_mask.reshape(all_clips, L) * (jnp.arange(L)[None, :] < lengths[:, None])
    ).astype(f32)
    valid_total = jnp.maximum(jnp.sum(valid_all), 1.0)
    first_row = ((dp * 2 + row) * 4 + col) * local_rows
    valid = lax.dynamic_slice_in_dim(valid_all.reshape(all_clips * L), first_row, local_rows)
    my_length = lax.dynamic_slice_in_dim(lengths, clip, 1)
    spot = jnp.arange(L)
    position = jnp.where(
        spot < local_rows, second * local_rows + spot, (1 - second) * local_rows + spot - local_rows
    )
    key_bias = jnp.where(position < my_length, 0.0, MASKED).astype(f32)
    key_bias = jnp.broadcast_to(key_bias[:, None], (L, 128))

    inputs = frame(states).astype(f32)
    norm_one, unit_one, spread_one = normalize(inputs, gain_one, shift_one)
    norm_other, unit_other, _ = normalize(frame(states_other).astype(f32), gain_one, shift_one)
    tokens_one = jnp.concatenate([norm_one.astype(bf16), norm_other.astype(bf16)], axis=0)

    zero_bias = jnp.zeros((head_width,), f32)
    score_scale = HD**-0.5
    scale = jnp.where(jnp.arange(3 * head_width) < head_width, score_scale, 1.0).astype(bf16)
    split = local_rows // QT * QT
    later = L - split
    over = local_rows - split

    def project(matrix, extra):
        q_add = extra[span : span + head_width].astype(f32)
        v_add = extra[span + head_width :].astype(f32)
        projected = jnp.dot(tokens_one, matrix, preferred_element_type=f32)
        packed = (projected + jnp.concatenate([q_add, zero_bias, v_add])[None]).astype(bf16)
        return packed * scale[None]

    packed_near = project(qkv_near, small)
    near_late, near_late_lse = attend(packed_near, key_bias, split, later)
    near_other = over_col(near_late[over:], 1)
    two_x, two_y = tie(two_x, near_late), tie(two_y, near_late)
    middle_row = two.shape[0] // 2
    two_low, two_high = over_dp(two_y[:middle_row], 1), over_dp(two_x[middle_row:], 2)
    near_soon, near_soon_lse = attend(tie(packed_near, two_x, two_y), key_bias, 0, split)
    one = tie(one, near_soon)
    one_x, one_y = over_dp(one, 1), over_dp(one, 2)
    packed_far = tie(project(qkv_far, smalls[2]), one, near_other)
    far_late, far_late_lse = attend(packed_far, key_bias, split, later)
    far_other = over_col(far_late[over:], 1)
    two_low, two_high = tie(two_low, far_late), tie(two_high, far_late)
    two_all = jnp.concatenate([two, two_x, two_y, two_low, two_high], axis=0)
    two_theirs = over_row(two_all)
    one_x, one_y = tie(one_x, far_late), tie(one_y, far_late)
    middle_row = one.shape[0] // 2
    one_low, one_high = over_dp(one_y[:middle_row], 1), over_dp(one_x[middle_row:], 2)
    far_soon, far_soon_lse = attend(tie(packed_far, two_all, one_x, one_y), key_bias, 0, split)
    one_low, one_high = tie(one_low, far_soon), tie(one_high, far_soon)
    one_all = jnp.concatenate([one, one_x, one_y, one_low, one_high], axis=0)
    one_theirs = over_row(one_all)

    def proj_rows(block, index, count):
        rows = []
        for s in range(4):
            at = (s * count + index) * slab_rows + half + 2 * sub
            rows.append(
                jnp.concatenate(
                    [block[at : at + part_rows], block[at + part_rows : at + 2 * part_rows]], axis=1
                )
            )
        return place(rows, quarter, 0)

    proj_whole = jnp.concatenate(
        [
            jnp.concatenate(
                [w, proj_rows(b, 0, 2), proj_rows(b, 1, 2), proj_rows(c, 0, 1)], axis=0
            )
            for w, b, c in ((w_proj, two_all, one_all), (proj_other, two_theirs, one_theirs))
        ],
        axis=1,
    )
    attended_rows = jnp.concatenate(
        [
            jnp.concatenate([near_soon, near_late[:over]], axis=0),
            near_other,
            jnp.concatenate([far_soon, far_late[:over]], axis=0),
            far_other,
        ],
        axis=1,
    )
    middle = inputs + (jnp.dot(attended_rows, proj_whole, preferred_element_type=f32) + bias_proj)
    norm_two, unit_two, spread_two = normalize(middle, gain_two, shift_two)
    norm_two = norm_two.astype(bf16)

    table = jnp.stack(
        [(dp ^ s) * 4 + (col ^ j) for s in range(4) for j in range(4)]
        + [a * 4 + col for a in range(4)]
    ).astype(jnp.int32)
    bias_blocks = jnp.stack([b[:span].reshape(4, sub) for b in smalls], axis=1)
    bias_blocks = jnp.concatenate(
        [lax.dynamic_index_in_dim(bias_blocks, col ^ b, 1) for b in range(4)], axis=1
    )
    loss_scale = all_clips * L * width / 2.0
    factor = (loss_scale * 2.0 / (valid_total * width)).reshape(1)
    outputs, hidden, grad_pre, grad_out, grad_low, grad_norm_two, fc1_bias_sum, sums = feed_forward(
        table,
        factor,
        norm_two,
        middle,
        frame(teacher),
        valid[:, None],
        bias_blocks.reshape(1, 4 * span).astype(f32),
        bias_two[None],
        (w_fc1, fc1_other, w_fc2, fc2_other, two_all, two_theirs, one_all, one_theirs),
    )
    numerator = jnp.sum(sums[0])
    back_two, gain_two_grad, shift_two_grad = norm_back(grad_norm_two, unit_two, spread_two, gain_two)
    grad_mid = grad_out + back_two
    mid_low = grad_mid.astype(bf16)
    grad_att_rows = jnp.dot(mid_low, proj_whole.T, preferred_element_type=f32).astype(bf16)
    ups = [
        grad_att_rows[:, 0:head_width],
        over_col(grad_att_rows[:, head_width : 2 * head_width], 1),
        grad_att_rows[:, 2 * head_width : 3 * head_width],
        over_col(grad_att_rows[:, 3 * head_width :], 1),
    ]

    def joined(kept, taken):
        return (kept + taken.astype(f32)).astype(bf16)

    give_fc2 = over_row(dot_tn(hidden, grad_low[:, half:]).astype(bf16))
    give_fc1 = over_row(dot_tn(grad_pre, norm_two[:, half:]).astype(bf16))
    give_proj = over_row(dot_tn(attended_rows, mid_low[:, half:]).astype(bf16))
    wide_fc2 = joined(dot_tn(hidden, grad_low[:, :half]), give_fc2)
    wide_fc1 = joined(dot_tn(grad_pre, norm_two[:, :half]), give_fc1)
    wide_proj = joined(dot_tn(attended_rows, mid_low[:, :half]), give_proj)

    def fc2_part(s, side):
        return cut(wide_fc2[:, side * sub : (side + 1) * sub], quarter(s), span, 0)

    def fc1_part(s, side):
        lanes = slice(side * sub, (side + 1) * sub)
        proj = [
            cut(wide_proj[j * head_width : (j + 1) * head_width, lanes], quarter(s), part_rows, 0)
            for j in range(4)
        ]
        return jnp.concatenate([cut(wide_fc1[:, lanes], quarter(s), span, 0), *proj], axis=0)

    STAY, GO = ((0, 2), (0, 1)), ((1, 3), (2, 3))

    def plane_first(part):
        give = [jnp.concatenate([part(s, side) for s in GO[side]], axis=0) for side in range(2)]
        return [over_dp(give[0], 1), over_dp(give[1], 2)], give

    def plane_second(part, taken):
        rows = taken[0].shape[0] // 2
        keep, give = [], []
        for side in range(2):
            first, second = STAY[side]
            keep.append(joined(part(first, side).astype(f32), taken[side][:rows]))
            give.append(joined(part(second, side).astype(f32), taken[side][rows:]))
        return keep, [over_dp(give[0], 2), over_dp(give[1], 1)], give

    fc2_taken, fc2_give = plane_first(fc2_part)
    fc1_taken, fc1_give = plane_first(fc1_part)

    def row_half(stacked):
        return stacked[:, :half].reshape(-1), stacked[:, half:].reshape(-1)

    keep, give = row_half(
        jnp.stack([gain_two_grad, shift_two_grad, jnp.sum(mid_low, axis=0, dtype=f32), sums[1]])
    )
    rest = jnp.concatenate([fc1_bias_sum[0], jnp.full((128,), numerator)])
    early = jnp.concatenate([keep, rest]) + over_row(jnp.concatenate([give, rest]))

    def cols_out(block_of):
        return [over_col(block_of(j), j) for j in (1, 2, 3)]

    packed_near = tie(packed_near, *fc2_give, *fc1_give)
    part_near = attend_back(packed_near, key_bias, near_soon_lse, near_soon, ups[0][:split], 0)
    fc2_taken = [tie(t, part_near[0]) for t in fc2_taken]
    fc2_keep, fc2_taken, fc2_give = plane_second(fc2_part, fc2_taken)
    early = early + over_dp(tie(early, part_near[0]), 1)

    packed_far = tie(packed_far, *fc2_give, early)
    part_far = attend_back(packed_far, key_bias, far_soon_lse, far_soon, ups[2][:split], 0)
    fc2_taken = [tie(t, part_far[0]) for t in fc2_taken]
    fc2_sum = jnp.concatenate(
        [joined(k.astype(f32), t) for k, t in zip(fc2_keep, fc2_taken, strict=True)], axis=1
    )
    fc2_cols = cols_out(lambda j: cut(fc2_sum, col ^ j, sub, 0))
    fc1_taken = [tie(t, part_far[0]) for t in fc1_taken]
    fc1_keep, fc1_taken, fc1_give = plane_second(fc1_part, fc1_taken)
    early = early + over_dp(tie(early, part_far[0]), 2)

    packed_near = tie(packed_near, fc2_sum, early, *fc1_give)
    up = jnp.concatenate([ups[0][split:], ups[1]], axis=0)
    grad_near = attend_back(packed_near, key_bias, near_late_lse, near_late, up, split, part_near)
    fc1_taken = [tie(t, grad_near) for t in fc1_taken]
    fc1_sum = jnp.concatenate(
        [joined(k.astype(f32), t) for k, t in zip(fc1_keep, fc1_taken, strict=True)], axis=1
    )

    def fc1_block(j):
        proj = fc1_sum[span + j * part_rows : span + (j + 1) * part_rows]
        return jnp.concatenate([cut(fc1_sum[:span], col ^ j, sub, 0), proj], axis=0)

    fc1_cols = cols_out(fc1_block)
    early = early + over_col(tie(early, grad_near), 1)

    def qkv_halves(grad):
        taken = over_row(dot_tn(tokens_one[:, half:], grad).astype(bf16))
        return joined(dot_tn(tokens_one[:, :half], grad), taken)

    deep = half // 4

    def plane_out(wide):
        return cut(wide, dp, deep), [over_dp(cut(wide, quarter(s), deep), s) for s in (1, 2, 3)]

    wide_near = qkv_halves(grad_near)
    near_keep, near_taken = plane_out(wide_near)
    norm_near = dot_nt(grad_near, qkv_near)

    packed_far = tie(packed_far, fc1_sum, wide_near, norm_near, early)
    up = jnp.concatenate([ups[2][split:], ups[3]], axis=0)
    grad_far = attend_back(packed_far, key_bias, far_late_lse, far_late, up, split, part_far)

    grad_norm_one = norm_near + dot_nt(grad_far, qkv_far)
    norm_give = grad_norm_one[local_rows:].astype(bf16)
    norm_taken = over_col(norm_give, 1)
    grad_far = tie(grad_far, norm_give)
    taken_far = over_row(dot_tn(tokens_one[:, half:], grad_far).astype(bf16))
    fc2_cols = [tie(t, grad_far) for t in fc2_cols]
    fc1_cols = [tie(t, grad_far) for t in fc1_cols]
    mine = jnp.concatenate(
        [add_up(cut(fc2_sum, col, sub, 0), fc2_cols), add_up(fc1_block(0), fc1_cols)], axis=0
    ).astype(bf16)
    mine_back = [over_dp(mine, s) for s in (1, 2, 3)]
    near_sum = add_up(near_keep, [tie(t, grad_far) for t in near_taken]).astype(bf16)
    early = early + over_col(tie(early, grad_far), 2)
    both = jnp.stack(
        [
            jnp.sum(grad_norm_one[:local_rows] * unit_one, axis=0)
            + jnp.sum(grad_norm_one[local_rows:] * unit_other, axis=0),
            jnp.sum(grad_norm_one, axis=0),
        ]
    )
    keep, give = row_half(both)
    heads = [
        jnp.sum(g[:, i : i + head_width], axis=0, dtype=f32)
        for g in (grad_near, grad_far)
        for i in (0, 2 * head_width)
    ]
    late_keep, late_give = jnp.concatenate([keep, *heads]), jnp.concatenate([give, *heads])
    late_taken = over_row(tie(late_give, mine))

    wide_far = joined(dot_tn(tokens_one[:, :half], grad_far), tie(taken_far, mine, late_give))
    far_keep, far_taken = plane_out(wide_far)
    late = late_keep + tie(late_taken, wide_far)
    late_parts = [over_dp(late, s) for s in (1, 2, 3)]
    far_taken = [tie(t, late) for t in far_taken]
    far_sum = add_up(far_keep, far_taken).astype(bf16)
    far_other = over_col(far_sum, 2)
    late_parts = [tie(t, far_sum) for t in late_parts]
    late = add_up(late, late_parts)
    flat, _, theirs = jnp.split(late, [2 * half, 2 * half + 2 * head_width])
    moved = [over_col(flat, 1), over_col(jnp.concatenate([flat, theirs]), 2), over_col(flat, 3)]
    qkv_sum = add_up(near_sum, [tie(far_other, flat, theirs)]).astype(bf16)
    qkv_back = [over_dp(qkv_sum, s) for s in (1, 2, 3)]

    norm_taken, *mine_back = lax.optimization_barrier((norm_taken, *mine_back, qkv_sum))[:4]
    places = jnp.stack([dp, dp ^ 1, dp ^ 2, dp ^ 3]).astype(jnp.int32)
    fc2_grad, fc1_grad, proj_grad = finish(places, [mine, *mine_back], part_rows)
    grad_norm_one = grad_norm_one[:local_rows] + norm_taken.astype(f32)
    back_one, _, _ = norm_back(grad_norm_one, unit_one, spread_one, gain_one)
    grad_states = frame((grad_mid + back_one).astype(bf16))
    moved = [tie(t, grad_states) for t in moved]
    heads = late[2 * half : 2 * half + 2 * head_width] + moved[1][2 * half :]
    late = (flat + moved[0] + moved[1][: 2 * half] + moved[2]).reshape(2, half)
    qkv_back = [tie(t, grad_states) for t in qkv_back]
    qkv_grad = finish_qkv(places, [qkv_sum, *qkv_back]).transpose(1, 0, 2)
    flat = early[: 4 * half].reshape(4, half)
    fc1_bias_grad = lax.dynamic_index_in_dim(
        early[4 * half : 4 * half + 4 * span].reshape(4, 4, sub), col, 1, False
    ).reshape(span)
    loss_value = early[4 * half + 4 * span] / (valid_total * width)
    return (
        frame(outputs),
        loss_value,
        grad_states,
        late[0],
        late[1],
        qkv_grad,
        heads[:head_width],
        heads[head_width:],
        proj_grad,
        flat[2],
        flat[0],
        flat[1],
        fc1_grad,
        fc1_bias_grad,
        fc2_grad,
        flat[3],
    )


def solution(mesh):
    sizes = (mesh.shape["dp"], mesh.shape["row"], mesh.shape["col"])
    body = local_paired if sizes == PAIRED_MESH else local_general
    in_specs = (
        P(("dp", "row", "col"), None),
        P("row"),
        P("row"),
        P("row", None, "col"),
        P("col"),
        P("col"),
        P("col", "row"),
        P("row"),
        P("row"),
        P("row"),
        P("row", "col"),
        P("col"),
        P("col", "row"),
        P("row"),
        P(("dp", "row", "col"), None),
        P(),
        P(),
    )
    out_specs = (
        P(("dp", "row", "col"), None),
        P(),
        P(("dp", "row", "col"), None),
        P("row"),
        P("row"),
        P("row", None, "col"),
        P("col"),
        P("col"),
        P("col", "row"),
        P("row"),
        P("row"),
        P("row"),
        P("row", "col"),
        P("col"),
        P("col", "row"),
        P("row"),
    )
    return jax.shard_map(body, mesh=mesh, in_specs=in_specs, out_specs=out_specs, check_vma=False)
```

```python
import functools

import jax
import jax.numpy as jnp
from jax import lax
from jax.experimental import pallas as pl
from jax.experimental.pallas import tpu as pltpu
from jax.sharding import PartitionSpec as P

HD = 64
L = 1568


EPSILON = 1e-06
MASKED = -1e30
ROOT_HALF = 0.7071067811865476
DENSITY_FACTOR = 0.3989422804014327


def normalize(values, factor, offset):
    centered = values - jnp.mean(values, axis=-1, keepdims=True)
    spread = lax.rsqrt(jnp.mean(centered * centered, axis=-1, keepdims=True) + EPSILON)
    normal = centered * spread
    return (normal * factor + offset, normal, spread)


def norm_back(upstream, normal, spread, factor):
    inner = upstream * factor
    center_term = jnp.mean(inner, axis=-1, keepdims=True)
    slope_term = jnp.mean(inner * normal, axis=-1, keepdims=True)
    back = spread * (inner - center_term - normal * slope_term)
    return (back, jnp.sum(upstream * normal, axis=0), jnp.sum(upstream, axis=0))


def gelu_value(values):
    return values * (0.5 * (1.0 + lax.erf(values * ROOT_HALF)))


def gelu_slope(values):
    normal_cdf = 0.5 * (1.0 + lax.erf(values * ROOT_HALF))
    return normal_cdf + values * jnp.exp(-0.5 * values * values) * DENSITY_FACTOR


def masked_scores(queries, key_rows, length, score_scale):
    logits = (
        jnp.einsum("ihd,jhd->hij", queries, key_rows, preferred_element_type=jnp.float32)
        * score_scale
    )
    keep = jnp.arange(key_rows.shape[0]) < length
    return jnp.where(keep[None, None, :], logits, MASKED)


def attend_clip(packed, length, score_scale):
    half_span = packed.shape[0] // 2
    key_rows = packed[:, 1]
    value_rows = packed[:, 2]
    pieces = []
    totals = []
    for block_index in range(2):
        queries = packed[block_index * half_span : (block_index + 1) * half_span, 0]
        logits = masked_scores(queries, key_rows, length, score_scale)
        peak = jnp.max(logits, axis=-1, keepdims=True)
        total = peak + jnp.log(jnp.sum(jnp.exp(logits - peak), axis=-1, keepdims=True))
        weights = jnp.exp(logits - total).astype(jnp.bfloat16)
        pieces.append(
            jnp.einsum("hij,jhd->ihd", weights, value_rows, preferred_element_type=jnp.float32)
        )
        totals.append(total[..., 0])
    return (jnp.concatenate(pieces, 0), jnp.concatenate(totals, 1))


def attend_clip_back(packed, length, totals, upstream, score_scale):
    half_span = packed.shape[0] // 2
    key_rows = packed[:, 1]
    value_rows = packed[:, 2]
    grad_keys = jnp.zeros(key_rows.shape, jnp.float32)
    grad_values = jnp.zeros(value_rows.shape, jnp.float32)
    grad_queries = []
    for block_index in range(2):
        first = block_index * half_span
        queries = packed[first : first + half_span, 0]
        logits = masked_scores(queries, key_rows, length, score_scale)
        probs = jnp.exp(logits - totals[:, first : first + half_span][..., None])
        incoming = upstream[first : first + half_span]
        grad_values = grad_values + jnp.einsum(
            "hij,ihd->jhd", probs.astype(jnp.bfloat16), incoming, preferred_element_type=jnp.float32
        )
        grad_probs = jnp.einsum(
            "ihd,jhd->hij", incoming, value_rows, preferred_element_type=jnp.float32
        )
        grad_logits = (
            probs * (grad_probs - jnp.sum(probs * grad_probs, axis=-1, keepdims=True))
        ).astype(jnp.bfloat16)
        grad_queries.append(
            jnp.einsum("hij,jhd->ihd", grad_logits, key_rows, preferred_element_type=jnp.float32)
            * score_scale
        )
        grad_keys = (
            grad_keys
            + jnp.einsum("hij,ihd->jhd", grad_logits, queries, preferred_element_type=jnp.float32)
            * score_scale
        )
    return jnp.stack([jnp.concatenate(grad_queries, 0), grad_keys, grad_values], axis=1)


def local_general(
    states,
    ln1_gain,
    ln1_bias,
    w_qkv,
    q_bias,
    v_bias,
    w_proj,
    proj_bias,
    ln2_gain,
    ln2_bias,
    w_fc1,
    fc1_bias,
    w_fc2,
    fc2_bias,
    teacher,
    loss_mask,
    lengths,
):
    row_count = lax.axis_size("row")
    col_count = lax.axis_size("col")
    col_index = lax.axis_index("col")
    group_index = lax.axis_index("dp") * row_count + lax.axis_index("row")
    local_rows = states.shape[0]
    width = states.shape[1]
    group_rows = local_rows * col_count
    clip_count = group_rows // L
    head_width = w_qkv.shape[2]
    heads_here = head_width // HD
    hidden_width = w_fc1.shape[1]
    score_scale = HD ** (-0.5)
    vectors = jnp.stack([ln1_gain, ln1_bias, proj_bias, ln2_gain, ln2_bias, fc2_bias])
    qkv_full, proj_full, fc1_full, fc2_full, vector_full = (
        lax.all_gather(w_qkv, "row", axis=0, tiled=True),
        lax.all_gather(w_proj, "row", axis=1, tiled=True),
        lax.all_gather(w_fc1, "row", axis=0, tiled=True),
        lax.all_gather(w_fc2, "row", axis=1, tiled=True),
        lax.all_gather(vectors, "row", axis=1, tiled=True),
    )
    vector_full = vector_full.astype(jnp.float32)
    gain_one = vector_full[0]
    shift_one = vector_full[1]
    bias_proj = vector_full[2]
    gain_two = vector_full[3]
    shift_two = vector_full[4]
    bias_two = vector_full[5]
    all_clips = lengths.shape[0]
    valid_all = (
        loss_mask.reshape(all_clips, L) * (jnp.arange(L)[None, :] < lengths[:, None])
    ).astype(jnp.float32)
    valid_total = jnp.maximum(jnp.sum(valid_all), 1.0)
    first_row = (group_index * col_count + col_index) * local_rows
    valid = lax.dynamic_slice_in_dim(valid_all.reshape(all_clips * L), first_row, local_rows)
    my_lengths = lax.dynamic_slice_in_dim(lengths, group_index * clip_count, clip_count)
    inputs = states.astype(jnp.float32)
    norm_one, unit_one, spread_one = normalize(inputs, gain_one, shift_one)
    norm_one = norm_one.astype(jnp.bfloat16)
    tokens_one = lax.all_gather(norm_one, "col", axis=0, tiled=True)
    qkv_matrix = qkv_full.reshape(width, 3 * head_width)
    projected = jnp.dot(tokens_one, qkv_matrix, preferred_element_type=jnp.float32).reshape(
        group_rows, 3, head_width
    )
    bias_rows = jnp.stack(
        [
            q_bias.astype(jnp.float32),
            jnp.zeros((head_width,), jnp.float32),
            v_bias.astype(jnp.float32),
        ]
    )
    packed = (projected + bias_rows[None]).astype(jnp.bfloat16)
    clips_packed = packed.reshape(clip_count, L, 3, heads_here, HD)
    attended, totals = lax.map(
        lambda element: attend_clip(element[0], element[1], score_scale), (clips_packed, my_lengths)
    )
    attended = attended.reshape(group_rows, head_width).astype(jnp.bfloat16)
    proj_whole, qkv_whole = (
        lax.all_gather(proj_full, "col", axis=0, tiled=True),
        lax.all_gather(qkv_full, "col", axis=2, tiled=True),
    )
    attended_rows = lax.all_to_all(attended, "col", split_axis=0, concat_axis=1, tiled=True)
    middle = inputs + (
        jnp.dot(attended_rows, proj_whole, preferred_element_type=jnp.float32) + bias_proj
    )
    norm_two, unit_two, spread_two = normalize(middle, gain_two, shift_two)
    norm_two = norm_two.astype(jnp.bfloat16)
    fc1_whole, fc2_whole, fc1_bias_whole = (
        lax.all_gather(fc1_full, "col", axis=1, tiled=True),
        lax.all_gather(fc2_full, "col", axis=0, tiled=True),
        lax.all_gather(fc1_bias, "col", axis=0, tiled=True),
    )
    hidden_pre = jnp.dot(
        norm_two, fc1_whole, preferred_element_type=jnp.float32
    ) + fc1_bias_whole.astype(jnp.float32)
    hidden = gelu_value(hidden_pre).astype(jnp.bfloat16)
    outputs = middle + (jnp.dot(hidden, fc2_whole, preferred_element_type=jnp.float32) + bias_two)
    differ = outputs - teacher.astype(jnp.float32)
    numerator = jnp.sum(valid[:, None] * differ * differ)
    loss_scale = all_clips * L * width / 2.0
    grad_out = loss_scale * 2.0 / (valid_total * width) * valid[:, None] * differ
    grad_low = grad_out.astype(jnp.bfloat16)
    grad_hidden = jnp.dot(grad_low, fc2_whole.T, preferred_element_type=jnp.float32)
    grad_pre = (grad_hidden * gelu_slope(hidden_pre)).astype(jnp.bfloat16)
    wide_fc2 = jnp.dot(hidden.T, grad_low, preferred_element_type=jnp.float32)
    wide_fc1 = jnp.dot(norm_two.T, grad_pre, preferred_element_type=jnp.float32)
    fc1_grad_part, fc2_grad_part = (
        lax.psum_scatter(
            wide_fc1.astype(jnp.bfloat16), "col", scatter_dimension=1, tiled=True
        ).astype(jnp.float32),
        lax.psum_scatter(
            wide_fc2.astype(jnp.bfloat16), "col", scatter_dimension=0, tiled=True
        ).astype(jnp.float32),
    )
    fc1_bias_sum = jnp.sum(grad_pre, axis=0, dtype=jnp.float32)
    grad_norm_two = jnp.dot(grad_pre, fc1_whole.T, preferred_element_type=jnp.float32)
    back_two, gain_two_grad, shift_two_grad = norm_back(
        grad_norm_two, unit_two, spread_two, gain_two
    )
    grad_mid = grad_out + back_two
    mid_low = grad_mid.astype(jnp.bfloat16)
    wide_proj = jnp.dot(attended_rows.T, mid_low, preferred_element_type=jnp.float32)
    proj_grad_part = lax.psum_scatter(
        wide_proj.astype(jnp.bfloat16), "col", scatter_dimension=0, tiled=True
    )
    grad_attended_rows = jnp.dot(mid_low, proj_whole.T, preferred_element_type=jnp.float32).astype(
        jnp.bfloat16
    )
    grad_attended = lax.all_to_all(
        grad_attended_rows, "col", split_axis=1, concat_axis=0, tiled=True
    )
    grads_packed = lax.map(
        lambda element: attend_clip_back(
            element[0], element[1], element[2], element[3], score_scale
        ),
        (clips_packed, my_lengths, totals, grad_attended.reshape(clip_count, L, heads_here, HD)),
    )
    grads_packed = grads_packed.reshape(group_rows, 3 * head_width).astype(jnp.bfloat16)
    qkv_grad_part = jnp.dot(tokens_one.T, grads_packed, preferred_element_type=jnp.float32).reshape(
        width, 3, head_width
    )
    bias_sums = jnp.sum(grads_packed.reshape(group_rows, 3, head_width), axis=0, dtype=jnp.float32)
    grads_rows = lax.all_to_all(
        grads_packed.reshape(group_rows, 3, head_width),
        "col",
        split_axis=0,
        concat_axis=2,
        tiled=True,
    )
    grad_norm_one = jnp.dot(
        grads_rows.reshape(local_rows, 3 * width),
        qkv_whole.reshape(width, 3 * width).T,
        preferred_element_type=jnp.float32,
    )
    back_one, gain_one_grad, shift_one_grad = norm_back(
        grad_norm_one, unit_one, spread_one, gain_one
    )
    grad_states = (grad_mid + back_one).astype(jnp.bfloat16)
    proj_bias_grad = jnp.sum(mid_low, axis=0, dtype=jnp.float32)
    fc2_bias_grad = jnp.sum(grad_low, axis=0, dtype=jnp.float32)
    token_vectors = jnp.stack(
        [
            gain_one_grad,
            shift_one_grad,
            proj_bias_grad,
            gain_two_grad,
            shift_two_grad,
            fc2_bias_grad,
        ]
    )
    head_vectors = lax.dynamic_update_slice(
        jnp.zeros((2, width), jnp.float32),
        jnp.stack([bias_sums[0], bias_sums[2]]),
        (0, col_index * head_width),
    )
    token_sums, head_sums, fc1_sums, loss_sum = lax.psum(
        (token_vectors, head_vectors, fc1_bias_sum, numerator), ("dp", "row", "col")
    )
    qkv_rows, proj_cols, fc1_rows, fc2_cols = (
        lax.psum_scatter(
            qkv_grad_part.astype(jnp.bfloat16), "row", scatter_dimension=0, tiled=True
        ).astype(jnp.float32),
        lax.psum_scatter(proj_grad_part, "row", scatter_dimension=1, tiled=True).astype(
            jnp.float32
        ),
        lax.psum_scatter(
            fc1_grad_part.astype(jnp.bfloat16), "row", scatter_dimension=0, tiled=True
        ).astype(jnp.float32),
        lax.psum_scatter(
            fc2_grad_part.astype(jnp.bfloat16), "row", scatter_dimension=1, tiled=True
        ).astype(jnp.float32),
    )
    qkv_grad, proj_grad, fc1_grad, fc2_grad = (
        lax.psum(qkv_rows.astype(jnp.bfloat16), "dp").astype(jnp.float32),
        lax.psum(proj_cols.astype(jnp.bfloat16), "dp").astype(jnp.float32),
        lax.psum(fc1_rows.astype(jnp.bfloat16), "dp").astype(jnp.float32),
        lax.psum(fc2_cols.astype(jnp.bfloat16), "dp").astype(jnp.float32),
    )
    half_width = width // row_count
    token_part = lax.dynamic_slice_in_dim(
        token_sums, lax.axis_index("row") * half_width, half_width, 1
    )
    head_part = lax.dynamic_slice_in_dim(head_sums, col_index * head_width, head_width, 1)
    fc1_part = lax.dynamic_slice_in_dim(fc1_sums, col_index * hidden_width, hidden_width, 0)
    loss_value = loss_sum / (valid_total * width)
    return (
        outputs.astype(jnp.bfloat16),
        loss_value,
        grad_states,
        token_part[0],
        token_part[1],
        qkv_grad,
        head_part[0],
        head_part[1],
        proj_grad,
        token_part[2],
        token_part[3],
        token_part[4],
        fc1_grad,
        fc1_part,
        fc2_grad,
        token_part[5],
    )


PAIRED_MESH = (4, 2, 4)
GROUP = 4


def small_cost(flops):
    return pl.CostEstimate(flops=flops, bytes_accessed=0, transcendentals=0)
QT = 128


def dot_nn(a, b):
    return lax.dot_general(a, b, (((1,), (0,)), ((), ())), preferred_element_type=jnp.float32)


def dot_nt(a, b):
    return lax.dot_general(a, b, (((1,), (1,)), ((), ())), preferred_element_type=jnp.float32)


def dot_tn(a, b):
    return lax.dot_general(a, b, (((0,), (0,)), ((), ())), preferred_element_type=jnp.float32)


def head_stack(values, zero):
    lane_head = lax.broadcasted_iota(jnp.int32, values.shape, 1) // HD
    return jnp.concatenate([jnp.where(lane_head == h, values, zero) for h in range(GROUP)], axis=0)


def head_unstack(wide, count):
    return jnp.concatenate(
        [wide[h * HD : (h + 1) * HD, h * count : (h + 1) * count] for h in range(GROUP)], axis=0
    ).T


def tiles_of(rows, tile):
    full = rows // QT

    @pl.loop(0, full)
    def _(index):
        tile(pl.multiple_of(index * QT, QT), QT, index)

    if rows > full * QT:
        tile(full * QT, rows - full * QT, full)


def attend_kernel(first, packed_ref, bias_ref, out_ref, lse_ref, vt_ref):
    width = GROUP * HD
    vt_ref[...] = packed_ref[:, 2 * width : 3 * width].T

    def tile(start, count, index):
        cols = GROUP * count
        stacked = head_stack(
            packed_ref[pl.ds(first + start, count), 0:width], jnp.zeros((), jnp.bfloat16)
        )
        keys = packed_ref[:, width : 2 * width]
        bias = bias_ref[...]
        scores = dot_nt(keys, stacked) + jnp.concatenate([bias] * (cols // 128), axis=1)
        peak = jnp.max(scores, axis=0, keepdims=True)
        weights = jnp.exp(scores - peak)
        total = jnp.sum(weights, axis=0, keepdims=True)
        wide = dot_nn(vt_ref[...], weights.astype(jnp.bfloat16)) * (1.0 / total)
        out_ref[pl.ds(start, count), :] = head_unstack(wide, count).astype(jnp.bfloat16)
        lse_ref[index, :, 0:cols] = jnp.broadcast_to(peak + jnp.log(total), (8, cols))

    tiles_of(out_ref.shape[0], tile)


def attend_back_kernel(
    first, lane, last, packed_ref, bias_ref, lse_ref, att_ref, up_own_ref, up_far_ref, *refs
):
    width = GROUP * HD
    lanes = slice(lane, lane + width)
    own_rows = up_own_ref.shape[0]
    if last:
        dq_in, dk_in, dv_in, out_ref, sum_ref, kt_ref, up_ref, dk_ref, dv_ref = refs
        dk_ref[...] = dk_in[...]
        dv_ref[...] = dv_in[...]
        out_ref[0:first, 0:width] = dq_in[...]
        rows = out_ref.shape[0] - first
        up_ref[0 : own_rows - first, :] = up_own_ref[first:own_rows, lanes]
        up_ref[own_rows - first :, :] = up_far_ref[:, lanes]
    else:
        out_ref, dk_ref, dv_ref, kt_ref, up_ref = refs
        dk_ref[...] = jnp.zeros_like(dk_ref)
        dv_ref[...] = jnp.zeros_like(dv_ref)
        rows = out_ref.shape[0]
        up_ref[...] = up_own_ref[0:rows, lanes]
    kt_ref[...] = packed_ref[:, width : 2 * width].T

    def tile(start, count, index):
        cols = GROUP * count
        zero = jnp.zeros((), jnp.bfloat16)
        up = up_ref[pl.ds(start, count), :]
        stacked = head_stack(packed_ref[pl.ds(first + start, count), 0:width], zero)
        up_stacked = head_stack(up, zero)
        product = head_stack(
            up.astype(jnp.float32) * att_ref[pl.ds(start, count), :].astype(jnp.float32),
            jnp.zeros((), jnp.float32),
        )
        high = product.astype(jnp.bfloat16)
        low = (product - high.astype(jnp.float32)).astype(jnp.bfloat16)
        ones = jnp.ones((8, width), jnp.bfloat16)
        delta = (dot_nt(ones, high) + dot_nt(ones, low))[0:1]
        keys = packed_ref[:, width : 2 * width]
        values = packed_ref[:, 2 * width : 3 * width]
        bias = bias_ref[...]
        scores = dot_nt(keys, stacked) + jnp.concatenate([bias] * (cols // 128), axis=1)
        weights = jnp.exp(scores - lse_ref[index, 0:1, 0:cols])
        dv_ref[...] += dot_nn(weights.astype(jnp.bfloat16), up_stacked)
        grad = (weights * (dot_nt(values, up_stacked) - delta)).astype(jnp.bfloat16)
        dk_ref[...] += dot_nn(grad, stacked)
        wide = dot_nn(kt_ref[...], grad) * (HD**-0.5)
        at = pl.ds(first + start if last else start, count)
        out_ref[at, 0:width] = head_unstack(wide, count).astype(jnp.bfloat16)

    tiles_of(rows, tile)
    if last:
        out_ref[:, width : 2 * width] = dk_ref[...].astype(jnp.bfloat16)
        out_ref[:, 2 * width : 3 * width] = dv_ref[...].astype(jnp.bfloat16)
        for k in range(3):
            part = out_ref[:, k * width : (k + 1) * width].astype(jnp.float32)
            sum_ref[:, k * width : (k + 1) * width] = jnp.sum(part, axis=0, keepdims=True)


def attend(packed, bias, first, rows):
    tokens, width = packed.shape[0], GROUP * HD
    tiles = -(-rows // QT)
    return pl.pallas_call(
        functools.partial(attend_kernel, first),
        out_shape=(
            jax.ShapeDtypeStruct((rows, width), jnp.bfloat16),
            jax.ShapeDtypeStruct((tiles, 8, GROUP * QT), jnp.float32),
        ),
        in_specs=[pl.BlockSpec(memory_space=pltpu.VMEM)] * 2,
        out_specs=[pl.BlockSpec(memory_space=pltpu.VMEM)] * 2,
        scratch_shapes=[pltpu.VMEM((width, tokens), jnp.bfloat16)],
        compiler_params=pltpu.CompilerParams(vmem_limit_bytes=32 << 20),
        cost_estimate=pl.CostEstimate(
            flops=2 * rows * tokens * width * 4, bytes_accessed=6 << 20, transcendentals=0
        ),
        name="attend",
    )(packed, bias)


def attend_back(packed, bias, lse, att, up_own, up_far, lane, first, before=None):
    tokens, width = packed.shape[0], GROUP * HD
    rows = att.shape[0]
    total = jax.ShapeDtypeStruct((tokens, width), jnp.float32)
    vmem = pl.BlockSpec(memory_space=pltpu.VMEM)
    scratch = [pltpu.VMEM((width, tokens), jnp.bfloat16), pltpu.VMEM((rows, width), jnp.bfloat16)]
    if before is None:
        extra = ()
        out_shape = (jax.ShapeDtypeStruct((rows, width), jnp.bfloat16), total, total)
        up_far = up_own
    else:
        extra = before
        out_shape = (
            jax.ShapeDtypeStruct((tokens, 3 * width), jnp.bfloat16),
            jax.ShapeDtypeStruct((1, 3 * width), jnp.float32),
        )
        scratch += [pltpu.VMEM((tokens, width), jnp.float32)] * 2
    return pl.pallas_call(
        functools.partial(attend_back_kernel, first, lane, before is not None),
        out_shape=out_shape,
        in_specs=[vmem] * (6 + len(extra)),
        out_specs=(vmem,) * len(out_shape),
        scratch_shapes=scratch,
        compiler_params=pltpu.CompilerParams(vmem_limit_bytes=52 << 20),
        cost_estimate=pl.CostEstimate(
            flops=4 * rows * tokens * width * 4, bytes_accessed=10 << 20, transcendentals=0
        ),
        name="attend_back",
    )(packed, bias, lse, att, up_own, up_far, *extra)


FF_CHUNK = 512
ROWS = 112


def rows_of(total, body):
    @pl.loop(0, total // ROWS)
    def _(index):
        body(pl.ds(pl.multiple_of(index * ROWS, ROWS), ROWS))


def unit_rows(values):
    centered = values - jnp.mean(values, axis=-1, keepdims=True)
    spread = lax.rsqrt(jnp.mean(centered * centered, axis=-1, keepdims=True) + EPSILON)
    return centered * spread, spread


def middle_kernel(
    table_ref,
    factor_ref,
    att_ref,
    input_ref,
    target_ref,
    valid_ref,
    vector_ref,
    small_ref,
    fc1_own,
    fc1_other,
    fc2_own,
    fc2_other,
    proj_own,
    proj_other,
    two_mine,
    two_theirs,
    one_mine,
    one_theirs,
    out_ref,
    hidden_ref,
    pre_ref,
    norm_ref,
    grad_low_ref,
    mid_low_ref,
    grad_mid_ref,
    up_own_ref,
    up_give_ref,
    hidden_sum_ref,
    sums_ref,
    fc1_v,
    fc2_v,
    proj_v,
    middle_v,
    back_v,
    sem_one,
    sem_two,
    sem_proj,
):
    f32, bf16 = jnp.float32, jnp.bfloat16
    total_rows = att_ref.shape[0]
    half = fc1_own.shape[0]
    sub = fc1_own.shape[1] // 4
    heads = proj_own.shape[0]
    part = heads // 4
    hidden_total = hidden_ref.shape[1]
    chunks = hidden_total // FF_CHUNK
    unit = half + 2 * sub + 2 * part + 16

    def fc1_copy(source, side, at):
        lanes = pl.ds(pl.multiple_of(at * sub, sub), sub)
        pltpu.make_async_copy(
            source, fc1_v.at[side * half : (side + 1) * half, lanes], sem_one.at[at // 2]
        ).start()

    def fc2_copy(source, side, i, at):
        lane = side * half + i * sub
        pltpu.make_async_copy(
            source, fc2_v.at[pl.ds(pl.multiple_of(at * sub, sub), sub), lane : lane + sub], sem_two
        ).start()

    sources = []
    for s in range(4):
        step = two_mine.shape[0] // 4
        sources.append((s, 2, two_mine, two_theirs, s * step))
        step = one_mine.shape[0] // 4
        sources.append((s, 1, one_mine, one_theirs, s * step))
        sources.append((s, 3, one_mine, one_theirs, s * step + unit))

    for side, ref in enumerate((proj_own, proj_other)):
        pltpu.make_async_copy(
            ref, proj_v.at[0:heads, side * half : (side + 1) * half], sem_proj
        ).start()
    for s, j, *refs, base in sources:
        rows = pl.ds(pl.multiple_of(j * heads + table_ref[20 + s] * part, part), part)
        for side in range(2):
            for i in range(2):
                low = base + half + 2 * sub + i * part
                lane = side * half + i * sub
                pltpu.make_async_copy(
                    refs[side].at[low : low + part, :], proj_v.at[rows, lane : lane + sub], sem_proj
                ).start()
    for a in range(4):
        for side, ref in enumerate((fc1_own, fc1_other)):
            fc1_copy(ref.at[:, a * sub : (a + 1) * sub], side, table_ref[16 + a])
    for s, j, *refs, base in sources:
        for side in range(2):
            fc1_copy(refs[side].at[base : base + half, :], side, table_ref[4 * s + j])
    for a in range(4):
        for side, ref in enumerate((fc2_own, fc2_other)):
            for i in range(2):
                fc2_copy(
                    ref.at[a * sub : (a + 1) * sub, i * sub : (i + 1) * sub], side, i, table_ref[16 + a]
                )
    for s, j, *refs, base in sources:
        for side in range(2):
            for i in range(2):
                low = base + half + i * sub
                fc2_copy(refs[side].at[low : low + sub, :], side, i, table_ref[4 * s + j])
    back_v[...] = jnp.zeros_like(back_v)

    def lanes_of(i):
        return pl.ds(pl.multiple_of((table_ref[28] ^ i) * half, half), half)

    sums_ref[...] = jnp.zeros_like(sums_ref)

    pltpu.make_async_copy(proj_v, proj_v, sem_proj).wait()
    for i in range(2):
        cols = slice(i * half, (i + 1) * half)
        middle_v[:, cols] = input_ref[:, lanes_of(i)].astype(f32) + (
            dot_nn(att_ref[...], proj_v[:, cols]) + vector_ref[2:3, cols]
        )

    @functools.partial(rows_of, total_rows)
    def _(rows):
        normal, _ = unit_rows(middle_v[rows, :])
        norm_ref[rows, :] = (normal * vector_ref[3:4, :] + vector_ref[4:5, :]).astype(bf16)

    @pl.loop(0, chunks)
    def _(k):
        span = pl.ds(pl.multiple_of(k * FF_CHUNK, FF_CHUNK), FF_CHUNK)
        pltpu.make_async_copy(fc1_v.at[:, span], fc1_v.at[:, span], sem_one.at[k]).wait()
        a = k // 2
        bias = jnp.concatenate(
            [
                small_ref[table_ref[24 + 2 * (k % 2) + i], pl.ds(a, 1), :]
                for i in range(FF_CHUNK // sub)
            ],
            axis=1,
        )
        pre = dot_nn(norm_ref[...], fc1_v[:, span]) + bias
        cdf = 0.5 * (1.0 + lax.erf(pre * ROOT_HALF))
        hidden_ref[:, span] = (pre * cdf).astype(bf16)
        slope = cdf + pre * jnp.exp(-0.5 * pre * pre) * DENSITY_FACTOR
        pre_ref[:, span] = slope.astype(bf16)

    pltpu.make_async_copy(fc2_v, fc2_v, sem_two).wait()
    for i in range(2):
        cols = slice(i * half, (i + 1) * half)
        total = middle_v[:, cols] + (dot_nn(hidden_ref[...], fc2_v[:, cols]) + vector_ref[5:6, cols])
        out_ref[:, lanes_of(i)] = total.astype(bf16)
        differ = total - target_ref[:, lanes_of(i)].astype(f32)
        weighted = valid_ref[...] * differ
        sums_ref[0:1, cols] = jnp.sum(weighted * differ, axis=0, keepdims=True)
        grad = factor_ref[0] * weighted
        grad_mid_ref[:, cols] = grad
        low = grad.astype(bf16)
        grad_low_ref[:, cols] = low
        sums_ref[1:2, cols] = jnp.sum(low.astype(f32), axis=0, keepdims=True)

    @pl.loop(0, chunks)
    def _(k):
        span = pl.ds(pl.multiple_of(k * FF_CHUNK, FF_CHUNK), FF_CHUNK)
        back = dot_nt(grad_low_ref[...], fc2_v[span, :])
        back = (back * pre_ref[:, span].astype(f32)).astype(bf16)
        pre_ref[:, span] = back
        hidden_sum_ref[0:1, span] = jnp.sum(back.astype(f32), axis=0, keepdims=True)
        back_v[...] += dot_nt(back, fc1_v[:, span])

    @functools.partial(rows_of, total_rows)
    def _(rows):
        normal, spread = unit_rows(middle_v[rows, :])
        upstream = back_v[rows, :]
        inner = upstream * vector_ref[3:4, :]
        center = jnp.mean(inner, axis=-1, keepdims=True)
        slope = jnp.mean(inner * normal, axis=-1, keepdims=True)
        grad = grad_mid_ref[rows, :] + spread * (inner - center - normal * slope)
        grad_mid_ref[rows, :] = grad
        low = grad.astype(bf16)
        mid_low_ref[rows, :] = low
        sums_ref[2:3, :] += jnp.sum(upstream * normal, axis=0, keepdims=True)
        sums_ref[3:4, :] += jnp.sum(upstream, axis=0, keepdims=True)
        sums_ref[4:5, :] += jnp.sum(low.astype(f32), axis=0, keepdims=True)

    for j, (ref, at) in enumerate(((up_own_ref, 0), (up_give_ref, 0), (up_own_ref, 1), (up_give_ref, 1))):
        grad = dot_nt(mid_low_ref[...], proj_v[j * heads : (j + 1) * heads, :])
        ref[:, at * heads : (at + 1) * heads] = grad.astype(bf16)


def middle_block(table, factor, att, inputs, target, valid, vectors, smalls, pieces):
    rows, width = att.shape
    hidden = 4 * pieces[0].shape[1]
    vmem = pl.BlockSpec(memory_space=pltpu.VMEM)
    smem = pl.BlockSpec(memory_space=pltpu.SMEM)
    anywhere = pl.BlockSpec(memory_space=pl.ANY)
    f32, bf16 = jnp.float32, jnp.bfloat16

    def result(columns, dtype):
        return jax.ShapeDtypeStruct((rows, columns), dtype)

    return pl.pallas_call(
        middle_kernel,
        out_shape=(
            result(width, bf16),
            result(hidden, bf16),
            result(hidden, bf16),
            result(width, bf16),
            result(width, bf16),
            result(width, bf16),
            result(width, f32),
            result(width // 2, bf16),
            result(width // 2, bf16),
            jax.ShapeDtypeStruct((1, hidden), f32),
            jax.ShapeDtypeStruct((8, width), f32),
        ),
        in_specs=[smem] * 2 + [vmem] * 6 + [anywhere] * 10,
        out_specs=[vmem] * 11,
        scratch_shapes=[
            pltpu.VMEM((width, hidden), bf16),
            pltpu.VMEM((hidden, width), bf16),
            pltpu.VMEM((width, width), bf16),
            pltpu.VMEM((rows, width), f32),
            pltpu.VMEM((rows, width), f32),
            pltpu.SemaphoreType.DMA((hidden // FF_CHUNK,)),
            pltpu.SemaphoreType.DMA,
            pltpu.SemaphoreType.DMA,
        ],
        compiler_params=pltpu.CompilerParams(vmem_limit_bytes=62 << 20),
        cost_estimate=pl.CostEstimate(
            flops=2 * rows * width * hidden, bytes_accessed=44 << 20, transcendentals=0
        ),
        name="middle_block",
    )(table, factor, att, inputs, target, valid, vectors, smalls, *pieces)


def swap(values, axis, mask, size):
    return lax.ppermute(values, axis, [(i, i ^ mask) for i in range(size)])


def over_row(values):
    return swap(values, "row", 1, 2)


def over_dp(values, mask):
    return swap(values, "dp", mask, 4)


def over_col(values, mask):
    return swap(values, "col", mask, 4)


def cut(values, index, size, axis=0):
    return lax.dynamic_slice_in_dim(values, index * size, size, axis)


def place(pieces, index_of, axis):
    size = pieces[0].shape[axis]
    shape = list(pieces[0].shape)
    shape[axis] = size * len(pieces)
    whole = jnp.zeros(shape, pieces[0].dtype)
    for s, piece in enumerate(pieces):
        whole = lax.dynamic_update_slice_in_dim(whole, piece, index_of(s) * size, axis)
    return whole


def copies(listed, sem_ref):
    for index, (source, target) in enumerate(listed):
        pltpu.make_async_copy(source, target, sem_ref.at[index]).start()
    for index, (source, target) in enumerate(listed):
        pltpu.make_async_copy(source, target, sem_ref.at[index]).wait()


def slab_kernel(places_ref, fc1_ref, fc2_ref, proj_ref, qkv_ref, small_ref, out_ref, sem_ref):
    half, sub = fc1_ref.shape[0], fc1_ref.shape[1] // 4
    part, deep = proj_ref.shape[0] // 4, half // 4
    mine = places_ref[0]
    fc2 = fc2_ref.at[pl.ds(pl.multiple_of(mine * sub, sub), sub)]
    proj = proj_ref.at[pl.ds(pl.multiple_of(mine * part, part), part)]
    listed = [(fc1_ref.at[:, pl.ds(pl.multiple_of(mine * sub, sub), sub)], half)]
    listed += [(fc2.at[:, i * sub : (i + 1) * sub], sub) for i in range(2)]
    listed += [(proj.at[:, i * sub : (i + 1) * sub], part) for i in range(2)]
    listed += [(small_ref, small_ref.shape[0])]
    rows = pl.ds(pl.multiple_of(mine * deep, deep), deep)
    listed += [(qkv_ref.at[k, rows], deep) for k in range(3)]
    pairs, at = [], 0
    for source, count in listed:
        pairs.append((source, out_ref.at[at : at + count]))
        at += count
    copies(pairs, sem_ref)


def make_slab(places, fc1, fc2, proj, qkv, small):
    half, sub = fc1.shape[0], fc1.shape[1] // 4
    rows = half + 2 * sub + proj.shape[0] // 2 + small.shape[0] + 3 * (half // 4)
    anywhere = pl.BlockSpec(memory_space=pl.ANY)
    return pl.pallas_call(
        slab_kernel,
        out_shape=jax.ShapeDtypeStruct((rows, sub), fc1.dtype),
        in_specs=[pl.BlockSpec(memory_space=pltpu.SMEM)] + [anywhere] * 5,
        out_specs=pl.BlockSpec(memory_space=pltpu.VMEM),
        scratch_shapes=[pltpu.SemaphoreType.DMA((9,))],
        cost_estimate=small_cost(100000000),
        name="make_slab",
    )(places, fc1, fc2, proj, qkv, small)


def far_qkv_kernel(base, places_ref, mine_ref, theirs_ref, out_ref, sem_ref):
    sub = mine_ref.shape[1]
    half = out_ref.shape[0] // 2
    deep, step = half // 4, mine_ref.shape[0] // 4
    pairs = []
    for side, ref in enumerate((mine_ref, theirs_ref)):
        for s in range(4):
            rows = pl.ds(pl.multiple_of(side * half + places_ref[s] * deep, deep), deep)
            for k in range(3):
                at = s * step + base + k * deep
                pairs.append((ref.at[at : at + deep], out_ref.at[rows, k * sub : (k + 1) * sub]))
    copies(pairs, sem_ref)


def far_qkv(places, mine, theirs, base, width):
    anywhere = pl.BlockSpec(memory_space=pl.ANY)
    return pl.pallas_call(
        functools.partial(far_qkv_kernel, base),
        out_shape=jax.ShapeDtypeStruct((width, 3 * mine.shape[1]), mine.dtype),
        in_specs=[pl.BlockSpec(memory_space=pltpu.SMEM)] + [anywhere] * 2,
        out_specs=pl.BlockSpec(memory_space=pltpu.VMEM),
        scratch_shapes=[pltpu.SemaphoreType.DMA((24,))],
        cost_estimate=small_cost(100000000),
        name="far_qkv",
    )(places, mine, theirs)


VECTORS = 32


def put_split(ref, at, values):
    high = values.astype(jnp.bfloat16)
    low = (values - high.astype(jnp.float32)).astype(jnp.bfloat16)
    columns = values.shape[1]
    ref[at : at + VECTORS, 0:columns] = high
    ref[at + VECTORS : at + 2 * VECTORS, 0:columns] = low
    rest = ref.shape[1] - columns
    if rest:
        ref[at : at + 2 * VECTORS, columns:] = jnp.zeros((2 * VECTORS, rest), jnp.bfloat16)


def get_split(ref, at, columns):
    high = ref[at : at + VECTORS, 0:columns].astype(jnp.float32)
    return high + ref[at + VECTORS : at + 2 * VECTORS, 0:columns].astype(jnp.float32)


def framed(ref, rows, flip, half):
    return jnp.concatenate(
        [ref[rows, pl.ds(pl.multiple_of((flip ^ i) * half, half), half)] for i in range(2)], axis=1
    ).astype(jnp.float32)


def token_back_kernel(
    flip_ref, near_ref, far_ref, w_near, w_far, own_states, other_states, own_ref, give_ref, sums_ref, other_v
):
    rows_all, half = own_ref.shape[0], own_ref.shape[1] // 2
    sums_ref[...] = jnp.zeros_like(sums_ref)
    for start, out_ref in ((rows_all, other_v), (0, own_ref)):
        rows = slice(start, start + rows_all)
        out_ref[...] = dot_nt(near_ref[rows, :], w_near[...]) + dot_nt(far_ref[rows, :], w_far[...])
    for out_ref, states in ((other_v, other_states), (own_ref, own_states)):

        @functools.partial(rows_of, rows_all)
        def _(rows, out_ref=out_ref, states=states):
            normal, _ = unit_rows(framed(states, rows, flip_ref[0], half))
            upstream = out_ref[rows, :]
            sums_ref[0:1, :] += jnp.sum(upstream * normal, axis=0, keepdims=True)
            sums_ref[1:2, :] += jnp.sum(upstream, axis=0, keepdims=True)
            if out_ref is other_v:
                give_ref[rows, :] = upstream.astype(jnp.bfloat16)


def token_back(flip, near, far, w_near, w_far, own_states, other_states):
    rows, width = own_states.shape
    vmem = pl.BlockSpec(memory_space=pltpu.VMEM)
    return pl.pallas_call(
        token_back_kernel,
        out_shape=(
            jax.ShapeDtypeStruct((rows, width), jnp.float32),
            jax.ShapeDtypeStruct((rows, width), jnp.bfloat16),
            jax.ShapeDtypeStruct((2, width), jnp.float32),
        ),
        in_specs=[pl.BlockSpec(memory_space=pltpu.SMEM)] + [vmem] * 6,
        out_specs=(vmem,) * 3,
        scratch_shapes=[pltpu.VMEM((rows, width), jnp.float32)],
        compiler_params=pltpu.CompilerParams(vmem_limit_bytes=40 << 20),
        cost_estimate=small_cost(100000000),
        name="token_back",
    )(flip, near, far, w_near, w_far, own_states, other_states)


def last_kernel(flip_ref, own_ref, taken_ref, states_ref, mid_ref, vector_ref, out_ref):
    half = own_ref.shape[1] // 2
    upstream = own_ref[...] + taken_ref[...].astype(jnp.float32)
    everything = slice(0, own_ref.shape[0])
    normal, spread = unit_rows(framed(states_ref, everything, flip_ref[0], half))
    inner = upstream * vector_ref[0:1, :]
    center = jnp.mean(inner, axis=-1, keepdims=True)
    slope = jnp.mean(inner * normal, axis=-1, keepdims=True)
    back = mid_ref[...] + spread * (inner - center - normal * slope)
    for i in range(2):
        lanes = pl.ds(pl.multiple_of((flip_ref[0] ^ i) * half, half), half)
        out_ref[:, lanes] = back[:, i * half : (i + 1) * half].astype(jnp.bfloat16)


def last_norm(flip, own, taken, states, mid, vectors):
    rows, width = own.shape
    block = pl.BlockSpec((ROWS, width), lambda i: (i, 0))
    whole = pl.BlockSpec(vectors.shape, lambda i: (0, 0))
    return pl.pallas_call(
        last_kernel,
        grid=(rows // ROWS,),
        out_shape=jax.ShapeDtypeStruct((rows, width), jnp.bfloat16),
        in_specs=[pl.BlockSpec(memory_space=pltpu.SMEM)] + [block] * 4 + [whole],
        out_specs=block,
        cost_estimate=small_cost(500000000),
        name="last_norm",
    )(flip, own, taken, states, mid, vectors)


def far_grads_kernel(
    turned_ref, grad_ref, sums_ref, hidden_ref, norm_ref, near_ref, far_ref, keep_ref, out_ref, kept_ref
):
    half = keep_ref.shape[1]
    width = near_ref.shape[1] // 3
    shared = [hidden_ref[0:1, i * half : (i + 1) * half] for i in range(8)]
    for ref in (near_ref, far_ref):
        shared.append(jnp.concatenate([ref[0:1, 0:width], ref[0:1, 2 * width :]], axis=1))
    shared.append(sums_ref[0:1, 0:half] + sums_ref[0:1, half:])
    blank = jnp.zeros((VECTORS - 6 - len(shared), half), jnp.float32)

    def rows(lanes):
        split = [sums_ref[i : i + 1, lanes] for i in (2, 3, 4, 1)]
        split += [norm_ref[i : i + 1, lanes] for i in range(2)]
        return jnp.concatenate(split + shared + [blank], axis=0)

    keep_ref[...] = rows(slice(0, half))
    put_split(out_ref, half, rows(slice(half, 2 * half)))
    out_ref[0:half, :] = dot_nn(turned_ref[half:, :], grad_ref[...]).astype(jnp.bfloat16)
    kept_ref[...] = dot_nn(turned_ref[0:half, :], grad_ref[...])


def after_row_kernel(
    places_ref, kept_ref, taken_ref, keep_ref, near_ref, near_taken, near_own_ref, far_own_ref, sum_ref, *outs
):
    deep = far_own_ref.shape[0]
    vectors = keep_ref[...] + get_split(taken_ref, 4 * deep, keep_ref.shape[1])
    sum_ref[...] = vectors
    for s in range(4):
        rows = pl.ds(pl.multiple_of(places_ref[s] * deep, deep), deep)
        far = kept_ref[rows, :] + taken_ref[rows, :].astype(jnp.float32)
        if s == 0:
            far_own_ref[...] = far
        else:
            outs[s - 1][0:deep, :] = far.astype(jnp.bfloat16)
            put_split(outs[s - 1], deep, vectors)
        if s % 2 == 0:
            at = slice(s // 2 * deep, (s // 2 + 1) * deep)
            near = near_ref[rows, :].astype(jnp.float32) + near_taken[at, :].astype(jnp.float32)
            if s == 0:
                near_own_ref[...] = near
            else:
                outs[s - 1][deep + 2 * VECTORS :, :] = near.astype(jnp.bfloat16)


def after_plane_kernel(near_ref, far_ref, sum_ref, *refs):
    takes, (keep_ref, vector_ref, give_ref, small_ref) = refs[:3], refs[3:]
    deep = far_ref.shape[0]
    vectors, far = sum_ref[...], far_ref[...]
    keep_ref[...] = near_ref[...] + takes[1][deep + 2 * VECTORS :, :].astype(jnp.float32)
    for take in takes:
        vectors = vectors + get_split(take, deep, vectors.shape[1])
        far = far + take[0:deep, :].astype(jnp.float32)
    vector_ref[...] = vectors
    give_ref[0:deep, :] = far.astype(jnp.bfloat16)
    put_split(give_ref, deep, vectors)
    put_split(small_ref, 0, vectors)


def after_cols_kernel(keep_ref, vector_ref, one_ref, two_ref, three_ref, out_ref, total_ref):
    deep = keep_ref.shape[0]
    out_ref[...] = (keep_ref[...] + two_ref[0:deep, :].astype(jnp.float32)).astype(jnp.bfloat16)
    columns = vector_ref.shape[1]
    far = get_split(two_ref, deep, columns)
    total = vector_ref[...] + far
    total = total + get_split(one_ref, 0, columns) + get_split(three_ref, 0, columns)
    total_ref[...] = total
    total_ref[14:15, :] = vector_ref[14:15, :] + far[15:16, :]


def on_chip(kernel, shapes, name, *args, tables=0):
    vmem = pl.BlockSpec(memory_space=pltpu.VMEM)
    return pl.pallas_call(
        kernel,
        out_shape=tuple(jax.ShapeDtypeStruct(*s) for s in shapes),
        in_specs=[pl.BlockSpec(memory_space=pltpu.SMEM)] * tables + [vmem] * (len(args) - tables),
        out_specs=(vmem,) * len(shapes),
        cost_estimate=small_cost(100000000),
        name=name,
    )(*args)


def wide_kernel(with_proj, places_ref, small_ref, big_ref, taken_ref, *refs):
    if with_proj:
        proj_kept, proj_taken, *refs = refs
    *outs, turned_v = refs
    half, sub = turned_v.shape[0], turned_v.shape[0] // 2
    span = big_ref.shape[1] // 4
    part = 256 // 4 if not with_proj else proj_kept.shape[0] // 16
    turned_v[...] = small_ref[:, 0:half].T
    for s in range(4):
        lanes = pl.ds(pl.multiple_of(places_ref[s] * span, span), span)
        block = dot_nn(turned_v[...], big_ref[:, lanes]) + taken_ref[:, lanes].astype(jnp.float32)
        block = block.astype(jnp.bfloat16)
        for side, (go, slot) in enumerate(((s % 2, s // 2), (s // 2, s % 2))):
            out = outs[2 * side + go]
            rows = slice(slot * sub, (slot + 1) * sub)
            out[rows, 0:span] = block[side * sub : (side + 1) * sub]
            if with_proj:
                at = side * sub
                for j in range(4):
                    start = pl.multiple_of(4 * j * part + places_ref[s] * part, part)
                    piece = proj_kept[pl.ds(start, part), at : at + sub] + proj_taken[
                        pl.ds(start, part), at : at + sub
                    ].astype(jnp.float32)
                    low = slot * sub + j * part
                    out[low : low + part, span:] = piece.astype(jnp.bfloat16)


def wide_grads(places, small, big, taken, proj=()):
    half = small.shape[1] // 2
    columns = big.shape[1] // 4 + (half // 2 if proj else 0)
    vmem = pl.BlockSpec(memory_space=pltpu.VMEM)
    return pl.pallas_call(
        functools.partial(wide_kernel, bool(proj)),
        out_shape=(jax.ShapeDtypeStruct((half, columns), jnp.bfloat16),) * 4,
        in_specs=[pl.BlockSpec(memory_space=pltpu.SMEM)] + [vmem] * (3 + len(proj)),
        out_specs=(vmem,) * 4,
        scratch_shapes=[pltpu.VMEM((half, small.shape[0]), jnp.bfloat16)],
        compiler_params=pltpu.CompilerParams(vmem_limit_bytes=44 << 20),
        cost_estimate=small_cost(3000000000),
        name="wide_grads",
    )(places, small, big, taken, *proj)


def plane_sum_kernel(*refs):
    sub = refs[4].shape[0]
    for side in range(2):
        kept, taken = refs[2 * side : 2 * side + 2]
        for slot in range(2):
            rows = slice(slot * sub, (slot + 1) * sub)
            total = kept[rows, :].astype(jnp.float32) + taken[rows, :].astype(jnp.float32)
            refs[4 + 2 * side + slot][...] = total.astype(jnp.bfloat16)


def cols_out_kernel(places_ref, *refs):
    outs = refs[4:]
    sub = refs[0].shape[0]
    columns = refs[0].shape[1]
    part = (outs[0].shape[0] - 2 * sub) // 2
    for side in range(2):
        kept, taken = refs[2 * side : 2 * side + 2]
        for j in range(4):
            lanes = pl.ds(pl.multiple_of(places_ref[4 + j] * sub, sub), sub)
            total = kept[:, lanes].astype(jnp.float32) + taken[:, lanes].astype(jnp.float32)
            outs[j][side * sub : (side + 1) * sub, :] = total.astype(jnp.bfloat16)
            if part:
                rows = slice(j * part, (j + 1) * part)
                total = kept[rows, columns - sub :].astype(jnp.float32)
                total = total + taken[rows, columns - sub :].astype(jnp.float32)
                low = 2 * sub + side * part
                outs[j][low : low + part, :] = total.astype(jnp.bfloat16)


def mine_kernel(*refs):
    out_ref, at = refs[8], 0
    for group in (refs[0:4], refs[4:8]):
        total = group[0][...].astype(jnp.float32)
        for ref in group[1:]:
            total = total + ref[...].astype(jnp.float32)
        out_ref[at : at + total.shape[0], :] = total.astype(jnp.bfloat16)
        at += total.shape[0]


def finish_kernel(part_rows, places_ref, *refs):
    pieces, (fc2_ref, fc1_ref, proj_ref) = refs[:4], refs[4:]
    half, sub = fc1_ref.shape[0], pieces[0].shape[1]
    for s, piece in enumerate(pieces):
        at = places_ref[s]
        rows = pl.ds(pl.multiple_of(at * sub, sub), sub)
        fc2_ref[rows, :] = piece[0:half, :].astype(jnp.float32).T
        fc1_ref[:, rows] = piece[half : 2 * half, :].astype(jnp.float32)
        rows = pl.ds(pl.multiple_of(at * part_rows, part_rows), part_rows)
        for i in range(2):
            low = 2 * half + i * part_rows
            proj_ref[rows, i * sub : (i + 1) * sub] = piece[low : low + part_rows, :].astype(jnp.float32)


def finish_qkv_kernel(places_ref, *refs):
    out_ref = refs[4]
    deep, width = refs[0].shape[0], out_ref.shape[2]
    for s in range(4):
        rows = pl.ds(pl.multiple_of(places_ref[s] * deep, deep), deep)
        for k in range(3):
            out_ref[k, rows, :] = refs[s][:, k * width : (k + 1) * width].astype(jnp.float32)


def finish(places, pieces, part_rows):
    rows, sub = pieces[0].shape
    half = (rows - 2 * part_rows) // 2
    vmem = pl.BlockSpec(memory_space=pltpu.VMEM)
    return pl.pallas_call(
        functools.partial(finish_kernel, part_rows),
        out_shape=(
            jax.ShapeDtypeStruct((4 * sub, half), jnp.float32),
            jax.ShapeDtypeStruct((half, 4 * sub), jnp.float32),
            jax.ShapeDtypeStruct((4 * part_rows, half), jnp.float32),
        ),
        in_specs=[pl.BlockSpec(memory_space=pltpu.SMEM)] + [vmem] * 4,
        out_specs=[vmem] * 3,
        cost_estimate=small_cost(100000000),
        name="finish",
    )(places, *pieces)


def finish_qkv(places, pieces):
    deep, width = pieces[0].shape
    vmem = pl.BlockSpec(memory_space=pltpu.VMEM)
    return pl.pallas_call(
        finish_qkv_kernel,
        out_shape=jax.ShapeDtypeStruct((3, 4 * deep, width // 3), jnp.float32),
        in_specs=[pl.BlockSpec(memory_space=pltpu.SMEM)] + [vmem] * 4,
        out_specs=vmem,
        cost_estimate=small_cost(100000000),
        name="finish_qkv",
    )(places, *pieces)


def tie(value, *others):
    return lax.optimization_barrier((value, *others))[0]


def add_up(own, taken):
    total = own.astype(jnp.float32)
    for piece in taken:
        total = total + piece.astype(jnp.float32)
    return total


def local_paired(
    states,
    ln1_gain,
    ln1_bias,
    w_qkv,
    q_bias,
    v_bias,
    w_proj,
    proj_bias,
    ln2_gain,
    ln2_bias,
    w_fc1,
    fc1_bias,
    w_fc2,
    fc2_bias,
    teacher,
    loss_mask,
    lengths,
):
    f32, bf16 = jnp.float32, jnp.bfloat16
    dp = lax.axis_index("dp")
    row = lax.axis_index("row")
    col = lax.axis_index("col")
    local_rows, width = states.shape
    half = width // 2
    head_width = w_qkv.shape[2]
    hidden_width = w_fc1.shape[1]
    sub = hidden_width // 4
    span = 4 * sub
    part_rows = head_width // 4
    clip = (dp * 2 + row) * 2 + col // 2
    second = col % 2

    def quarter(s):
        return dp ^ s

    def frame(values):
        return jnp.where(
            row == 0, values, jnp.concatenate([values[:, half:], values[:, :half]], axis=1)
        )

    places = jnp.stack([dp ^ s for s in range(4)] + [col ^ j for j in range(4)]).astype(jnp.int32)
    flip = row.reshape(1).astype(jnp.int32)
    states_other = over_col(states, 1)
    small = jnp.concatenate(
        [
            fc1_bias.reshape(4, sub),
            q_bias.reshape(1, sub),
            v_bias.reshape(1, sub),
            jnp.zeros((10, sub), bf16),
        ],
        axis=0,
    )
    slab = make_slab(places, w_fc1, w_fc2, w_proj, w_qkv.transpose(1, 0, 2), small)
    unit_rows_total = half + 2 * sub + 2 * part_rows + small.shape[0]
    small_at = unit_rows_total - small.shape[0]
    two = over_col(slab, 2)
    w_qkv2 = w_qkv.reshape(half, 3 * head_width)
    w_qkv2 = tie(w_qkv2, slab)
    qkv_near = jnp.concatenate([w_qkv2, over_row(w_qkv2)], axis=0)
    vectors = jnp.stack([ln1_gain, ln1_bias, proj_bias, ln2_gain, ln2_bias, fc2_bias])
    vectors, states, teacher, loss_mask = lax.optimization_barrier(
        (vectors, states, teacher, loss_mask, slab)
    )[:4]
    vectors = jnp.concatenate([vectors, over_row(vectors)], axis=1).astype(f32)
    fc1_other, fc2_other, proj_other = over_row(w_fc1), over_row(w_fc2), over_row(w_proj)
    two = tie(two, fc1_other, fc2_other, proj_other)
    two_x, two_y = over_dp(two, 1), over_dp(two, 2)
    states_other = tie(states_other, two)

    all_clips = lengths.shape[0]
    valid_all = (
        loss_mask.reshape(all_clips, L) * (jnp.arange(L)[None, :] < lengths[:, None])
    ).astype(f32)
    valid_total = jnp.maximum(jnp.sum(valid_all), 1.0)
    first_row = ((dp * 2 + row) * 4 + col) * local_rows
    valid = lax.dynamic_slice_in_dim(valid_all.reshape(all_clips * L), first_row, local_rows)
    my_length = lax.dynamic_slice_in_dim(lengths, clip, 1)
    spot = jnp.arange(L)
    position = jnp.where(
        spot < local_rows, second * local_rows + spot, (1 - second) * local_rows + spot - local_rows
    )
    key_bias = jnp.where(position < my_length, 0.0, MASKED).astype(f32)
    key_bias = jnp.broadcast_to(key_bias[:, None], (L, 128))

    gain_one, shift_one = vectors[0], vectors[1]
    norm_one, _, _ = normalize(frame(states).astype(f32), gain_one, shift_one)
    norm_other, _, _ = normalize(frame(states_other).astype(f32), gain_one, shift_one)
    tokens_one = jnp.concatenate([norm_one.astype(bf16), norm_other.astype(bf16)], axis=0)

    zero_bias = jnp.zeros((head_width,), f32)
    score_scale = HD**-0.5
    scale = jnp.where(jnp.arange(3 * head_width) < head_width, score_scale, 1.0).astype(bf16)
    split = local_rows // QT * QT
    later = L - split
    over = local_rows - split

    def project(matrix, q_add, v_add):
        projected = jnp.dot(tokens_one, matrix, preferred_element_type=f32)
        add = jnp.concatenate([q_add.astype(f32), zero_bias, v_add.astype(f32)])
        return (projected + add[None]).astype(bf16) * scale[None]

    packed_near = project(qkv_near, q_bias, v_bias)
    cut_at = two.shape[0] // 32 * 16
    two_x, two_y = tie(two_x, packed_near), tie(two_y, packed_near)
    two_low, two_high = over_dp(two_y[:cut_at], 1), over_dp(two_x[cut_at:], 2)
    one_give = jnp.concatenate([slab[:unit_rows_total], two[:unit_rows_total]], axis=0)
    one = over_col(tie(one_give, states_other), 1)
    near_late, near_late_lse = attend(tie(packed_near, two_x, two_y, one), key_bias, split, later)
    two_low, two_high = tie(two_low, near_late), tie(two_high, near_late)
    two_all = jnp.concatenate([two, two_x, two_y, two_low, two_high], axis=0)
    two_theirs = over_row(two_all)
    near_other = over_col(near_late[over:], 1)
    one_x, one_y = over_dp(one, 1), over_dp(one, 2)
    near_soon, near_soon_lse = attend(
        tie(packed_near, two_all, near_late, one), key_bias, 0, split
    )
    two_theirs = tie(two_theirs, near_soon)
    qkv_far = far_qkv(places, two_all, two_theirs, unit_rows_total, width)
    far_small = two_all[small_at : small_at + small.shape[0]]
    packed_far = project(qkv_far, far_small[4], far_small[5])
    packed_far = tie(packed_far, one, near_other)
    far_late, far_late_lse = attend(packed_far, key_bias, split, later)
    far_other = over_col(far_late[over:], 1)
    one_x, one_y = tie(one_x, far_late), tie(one_y, far_late)
    cut_at = one.shape[0] // 2
    one_low, one_high = over_dp(one_y[:cut_at], 1), over_dp(one_x[cut_at:], 2)
    far_soon, far_soon_lse = attend(tie(packed_far, one_x, one_y, far_late), key_bias, 0, split)
    one_low, one_high = tie(one_low, far_soon), tie(one_high, far_soon)
    one_all = jnp.concatenate([one, one_x, one_y, one_low, one_high], axis=0)
    one_all = tie(one_all, far_other)
    turned = tie(tokens_one, far_late).T
    one_theirs = over_row(one_all)
    attended_rows = jnp.concatenate(
        [
            jnp.concatenate([near_soon, near_late[:over]], axis=0),
            near_other,
            jnp.concatenate([far_soon, far_late[:over]], axis=0),
            far_other,
        ],
        axis=1,
    )

    table = jnp.stack(
        [(dp ^ s) * 4 + (col ^ j) for s in range(4) for j in range(4)]
        + [a * 4 + col for a in range(4)]
        + [dp ^ s for s in range(4)]
        + [col ^ b for b in range(4)]
        + [row]
    ).astype(jnp.int32)
    at = unit_rows_total + small_at
    smalls = jnp.stack(
        [small, one_all[small_at : small_at + 16], two_all[small_at : small_at + 16], one_all[at : at + 16]]
    ).astype(f32)
    loss_scale = all_clips * L * width / 2.0
    factor = (loss_scale * 2.0 / (valid_total * width)).reshape(1)
    (
        outputs,
        hidden,
        grad_pre,
        norm_two,
        grad_low,
        mid_low,
        grad_mid,
        up_own,
        up_give,
        hidden_sum,
        sums,
    ) = middle_block(
        table,
        factor,
        attended_rows,
        states,
        teacher,
        valid[:, None],
        vectors,
        smalls,
        (
            w_fc1,
            fc1_other,
            w_fc2,
            fc2_other,
            w_proj,
            proj_other,
            two_all,
            two_theirs,
            one_all,
            one_theirs,
        ),
    )
    up_far = over_col(up_give, 1)

    def joined(kept, taken):
        return (kept.astype(f32) + taken.astype(f32)).astype(bf16)

    give_fc2 = over_row(dot_tn(grad_low[:, half:], hidden).astype(bf16))
    give_fc1 = over_row(dot_tn(norm_two[:, half:], grad_pre).astype(bf16))
    give_proj = over_row(dot_tn(attended_rows, mid_low[:, half:]).astype(bf16))
    kept_proj = dot_tn(attended_rows, mid_low[:, :half])

    def plane_first(wide):
        keep_x, give_x, keep_y, give_y = wide
        return (keep_x, keep_y), (give_x, give_y), (over_dp(give_x, 1), over_dp(give_y, 2))

    def plane_second(keep, taken):
        shape = ((keep[0].shape[0] // 2, keep[0].shape[1]), bf16)
        keep_x, give_x, keep_y, give_y = on_chip(
            plane_sum_kernel, [shape] * 4, "plane_sum", keep[0], taken[0], keep[1], taken[1]
        )
        return (keep_x, keep_y), (give_x, give_y), (over_dp(give_x, 2), over_dp(give_y, 1))

    def cols_out(keep, taken, rows):
        blocks = on_chip(
            cols_out_kernel,
            [((rows, sub), bf16)] * 4,
            "cols_out",
            *(places, keep[0], taken[0], keep[1], taken[1]),
            tables=1,
        )
        return blocks, [over_col(blocks[j], j) for j in (1, 2, 3)]

    def all_tied(values, *others):
        return [tie(v, *others) for v in values]

    wide = wide_grads(places, grad_low, hidden, give_fc2)
    fc2_keep, fc2_give, fc2_taken = plane_first(wide)
    wide = wide_grads(
        places, tie(norm_two, *fc2_give), grad_pre, give_fc1, (kept_proj, give_proj)
    )
    fc1_keep, fc1_give, fc1_taken = plane_first(wide)

    packed_near = tie(packed_near, *fc2_give, *fc1_give)
    part_near = attend_back(packed_near, key_bias, near_soon_lse, near_soon, up_own, None, 0, 0)
    fc2_keep, fc2_give, fc2_taken = plane_second(fc2_keep, all_tied(fc2_taken, part_near[0]))

    packed_far = tie(packed_far, *fc2_give, part_near[0])
    part_far = attend_back(
        packed_far, key_bias, far_soon_lse, far_soon, up_own, None, head_width, 0
    )
    fc2_blocks, fc2_cols = cols_out(fc2_keep, all_tied(fc2_taken, part_far[0]), 2 * sub)
    fc1_keep, fc1_give, fc1_taken = plane_second(fc1_keep, all_tied(fc1_taken, part_far[0]))

    packed_near = tie(packed_near, *fc2_blocks, *fc1_give)
    grad_near, near_sums = attend_back(
        packed_near, key_bias, near_late_lse, near_late, up_own, up_far, 0, split, part_near
    )
    fc2_cols = all_tied(fc2_cols, grad_near)
    fc1_blocks, fc1_cols = cols_out(
        fc1_keep, all_tied(fc1_taken, grad_near, *fc2_cols), 2 * sub + 2 * part_rows
    )
    near_tied = tie(grad_near, *fc1_blocks)
    near_row = over_row(dot_tn(tokens_one[:, half:], near_tied).astype(bf16))
    wide_near = joined(dot_tn(tokens_one[:, :half], near_tied), near_row)
    deep = half // 4
    near_give = jnp.concatenate([cut(wide_near, quarter(s), deep) for s in (1, 3)], axis=0)
    near_taken = over_dp(near_give, 1)

    packed_far = tie(packed_far, near_give, *fc1_blocks, *fc2_cols)
    grad_far, far_sums = attend_back(
        packed_far, key_bias, far_late_lse, far_late, up_own, up_far, head_width, split, part_far
    )

    norm_own, norm_give, norm_sums = token_back(
        flip, grad_near, grad_far, qkv_near, qkv_far, states, states_other
    )
    norm_taken = over_col(norm_give, 1)
    columns, slots = grad_far.shape[1], 2 * VECTORS
    vec_keep, row_give, kept = on_chip(
        far_grads_kernel,
        [((VECTORS, half), f32), ((half + slots, columns), bf16), ((half, columns), f32)],
        "far_grads",
        *(turned, tie(grad_far, norm_give, near_taken), sums, hidden_sum, norm_sums, near_sums, far_sums),
    )
    row_taken = over_row(row_give)
    fc1_cols = all_tied(fc1_cols, row_give)
    mine_rows = fc2_blocks[0].shape[0] + fc1_blocks[0].shape[0]
    (mine,) = on_chip(
        mine_kernel,
        [((mine_rows, sub), bf16)],
        "mine",
        *(fc2_blocks[0], *fc2_cols, fc1_blocks[0], *fc1_cols),
    )
    mine_x = over_dp(mine, 1)
    near_own, far_own, vec_sum, *plane_give = on_chip(
        after_row_kernel,
        [((deep, columns), f32)] * 2
        + [((VECTORS, half), f32)]
        + [((deep + slots + (deep if s == 2 else 0), columns), bf16) for s in (1, 2, 3)],
        "after_row",
        *(places, kept, tie(row_taken, mine), vec_keep, wide_near, tie(near_taken, mine)),
        tables=1,
    )
    plane_taken = [over_dp(plane_give[s - 1], s) for s in (1, 2, 3)]
    mine_two = jnp.concatenate([mine, tie(mine_x, *plane_give)], axis=0)
    plane_taken = all_tied(plane_taken, mine_two, norm_taken)
    near_own, vec_sum, col_give, vec_give = on_chip(
        after_plane_kernel,
        [
            ((deep, columns), f32),
            ((VECTORS, half), f32),
            ((deep + slots, columns), bf16),
            ((slots, half), bf16),
        ],
        "after_plane",
        *(near_own, far_own, vec_sum, *plane_taken),
    )
    mine_y = over_dp(mine_two, 2)
    col_taken = [over_col(vec_give, 1), over_col(col_give, 2), over_col(vec_give, 3)]
    norm_taken = tie(norm_taken, col_give)
    grad_states = last_norm(flip, norm_own, norm_taken, states, grad_mid, vectors)

    qkv_mine, vec_total = on_chip(
        after_cols_kernel,
        [((deep, columns), bf16), ((VECTORS, half), f32)],
        "after_cols",
        *(near_own, vec_sum, *all_tied(col_taken, grad_states)),
    )
    qkv_back = [over_dp(qkv_mine, s) for s in (1, 2, 3)]
    mine_y = tie(mine_y, qkv_mine)
    rows = mine.shape[0]
    pieces = [mine_two[:rows], mine_two[rows:], mine_y[:rows], mine_y[rows:]]
    fc2_grad, fc1_grad, proj_grad = finish(places, pieces, part_rows)
    qkv_grad = finish_qkv(places, [qkv_mine, *all_tied(qkv_back, fc2_grad)]).transpose(1, 0, 2)

    fc1_bias_grad = lax.dynamic_index_in_dim(vec_total[6:14].reshape(4, 4, sub), col, 1, False)
    loss_value = jnp.sum(vec_total[16]) / (valid_total * width)
    return (
        outputs,
        loss_value,
        grad_states,
        vec_total[4],
        vec_total[5],
        qkv_grad,
        vec_total[14, :head_width],
        vec_total[14, head_width:],
        proj_grad,
        vec_total[2],
        vec_total[0],
        vec_total[1],
        fc1_grad,
        fc1_bias_grad.reshape(span),
        fc2_grad,
        vec_total[3],
    )


def solution(mesh):
    sizes = (mesh.shape["dp"], mesh.shape["row"], mesh.shape["col"])
    body = local_paired if sizes == PAIRED_MESH else local_general
    in_specs = (
        P(("dp", "row", "col"), None),
        P("row"),
        P("row"),
        P("row", None, "col"),
        P("col"),
        P("col"),
        P("col", "row"),
        P("row"),
        P("row"),
        P("row"),
        P("row", "col"),
        P("col"),
        P("col", "row"),
        P("row"),
        P(("dp", "row", "col"), None),
        P(),
        P(),
    )
    out_specs = (
        P(("dp", "row", "col"), None),
        P(),
        P(("dp", "row", "col"), None),
        P("row"),
        P("row"),
        P("row", None, "col"),
        P("col"),
        P("col"),
        P("col", "row"),
        P("row"),
        P("row"),
        P("row"),
        P("row", "col"),
        P("col"),
        P("col", "row"),
        P("row"),
    )
    return jax.shard_map(body, mesh=mesh, in_specs=in_specs, out_specs=out_specs, check_vma=False)
```

```python
import functools

import jax
import jax.numpy as jnp
from jax import lax
from jax.experimental import pallas as pl
from jax.experimental.pallas import tpu as pltpu
from jax.sharding import PartitionSpec as P

HD = 64
L = 1568


EPSILON = 1e-06
MASKED = -1e30
ROOT_HALF = 0.7071067811865476
DENSITY_FACTOR = 0.3989422804014327


def normalize(values, factor, offset):
    centered = values - jnp.mean(values, axis=-1, keepdims=True)
    spread = lax.rsqrt(jnp.mean(centered * centered, axis=-1, keepdims=True) + EPSILON)
    normal = centered * spread
    return (normal * factor + offset, normal, spread)


def norm_back(upstream, normal, spread, factor):
    inner = upstream * factor
    center_term = jnp.mean(inner, axis=-1, keepdims=True)
    slope_term = jnp.mean(inner * normal, axis=-1, keepdims=True)
    back = spread * (inner - center_term - normal * slope_term)
    return (back, jnp.sum(upstream * normal, axis=0), jnp.sum(upstream, axis=0))


def gelu_value(values):
    return values * (0.5 * (1.0 + lax.erf(values * ROOT_HALF)))


def gelu_slope(values):
    normal_cdf = 0.5 * (1.0 + lax.erf(values * ROOT_HALF))
    return normal_cdf + values * jnp.exp(-0.5 * values * values) * DENSITY_FACTOR


def masked_scores(queries, key_rows, length, score_scale):
    logits = (
        jnp.einsum("ihd,jhd->hij", queries, key_rows, preferred_element_type=jnp.float32)
        * score_scale
    )
    keep = jnp.arange(key_rows.shape[0]) < length
    return jnp.where(keep[None, None, :], logits, MASKED)


def attend_clip(packed, length, score_scale):
    half_span = packed.shape[0] // 2
    key_rows = packed[:, 1]
    value_rows = packed[:, 2]
    pieces = []
    totals = []
    for block_index in range(2):
        queries = packed[block_index * half_span : (block_index + 1) * half_span, 0]
        logits = masked_scores(queries, key_rows, length, score_scale)
        peak = jnp.max(logits, axis=-1, keepdims=True)
        total = peak + jnp.log(jnp.sum(jnp.exp(logits - peak), axis=-1, keepdims=True))
        weights = jnp.exp(logits - total).astype(jnp.bfloat16)
        pieces.append(
            jnp.einsum("hij,jhd->ihd", weights, value_rows, preferred_element_type=jnp.float32)
        )
        totals.append(total[..., 0])
    return (jnp.concatenate(pieces, 0), jnp.concatenate(totals, 1))


def attend_clip_back(packed, length, totals, upstream, score_scale):
    half_span = packed.shape[0] // 2
    key_rows = packed[:, 1]
    value_rows = packed[:, 2]
    grad_keys = jnp.zeros(key_rows.shape, jnp.float32)
    grad_values = jnp.zeros(value_rows.shape, jnp.float32)
    grad_queries = []
    for block_index in range(2):
        first = block_index * half_span
        queries = packed[first : first + half_span, 0]
        logits = masked_scores(queries, key_rows, length, score_scale)
        probs = jnp.exp(logits - totals[:, first : first + half_span][..., None])
        incoming = upstream[first : first + half_span]
        grad_values = grad_values + jnp.einsum(
            "hij,ihd->jhd", probs.astype(jnp.bfloat16), incoming, preferred_element_type=jnp.float32
        )
        grad_probs = jnp.einsum(
            "ihd,jhd->hij", incoming, value_rows, preferred_element_type=jnp.float32
        )
        grad_logits = (
            probs * (grad_probs - jnp.sum(probs * grad_probs, axis=-1, keepdims=True))
        ).astype(jnp.bfloat16)
        grad_queries.append(
            jnp.einsum("hij,jhd->ihd", grad_logits, key_rows, preferred_element_type=jnp.float32)
            * score_scale
        )
        grad_keys = (
            grad_keys
            + jnp.einsum("hij,ihd->jhd", grad_logits, queries, preferred_element_type=jnp.float32)
            * score_scale
        )
    return jnp.stack([jnp.concatenate(grad_queries, 0), grad_keys, grad_values], axis=1)


def local_general(
    states,
    ln1_gain,
    ln1_bias,
    w_qkv,
    q_bias,
    v_bias,
    w_proj,
    proj_bias,
    ln2_gain,
    ln2_bias,
    w_fc1,
    fc1_bias,
    w_fc2,
    fc2_bias,
    teacher,
    loss_mask,
    lengths,
):
    row_count = lax.axis_size("row")
    col_count = lax.axis_size("col")
    col_index = lax.axis_index("col")
    group_index = lax.axis_index("dp") * row_count + lax.axis_index("row")
    local_rows = states.shape[0]
    width = states.shape[1]
    group_rows = local_rows * col_count
    clip_count = group_rows // L
    head_width = w_qkv.shape[2]
    heads_here = head_width // HD
    hidden_width = w_fc1.shape[1]
    score_scale = HD ** (-0.5)
    vectors = jnp.stack([ln1_gain, ln1_bias, proj_bias, ln2_gain, ln2_bias, fc2_bias])
    qkv_full, proj_full, fc1_full, fc2_full, vector_full = (
        lax.all_gather(w_qkv, "row", axis=0, tiled=True),
        lax.all_gather(w_proj, "row", axis=1, tiled=True),
        lax.all_gather(w_fc1, "row", axis=0, tiled=True),
        lax.all_gather(w_fc2, "row", axis=1, tiled=True),
        lax.all_gather(vectors, "row", axis=1, tiled=True),
    )
    vector_full = vector_full.astype(jnp.float32)
    gain_one = vector_full[0]
    shift_one = vector_full[1]
    bias_proj = vector_full[2]
    gain_two = vector_full[3]
    shift_two = vector_full[4]
    bias_two = vector_full[5]
    all_clips = lengths.shape[0]
    valid_all = (
        loss_mask.reshape(all_clips, L) * (jnp.arange(L)[None, :] < lengths[:, None])
    ).astype(jnp.float32)
    valid_total = jnp.maximum(jnp.sum(valid_all), 1.0)
    first_row = (group_index * col_count + col_index) * local_rows
    valid = lax.dynamic_slice_in_dim(valid_all.reshape(all_clips * L), first_row, local_rows)
    my_lengths = lax.dynamic_slice_in_dim(lengths, group_index * clip_count, clip_count)
    inputs = states.astype(jnp.float32)
    norm_one, unit_one, spread_one = normalize(inputs, gain_one, shift_one)
    norm_one = norm_one.astype(jnp.bfloat16)
    tokens_one = lax.all_gather(norm_one, "col", axis=0, tiled=True)
    qkv_matrix = qkv_full.reshape(width, 3 * head_width)
    projected = jnp.dot(tokens_one, qkv_matrix, preferred_element_type=jnp.float32).reshape(
        group_rows, 3, head_width
    )
    bias_rows = jnp.stack(
        [
            q_bias.astype(jnp.float32),
            jnp.zeros((head_width,), jnp.float32),
            v_bias.astype(jnp.float32),
        ]
    )
    packed = (projected + bias_rows[None]).astype(jnp.bfloat16)
    clips_packed = packed.reshape(clip_count, L, 3, heads_here, HD)
    attended, totals = lax.map(
        lambda element: attend_clip(element[0], element[1], score_scale), (clips_packed, my_lengths)
    )
    attended = attended.reshape(group_rows, head_width).astype(jnp.bfloat16)
    proj_whole, qkv_whole = (
        lax.all_gather(proj_full, "col", axis=0, tiled=True),
        lax.all_gather(qkv_full, "col", axis=2, tiled=True),
    )
    attended_rows = lax.all_to_all(attended, "col", split_axis=0, concat_axis=1, tiled=True)
    middle = inputs + (
        jnp.dot(attended_rows, proj_whole, preferred_element_type=jnp.float32) + bias_proj
    )
    norm_two, unit_two, spread_two = normalize(middle, gain_two, shift_two)
    norm_two = norm_two.astype(jnp.bfloat16)
    fc1_whole, fc2_whole, fc1_bias_whole = (
        lax.all_gather(fc1_full, "col", axis=1, tiled=True),
        lax.all_gather(fc2_full, "col", axis=0, tiled=True),
        lax.all_gather(fc1_bias, "col", axis=0, tiled=True),
    )
    hidden_pre = jnp.dot(
        norm_two, fc1_whole, preferred_element_type=jnp.float32
    ) + fc1_bias_whole.astype(jnp.float32)
    hidden = gelu_value(hidden_pre).astype(jnp.bfloat16)
    outputs = middle + (jnp.dot(hidden, fc2_whole, preferred_element_type=jnp.float32) + bias_two)
    differ = outputs - teacher.astype(jnp.float32)
    numerator = jnp.sum(valid[:, None] * differ * differ)
    loss_scale = all_clips * L * width / 2.0
    grad_out = loss_scale * 2.0 / (valid_total * width) * valid[:, None] * differ
    grad_low = grad_out.astype(jnp.bfloat16)
    grad_hidden = jnp.dot(grad_low, fc2_whole.T, preferred_element_type=jnp.float32)
    grad_pre = (grad_hidden * gelu_slope(hidden_pre)).astype(jnp.bfloat16)
    wide_fc2 = jnp.dot(hidden.T, grad_low, preferred_element_type=jnp.float32)
    wide_fc1 = jnp.dot(norm_two.T, grad_pre, preferred_element_type=jnp.float32)
    fc1_grad_part, fc2_grad_part = (
        lax.psum_scatter(
            wide_fc1.astype(jnp.bfloat16), "col", scatter_dimension=1, tiled=True
        ).astype(jnp.float32),
        lax.psum_scatter(
            wide_fc2.astype(jnp.bfloat16), "col", scatter_dimension=0, tiled=True
        ).astype(jnp.float32),
    )
    fc1_bias_sum = jnp.sum(grad_pre, axis=0, dtype=jnp.float32)
    grad_norm_two = jnp.dot(grad_pre, fc1_whole.T, preferred_element_type=jnp.float32)
    back_two, gain_two_grad, shift_two_grad = norm_back(
        grad_norm_two, unit_two, spread_two, gain_two
    )
    grad_mid = grad_out + back_two
    mid_low = grad_mid.astype(jnp.bfloat16)
    wide_proj = jnp.dot(attended_rows.T, mid_low, preferred_element_type=jnp.float32)
    proj_grad_part = lax.psum_scatter(
        wide_proj.astype(jnp.bfloat16), "col", scatter_dimension=0, tiled=True
    )
    grad_attended_rows = jnp.dot(mid_low, proj_whole.T, preferred_element_type=jnp.float32).astype(
        jnp.bfloat16
    )
    grad_attended = lax.all_to_all(
        grad_attended_rows, "col", split_axis=1, concat_axis=0, tiled=True
    )
    grads_packed = lax.map(
        lambda element: attend_clip_back(
            element[0], element[1], element[2], element[3], score_scale
        ),
        (clips_packed, my_lengths, totals, grad_attended.reshape(clip_count, L, heads_here, HD)),
    )
    grads_packed = grads_packed.reshape(group_rows, 3 * head_width).astype(jnp.bfloat16)
    qkv_grad_part = jnp.dot(tokens_one.T, grads_packed, preferred_element_type=jnp.float32).reshape(
        width, 3, head_width
    )
    bias_sums = jnp.sum(grads_packed.reshape(group_rows, 3, head_width), axis=0, dtype=jnp.float32)
    grads_rows = lax.all_to_all(
        grads_packed.reshape(group_rows, 3, head_width),
        "col",
        split_axis=0,
        concat_axis=2,
        tiled=True,
    )
    grad_norm_one = jnp.dot(
        grads_rows.reshape(local_rows, 3 * width),
        qkv_whole.reshape(width, 3 * width).T,
        preferred_element_type=jnp.float32,
    )
    back_one, gain_one_grad, shift_one_grad = norm_back(
        grad_norm_one, unit_one, spread_one, gain_one
    )
    grad_states = (grad_mid + back_one).astype(jnp.bfloat16)
    proj_bias_grad = jnp.sum(mid_low, axis=0, dtype=jnp.float32)
    fc2_bias_grad = jnp.sum(grad_low, axis=0, dtype=jnp.float32)
    token_vectors = jnp.stack(
        [
            gain_one_grad,
            shift_one_grad,
            proj_bias_grad,
            gain_two_grad,
            shift_two_grad,
            fc2_bias_grad,
        ]
    )
    head_vectors = lax.dynamic_update_slice(
        jnp.zeros((2, width), jnp.float32),
        jnp.stack([bias_sums[0], bias_sums[2]]),
        (0, col_index * head_width),
    )
    token_sums, head_sums, fc1_sums, loss_sum = lax.psum(
        (token_vectors, head_vectors, fc1_bias_sum, numerator), ("dp", "row", "col")
    )
    qkv_rows, proj_cols, fc1_rows, fc2_cols = (
        lax.psum_scatter(
            qkv_grad_part.astype(jnp.bfloat16), "row", scatter_dimension=0, tiled=True
        ).astype(jnp.float32),
        lax.psum_scatter(proj_grad_part, "row", scatter_dimension=1, tiled=True).astype(
            jnp.float32
        ),
        lax.psum_scatter(
            fc1_grad_part.astype(jnp.bfloat16), "row", scatter_dimension=0, tiled=True
        ).astype(jnp.float32),
        lax.psum_scatter(
            fc2_grad_part.astype(jnp.bfloat16), "row", scatter_dimension=1, tiled=True
        ).astype(jnp.float32),
    )
    qkv_grad, proj_grad, fc1_grad, fc2_grad = (
        lax.psum(qkv_rows.astype(jnp.bfloat16), "dp").astype(jnp.float32),
        lax.psum(proj_cols.astype(jnp.bfloat16), "dp").astype(jnp.float32),
        lax.psum(fc1_rows.astype(jnp.bfloat16), "dp").astype(jnp.float32),
        lax.psum(fc2_cols.astype(jnp.bfloat16), "dp").astype(jnp.float32),
    )
    half_width = width // row_count
    token_part = lax.dynamic_slice_in_dim(
        token_sums, lax.axis_index("row") * half_width, half_width, 1
    )
    head_part = lax.dynamic_slice_in_dim(head_sums, col_index * head_width, head_width, 1)
    fc1_part = lax.dynamic_slice_in_dim(fc1_sums, col_index * hidden_width, hidden_width, 0)
    loss_value = loss_sum / (valid_total * width)
    return (
        outputs.astype(jnp.bfloat16),
        loss_value,
        grad_states,
        token_part[0],
        token_part[1],
        qkv_grad,
        head_part[0],
        head_part[1],
        proj_grad,
        token_part[2],
        token_part[3],
        token_part[4],
        fc1_grad,
        fc1_part,
        fc2_grad,
        token_part[5],
    )


PAIRED_MESH = (4, 2, 4)
GROUP = 4


def small_cost(flops):
    return pl.CostEstimate(flops=flops, bytes_accessed=0, transcendentals=0)
QT = 128


def dot_nn(a, b):
    return lax.dot_general(a, b, (((1,), (0,)), ((), ())), preferred_element_type=jnp.float32)


def dot_nt(a, b):
    return lax.dot_general(a, b, (((1,), (1,)), ((), ())), preferred_element_type=jnp.float32)


def dot_tn(a, b):
    return lax.dot_general(a, b, (((0,), (0,)), ((), ())), preferred_element_type=jnp.float32)


def head_stack(values, zero):
    lane_head = lax.broadcasted_iota(jnp.int32, values.shape, 1) // HD
    return jnp.concatenate([jnp.where(lane_head == h, values, zero) for h in range(GROUP)], axis=0)


def head_unstack(wide, count):
    return jnp.concatenate(
        [wide[h * HD : (h + 1) * HD, h * count : (h + 1) * count] for h in range(GROUP)], axis=0
    ).T


def tiles_of(rows, tile):
    full = rows // QT

    @pl.loop(0, full)
    def _(index):
        tile(pl.multiple_of(index * QT, QT), QT, index)

    if rows > full * QT:
        tile(full * QT, rows - full * QT, full)


def attend_kernel(first, packed_ref, bias_ref, out_ref, lse_ref, vt_ref):
    width = GROUP * HD
    vt_ref[...] = packed_ref[:, 2 * width : 3 * width].T

    def tile(start, count, index):
        cols = GROUP * count
        stacked = head_stack(
            packed_ref[pl.ds(first + start, count), 0:width], jnp.zeros((), jnp.bfloat16)
        )
        keys = packed_ref[:, width : 2 * width]
        bias = bias_ref[...]
        scores = dot_nt(keys, stacked) + jnp.concatenate([bias] * (cols // 128), axis=1)
        peak = jnp.max(scores, axis=0, keepdims=True)
        weights = jnp.exp(scores - peak)
        total = jnp.sum(weights, axis=0, keepdims=True)
        wide = dot_nn(vt_ref[...], weights.astype(jnp.bfloat16)) * (1.0 / total)
        out_ref[pl.ds(start, count), :] = head_unstack(wide, count).astype(jnp.bfloat16)
        lse_ref[index, :, 0:cols] = jnp.broadcast_to(peak + jnp.log(total), (8, cols))

    tiles_of(out_ref.shape[0], tile)


def attend_back_kernel(
    first, lane, last, packed_ref, bias_ref, lse_ref, att_ref, up_own_ref, up_far_ref, *refs
):
    width = GROUP * HD
    lanes = slice(lane, lane + width)
    own_rows = up_own_ref.shape[0]
    if last:
        dq_in, dk_in, dv_in, out_ref, sum_ref, kt_ref, up_ref, dk_ref, dv_ref = refs
        dk_ref[...] = dk_in[...]
        dv_ref[...] = dv_in[...]
        out_ref[0:first, 0:width] = dq_in[...]
        rows = out_ref.shape[0] - first
        up_ref[0 : own_rows - first, :] = up_own_ref[first:own_rows, lanes]
        up_ref[own_rows - first :, :] = up_far_ref[:, lanes]
    else:
        out_ref, dk_ref, dv_ref, kt_ref, up_ref = refs
        dk_ref[...] = jnp.zeros_like(dk_ref)
        dv_ref[...] = jnp.zeros_like(dv_ref)
        rows = out_ref.shape[0]
        up_ref[...] = up_own_ref[0:rows, lanes]
    kt_ref[...] = packed_ref[:, width : 2 * width].T

    def tile(start, count, index):
        cols = GROUP * count
        zero = jnp.zeros((), jnp.bfloat16)
        up = up_ref[pl.ds(start, count), :]
        stacked = head_stack(packed_ref[pl.ds(first + start, count), 0:width], zero)
        up_stacked = head_stack(up, zero)
        product = head_stack(
            up.astype(jnp.float32) * att_ref[pl.ds(start, count), :].astype(jnp.float32),
            jnp.zeros((), jnp.float32),
        )
        high = product.astype(jnp.bfloat16)
        low = (product - high.astype(jnp.float32)).astype(jnp.bfloat16)
        ones = jnp.ones((8, width), jnp.bfloat16)
        delta = (dot_nt(ones, high) + dot_nt(ones, low))[0:1]
        keys = packed_ref[:, width : 2 * width]
        values = packed_ref[:, 2 * width : 3 * width]
        bias = bias_ref[...]
        scores = dot_nt(keys, stacked) + jnp.concatenate([bias] * (cols // 128), axis=1)
        weights = jnp.exp(scores - lse_ref[index, 0:1, 0:cols])
        dv_ref[...] += dot_nn(weights.astype(jnp.bfloat16), up_stacked)
        grad = (weights * (dot_nt(values, up_stacked) - delta)).astype(jnp.bfloat16)
        dk_ref[...] += dot_nn(grad, stacked)
        wide = dot_nn(kt_ref[...], grad) * (HD**-0.5)
        at = pl.ds(first + start if last else start, count)
        out_ref[at, 0:width] = head_unstack(wide, count).astype(jnp.bfloat16)

    tiles_of(rows, tile)
    if last:
        out_ref[:, width : 2 * width] = dk_ref[...].astype(jnp.bfloat16)
        out_ref[:, 2 * width : 3 * width] = dv_ref[...].astype(jnp.bfloat16)
        for k in range(3):
            part = out_ref[:, k * width : (k + 1) * width].astype(jnp.float32)
            sum_ref[:, k * width : (k + 1) * width] = jnp.sum(part, axis=0, keepdims=True)


def attend(packed, bias, first, rows):
    tokens, width = packed.shape[0], GROUP * HD
    tiles = -(-rows // QT)
    return pl.pallas_call(
        functools.partial(attend_kernel, first),
        out_shape=(
            jax.ShapeDtypeStruct((rows, width), jnp.bfloat16),
            jax.ShapeDtypeStruct((tiles, 8, GROUP * QT), jnp.float32),
        ),
        in_specs=[pl.BlockSpec(memory_space=pltpu.VMEM)] * 2,
        out_specs=[pl.BlockSpec(memory_space=pltpu.VMEM)] * 2,
        scratch_shapes=[pltpu.VMEM((width, tokens), jnp.bfloat16)],
        compiler_params=pltpu.CompilerParams(vmem_limit_bytes=32 << 20),
        cost_estimate=pl.CostEstimate(
            flops=2 * rows * tokens * width * 4, bytes_accessed=6 << 20, transcendentals=0
        ),
        name="attend",
    )(packed, bias)


def attend_back(packed, bias, lse, att, up_own, up_far, lane, first, before=None):
    tokens, width = packed.shape[0], GROUP * HD
    rows = att.shape[0]
    total = jax.ShapeDtypeStruct((tokens, width), jnp.float32)
    vmem = pl.BlockSpec(memory_space=pltpu.VMEM)
    scratch = [pltpu.VMEM((width, tokens), jnp.bfloat16), pltpu.VMEM((rows, width), jnp.bfloat16)]
    if before is None:
        extra = ()
        out_shape = (jax.ShapeDtypeStruct((rows, width), jnp.bfloat16), total, total)
        up_far = up_own
    else:
        extra = before
        out_shape = (
            jax.ShapeDtypeStruct((tokens, 3 * width), jnp.bfloat16),
            jax.ShapeDtypeStruct((1, 3 * width), jnp.float32),
        )
        scratch += [pltpu.VMEM((tokens, width), jnp.float32)] * 2
    return pl.pallas_call(
        functools.partial(attend_back_kernel, first, lane, before is not None),
        out_shape=out_shape,
        in_specs=[vmem] * (6 + len(extra)),
        out_specs=(vmem,) * len(out_shape),
        scratch_shapes=scratch,
        compiler_params=pltpu.CompilerParams(vmem_limit_bytes=52 << 20),
        cost_estimate=pl.CostEstimate(
            flops=4 * rows * tokens * width * 4, bytes_accessed=10 << 20, transcendentals=0
        ),
        name="attend_back",
    )(packed, bias, lse, att, up_own, up_far, *extra)


FF_CHUNK = 512
ROWS = 112


def rows_of(total, body):
    @pl.loop(0, total // ROWS)
    def _(index):
        body(pl.ds(pl.multiple_of(index * ROWS, ROWS), ROWS))


def unit_rows(values):
    centered = values - jnp.mean(values, axis=-1, keepdims=True)
    spread = lax.rsqrt(jnp.mean(centered * centered, axis=-1, keepdims=True) + EPSILON)
    return centered * spread, spread


def middle_kernel(
    table_ref,
    factor_ref,
    att_ref,
    input_ref,
    target_ref,
    valid_ref,
    vector_ref,
    small_ref,
    fc1_own,
    fc1_other,
    fc2_own,
    fc2_other,
    proj_own,
    proj_other,
    two_mine,
    two_theirs,
    one_mine,
    one_theirs,
    out_hbm,
    hidden_hbm,
    pre_hbm,
    norm_hbm,
    grad_low_hbm,
    mid_low_ref,
    grad_mid_ref,
    up_own_ref,
    up_give_ref,
    hidden_sum_ref,
    sums_ref,
    fc1_v,
    fc2_v,
    proj_v,
    middle_v,
    back_v,
    out_ref,
    hidden_ref,
    pre_ref,
    norm_ref,
    grad_low_ref,
    sem_one,
    sem_two,
    sem_proj,
    sem_out,
):
    stores = [
        pltpu.make_async_copy(source, target, sem_out.at[i])
        for i, (source, target) in enumerate(
            (
                (norm_ref, norm_hbm),
                (hidden_ref, hidden_hbm),
                (out_ref, out_hbm),
                (grad_low_ref, grad_low_hbm),
                (pre_ref, pre_hbm),
            )
        )
    ]
    f32, bf16 = jnp.float32, jnp.bfloat16
    total_rows = att_ref.shape[0]
    half = fc1_own.shape[0]
    sub = fc1_own.shape[1] // 4
    heads = proj_own.shape[0]
    part = heads // 4
    hidden_total = hidden_ref.shape[1]
    chunks = hidden_total // FF_CHUNK
    unit = half + 2 * sub + 2 * part + 16

    def fc1_copy(source, side, at):
        lanes = pl.ds(pl.multiple_of(at * sub, sub), sub)
        pltpu.make_async_copy(
            source, fc1_v.at[side * half : (side + 1) * half, lanes], sem_one.at[at // 2]
        ).start()

    def fc2_copy(source, side, i, at):
        lane = side * half + i * sub
        pltpu.make_async_copy(
            source, fc2_v.at[pl.ds(pl.multiple_of(at * sub, sub), sub), lane : lane + sub], sem_two
        ).start()

    sources = []
    for s in range(4):
        step = two_mine.shape[0] // 4
        sources.append((s, 2, two_mine, two_theirs, s * step))
        step = one_mine.shape[0] // 4
        sources.append((s, 1, one_mine, one_theirs, s * step))
        sources.append((s, 3, one_mine, one_theirs, s * step + unit))

    for side, ref in enumerate((proj_own, proj_other)):
        pltpu.make_async_copy(
            ref, proj_v.at[0:heads, side * half : (side + 1) * half], sem_proj
        ).start()
    for s, j, *refs, base in sources:
        rows = pl.ds(pl.multiple_of(j * heads + table_ref[20 + s] * part, part), part)
        for side in range(2):
            for i in range(2):
                low = base + half + 2 * sub + i * part
                lane = side * half + i * sub
                pltpu.make_async_copy(
                    refs[side].at[low : low + part, :], proj_v.at[rows, lane : lane + sub], sem_proj
                ).start()
    for a in range(4):
        for side, ref in enumerate((fc1_own, fc1_other)):
            fc1_copy(ref.at[:, a * sub : (a + 1) * sub], side, table_ref[16 + a])
    for s, j, *refs, base in sources:
        for side in range(2):
            fc1_copy(refs[side].at[base : base + half, :], side, table_ref[4 * s + j])
    for a in range(4):
        for side, ref in enumerate((fc2_own, fc2_other)):
            for i in range(2):
                fc2_copy(
                    ref.at[a * sub : (a + 1) * sub, i * sub : (i + 1) * sub], side, i, table_ref[16 + a]
                )
    for s, j, *refs, base in sources:
        for side in range(2):
            for i in range(2):
                low = base + half + i * sub
                fc2_copy(refs[side].at[low : low + sub, :], side, i, table_ref[4 * s + j])

    def lanes_of(i):
        return pl.ds(pl.multiple_of((table_ref[28] ^ i) * half, half), half)

    sums_ref[...] = jnp.zeros_like(sums_ref)

    pltpu.make_async_copy(proj_v, proj_v, sem_proj).wait()
    for i in range(2):
        cols = slice(i * half, (i + 1) * half)
        middle_v[:, cols] = input_ref[:, lanes_of(i)].astype(f32) + (
            dot_nn(att_ref[...], proj_v[:, cols]) + vector_ref[2:3, cols]
        )

    @functools.partial(rows_of, total_rows)
    def _(rows):
        normal, _ = unit_rows(middle_v[rows, :])
        norm_ref[rows, :] = (normal * vector_ref[3:4, :] + vector_ref[4:5, :]).astype(bf16)

    stores[0].start()

    @pl.loop(0, chunks)
    def _(k):
        span = pl.ds(pl.multiple_of(k * FF_CHUNK, FF_CHUNK), FF_CHUNK)
        pltpu.make_async_copy(fc1_v.at[:, span], fc1_v.at[:, span], sem_one.at[k]).wait()
        a = k // 2
        bias = jnp.concatenate(
            [
                small_ref[table_ref[24 + 2 * (k % 2) + i], pl.ds(a, 1), :]
                for i in range(FF_CHUNK // sub)
            ],
            axis=1,
        )
        pre = dot_nn(norm_ref[...], fc1_v[:, span]) + bias
        cdf = 0.5 * (1.0 + lax.erf(pre * ROOT_HALF))
        hidden_ref[:, span] = (pre * cdf).astype(bf16)
        slope = cdf + pre * jnp.exp(-0.5 * pre * pre) * DENSITY_FACTOR
        pre_ref[:, span] = slope.astype(bf16)

    stores[1].start()
    pltpu.make_async_copy(fc2_v, fc2_v, sem_two).wait()
    for i in range(2):
        cols = slice(i * half, (i + 1) * half)
        total = middle_v[:, cols] + (dot_nn(hidden_ref[...], fc2_v[:, cols]) + vector_ref[5:6, cols])
        out_ref[:, lanes_of(i)] = total.astype(bf16)
        differ = total - target_ref[:, lanes_of(i)].astype(f32)
        weighted = valid_ref[...] * differ
        sums_ref[0:1, cols] = jnp.sum(weighted * differ, axis=0, keepdims=True)
        grad = factor_ref[0] * weighted
        grad_mid_ref[:, cols] = grad
        low = grad.astype(bf16)
        grad_low_ref[:, cols] = low
        sums_ref[1:2, cols] = jnp.sum(low.astype(f32), axis=0, keepdims=True)

    stores[2].start()
    stores[3].start()

    @pl.loop(0, chunks)
    def _(k):
        span = pl.ds(pl.multiple_of(k * FF_CHUNK, FF_CHUNK), FF_CHUNK)
        back = dot_nt(grad_low_ref[...], fc2_v[span, :])
        back = (back * pre_ref[:, span].astype(f32)).astype(bf16)
        pre_ref[:, span] = back
        hidden_sum_ref[0:1, span] = jnp.sum(back.astype(f32), axis=0, keepdims=True)

    stores[4].start()
    for i in range(2):
        cols = slice(i * half, (i + 1) * half)
        back_v[:, cols] = dot_nt(pre_ref[...], fc1_v[cols, :])

    @functools.partial(rows_of, total_rows)
    def _(rows):
        normal, spread = unit_rows(middle_v[rows, :])
        upstream = back_v[rows, :]
        inner = upstream * vector_ref[3:4, :]
        center = jnp.mean(inner, axis=-1, keepdims=True)
        slope = jnp.mean(inner * normal, axis=-1, keepdims=True)
        grad = grad_mid_ref[rows, :] + spread * (inner - center - normal * slope)
        grad_mid_ref[rows, :] = grad
        low = grad.astype(bf16)
        mid_low_ref[rows, :] = low
        sums_ref[2:3, :] += jnp.sum(upstream * normal, axis=0, keepdims=True)
        sums_ref[3:4, :] += jnp.sum(upstream, axis=0, keepdims=True)
        sums_ref[4:5, :] += jnp.sum(low.astype(f32), axis=0, keepdims=True)

    for j, (ref, at) in enumerate(((up_own_ref, 0), (up_give_ref, 0), (up_own_ref, 1), (up_give_ref, 1))):
        grad = dot_nt(mid_low_ref[...], proj_v[j * heads : (j + 1) * heads, :])
        ref[:, at * heads : (at + 1) * heads] = grad.astype(bf16)
    for store in stores:
        store.wait()


def middle_block(table, factor, att, inputs, target, valid, vectors, smalls, pieces):
    rows, width = att.shape
    hidden = 4 * pieces[0].shape[1]
    vmem = pl.BlockSpec(memory_space=pltpu.VMEM)
    smem = pl.BlockSpec(memory_space=pltpu.SMEM)
    anywhere = pl.BlockSpec(memory_space=pl.ANY)
    f32, bf16 = jnp.float32, jnp.bfloat16

    def result(columns, dtype):
        return jax.ShapeDtypeStruct((rows, columns), dtype)

    return pl.pallas_call(
        middle_kernel,
        out_shape=(
            result(width, bf16),
            result(hidden, bf16),
            result(hidden, bf16),
            result(width, bf16),
            result(width, bf16),
            result(width, bf16),
            result(width, f32),
            result(width // 2, bf16),
            result(width // 2, bf16),
            jax.ShapeDtypeStruct((1, hidden), f32),
            jax.ShapeDtypeStruct((8, width), f32),
        ),
        in_specs=[smem] * 2 + [vmem] * 6 + [anywhere] * 10,
        out_specs=[anywhere] * 5 + [vmem] * 6,
        scratch_shapes=[
            pltpu.VMEM((width, hidden), bf16),
            pltpu.VMEM((hidden, width), bf16),
            pltpu.VMEM((width, width), bf16),
            pltpu.VMEM((rows, width), f32),
            pltpu.VMEM((rows, width), f32),
            pltpu.VMEM((rows, width), bf16),
            pltpu.VMEM((rows, hidden), bf16),
            pltpu.VMEM((rows, hidden), bf16),
            pltpu.VMEM((rows, width), bf16),
            pltpu.VMEM((rows, width), bf16),
            pltpu.SemaphoreType.DMA((hidden // FF_CHUNK,)),
            pltpu.SemaphoreType.DMA,
            pltpu.SemaphoreType.DMA,
            pltpu.SemaphoreType.DMA((5,)),
        ],
        compiler_params=pltpu.CompilerParams(vmem_limit_bytes=62 << 20),
        cost_estimate=pl.CostEstimate(
            flops=2 * rows * width * hidden, bytes_accessed=44 << 20, transcendentals=0
        ),
        name="middle_block",
    )(table, factor, att, inputs, target, valid, vectors, smalls, *pieces)


def swap(values, axis, mask, size):
    return lax.ppermute(values, axis, [(i, i ^ mask) for i in range(size)])


def over_row(values):
    return swap(values, "row", 1, 2)


def over_dp(values, mask):
    return swap(values, "dp", mask, 4)


def over_col(values, mask):
    return swap(values, "col", mask, 4)


def cut(values, index, size, axis=0):
    return lax.dynamic_slice_in_dim(values, index * size, size, axis)


def place(pieces, index_of, axis):
    size = pieces[0].shape[axis]
    shape = list(pieces[0].shape)
    shape[axis] = size * len(pieces)
    whole = jnp.zeros(shape, pieces[0].dtype)
    for s, piece in enumerate(pieces):
        whole = lax.dynamic_update_slice_in_dim(whole, piece, index_of(s) * size, axis)
    return whole


def copies(listed, sem_ref):
    for index, (source, target) in enumerate(listed):
        pltpu.make_async_copy(source, target, sem_ref.at[index]).start()
    for index, (source, target) in enumerate(listed):
        pltpu.make_async_copy(source, target, sem_ref.at[index]).wait()


def slab_kernel(places_ref, fc1_ref, fc2_ref, proj_ref, qkv_ref, small_ref, out_ref, sem_ref):
    half, sub = fc1_ref.shape[0], fc1_ref.shape[1] // 4
    part, deep = proj_ref.shape[0] // 4, half // 4
    mine = places_ref[0]
    fc2 = fc2_ref.at[pl.ds(pl.multiple_of(mine * sub, sub), sub)]
    proj = proj_ref.at[pl.ds(pl.multiple_of(mine * part, part), part)]
    listed = [(fc1_ref.at[:, pl.ds(pl.multiple_of(mine * sub, sub), sub)], half)]
    listed += [(fc2.at[:, i * sub : (i + 1) * sub], sub) for i in range(2)]
    listed += [(proj.at[:, i * sub : (i + 1) * sub], part) for i in range(2)]
    listed += [(small_ref, small_ref.shape[0])]
    rows = pl.ds(pl.multiple_of(mine * deep, deep), deep)
    listed += [(qkv_ref.at[k, rows], deep) for k in range(3)]
    pairs, at = [], 0
    for source, count in listed:
        pairs.append((source, out_ref.at[at : at + count]))
        at += count
    copies(pairs, sem_ref)


def make_slab(places, fc1, fc2, proj, qkv, small):
    half, sub = fc1.shape[0], fc1.shape[1] // 4
    rows = half + 2 * sub + proj.shape[0] // 2 + small.shape[0] + 3 * (half // 4)
    anywhere = pl.BlockSpec(memory_space=pl.ANY)
    return pl.pallas_call(
        slab_kernel,
        out_shape=jax.ShapeDtypeStruct((rows, sub), fc1.dtype),
        in_specs=[pl.BlockSpec(memory_space=pltpu.SMEM)] + [anywhere] * 5,
        out_specs=pl.BlockSpec(memory_space=pltpu.VMEM),
        scratch_shapes=[pltpu.SemaphoreType.DMA((9,))],
        cost_estimate=small_cost(100000000),
        name="make_slab",
    )(places, fc1, fc2, proj, qkv, small)


def far_qkv_kernel(base, places_ref, mine_ref, theirs_ref, out_ref, sem_ref):
    sub = mine_ref.shape[1]
    half = out_ref.shape[0] // 2
    deep, step = half // 4, mine_ref.shape[0] // 4
    pairs = []
    for side, ref in enumerate((mine_ref, theirs_ref)):
        for s in range(4):
            rows = pl.ds(pl.multiple_of(side * half + places_ref[s] * deep, deep), deep)
            for k in range(3):
                at = s * step + base + k * deep
                pairs.append((ref.at[at : at + deep], out_ref.at[rows, k * sub : (k + 1) * sub]))
    copies(pairs, sem_ref)


def far_qkv(places, mine, theirs, base, width):
    anywhere = pl.BlockSpec(memory_space=pl.ANY)
    return pl.pallas_call(
        functools.partial(far_qkv_kernel, base),
        out_shape=jax.ShapeDtypeStruct((width, 3 * mine.shape[1]), mine.dtype),
        in_specs=[pl.BlockSpec(memory_space=pltpu.SMEM)] + [anywhere] * 2,
        out_specs=pl.BlockSpec(memory_space=pltpu.VMEM),
        scratch_shapes=[pltpu.SemaphoreType.DMA((24,))],
        cost_estimate=small_cost(100000000),
        name="far_qkv",
    )(places, mine, theirs)


VECTORS = 32


def put_split(ref, at, values):
    high = values.astype(jnp.bfloat16)
    low = (values - high.astype(jnp.float32)).astype(jnp.bfloat16)
    columns = values.shape[1]
    ref[at : at + VECTORS, 0:columns] = high
    ref[at + VECTORS : at + 2 * VECTORS, 0:columns] = low
    rest = ref.shape[1] - columns
    if rest:
        ref[at : at + 2 * VECTORS, columns:] = jnp.zeros((2 * VECTORS, rest), jnp.bfloat16)


def get_split(ref, at, columns):
    high = ref[at : at + VECTORS, 0:columns].astype(jnp.float32)
    return high + ref[at + VECTORS : at + 2 * VECTORS, 0:columns].astype(jnp.float32)


def framed(ref, rows, flip, half):
    return jnp.concatenate(
        [ref[rows, pl.ds(pl.multiple_of((flip ^ i) * half, half), half)] for i in range(2)], axis=1
    ).astype(jnp.float32)


def token_back_kernel(
    flip_ref, near_ref, far_ref, w_near, w_far, own_states, other_states, own_ref, give_ref, sums_ref, other_v
):
    rows_all, half = own_ref.shape[0], own_ref.shape[1] // 2
    sums_ref[...] = jnp.zeros_like(sums_ref)
    for start, out_ref in ((rows_all, other_v), (0, own_ref)):
        rows = slice(start, start + rows_all)
        out_ref[...] = dot_nt(near_ref[rows, :], w_near[...]) + dot_nt(far_ref[rows, :], w_far[...])
    for out_ref, states in ((other_v, other_states), (own_ref, own_states)):

        @functools.partial(rows_of, rows_all)
        def _(rows, out_ref=out_ref, states=states):
            normal, _ = unit_rows(framed(states, rows, flip_ref[0], half))
            upstream = out_ref[rows, :]
            sums_ref[0:1, :] += jnp.sum(upstream * normal, axis=0, keepdims=True)
            sums_ref[1:2, :] += jnp.sum(upstream, axis=0, keepdims=True)
            if out_ref is other_v:
                give_ref[rows, :] = upstream.astype(jnp.bfloat16)


def token_back(flip, near, far, w_near, w_far, own_states, other_states):
    rows, width = own_states.shape
    vmem = pl.BlockSpec(memory_space=pltpu.VMEM)
    return pl.pallas_call(
        token_back_kernel,
        out_shape=(
            jax.ShapeDtypeStruct((rows, width), jnp.float32),
            jax.ShapeDtypeStruct((rows, width), jnp.bfloat16),
            jax.ShapeDtypeStruct((2, width), jnp.float32),
        ),
        in_specs=[pl.BlockSpec(memory_space=pltpu.SMEM)] + [vmem] * 6,
        out_specs=(vmem,) * 3,
        scratch_shapes=[pltpu.VMEM((rows, width), jnp.float32)],
        compiler_params=pltpu.CompilerParams(vmem_limit_bytes=40 << 20),
        cost_estimate=small_cost(100000000),
        name="token_back",
    )(flip, near, far, w_near, w_far, own_states, other_states)


def last_kernel(flip_ref, own_ref, taken_ref, states_ref, mid_ref, vector_ref, out_ref):
    half = own_ref.shape[1] // 2
    upstream = own_ref[...] + taken_ref[...].astype(jnp.float32)
    everything = slice(0, own_ref.shape[0])
    normal, spread = unit_rows(framed(states_ref, everything, flip_ref[0], half))
    inner = upstream * vector_ref[0:1, :]
    center = jnp.mean(inner, axis=-1, keepdims=True)
    slope = jnp.mean(inner * normal, axis=-1, keepdims=True)
    back = mid_ref[...] + spread * (inner - center - normal * slope)
    for i in range(2):
        lanes = pl.ds(pl.multiple_of((flip_ref[0] ^ i) * half, half), half)
        out_ref[:, lanes] = back[:, i * half : (i + 1) * half].astype(jnp.bfloat16)


def last_norm(flip, own, taken, states, mid, vectors):
    rows, width = own.shape
    block = pl.BlockSpec((ROWS, width), lambda i: (i, 0))
    whole = pl.BlockSpec(vectors.shape, lambda i: (0, 0))
    return pl.pallas_call(
        last_kernel,
        grid=(rows // ROWS,),
        out_shape=jax.ShapeDtypeStruct((rows, width), jnp.bfloat16),
        in_specs=[pl.BlockSpec(memory_space=pltpu.SMEM)] + [block] * 4 + [whole],
        out_specs=block,
        cost_estimate=small_cost(500000000),
        name="last_norm",
    )(flip, own, taken, states, mid, vectors)


def far_grads_kernel(
    turned_ref, grad_ref, sums_ref, hidden_ref, norm_ref, near_ref, far_ref, keep_ref, out_ref, kept_ref
):
    half = keep_ref.shape[1]
    width = near_ref.shape[1] // 3
    shared = [hidden_ref[0:1, i * half : (i + 1) * half] for i in range(8)]
    for ref in (near_ref, far_ref):
        shared.append(jnp.concatenate([ref[0:1, 0:width], ref[0:1, 2 * width :]], axis=1))
    shared.append(sums_ref[0:1, 0:half] + sums_ref[0:1, half:])
    blank = jnp.zeros((VECTORS - 6 - len(shared), half), jnp.float32)

    def rows(lanes):
        split = [sums_ref[i : i + 1, lanes] for i in (2, 3, 4, 1)]
        split += [norm_ref[i : i + 1, lanes] for i in range(2)]
        return jnp.concatenate(split + shared + [blank], axis=0)

    keep_ref[...] = rows(slice(0, half))
    put_split(out_ref, half, rows(slice(half, 2 * half)))
    out_ref[0:half, :] = dot_nn(turned_ref[half:, :], grad_ref[...]).astype(jnp.bfloat16)
    kept_ref[...] = dot_nn(turned_ref[0:half, :], grad_ref[...])


def after_row_kernel(
    places_ref, kept_ref, taken_ref, keep_ref, near_ref, near_taken, near_own_ref, far_own_ref, sum_ref, *outs
):
    deep = far_own_ref.shape[0]
    vectors = keep_ref[...] + get_split(taken_ref, 4 * deep, keep_ref.shape[1])
    sum_ref[...] = vectors
    for s in range(4):
        rows = pl.ds(pl.multiple_of(places_ref[s] * deep, deep), deep)
        far = kept_ref[rows, :] + taken_ref[rows, :].astype(jnp.float32)
        if s == 0:
            far_own_ref[...] = far
        else:
            outs[s - 1][0:deep, :] = far.astype(jnp.bfloat16)
            put_split(outs[s - 1], deep, vectors)
        if s % 2 == 0:
            at = slice(s // 2 * deep, (s // 2 + 1) * deep)
            near = near_ref[rows, :].astype(jnp.float32) + near_taken[at, :].astype(jnp.float32)
            if s == 0:
                near_own_ref[...] = near
            else:
                outs[s - 1][deep + 2 * VECTORS :, :] = near.astype(jnp.bfloat16)


def after_plane_kernel(near_ref, far_ref, sum_ref, *refs):
    takes, (keep_ref, vector_ref, give_ref, small_ref) = refs[:3], refs[3:]
    deep = far_ref.shape[0]
    vectors, far = sum_ref[...], far_ref[...]
    keep_ref[...] = near_ref[...] + takes[1][deep + 2 * VECTORS :, :].astype(jnp.float32)
    for take in takes:
        vectors = vectors + get_split(take, deep, vectors.shape[1])
        far = far + take[0:deep, :].astype(jnp.float32)
    vector_ref[...] = vectors
    give_ref[0:deep, :] = far.astype(jnp.bfloat16)
    put_split(give_ref, deep, vectors)
    put_split(small_ref, 0, vectors)


def after_cols_kernel(keep_ref, vector_ref, one_ref, two_ref, three_ref, out_ref, total_ref):
    deep = keep_ref.shape[0]
    out_ref[...] = (keep_ref[...] + two_ref[0:deep, :].astype(jnp.float32)).astype(jnp.bfloat16)
    columns = vector_ref.shape[1]
    far = get_split(two_ref, deep, columns)
    total = vector_ref[...] + far
    total = total + get_split(one_ref, 0, columns) + get_split(three_ref, 0, columns)
    total_ref[...] = total
    total_ref[14:15, :] = vector_ref[14:15, :] + far[15:16, :]


def on_chip(kernel, shapes, name, *args, tables=0):
    vmem = pl.BlockSpec(memory_space=pltpu.VMEM)
    return pl.pallas_call(
        kernel,
        out_shape=tuple(jax.ShapeDtypeStruct(*s) for s in shapes),
        in_specs=[pl.BlockSpec(memory_space=pltpu.SMEM)] * tables + [vmem] * (len(args) - tables),
        out_specs=(vmem,) * len(shapes),
        cost_estimate=small_cost(100000000),
        name=name,
    )(*args)


def wide_kernel(with_proj, places_ref, small_ref, big_ref, taken_ref, *refs):
    if with_proj:
        proj_kept, proj_taken, *refs = refs
    *outs, turned_v = refs
    half, sub = turned_v.shape[0], turned_v.shape[0] // 2
    span = big_ref.shape[1] // 4
    part = 256 // 4 if not with_proj else proj_kept.shape[0] // 16
    turned_v[...] = small_ref[:, 0:half].T
    for s in range(4):
        lanes = pl.ds(pl.multiple_of(places_ref[s] * span, span), span)
        block = dot_nn(turned_v[...], big_ref[:, lanes]) + taken_ref[:, lanes].astype(jnp.float32)
        block = block.astype(jnp.bfloat16)
        for side, (go, slot) in enumerate(((s % 2, s // 2), (s // 2, s % 2))):
            out = outs[2 * side + go]
            rows = slice(slot * sub, (slot + 1) * sub)
            out[rows, 0:span] = block[side * sub : (side + 1) * sub]
            if with_proj:
                at = side * sub
                for j in range(4):
                    start = pl.multiple_of(4 * j * part + places_ref[s] * part, part)
                    piece = proj_kept[pl.ds(start, part), at : at + sub] + proj_taken[
                        pl.ds(start, part), at : at + sub
                    ].astype(jnp.float32)
                    low = slot * sub + j * part
                    out[low : low + part, span:] = piece.astype(jnp.bfloat16)


def wide_grads(places, small, big, taken, proj=()):
    half = small.shape[1] // 2
    columns = big.shape[1] // 4 + (half // 2 if proj else 0)
    vmem = pl.BlockSpec(memory_space=pltpu.VMEM)
    return pl.pallas_call(
        functools.partial(wide_kernel, bool(proj)),
        out_shape=(jax.ShapeDtypeStruct((half, columns), jnp.bfloat16),) * 4,
        in_specs=[pl.BlockSpec(memory_space=pltpu.SMEM)] + [vmem] * (3 + len(proj)),
        out_specs=(vmem,) * 4,
        scratch_shapes=[pltpu.VMEM((half, small.shape[0]), jnp.bfloat16)],
        compiler_params=pltpu.CompilerParams(vmem_limit_bytes=44 << 20),
        cost_estimate=small_cost(3000000000),
        name="wide_grads",
    )(places, small, big, taken, *proj)


def plane_sum_kernel(*refs):
    sub = refs[4].shape[0]
    for side in range(2):
        kept, taken = refs[2 * side : 2 * side + 2]
        for slot in range(2):
            rows = slice(slot * sub, (slot + 1) * sub)
            total = kept[rows, :].astype(jnp.float32) + taken[rows, :].astype(jnp.float32)
            refs[4 + 2 * side + slot][...] = total.astype(jnp.bfloat16)


def cols_out_kernel(places_ref, *refs):
    outs = refs[4:]
    sub = refs[0].shape[0]
    columns = refs[0].shape[1]
    part = (outs[0].shape[0] - 2 * sub) // 2
    for side in range(2):
        kept, taken = refs[2 * side : 2 * side + 2]
        for j in range(4):
            lanes = pl.ds(pl.multiple_of(places_ref[4 + j] * sub, sub), sub)
            total = kept[:, lanes].astype(jnp.float32) + taken[:, lanes].astype(jnp.float32)
            outs[j][side * sub : (side + 1) * sub, :] = total.astype(jnp.bfloat16)
            if part:
                rows = slice(j * part, (j + 1) * part)
                total = kept[rows, columns - sub :].astype(jnp.float32)
                total = total + taken[rows, columns - sub :].astype(jnp.float32)
                low = 2 * sub + side * part
                outs[j][low : low + part, :] = total.astype(jnp.bfloat16)


def mine_kernel(*refs):
    out_ref, at = refs[8], 0
    for group in (refs[0:4], refs[4:8]):
        total = group[0][...].astype(jnp.float32)
        for ref in group[1:]:
            total = total + ref[...].astype(jnp.float32)
        out_ref[at : at + total.shape[0], :] = total.astype(jnp.bfloat16)
        at += total.shape[0]


def finish_kernel(part_rows, places_ref, *refs):
    pieces, (fc2_ref, fc1_ref, proj_ref) = refs[:2], refs[2:]
    half, sub = fc1_ref.shape[0], pieces[0].shape[1]
    for s in range(4):
        piece, base = pieces[s // 2], (s % 2) * (pieces[0].shape[0] // 2)
        at = places_ref[s]
        rows = pl.ds(pl.multiple_of(at * sub, sub), sub)
        fc2_ref[rows, :] = piece[base : base + half, :].astype(jnp.float32).T
        fc1_ref[:, rows] = piece[base + half : base + 2 * half, :].astype(jnp.float32)
        rows = pl.ds(pl.multiple_of(at * part_rows, part_rows), part_rows)
        for i in range(2):
            low = base + 2 * half + i * part_rows
            proj_ref[rows, i * sub : (i + 1) * sub] = piece[low : low + part_rows, :].astype(jnp.float32)


def finish_qkv_kernel(places_ref, *refs):
    out_ref = refs[4]
    deep, width = refs[0].shape[0], out_ref.shape[2]
    for s in range(4):
        rows = pl.ds(pl.multiple_of(places_ref[s] * deep, deep), deep)
        for k in range(3):
            out_ref[k, rows, :] = refs[s][:, k * width : (k + 1) * width].astype(jnp.float32)


def finish(places, pieces, part_rows):
    rows, sub = pieces[0].shape
    half = (rows // 2 - 2 * part_rows) // 2
    vmem = pl.BlockSpec(memory_space=pltpu.VMEM)
    return pl.pallas_call(
        functools.partial(finish_kernel, part_rows),
        out_shape=(
            jax.ShapeDtypeStruct((4 * sub, half), jnp.float32),
            jax.ShapeDtypeStruct((half, 4 * sub), jnp.float32),
            jax.ShapeDtypeStruct((4 * part_rows, half), jnp.float32),
        ),
        in_specs=[pl.BlockSpec(memory_space=pltpu.SMEM)] + [vmem] * 2,
        out_specs=[vmem] * 3,
        cost_estimate=small_cost(100000000),
        name="finish",
    )(places, *pieces)


def finish_qkv(places, pieces):
    deep, width = pieces[0].shape
    vmem = pl.BlockSpec(memory_space=pltpu.VMEM)
    return pl.pallas_call(
        finish_qkv_kernel,
        out_shape=jax.ShapeDtypeStruct((3, 4 * deep, width // 3), jnp.float32),
        in_specs=[pl.BlockSpec(memory_space=pltpu.SMEM)] + [vmem] * 4,
        out_specs=vmem,
        cost_estimate=small_cost(100000000),
        name="finish_qkv",
    )(places, *pieces)


def tie(value, *others):
    return lax.optimization_barrier((value, *others))[0]


def add_up(own, taken):
    total = own.astype(jnp.float32)
    for piece in taken:
        total = total + piece.astype(jnp.float32)
    return total


def local_paired(
    states,
    ln1_gain,
    ln1_bias,
    w_qkv,
    q_bias,
    v_bias,
    w_proj,
    proj_bias,
    ln2_gain,
    ln2_bias,
    w_fc1,
    fc1_bias,
    w_fc2,
    fc2_bias,
    teacher,
    loss_mask,
    lengths,
):
    f32, bf16 = jnp.float32, jnp.bfloat16
    dp = lax.axis_index("dp")
    row = lax.axis_index("row")
    col = lax.axis_index("col")
    local_rows, width = states.shape
    half = width // 2
    head_width = w_qkv.shape[2]
    hidden_width = w_fc1.shape[1]
    sub = hidden_width // 4
    span = 4 * sub
    part_rows = head_width // 4
    clip = (dp * 2 + row) * 2 + col // 2
    second = col % 2

    def quarter(s):
        return dp ^ s

    def frame(values):
        return jnp.where(
            row == 0, values, jnp.concatenate([values[:, half:], values[:, :half]], axis=1)
        )

    places = jnp.stack([dp ^ s for s in range(4)] + [col ^ j for j in range(4)]).astype(jnp.int32)
    flip = row.reshape(1).astype(jnp.int32)
    states_other = over_col(states, 1)
    small = jnp.concatenate(
        [
            fc1_bias.reshape(4, sub),
            q_bias.reshape(1, sub),
            v_bias.reshape(1, sub),
            jnp.zeros((10, sub), bf16),
        ],
        axis=0,
    )
    slab = make_slab(places, w_fc1, w_fc2, w_proj, w_qkv.transpose(1, 0, 2), small)
    unit_rows_total = half + 2 * sub + 2 * part_rows + small.shape[0]
    small_at = unit_rows_total - small.shape[0]
    two = over_col(slab, 2)
    w_qkv2 = w_qkv.reshape(half, 3 * head_width)
    w_qkv2 = tie(w_qkv2, slab)
    qkv_near = jnp.concatenate([w_qkv2, over_row(w_qkv2)], axis=0)
    vectors = jnp.stack([ln1_gain, ln1_bias, proj_bias, ln2_gain, ln2_bias, fc2_bias])
    vectors, states, teacher, loss_mask = lax.optimization_barrier(
        (vectors, states, teacher, loss_mask, slab)
    )[:4]
    vectors = jnp.concatenate([vectors, over_row(vectors)], axis=1).astype(f32)
    fc1_other, fc2_other, proj_other = over_row(w_fc1), over_row(w_fc2), over_row(w_proj)
    two = tie(two, fc1_other, fc2_other, proj_other)
    two_x, two_y = over_dp(two, 1), over_dp(two, 2)
    states_other = tie(states_other, two)

    all_clips = lengths.shape[0]
    valid_all = (
        loss_mask.reshape(all_clips, L) * (jnp.arange(L)[None, :] < lengths[:, None])
    ).astype(f32)
    valid_total = jnp.maximum(jnp.sum(valid_all), 1.0)
    first_row = ((dp * 2 + row) * 4 + col) * local_rows
    valid = lax.dynamic_slice_in_dim(valid_all.reshape(all_clips * L), first_row, local_rows)
    my_length = lax.dynamic_slice_in_dim(lengths, clip, 1)
    spot = jnp.arange(L)
    position = jnp.where(
        spot < local_rows, second * local_rows + spot, (1 - second) * local_rows + spot - local_rows
    )
    key_bias = jnp.where(position < my_length, 0.0, MASKED).astype(f32)
    key_bias = jnp.broadcast_to(key_bias[:, None], (L, 128))

    gain_one, shift_one = vectors[0], vectors[1]
    norm_one, _, _ = normalize(frame(states).astype(f32), gain_one, shift_one)
    norm_other, _, _ = normalize(frame(states_other).astype(f32), gain_one, shift_one)
    tokens_one = jnp.concatenate([norm_one.astype(bf16), norm_other.astype(bf16)], axis=0)

    zero_bias = jnp.zeros((head_width,), f32)
    score_scale = HD**-0.5
    scale = jnp.where(jnp.arange(3 * head_width) < head_width, score_scale, 1.0).astype(bf16)
    split = local_rows // QT * QT
    later = L - split
    over = local_rows - split

    def project(matrix, q_add, v_add):
        projected = jnp.dot(tokens_one, matrix, preferred_element_type=f32)
        add = jnp.concatenate([q_add.astype(f32), zero_bias, v_add.astype(f32)])
        return (projected + add[None]).astype(bf16) * scale[None]

    packed_near = project(qkv_near, q_bias, v_bias)
    cut_at = two.shape[0] // 32 * 16
    two_x, two_y = tie(two_x, packed_near), tie(two_y, packed_near)
    two_low, two_high = over_dp(two_y[:cut_at], 1), over_dp(two_x[cut_at:], 2)
    one_give = jnp.concatenate([slab[:unit_rows_total], two[:unit_rows_total]], axis=0)
    one = over_col(tie(one_give, states_other), 1)
    near_late, near_late_lse = attend(tie(packed_near, two_x, two_y, one), key_bias, split, later)
    two_low, two_high = tie(two_low, near_late), tie(two_high, near_late)
    two_all = jnp.concatenate([two, two_x, two_y, two_low, two_high], axis=0)
    two_theirs = over_row(two_all)
    near_other = over_col(near_late[over:], 1)
    one_x, one_y = over_dp(one, 1), over_dp(one, 2)
    near_soon, near_soon_lse = attend(
        tie(packed_near, two_all, near_late, one), key_bias, 0, split
    )
    two_theirs = tie(two_theirs, near_soon)
    qkv_far = far_qkv(places, two_all, two_theirs, unit_rows_total, width)
    far_small = two_all[small_at : small_at + small.shape[0]]
    packed_far = project(qkv_far, far_small[4], far_small[5])
    packed_far = tie(packed_far, one, near_other)
    far_late, far_late_lse = attend(packed_far, key_bias, split, later)
    far_other = over_col(far_late[over:], 1)
    one_x, one_y = tie(one_x, far_late), tie(one_y, far_late)
    cut_at = one.shape[0] // 2
    one_low, one_high = over_dp(one_y[:cut_at], 1), over_dp(one_x[cut_at:], 2)
    far_soon, far_soon_lse = attend(tie(packed_far, one_x, one_y, far_late), key_bias, 0, split)
    one_low, one_high = tie(one_low, far_soon), tie(one_high, far_soon)
    one_all = jnp.concatenate([one, one_x, one_y, one_low, one_high], axis=0)
    one_all = tie(one_all, far_other)
    turned = tie(tokens_one, far_late).T
    one_theirs = over_row(one_all)
    attended_rows = jnp.concatenate(
        [
            jnp.concatenate([near_soon, near_late[:over]], axis=0),
            near_other,
            jnp.concatenate([far_soon, far_late[:over]], axis=0),
            far_other,
        ],
        axis=1,
    )

    table = jnp.stack(
        [(dp ^ s) * 4 + (col ^ j) for s in range(4) for j in range(4)]
        + [a * 4 + col for a in range(4)]
        + [dp ^ s for s in range(4)]
        + [col ^ b for b in range(4)]
        + [row]
    ).astype(jnp.int32)
    at = unit_rows_total + small_at
    smalls = jnp.stack(
        [small, one_all[small_at : small_at + 16], two_all[small_at : small_at + 16], one_all[at : at + 16]]
    ).astype(f32)
    loss_scale = all_clips * L * width / 2.0
    factor = (loss_scale * 2.0 / (valid_total * width)).reshape(1)
    (
        outputs,
        hidden,
        grad_pre,
        norm_two,
        grad_low,
        mid_low,
        grad_mid,
        up_own,
        up_give,
        hidden_sum,
        sums,
    ) = middle_block(
        table,
        factor,
        attended_rows,
        states,
        teacher,
        valid[:, None],
        vectors,
        smalls,
        (
            w_fc1,
            fc1_other,
            w_fc2,
            fc2_other,
            w_proj,
            proj_other,
            two_all,
            two_theirs,
            one_all,
            one_theirs,
        ),
    )
    up_far = over_col(up_give, 1)

    def joined(kept, taken):
        return (kept.astype(f32) + taken.astype(f32)).astype(bf16)

    give_fc2 = over_row(dot_tn(grad_low[:, half:], hidden).astype(bf16))
    give_fc1 = over_row(dot_tn(norm_two[:, half:], grad_pre).astype(bf16))
    give_proj = over_row(dot_tn(attended_rows, mid_low[:, half:]).astype(bf16))
    kept_proj = dot_tn(attended_rows, mid_low[:, :half])

    def plane_first(wide):
        keep_x, give_x, keep_y, give_y = wide
        return (keep_x, keep_y), (give_x, give_y), (over_dp(give_x, 1), over_dp(give_y, 2))

    def plane_second(keep, taken):
        shape = ((keep[0].shape[0] // 2, keep[0].shape[1]), bf16)
        keep_x, give_x, keep_y, give_y = on_chip(
            plane_sum_kernel, [shape] * 4, "plane_sum", keep[0], taken[0], keep[1], taken[1]
        )
        return (keep_x, keep_y), (give_x, give_y), (over_dp(give_x, 2), over_dp(give_y, 1))

    def cols_out(keep, taken, rows):
        blocks = on_chip(
            cols_out_kernel,
            [((rows, sub), bf16)] * 4,
            "cols_out",
            *(places, keep[0], taken[0], keep[1], taken[1]),
            tables=1,
        )
        return blocks, [over_col(blocks[j], j) for j in (1, 2, 3)]

    def all_tied(values, *others):
        return [tie(v, *others) for v in values]

    wide = wide_grads(places, grad_low, hidden, give_fc2)
    fc2_keep, fc2_give, fc2_taken = plane_first(wide)
    wide = wide_grads(
        places, tie(norm_two, *fc2_give), grad_pre, give_fc1, (kept_proj, give_proj)
    )
    fc1_keep, fc1_give, fc1_taken = plane_first(wide)

    packed_near = tie(packed_near, *fc2_give, *fc1_give)
    part_near = attend_back(packed_near, key_bias, near_soon_lse, near_soon, up_own, None, 0, 0)
    fc2_keep, fc2_give, fc2_taken = plane_second(fc2_keep, all_tied(fc2_taken, part_near[0]))

    packed_far = tie(packed_far, *fc2_give, part_near[0])
    part_far = attend_back(
        packed_far, key_bias, far_soon_lse, far_soon, up_own, None, head_width, 0
    )
    fc2_blocks, fc2_cols = cols_out(fc2_keep, all_tied(fc2_taken, part_far[0]), 2 * sub)
    fc1_keep, fc1_give, fc1_taken = plane_second(fc1_keep, all_tied(fc1_taken, part_far[0]))

    packed_near = tie(packed_near, *fc2_blocks, *fc1_give)
    grad_near, near_sums = attend_back(
        packed_near, key_bias, near_late_lse, near_late, up_own, up_far, 0, split, part_near
    )
    fc2_cols = all_tied(fc2_cols, grad_near)
    fc1_blocks, fc1_cols = cols_out(
        fc1_keep, all_tied(fc1_taken, grad_near, *fc2_cols), 2 * sub + 2 * part_rows
    )
    near_tied = tie(grad_near, *fc1_blocks)
    near_row = over_row(dot_tn(tokens_one[:, half:], near_tied).astype(bf16))
    wide_near = joined(dot_tn(tokens_one[:, :half], near_tied), near_row)
    deep = half // 4
    near_give = jnp.concatenate([cut(wide_near, quarter(s), deep) for s in (1, 3)], axis=0)
    near_taken = over_dp(near_give, 1)

    packed_far = tie(packed_far, near_give, *fc1_blocks, *fc2_cols)
    grad_far, far_sums = attend_back(
        packed_far, key_bias, far_late_lse, far_late, up_own, up_far, head_width, split, part_far
    )

    norm_own, norm_give, norm_sums = token_back(
        flip, grad_near, grad_far, qkv_near, qkv_far, states, states_other
    )
    norm_taken = over_col(norm_give, 1)
    columns, slots = grad_far.shape[1], 2 * VECTORS
    vec_keep, row_give, kept = on_chip(
        far_grads_kernel,
        [((VECTORS, half), f32), ((half + slots, columns), bf16), ((half, columns), f32)],
        "far_grads",
        *(turned, tie(grad_far, norm_give, near_taken, *fc1_cols), sums, hidden_sum, norm_sums, near_sums, far_sums),
    )
    row_taken = over_row(row_give)
    fc1_cols = all_tied(fc1_cols, row_give)
    mine_rows = fc2_blocks[0].shape[0] + fc1_blocks[0].shape[0]
    (mine,) = on_chip(
        mine_kernel,
        [((mine_rows, sub), bf16)],
        "mine",
        *(fc2_blocks[0], *fc2_cols, fc1_blocks[0], *fc1_cols),
    )
    mine_x = over_dp(mine, 1)
    near_own, far_own, vec_sum, *plane_give = on_chip(
        after_row_kernel,
        [((deep, columns), f32)] * 2
        + [((VECTORS, half), f32)]
        + [((deep + slots + (deep if s == 2 else 0), columns), bf16) for s in (1, 2, 3)],
        "after_row",
        *(places, kept, tie(row_taken, mine), vec_keep, wide_near, tie(near_taken, mine)),
        tables=1,
    )
    plane_taken = [over_dp(plane_give[s - 1], s) for s in (1, 2, 3)]
    mine_two = jnp.concatenate([mine, tie(mine_x, *plane_give)], axis=0)
    plane_taken = all_tied(plane_taken, mine_two, norm_taken)
    near_own, vec_sum, col_give, vec_give = on_chip(
        after_plane_kernel,
        [
            ((deep, columns), f32),
            ((VECTORS, half), f32),
            ((deep + slots, columns), bf16),
            ((slots, half), bf16),
        ],
        "after_plane",
        *(near_own, far_own, vec_sum, *plane_taken),
    )
    mine_y = over_dp(tie(mine_two, col_give), 2)
    col_taken = [over_col(vec_give, 1), over_col(col_give, 2), over_col(vec_give, 3)]
    norm_taken = tie(norm_taken, col_give)
    grad_states = last_norm(flip, norm_own, norm_taken, states, grad_mid, vectors)

    qkv_mine, vec_total = on_chip(
        after_cols_kernel,
        [((deep, columns), bf16), ((VECTORS, half), f32)],
        "after_cols",
        *(near_own, vec_sum, *all_tied(col_taken, grad_states)),
    )
    qkv_back = [over_dp(qkv_mine, s) for s in (1, 2, 3)]
    fc2_grad, fc1_grad, proj_grad = finish(places, [mine_two, tie(mine_y, qkv_mine)], part_rows)
    qkv_grad = finish_qkv(places, [qkv_mine, *all_tied(qkv_back, fc2_grad)]).transpose(1, 0, 2)

    fc1_bias_grad = lax.dynamic_index_in_dim(vec_total[6:14].reshape(4, 4, sub), col, 1, False)
    loss_value = jnp.sum(vec_total[16]) / (valid_total * width)
    return (
        outputs,
        loss_value,
        grad_states,
        vec_total[4],
        vec_total[5],
        qkv_grad,
        vec_total[14, :head_width],
        vec_total[14, head_width:],
        proj_grad,
        vec_total[2],
        vec_total[0],
        vec_total[1],
        fc1_grad,
        fc1_bias_grad.reshape(span),
        fc2_grad,
        vec_total[3],
    )


def solution(mesh):
    sizes = (mesh.shape["dp"], mesh.shape["row"], mesh.shape["col"])
    body = local_paired if sizes == PAIRED_MESH else local_general
    in_specs = (
        P(("dp", "row", "col"), None),
        P("row"),
        P("row"),
        P("row", None, "col"),
        P("col"),
        P("col"),
        P("col", "row"),
        P("row"),
        P("row"),
        P("row"),
        P("row", "col"),
        P("col"),
        P("col", "row"),
        P("row"),
        P(("dp", "row", "col"), None),
        P(),
        P(),
    )
    out_specs = (
        P(("dp", "row", "col"), None),
        P(),
        P(("dp", "row", "col"), None),
        P("row"),
        P("row"),
        P("row", None, "col"),
        P("col"),
        P("col"),
        P("col", "row"),
        P("row"),
        P("row"),
        P("row"),
        P("row", "col"),
        P("col"),
        P("col", "row"),
        P("row"),
    )
    return jax.shard_map(body, mesh=mesh, in_specs=in_specs, out_specs=out_specs, check_vma=False)
```

```python
import functools

import jax
import jax.numpy as jnp
from jax import lax
from jax.experimental import pallas as pl
from jax.experimental.pallas import tpu as pltpu
from jax.sharding import PartitionSpec as P

HD = 64
L = 1568


EPSILON = 1e-06
MASKED = -1e30
ROOT_HALF = 0.7071067811865476
DENSITY_FACTOR = 0.3989422804014327


def normalize(values, factor, offset):
    centered = values - jnp.mean(values, axis=-1, keepdims=True)
    spread = lax.rsqrt(jnp.mean(centered * centered, axis=-1, keepdims=True) + EPSILON)
    normal = centered * spread
    return (normal * factor + offset, normal, spread)


def norm_back(upstream, normal, spread, factor):
    inner = upstream * factor
    center_term = jnp.mean(inner, axis=-1, keepdims=True)
    slope_term = jnp.mean(inner * normal, axis=-1, keepdims=True)
    back = spread * (inner - center_term - normal * slope_term)
    return (back, jnp.sum(upstream * normal, axis=0), jnp.sum(upstream, axis=0))


def gelu_value(values):
    return values * (0.5 * (1.0 + lax.erf(values * ROOT_HALF)))


def gelu_slope(values):
    normal_cdf = 0.5 * (1.0 + lax.erf(values * ROOT_HALF))
    return normal_cdf + values * jnp.exp(-0.5 * values * values) * DENSITY_FACTOR


def masked_scores(queries, key_rows, length, score_scale):
    logits = (
        jnp.einsum("ihd,jhd->hij", queries, key_rows, preferred_element_type=jnp.float32)
        * score_scale
    )
    keep = jnp.arange(key_rows.shape[0]) < length
    return jnp.where(keep[None, None, :], logits, MASKED)


def attend_clip(packed, length, score_scale):
    half_span = packed.shape[0] // 2
    key_rows = packed[:, 1]
    value_rows = packed[:, 2]
    pieces = []
    totals = []
    for block_index in range(2):
        queries = packed[block_index * half_span : (block_index + 1) * half_span, 0]
        logits = masked_scores(queries, key_rows, length, score_scale)
        peak = jnp.max(logits, axis=-1, keepdims=True)
        total = peak + jnp.log(jnp.sum(jnp.exp(logits - peak), axis=-1, keepdims=True))
        weights = jnp.exp(logits - total).astype(jnp.bfloat16)
        pieces.append(
            jnp.einsum("hij,jhd->ihd", weights, value_rows, preferred_element_type=jnp.float32)
        )
        totals.append(total[..., 0])
    return (jnp.concatenate(pieces, 0), jnp.concatenate(totals, 1))


def attend_clip_back(packed, length, totals, upstream, score_scale):
    half_span = packed.shape[0] // 2
    key_rows = packed[:, 1]
    value_rows = packed[:, 2]
    grad_keys = jnp.zeros(key_rows.shape, jnp.float32)
    grad_values = jnp.zeros(value_rows.shape, jnp.float32)
    grad_queries = []
    for block_index in range(2):
        first = block_index * half_span
        queries = packed[first : first + half_span, 0]
        logits = masked_scores(queries, key_rows, length, score_scale)
        probs = jnp.exp(logits - totals[:, first : first + half_span][..., None])
        incoming = upstream[first : first + half_span]
        grad_values = grad_values + jnp.einsum(
            "hij,ihd->jhd", probs.astype(jnp.bfloat16), incoming, preferred_element_type=jnp.float32
        )
        grad_probs = jnp.einsum(
            "ihd,jhd->hij", incoming, value_rows, preferred_element_type=jnp.float32
        )
        grad_logits = (
            probs * (grad_probs - jnp.sum(probs * grad_probs, axis=-1, keepdims=True))
        ).astype(jnp.bfloat16)
        grad_queries.append(
            jnp.einsum("hij,jhd->ihd", grad_logits, key_rows, preferred_element_type=jnp.float32)
            * score_scale
        )
        grad_keys = (
            grad_keys
            + jnp.einsum("hij,ihd->jhd", grad_logits, queries, preferred_element_type=jnp.float32)
            * score_scale
        )
    return jnp.stack([jnp.concatenate(grad_queries, 0), grad_keys, grad_values], axis=1)


def local_general(
    states,
    ln1_gain,
    ln1_bias,
    w_qkv,
    q_bias,
    v_bias,
    w_proj,
    proj_bias,
    ln2_gain,
    ln2_bias,
    w_fc1,
    fc1_bias,
    w_fc2,
    fc2_bias,
    teacher,
    loss_mask,
    lengths,
):
    row_count = lax.axis_size("row")
    col_count = lax.axis_size("col")
    col_index = lax.axis_index("col")
    group_index = lax.axis_index("dp") * row_count + lax.axis_index("row")
    local_rows = states.shape[0]
    width = states.shape[1]
    group_rows = local_rows * col_count
    clip_count = group_rows // L
    head_width = w_qkv.shape[2]
    heads_here = head_width // HD
    hidden_width = w_fc1.shape[1]
    score_scale = HD ** (-0.5)
    vectors = jnp.stack([ln1_gain, ln1_bias, proj_bias, ln2_gain, ln2_bias, fc2_bias])
    qkv_full, proj_full, fc1_full, fc2_full, vector_full = (
        lax.all_gather(w_qkv, "row", axis=0, tiled=True),
        lax.all_gather(w_proj, "row", axis=1, tiled=True),
        lax.all_gather(w_fc1, "row", axis=0, tiled=True),
        lax.all_gather(w_fc2, "row", axis=1, tiled=True),
        lax.all_gather(vectors, "row", axis=1, tiled=True),
    )
    vector_full = vector_full.astype(jnp.float32)
    gain_one = vector_full[0]
    shift_one = vector_full[1]
    bias_proj = vector_full[2]
    gain_two = vector_full[3]
    shift_two = vector_full[4]
    bias_two = vector_full[5]
    all_clips = lengths.shape[0]
    valid_all = (
        loss_mask.reshape(all_clips, L) * (jnp.arange(L)[None, :] < lengths[:, None])
    ).astype(jnp.float32)
    valid_total = jnp.maximum(jnp.sum(valid_all), 1.0)
    first_row = (group_index * col_count + col_index) * local_rows
    valid = lax.dynamic_slice_in_dim(valid_all.reshape(all_clips * L), first_row, local_rows)
    my_lengths = lax.dynamic_slice_in_dim(lengths, group_index * clip_count, clip_count)
    inputs = states.astype(jnp.float32)
    norm_one, unit_one, spread_one = normalize(inputs, gain_one, shift_one)
    norm_one = norm_one.astype(jnp.bfloat16)
    tokens_one = lax.all_gather(norm_one, "col", axis=0, tiled=True)
    qkv_matrix = qkv_full.reshape(width, 3 * head_width)
    projected = jnp.dot(tokens_one, qkv_matrix, preferred_element_type=jnp.float32).reshape(
        group_rows, 3, head_width
    )
    bias_rows = jnp.stack(
        [
            q_bias.astype(jnp.float32),
            jnp.zeros((head_width,), jnp.float32),
            v_bias.astype(jnp.float32),
        ]
    )
    packed = (projected + bias_rows[None]).astype(jnp.bfloat16)
    clips_packed = packed.reshape(clip_count, L, 3, heads_here, HD)
    attended, totals = lax.map(
        lambda element: attend_clip(element[0], element[1], score_scale), (clips_packed, my_lengths)
    )
    attended = attended.reshape(group_rows, head_width).astype(jnp.bfloat16)
    proj_whole, qkv_whole = (
        lax.all_gather(proj_full, "col", axis=0, tiled=True),
        lax.all_gather(qkv_full, "col", axis=2, tiled=True),
    )
    attended_rows = lax.all_to_all(attended, "col", split_axis=0, concat_axis=1, tiled=True)
    middle = inputs + (
        jnp.dot(attended_rows, proj_whole, preferred_element_type=jnp.float32) + bias_proj
    )
    norm_two, unit_two, spread_two = normalize(middle, gain_two, shift_two)
    norm_two = norm_two.astype(jnp.bfloat16)
    fc1_whole, fc2_whole, fc1_bias_whole = (
        lax.all_gather(fc1_full, "col", axis=1, tiled=True),
        lax.all_gather(fc2_full, "col", axis=0, tiled=True),
        lax.all_gather(fc1_bias, "col", axis=0, tiled=True),
    )
    hidden_pre = jnp.dot(
        norm_two, fc1_whole, preferred_element_type=jnp.float32
    ) + fc1_bias_whole.astype(jnp.float32)
    hidden = gelu_value(hidden_pre).astype(jnp.bfloat16)
    outputs = middle + (jnp.dot(hidden, fc2_whole, preferred_element_type=jnp.float32) + bias_two)
    differ = outputs - teacher.astype(jnp.float32)
    numerator = jnp.sum(valid[:, None] * differ * differ)
    loss_scale = all_clips * L * width / 2.0
    grad_out = loss_scale * 2.0 / (valid_total * width) * valid[:, None] * differ
    grad_low = grad_out.astype(jnp.bfloat16)
    grad_hidden = jnp.dot(grad_low, fc2_whole.T, preferred_element_type=jnp.float32)
    grad_pre = (grad_hidden * gelu_slope(hidden_pre)).astype(jnp.bfloat16)
    wide_fc2 = jnp.dot(hidden.T, grad_low, preferred_element_type=jnp.float32)
    wide_fc1 = jnp.dot(norm_two.T, grad_pre, preferred_element_type=jnp.float32)
    fc1_grad_part, fc2_grad_part = (
        lax.psum_scatter(
            wide_fc1.astype(jnp.bfloat16), "col", scatter_dimension=1, tiled=True
        ).astype(jnp.float32),
        lax.psum_scatter(
            wide_fc2.astype(jnp.bfloat16), "col", scatter_dimension=0, tiled=True
        ).astype(jnp.float32),
    )
    fc1_bias_sum = jnp.sum(grad_pre, axis=0, dtype=jnp.float32)
    grad_norm_two = jnp.dot(grad_pre, fc1_whole.T, preferred_element_type=jnp.float32)
    back_two, gain_two_grad, shift_two_grad = norm_back(
        grad_norm_two, unit_two, spread_two, gain_two
    )
    grad_mid = grad_out + back_two
    mid_low = grad_mid.astype(jnp.bfloat16)
    wide_proj = jnp.dot(attended_rows.T, mid_low, preferred_element_type=jnp.float32)
    proj_grad_part = lax.psum_scatter(
        wide_proj.astype(jnp.bfloat16), "col", scatter_dimension=0, tiled=True
    )
    grad_attended_rows = jnp.dot(mid_low, proj_whole.T, preferred_element_type=jnp.float32).astype(
        jnp.bfloat16
    )
    grad_attended = lax.all_to_all(
        grad_attended_rows, "col", split_axis=1, concat_axis=0, tiled=True
    )
    grads_packed = lax.map(
        lambda element: attend_clip_back(
            element[0], element[1], element[2], element[3], score_scale
        ),
        (clips_packed, my_lengths, totals, grad_attended.reshape(clip_count, L, heads_here, HD)),
    )
    grads_packed = grads_packed.reshape(group_rows, 3 * head_width).astype(jnp.bfloat16)
    qkv_grad_part = jnp.dot(tokens_one.T, grads_packed, preferred_element_type=jnp.float32).reshape(
        width, 3, head_width
    )
    bias_sums = jnp.sum(grads_packed.reshape(group_rows, 3, head_width), axis=0, dtype=jnp.float32)
    grads_rows = lax.all_to_all(
        grads_packed.reshape(group_rows, 3, head_width),
        "col",
        split_axis=0,
        concat_axis=2,
        tiled=True,
    )
    grad_norm_one = jnp.dot(
        grads_rows.reshape(local_rows, 3 * width),
        qkv_whole.reshape(width, 3 * width).T,
        preferred_element_type=jnp.float32,
    )
    back_one, gain_one_grad, shift_one_grad = norm_back(
        grad_norm_one, unit_one, spread_one, gain_one
    )
    grad_states = (grad_mid + back_one).astype(jnp.bfloat16)
    proj_bias_grad = jnp.sum(mid_low, axis=0, dtype=jnp.float32)
    fc2_bias_grad = jnp.sum(grad_low, axis=0, dtype=jnp.float32)
    token_vectors = jnp.stack(
        [
            gain_one_grad,
            shift_one_grad,
            proj_bias_grad,
            gain_two_grad,
            shift_two_grad,
            fc2_bias_grad,
        ]
    )
    head_vectors = lax.dynamic_update_slice(
        jnp.zeros((2, width), jnp.float32),
        jnp.stack([bias_sums[0], bias_sums[2]]),
        (0, col_index * head_width),
    )
    token_sums, head_sums, fc1_sums, loss_sum = lax.psum(
        (token_vectors, head_vectors, fc1_bias_sum, numerator), ("dp", "row", "col")
    )
    qkv_rows, proj_cols, fc1_rows, fc2_cols = (
        lax.psum_scatter(
            qkv_grad_part.astype(jnp.bfloat16), "row", scatter_dimension=0, tiled=True
        ).astype(jnp.float32),
        lax.psum_scatter(proj_grad_part, "row", scatter_dimension=1, tiled=True).astype(
            jnp.float32
        ),
        lax.psum_scatter(
            fc1_grad_part.astype(jnp.bfloat16), "row", scatter_dimension=0, tiled=True
        ).astype(jnp.float32),
        lax.psum_scatter(
            fc2_grad_part.astype(jnp.bfloat16), "row", scatter_dimension=1, tiled=True
        ).astype(jnp.float32),
    )
    qkv_grad, proj_grad, fc1_grad, fc2_grad = (
        lax.psum(qkv_rows.astype(jnp.bfloat16), "dp").astype(jnp.float32),
        lax.psum(proj_cols.astype(jnp.bfloat16), "dp").astype(jnp.float32),
        lax.psum(fc1_rows.astype(jnp.bfloat16), "dp").astype(jnp.float32),
        lax.psum(fc2_cols.astype(jnp.bfloat16), "dp").astype(jnp.float32),
    )
    half_width = width // row_count
    token_part = lax.dynamic_slice_in_dim(
        token_sums, lax.axis_index("row") * half_width, half_width, 1
    )
    head_part = lax.dynamic_slice_in_dim(head_sums, col_index * head_width, head_width, 1)
    fc1_part = lax.dynamic_slice_in_dim(fc1_sums, col_index * hidden_width, hidden_width, 0)
    loss_value = loss_sum / (valid_total * width)
    return (
        outputs.astype(jnp.bfloat16),
        loss_value,
        grad_states,
        token_part[0],
        token_part[1],
        qkv_grad,
        head_part[0],
        head_part[1],
        proj_grad,
        token_part[2],
        token_part[3],
        token_part[4],
        fc1_grad,
        fc1_part,
        fc2_grad,
        token_part[5],
    )


PAIRED_MESH = (4, 2, 4)
GROUP = 4


def small_cost(flops):
    return pl.CostEstimate(flops=flops, bytes_accessed=0, transcendentals=0)
QT = 128


def dot_nn(a, b):
    return lax.dot_general(a, b, (((1,), (0,)), ((), ())), preferred_element_type=jnp.float32)


def dot_nt(a, b):
    return lax.dot_general(a, b, (((1,), (1,)), ((), ())), preferred_element_type=jnp.float32)


def dot_tn(a, b):
    return lax.dot_general(a, b, (((0,), (0,)), ((), ())), preferred_element_type=jnp.float32)


def head_stack(values, zero):
    lane_head = lax.broadcasted_iota(jnp.int32, values.shape, 1) // HD
    return jnp.concatenate([jnp.where(lane_head == h, values, zero) for h in range(GROUP)], axis=0)


def head_unstack(wide, count):
    return jnp.concatenate(
        [wide[h * HD : (h + 1) * HD, h * count : (h + 1) * count] for h in range(GROUP)], axis=0
    ).T


def tiles_of(rows, tile):
    full = rows // QT

    @pl.loop(0, full)
    def _(index):
        tile(pl.multiple_of(index * QT, QT), QT, index)

    if rows > full * QT:
        tile(full * QT, rows - full * QT, full)


def attend_kernel(first, packed_ref, bias_ref, out_ref, lse_ref, vt_ref):
    width = GROUP * HD
    vt_ref[...] = packed_ref[:, 2 * width : 3 * width].T

    def tile(start, count, index):
        cols = GROUP * count
        stacked = head_stack(
            packed_ref[pl.ds(first + start, count), 0:width], jnp.zeros((), jnp.bfloat16)
        )
        keys = packed_ref[:, width : 2 * width]
        bias = bias_ref[...]
        scores = dot_nt(keys, stacked) + jnp.concatenate([bias] * (cols // 128), axis=1)
        peak = jnp.max(scores, axis=0, keepdims=True)
        weights = jnp.exp(scores - peak)
        total = jnp.sum(weights, axis=0, keepdims=True)
        wide = dot_nn(vt_ref[...], weights.astype(jnp.bfloat16)) * (1.0 / total)
        out_ref[pl.ds(start, count), :] = head_unstack(wide, count).astype(jnp.bfloat16)
        lse_ref[index, :, 0:cols] = jnp.broadcast_to(peak + jnp.log(total), (8, cols))

    tiles_of(out_ref.shape[0], tile)


def attend_back_kernel(
    first, lane, last, packed_ref, bias_ref, lse_ref, att_ref, up_own_ref, up_far_ref, *refs
):
    width = GROUP * HD
    lanes = slice(lane, lane + width)
    own_rows = up_own_ref.shape[0]
    if last:
        dq_in, dk_in, dv_in, out_ref, sum_ref, kt_ref, up_ref, dk_ref, dv_ref = refs
        dk_ref[...] = dk_in[...]
        dv_ref[...] = dv_in[...]
        out_ref[0:first, 0:width] = dq_in[...]
        rows = out_ref.shape[0] - first
        up_ref[0 : own_rows - first, :] = up_own_ref[first:own_rows, lanes]
        up_ref[own_rows - first :, :] = up_far_ref[:, lanes]
    else:
        out_ref, dk_ref, dv_ref, kt_ref, up_ref = refs
        dk_ref[...] = jnp.zeros_like(dk_ref)
        dv_ref[...] = jnp.zeros_like(dv_ref)
        rows = out_ref.shape[0]
        up_ref[...] = up_own_ref[0:rows, lanes]
    kt_ref[...] = packed_ref[:, width : 2 * width].T

    def tile(start, count, index):
        cols = GROUP * count
        zero = jnp.zeros((), jnp.bfloat16)
        up = up_ref[pl.ds(start, count), :]
        stacked = head_stack(packed_ref[pl.ds(first + start, count), 0:width], zero)
        up_stacked = head_stack(up, zero)
        product = head_stack(
            up.astype(jnp.float32) * att_ref[pl.ds(start, count), :].astype(jnp.float32),
            jnp.zeros((), jnp.float32),
        )
        high = product.astype(jnp.bfloat16)
        low = (product - high.astype(jnp.float32)).astype(jnp.bfloat16)
        ones = jnp.ones((8, width), jnp.bfloat16)
        delta = (dot_nt(ones, high) + dot_nt(ones, low))[0:1]
        keys = packed_ref[:, width : 2 * width]
        values = packed_ref[:, 2 * width : 3 * width]
        bias = bias_ref[...]
        scores = dot_nt(keys, stacked) + jnp.concatenate([bias] * (cols // 128), axis=1)
        weights = jnp.exp(scores - lse_ref[index, 0:1, 0:cols])
        dv_ref[...] += dot_nn(weights.astype(jnp.bfloat16), up_stacked)
        grad = (weights * (dot_nt(values, up_stacked) - delta)).astype(jnp.bfloat16)
        dk_ref[...] += dot_nn(grad, stacked)
        wide = dot_nn(kt_ref[...], grad) * (HD**-0.5)
        at = pl.ds(first + start if last else start, count)
        out_ref[at, 0:width] = head_unstack(wide, count).astype(jnp.bfloat16)

    tiles_of(rows, tile)
    if last:
        out_ref[:, width : 2 * width] = dk_ref[...].astype(jnp.bfloat16)
        out_ref[:, 2 * width : 3 * width] = dv_ref[...].astype(jnp.bfloat16)
        for k in range(3):
            part = out_ref[:, k * width : (k + 1) * width].astype(jnp.float32)
            sum_ref[:, k * width : (k + 1) * width] = jnp.sum(part, axis=0, keepdims=True)


def attend(packed, bias, first, rows):
    tokens, width = packed.shape[0], GROUP * HD
    tiles = -(-rows // QT)
    return pl.pallas_call(
        functools.partial(attend_kernel, first),
        out_shape=(
            jax.ShapeDtypeStruct((rows, width), jnp.bfloat16),
            jax.ShapeDtypeStruct((tiles, 8, GROUP * QT), jnp.float32),
        ),
        in_specs=[pl.BlockSpec(memory_space=pltpu.VMEM)] * 2,
        out_specs=[pl.BlockSpec(memory_space=pltpu.VMEM)] * 2,
        scratch_shapes=[pltpu.VMEM((width, tokens), jnp.bfloat16)],
        compiler_params=pltpu.CompilerParams(vmem_limit_bytes=32 << 20),
        cost_estimate=pl.CostEstimate(
            flops=2 * rows * tokens * width * 4, bytes_accessed=6 << 20, transcendentals=0
        ),
        name="attend",
    )(packed, bias)


def attend_back(packed, bias, lse, att, up_own, up_far, lane, first, before=None):
    tokens, width = packed.shape[0], GROUP * HD
    rows = att.shape[0]
    total = jax.ShapeDtypeStruct((tokens, width), jnp.float32)
    vmem = pl.BlockSpec(memory_space=pltpu.VMEM)
    scratch = [pltpu.VMEM((width, tokens), jnp.bfloat16), pltpu.VMEM((rows, width), jnp.bfloat16)]
    if before is None:
        extra = ()
        out_shape = (jax.ShapeDtypeStruct((rows, width), jnp.bfloat16), total, total)
        up_far = up_own
    else:
        extra = before
        out_shape = (
            jax.ShapeDtypeStruct((tokens, 3 * width), jnp.bfloat16),
            jax.ShapeDtypeStruct((1, 3 * width), jnp.float32),
        )
        scratch += [pltpu.VMEM((tokens, width), jnp.float32)] * 2
    return pl.pallas_call(
        functools.partial(attend_back_kernel, first, lane, before is not None),
        out_shape=out_shape,
        in_specs=[vmem] * (6 + len(extra)),
        out_specs=(vmem,) * len(out_shape),
        scratch_shapes=scratch,
        compiler_params=pltpu.CompilerParams(vmem_limit_bytes=52 << 20),
        cost_estimate=pl.CostEstimate(
            flops=4 * rows * tokens * width * 4, bytes_accessed=10 << 20, transcendentals=0
        ),
        name="attend_back",
    )(packed, bias, lse, att, up_own, up_far, *extra)


FF_CHUNK = 512
ROWS = 112


def rows_of(total, body):
    @pl.loop(0, total // ROWS)
    def _(index):
        body(pl.ds(pl.multiple_of(index * ROWS, ROWS), ROWS))


def unit_rows(values):
    centered = values - jnp.mean(values, axis=-1, keepdims=True)
    spread = lax.rsqrt(jnp.mean(centered * centered, axis=-1, keepdims=True) + EPSILON)
    return centered * spread, spread


def middle_kernel(
    table_ref,
    factor_ref,
    input_ref,
    target_ref,
    valid_ref,
    vector_ref,
    small_ref,
    fc1_own,
    fc1_other,
    fc2_own,
    fc2_other,
    proj_own,
    proj_other,
    two_mine,
    two_theirs,
    *refs,
):
    one_mine, one_theirs, att_parts, refs = refs[:5], refs[5:10], refs[10:16], refs[16:]
    (
        att_hbm,
        out_hbm,
        hidden_hbm,
        pre_hbm,
        norm_hbm,
        grad_low_hbm,
        mid_low_ref,
        grad_mid_ref,
        up_own_ref,
        up_give_ref,
        hidden_sum_ref,
        sums_ref,
        fc1_v,
        fc2_v,
        proj_v,
        middle_v,
        back_v,
        out_ref,
        hidden_ref,
        pre_ref,
        norm_ref,
        grad_low_ref,
        att_ref,
        sem_one,
        sem_two,
        sem_proj,
        sem_att,
        sem_out,
    ) = refs
    stores = [
        pltpu.make_async_copy(source, target, sem_out.at[i])
        for i, (source, target) in enumerate(
            (
                (norm_ref, norm_hbm),
                (hidden_ref, hidden_hbm),
                (out_ref, out_hbm),
                (grad_low_ref, grad_low_hbm),
                (pre_ref, pre_hbm),
                (att_ref, att_hbm),
            )
        )
    ]
    f32, bf16 = jnp.float32, jnp.bfloat16
    total_rows = input_ref.shape[0]
    half = fc1_own.shape[0]
    sub = fc1_own.shape[1] // 4
    heads = proj_own.shape[0]
    part = heads // 4
    hidden_total = hidden_ref.shape[1]
    chunks = hidden_total // FF_CHUNK
    unit = half + 2 * sub + 2 * part + 16

    def fc1_copy(source, side, at):
        lanes = pl.ds(pl.multiple_of(at * sub, sub), sub)
        pltpu.make_async_copy(
            source, fc1_v.at[side * half : (side + 1) * half, lanes], sem_one.at[at // 2]
        ).start()

    def fc2_copy(source, side, i, at):
        lane = side * half + i * sub
        pltpu.make_async_copy(
            source, fc2_v.at[pl.ds(pl.multiple_of(at * sub, sub), sub), lane : lane + sub], sem_two
        ).start()

    sources = []
    for s in range(4):
        step = two_mine.shape[0] // 4
        sources.append((s, 2, two_mine, two_theirs, s * step))
        low, high = (3, 4) if s == 3 else (s, s)
        sources.append((s, 1, one_mine[low], one_theirs[low], 0))
        sources.append((s, 3, one_mine[high], one_theirs[high], 0 if s == 3 else unit))

    early_rows = att_parts[0].shape[0]
    for at in range(2):
        soon, late, other = att_parts[3 * at : 3 * at + 3]
        lanes = slice(2 * at * heads, (2 * at + 1) * heads)
        pltpu.make_async_copy(soon, att_ref.at[0:early_rows, lanes], sem_att).start()
        pltpu.make_async_copy(
            late.at[0 : total_rows - early_rows], att_ref.at[early_rows:total_rows, lanes], sem_att
        ).start()
        lanes = slice((2 * at + 1) * heads, (2 * at + 2) * heads)
        pltpu.make_async_copy(other, att_ref.at[:, lanes], sem_att).start()
    for side, ref in enumerate((proj_own, proj_other)):
        pltpu.make_async_copy(
            ref, proj_v.at[0:heads, side * half : (side + 1) * half], sem_proj
        ).start()
    for s, j, *refs, base in sources:
        rows = pl.ds(pl.multiple_of(j * heads + table_ref[20 + s] * part, part), part)
        for side in range(2):
            for i in range(2):
                low = base + half + 2 * sub + i * part
                lane = side * half + i * sub
                pltpu.make_async_copy(
                    refs[side].at[low : low + part, :], proj_v.at[rows, lane : lane + sub], sem_proj
                ).start()
    for a in range(4):
        for side, ref in enumerate((fc1_own, fc1_other)):
            fc1_copy(ref.at[:, a * sub : (a + 1) * sub], side, table_ref[16 + a])
    for s, j, *refs, base in sources:
        for side in range(2):
            fc1_copy(refs[side].at[base : base + half, :], side, table_ref[4 * s + j])
    for a in range(4):
        for side, ref in enumerate((fc2_own, fc2_other)):
            for i in range(2):
                fc2_copy(
                    ref.at[a * sub : (a + 1) * sub, i * sub : (i + 1) * sub], side, i, table_ref[16 + a]
                )
    for s, j, *refs, base in sources:
        for side in range(2):
            for i in range(2):
                low = base + half + i * sub
                fc2_copy(refs[side].at[low : low + sub, :], side, i, table_ref[4 * s + j])

    def lanes_of(i):
        return pl.ds(pl.multiple_of((table_ref[28] ^ i) * half, half), half)

    sums_ref[...] = jnp.zeros_like(sums_ref)

    pltpu.make_async_copy(att_ref, att_ref, sem_att).wait()
    stores[5].start()
    pltpu.make_async_copy(proj_v, proj_v, sem_proj).wait()
    for i in range(2):
        cols = slice(i * half, (i + 1) * half)
        middle_v[:, cols] = input_ref[:, lanes_of(i)].astype(f32) + (
            dot_nn(att_ref[...], proj_v[:, cols]) + vector_ref[2:3, cols]
        )

    @functools.partial(rows_of, total_rows)
    def _(rows):
        normal, _ = unit_rows(middle_v[rows, :])
        norm_ref[rows, :] = (normal * vector_ref[3:4, :] + vector_ref[4:5, :]).astype(bf16)

    stores[0].start()

    @pl.loop(0, chunks)
    def _(k):
        span = pl.ds(pl.multiple_of(k * FF_CHUNK, FF_CHUNK), FF_CHUNK)
        pltpu.make_async_copy(fc1_v.at[:, span], fc1_v.at[:, span], sem_one.at[k]).wait()
        a = k // 2
        bias = jnp.concatenate(
            [
                small_ref[table_ref[24 + 2 * (k % 2) + i], pl.ds(a, 1), :]
                for i in range(FF_CHUNK // sub)
            ],
            axis=1,
        )
        pre = dot_nn(norm_ref[...], fc1_v[:, span]) + bias
        cdf = 0.5 * (1.0 + lax.erf(pre * ROOT_HALF))
        hidden_ref[:, span] = (pre * cdf).astype(bf16)
        slope = cdf + pre * jnp.exp(-0.5 * pre * pre) * DENSITY_FACTOR
        pre_ref[:, span] = slope.astype(bf16)

    stores[1].start()
    pltpu.make_async_copy(fc2_v, fc2_v, sem_two).wait()
    for i in range(2):
        cols = slice(i * half, (i + 1) * half)
        total = middle_v[:, cols] + (dot_nn(hidden_ref[...], fc2_v[:, cols]) + vector_ref[5:6, cols])
        out_ref[:, lanes_of(i)] = total.astype(bf16)
        differ = total - target_ref[:, lanes_of(i)].astype(f32)
        weighted = valid_ref[...] * differ
        sums_ref[0:1, cols] = jnp.sum(weighted * differ, axis=0, keepdims=True)
        grad = factor_ref[0] * weighted
        grad_mid_ref[:, cols] = grad
        low = grad.astype(bf16)
        grad_low_ref[:, cols] = low
        sums_ref[1:2, cols] = jnp.sum(low.astype(f32), axis=0, keepdims=True)

    stores[2].start()
    stores[3].start()

    @pl.loop(0, chunks)
    def _(k):
        span = pl.ds(pl.multiple_of(k * FF_CHUNK, FF_CHUNK), FF_CHUNK)
        back = dot_nt(grad_low_ref[...], fc2_v[span, :])
        back = (back * pre_ref[:, span].astype(f32)).astype(bf16)
        pre_ref[:, span] = back
        hidden_sum_ref[0:1, span] = jnp.sum(back.astype(f32), axis=0, keepdims=True)

    stores[4].start()
    for i in range(2):
        cols = slice(i * half, (i + 1) * half)
        back_v[:, cols] = dot_nt(pre_ref[...], fc1_v[cols, :])

    @functools.partial(rows_of, total_rows)
    def _(rows):
        normal, spread = unit_rows(middle_v[rows, :])
        upstream = back_v[rows, :]
        inner = upstream * vector_ref[3:4, :]
        center = jnp.mean(inner, axis=-1, keepdims=True)
        slope = jnp.mean(inner * normal, axis=-1, keepdims=True)
        grad = grad_mid_ref[rows, :] + spread * (inner - center - normal * slope)
        grad_mid_ref[rows, :] = grad
        low = grad.astype(bf16)
        mid_low_ref[rows, :] = low
        sums_ref[2:3, :] += jnp.sum(upstream * normal, axis=0, keepdims=True)
        sums_ref[3:4, :] += jnp.sum(upstream, axis=0, keepdims=True)
        sums_ref[4:5, :] += jnp.sum(low.astype(f32), axis=0, keepdims=True)

    for j, (ref, at) in enumerate(((up_own_ref, 0), (up_give_ref, 0), (up_own_ref, 1), (up_give_ref, 1))):
        grad = dot_nt(mid_low_ref[...], proj_v[j * heads : (j + 1) * heads, :])
        ref[:, at * heads : (at + 1) * heads] = grad.astype(bf16)
    for store in stores:
        store.wait()


def middle_block(table, factor, inputs, target, valid, vectors, smalls, pieces):
    rows, width = inputs.shape
    hidden = 4 * pieces[0].shape[1]
    vmem = pl.BlockSpec(memory_space=pltpu.VMEM)
    smem = pl.BlockSpec(memory_space=pltpu.SMEM)
    anywhere = pl.BlockSpec(memory_space=pl.ANY)
    f32, bf16 = jnp.float32, jnp.bfloat16

    def result(columns, dtype):
        return jax.ShapeDtypeStruct((rows, columns), dtype)

    return pl.pallas_call(
        middle_kernel,
        out_shape=(
            result(width, bf16),
            result(width, bf16),
            result(hidden, bf16),
            result(hidden, bf16),
            result(width, bf16),
            result(width, bf16),
            result(width, bf16),
            result(width, f32),
            result(width // 2, bf16),
            result(width // 2, bf16),
            jax.ShapeDtypeStruct((1, hidden), f32),
            jax.ShapeDtypeStruct((8, width), f32),
        ),
        in_specs=[smem] * 2 + [vmem] * 5 + [anywhere] * len(pieces),
        out_specs=[anywhere] * 6 + [vmem] * 6,
        scratch_shapes=[
            pltpu.VMEM((width, hidden), bf16),
            pltpu.VMEM((hidden, width), bf16),
            pltpu.VMEM((width, width), bf16),
            pltpu.VMEM((rows, width), f32),
            pltpu.VMEM((rows, width), f32),
            pltpu.VMEM((rows, width), bf16),
            pltpu.VMEM((rows, hidden), bf16),
            pltpu.VMEM((rows, hidden), bf16),
            pltpu.VMEM((rows, width), bf16),
            pltpu.VMEM((rows, width), bf16),
            pltpu.VMEM((rows, width), bf16),
            pltpu.SemaphoreType.DMA((hidden // FF_CHUNK,)),
            pltpu.SemaphoreType.DMA,
            pltpu.SemaphoreType.DMA,
            pltpu.SemaphoreType.DMA,
            pltpu.SemaphoreType.DMA((6,)),
        ],
        compiler_params=pltpu.CompilerParams(vmem_limit_bytes=62 << 20),
        cost_estimate=pl.CostEstimate(
            flops=2 * rows * width * hidden, bytes_accessed=44 << 20, transcendentals=0
        ),
        name="middle_block",
    )(table, factor, inputs, target, valid, vectors, smalls, *pieces)


def swap(values, axis, mask, size):
    return lax.ppermute(values, axis, [(i, i ^ mask) for i in range(size)])


def over_row(values):
    return swap(values, "row", 1, 2)


def over_dp(values, mask):
    return swap(values, "dp", mask, 4)


def over_col(values, mask):
    return swap(values, "col", mask, 4)


def cut(values, index, size, axis=0):
    return lax.dynamic_slice_in_dim(values, index * size, size, axis)


def place(pieces, index_of, axis):
    size = pieces[0].shape[axis]
    shape = list(pieces[0].shape)
    shape[axis] = size * len(pieces)
    whole = jnp.zeros(shape, pieces[0].dtype)
    for s, piece in enumerate(pieces):
        whole = lax.dynamic_update_slice_in_dim(whole, piece, index_of(s) * size, axis)
    return whole


def copies(listed, sem_ref):
    for index, (source, target) in enumerate(listed):
        pltpu.make_async_copy(source, target, sem_ref.at[index]).start()
    for index, (source, target) in enumerate(listed):
        pltpu.make_async_copy(source, target, sem_ref.at[index]).wait()


def slab_kernel(places_ref, fc1_ref, fc2_ref, proj_ref, qkv_ref, small_ref, out_ref, sem_ref):
    half, sub = fc1_ref.shape[0], fc1_ref.shape[1] // 4
    part, deep = proj_ref.shape[0] // 4, half // 4
    mine = places_ref[0]
    fc2 = fc2_ref.at[pl.ds(pl.multiple_of(mine * sub, sub), sub)]
    proj = proj_ref.at[pl.ds(pl.multiple_of(mine * part, part), part)]
    listed = [(fc1_ref.at[:, pl.ds(pl.multiple_of(mine * sub, sub), sub)], half)]
    listed += [(fc2.at[:, i * sub : (i + 1) * sub], sub) for i in range(2)]
    listed += [(proj.at[:, i * sub : (i + 1) * sub], part) for i in range(2)]
    listed += [(small_ref, small_ref.shape[0])]
    rows = pl.ds(pl.multiple_of(mine * deep, deep), deep)
    listed += [(qkv_ref.at[k, rows], deep) for k in range(3)]
    pairs, at = [], 0
    for source, count in listed:
        pairs.append((source, out_ref.at[at : at + count]))
        at += count
    copies(pairs, sem_ref)


def make_slab(places, fc1, fc2, proj, qkv, small):
    half, sub = fc1.shape[0], fc1.shape[1] // 4
    rows = half + 2 * sub + proj.shape[0] // 2 + small.shape[0] + 3 * (half // 4)
    anywhere = pl.BlockSpec(memory_space=pl.ANY)
    return pl.pallas_call(
        slab_kernel,
        out_shape=jax.ShapeDtypeStruct((rows, sub), fc1.dtype),
        in_specs=[pl.BlockSpec(memory_space=pltpu.SMEM)] + [anywhere] * 5,
        out_specs=pl.BlockSpec(memory_space=pltpu.VMEM),
        scratch_shapes=[pltpu.SemaphoreType.DMA((9,))],
        cost_estimate=small_cost(100000000),
        name="make_slab",
    )(places, fc1, fc2, proj, qkv, small)


def far_qkv_kernel(base, places_ref, mine_ref, theirs_ref, out_ref, sem_ref):
    sub = mine_ref.shape[1]
    half = out_ref.shape[0] // 2
    deep, step = half // 4, mine_ref.shape[0] // 4
    pairs = []
    for side, ref in enumerate((mine_ref, theirs_ref)):
        for s in range(4):
            rows = pl.ds(pl.multiple_of(side * half + places_ref[s] * deep, deep), deep)
            for k in range(3):
                at = s * step + base + k * deep
                pairs.append((ref.at[at : at + deep], out_ref.at[rows, k * sub : (k + 1) * sub]))
    copies(pairs, sem_ref)


def far_qkv(places, mine, theirs, base, width):
    anywhere = pl.BlockSpec(memory_space=pl.ANY)
    return pl.pallas_call(
        functools.partial(far_qkv_kernel, base),
        out_shape=jax.ShapeDtypeStruct((width, 3 * mine.shape[1]), mine.dtype),
        in_specs=[pl.BlockSpec(memory_space=pltpu.SMEM)] + [anywhere] * 2,
        out_specs=pl.BlockSpec(memory_space=pltpu.VMEM),
        scratch_shapes=[pltpu.SemaphoreType.DMA((24,))],
        cost_estimate=small_cost(100000000),
        name="far_qkv",
    )(places, mine, theirs)


VECTORS = 32


def put_split(ref, at, values):
    high = values.astype(jnp.bfloat16)
    low = (values - high.astype(jnp.float32)).astype(jnp.bfloat16)
    columns = values.shape[1]
    ref[at : at + VECTORS, 0:columns] = high
    ref[at + VECTORS : at + 2 * VECTORS, 0:columns] = low
    rest = ref.shape[1] - columns
    if rest:
        ref[at : at + 2 * VECTORS, columns:] = jnp.zeros((2 * VECTORS, rest), jnp.bfloat16)


def get_split(ref, at, columns):
    high = ref[at : at + VECTORS, 0:columns].astype(jnp.float32)
    return high + ref[at + VECTORS : at + 2 * VECTORS, 0:columns].astype(jnp.float32)


def framed(ref, rows, flip, half):
    return jnp.concatenate(
        [ref[rows, pl.ds(pl.multiple_of((flip ^ i) * half, half), half)] for i in range(2)], axis=1
    ).astype(jnp.float32)


def token_back_kernel(
    flip_ref, near_ref, far_ref, w_near, w_far, own_states, other_states, own_ref, give_ref, sums_ref, other_v
):
    rows_all, half = own_ref.shape[0], own_ref.shape[1] // 2
    sums_ref[...] = jnp.zeros_like(sums_ref)
    for start, out_ref in ((rows_all, other_v), (0, own_ref)):
        rows = slice(start, start + rows_all)
        out_ref[...] = dot_nt(near_ref[rows, :], w_near[...]) + dot_nt(far_ref[rows, :], w_far[...])
    for out_ref, states in ((other_v, other_states), (own_ref, own_states)):

        @functools.partial(rows_of, rows_all)
        def _(rows, out_ref=out_ref, states=states):
            normal, _ = unit_rows(framed(states, rows, flip_ref[0], half))
            upstream = out_ref[rows, :]
            sums_ref[0:1, :] += jnp.sum(upstream * normal, axis=0, keepdims=True)
            sums_ref[1:2, :] += jnp.sum(upstream, axis=0, keepdims=True)
            if out_ref is other_v:
                give_ref[rows, :] = upstream.astype(jnp.bfloat16)


def token_back(flip, near, far, w_near, w_far, own_states, other_states):
    rows, width = own_states.shape
    vmem = pl.BlockSpec(memory_space=pltpu.VMEM)
    return pl.pallas_call(
        token_back_kernel,
        out_shape=(
            jax.ShapeDtypeStruct((rows, width), jnp.float32),
            jax.ShapeDtypeStruct((rows, width), jnp.bfloat16),
            jax.ShapeDtypeStruct((2, width), jnp.float32),
        ),
        in_specs=[pl.BlockSpec(memory_space=pltpu.SMEM)] + [vmem] * 6,
        out_specs=(vmem,) * 3,
        scratch_shapes=[pltpu.VMEM((rows, width), jnp.float32)],
        compiler_params=pltpu.CompilerParams(vmem_limit_bytes=40 << 20),
        cost_estimate=small_cost(100000000),
        name="token_back",
    )(flip, near, far, w_near, w_far, own_states, other_states)


def last_kernel(flip_ref, own_ref, taken_ref, states_ref, mid_ref, vector_ref, out_ref):
    half = own_ref.shape[1] // 2
    upstream = own_ref[...] + taken_ref[...].astype(jnp.float32)
    everything = slice(0, own_ref.shape[0])
    normal, spread = unit_rows(framed(states_ref, everything, flip_ref[0], half))
    inner = upstream * vector_ref[0:1, :]
    center = jnp.mean(inner, axis=-1, keepdims=True)
    slope = jnp.mean(inner * normal, axis=-1, keepdims=True)
    back = mid_ref[...] + spread * (inner - center - normal * slope)
    for i in range(2):
        lanes = pl.ds(pl.multiple_of((flip_ref[0] ^ i) * half, half), half)
        out_ref[:, lanes] = back[:, i * half : (i + 1) * half].astype(jnp.bfloat16)


def last_norm(flip, own, taken, states, mid, vectors):
    rows, width = own.shape
    block = pl.BlockSpec((ROWS, width), lambda i: (i, 0))
    whole = pl.BlockSpec(vectors.shape, lambda i: (0, 0))
    return pl.pallas_call(
        last_kernel,
        grid=(rows // ROWS,),
        out_shape=jax.ShapeDtypeStruct((rows, width), jnp.bfloat16),
        in_specs=[pl.BlockSpec(memory_space=pltpu.SMEM)] + [block] * 4 + [whole],
        out_specs=block,
        cost_estimate=small_cost(500000000),
        name="last_norm",
    )(flip, own, taken, states, mid, vectors)


def far_grads_kernel(
    turned_ref, grad_ref, sums_ref, hidden_ref, norm_ref, near_ref, far_ref, keep_ref, out_ref, kept_ref
):
    half = keep_ref.shape[1]
    width = near_ref.shape[1] // 3
    shared = [hidden_ref[0:1, i * half : (i + 1) * half] for i in range(8)]
    for ref in (near_ref, far_ref):
        shared.append(jnp.concatenate([ref[0:1, 0:width], ref[0:1, 2 * width :]], axis=1))
    shared.append(sums_ref[0:1, 0:half] + sums_ref[0:1, half:])
    blank = jnp.zeros((VECTORS - 6 - len(shared), half), jnp.float32)

    def rows(lanes):
        split = [sums_ref[i : i + 1, lanes] for i in (2, 3, 4, 1)]
        split += [norm_ref[i : i + 1, lanes] for i in range(2)]
        return jnp.concatenate(split + shared + [blank], axis=0)

    keep_ref[...] = rows(slice(0, half))
    put_split(out_ref, half, rows(slice(half, 2 * half)))
    out_ref[0:half, :] = dot_nn(turned_ref[half:, :], grad_ref[...]).astype(jnp.bfloat16)
    kept_ref[...] = dot_nn(turned_ref[0:half, :], grad_ref[...])


def after_row_kernel(
    places_ref, kept_ref, taken_ref, keep_ref, near_ref, near_taken, near_own_ref, far_own_ref, sum_ref, *outs
):
    deep = far_own_ref.shape[0]
    vectors = keep_ref[...] + get_split(taken_ref, 4 * deep, keep_ref.shape[1])
    sum_ref[...] = vectors
    for s in range(4):
        rows = pl.ds(pl.multiple_of(places_ref[s] * deep, deep), deep)
        far = kept_ref[rows, :] + taken_ref[rows, :].astype(jnp.float32)
        if s == 0:
            far_own_ref[...] = far
        else:
            outs[s - 1][0:deep, :] = far.astype(jnp.bfloat16)
            put_split(outs[s - 1], deep, vectors)
        if s % 2 == 0:
            at = slice(s // 2 * deep, (s // 2 + 1) * deep)
            near = near_ref[rows, :].astype(jnp.float32) + near_taken[at, :].astype(jnp.float32)
            if s == 0:
                near_own_ref[...] = near
            else:
                outs[s - 1][deep + 2 * VECTORS :, :] = near.astype(jnp.bfloat16)


def after_plane_kernel(near_ref, far_ref, sum_ref, *refs):
    takes, (keep_ref, vector_ref, give_ref, small_ref) = refs[:3], refs[3:]
    deep = far_ref.shape[0]
    vectors, far = sum_ref[...], far_ref[...]
    keep_ref[...] = near_ref[...] + takes[1][deep + 2 * VECTORS :, :].astype(jnp.float32)
    for take in takes:
        vectors = vectors + get_split(take, deep, vectors.shape[1])
        far = far + take[0:deep, :].astype(jnp.float32)
    vector_ref[...] = vectors
    give_ref[0:deep, :] = far.astype(jnp.bfloat16)
    put_split(give_ref, deep, vectors)
    put_split(small_ref, 0, vectors)


def after_cols_kernel(keep_ref, vector_ref, one_ref, two_ref, three_ref, out_ref, total_ref):
    deep = keep_ref.shape[0]
    out_ref[...] = (keep_ref[...] + two_ref[0:deep, :].astype(jnp.float32)).astype(jnp.bfloat16)
    columns = vector_ref.shape[1]
    far = get_split(two_ref, deep, columns)
    total = vector_ref[...] + far
    total = total + get_split(one_ref, 0, columns) + get_split(three_ref, 0, columns)
    total_ref[...] = total
    total_ref[14:15, :] = vector_ref[14:15, :] + far[15:16, :]


def on_chip(kernel, shapes, name, *args, tables=0):
    vmem = pl.BlockSpec(memory_space=pltpu.VMEM)
    return pl.pallas_call(
        kernel,
        out_shape=tuple(jax.ShapeDtypeStruct(*s) for s in shapes),
        in_specs=[pl.BlockSpec(memory_space=pltpu.SMEM)] * tables + [vmem] * (len(args) - tables),
        out_specs=(vmem,) * len(shapes),
        cost_estimate=small_cost(100000000),
        name=name,
    )(*args)


def wide_kernel(with_proj, places_ref, small_ref, big_ref, taken_ref, *refs):
    if with_proj:
        proj_kept, proj_taken, *refs = refs
    *outs, turned_v = refs
    half, sub = turned_v.shape[0], turned_v.shape[0] // 2
    span = big_ref.shape[1] // 4
    part = 256 // 4 if not with_proj else proj_kept.shape[0] // 16
    turned_v[...] = small_ref[:, 0:half].T
    for s in range(4):
        lanes = pl.ds(pl.multiple_of(places_ref[s] * span, span), span)
        block = dot_nn(turned_v[...], big_ref[:, lanes]) + taken_ref[:, lanes].astype(jnp.float32)
        block = block.astype(jnp.bfloat16)
        for side, (go, slot) in enumerate(((s % 2, s // 2), (s // 2, s % 2))):
            out = outs[2 * side + go]
            rows = slice(slot * sub, (slot + 1) * sub)
            out[rows, 0:span] = block[side * sub : (side + 1) * sub]
            if with_proj:
                at = side * sub
                for j in range(4):
                    start = pl.multiple_of(4 * j * part + places_ref[s] * part, part)
                    piece = proj_kept[pl.ds(start, part), at : at + sub] + proj_taken[
                        pl.ds(start, part), at : at + sub
                    ].astype(jnp.float32)
                    low = slot * sub + j * part
                    out[low : low + part, span:] = piece.astype(jnp.bfloat16)


def wide_grads(places, small, big, taken, proj=()):
    half = small.shape[1] // 2
    columns = big.shape[1] // 4 + (half // 2 if proj else 0)
    vmem = pl.BlockSpec(memory_space=pltpu.VMEM)
    return pl.pallas_call(
        functools.partial(wide_kernel, bool(proj)),
        out_shape=(jax.ShapeDtypeStruct((half, columns), jnp.bfloat16),) * 4,
        in_specs=[pl.BlockSpec(memory_space=pltpu.SMEM)] + [vmem] * (3 + len(proj)),
        out_specs=(vmem,) * 4,
        scratch_shapes=[pltpu.VMEM((half, small.shape[0]), jnp.bfloat16)],
        compiler_params=pltpu.CompilerParams(vmem_limit_bytes=44 << 20),
        cost_estimate=small_cost(3000000000),
        name="wide_grads",
    )(places, small, big, taken, *proj)


def plane_sum_kernel(*refs):
    sub = refs[4].shape[0]
    for side in range(2):
        kept, taken = refs[2 * side : 2 * side + 2]
        for slot in range(2):
            rows = slice(slot * sub, (slot + 1) * sub)
            total = kept[rows, :].astype(jnp.float32) + taken[rows, :].astype(jnp.float32)
            refs[4 + 2 * side + slot][...] = total.astype(jnp.bfloat16)


def cols_out_kernel(places_ref, *refs):
    outs = refs[4:]
    sub = refs[0].shape[0]
    columns = refs[0].shape[1]
    part = (outs[0].shape[0] - 2 * sub) // 2
    for side in range(2):
        kept, taken = refs[2 * side : 2 * side + 2]
        for j in range(4):
            lanes = pl.ds(pl.multiple_of(places_ref[4 + j] * sub, sub), sub)
            total = kept[:, lanes].astype(jnp.float32) + taken[:, lanes].astype(jnp.float32)
            outs[j][side * sub : (side + 1) * sub, :] = total.astype(jnp.bfloat16)
            if part:
                rows = slice(j * part, (j + 1) * part)
                total = kept[rows, columns - sub :].astype(jnp.float32)
                total = total + taken[rows, columns - sub :].astype(jnp.float32)
                low = 2 * sub + side * part
                outs[j][low : low + part, :] = total.astype(jnp.bfloat16)


def mine_kernel(*refs):
    out_ref, at = refs[8], 0
    for group in (refs[0:4], refs[4:8]):
        total = group[0][...].astype(jnp.float32)
        for ref in group[1:]:
            total = total + ref[...].astype(jnp.float32)
        out_ref[at : at + total.shape[0], :] = total.astype(jnp.bfloat16)
        at += total.shape[0]


def finish_kernel(part_rows, places_ref, *refs):
    pieces, (fc2_ref, fc1_ref, proj_ref) = refs[:2], refs[2:]
    half, sub = fc1_ref.shape[0], pieces[0].shape[1]
    for s in range(4):
        piece, base = pieces[s // 2], (s % 2) * (pieces[0].shape[0] // 2)
        at = places_ref[s]
        rows = pl.ds(pl.multiple_of(at * sub, sub), sub)
        fc2_ref[rows, :] = piece[base : base + half, :].astype(jnp.float32).T
        fc1_ref[:, rows] = piece[base + half : base + 2 * half, :].astype(jnp.float32)
        rows = pl.ds(pl.multiple_of(at * part_rows, part_rows), part_rows)
        for i in range(2):
            low = base + 2 * half + i * part_rows
            proj_ref[rows, i * sub : (i + 1) * sub] = piece[low : low + part_rows, :].astype(jnp.float32)


def finish_qkv_kernel(places_ref, *refs):
    out_ref = refs[4]
    deep, width = refs[0].shape[0], out_ref.shape[2]
    for s in range(4):
        rows = pl.ds(pl.multiple_of(places_ref[s] * deep, deep), deep)
        for k in range(3):
            out_ref[k, rows, :] = refs[s][:, k * width : (k + 1) * width].astype(jnp.float32)


def finish(places, pieces, part_rows):
    rows, sub = pieces[0].shape
    half = (rows // 2 - 2 * part_rows) // 2
    vmem = pl.BlockSpec(memory_space=pltpu.VMEM)
    return pl.pallas_call(
        functools.partial(finish_kernel, part_rows),
        out_shape=(
            jax.ShapeDtypeStruct((4 * sub, half), jnp.float32),
            jax.ShapeDtypeStruct((half, 4 * sub), jnp.float32),
            jax.ShapeDtypeStruct((4 * part_rows, half), jnp.float32),
        ),
        in_specs=[pl.BlockSpec(memory_space=pltpu.SMEM)] + [vmem] * 2,
        out_specs=[vmem] * 3,
        cost_estimate=small_cost(100000000),
        name="finish",
    )(places, *pieces)


def finish_qkv(places, pieces):
    deep, width = pieces[0].shape
    vmem = pl.BlockSpec(memory_space=pltpu.VMEM)
    return pl.pallas_call(
        finish_qkv_kernel,
        out_shape=jax.ShapeDtypeStruct((3, 4 * deep, width // 3), jnp.float32),
        in_specs=[pl.BlockSpec(memory_space=pltpu.SMEM)] + [vmem] * 4,
        out_specs=vmem,
        cost_estimate=small_cost(100000000),
        name="finish_qkv",
    )(places, *pieces)


def tie(value, *others):
    return lax.optimization_barrier((value, *others))[0]


def add_up(own, taken):
    total = own.astype(jnp.float32)
    for piece in taken:
        total = total + piece.astype(jnp.float32)
    return total


def local_paired(
    states,
    ln1_gain,
    ln1_bias,
    w_qkv,
    q_bias,
    v_bias,
    w_proj,
    proj_bias,
    ln2_gain,
    ln2_bias,
    w_fc1,
    fc1_bias,
    w_fc2,
    fc2_bias,
    teacher,
    loss_mask,
    lengths,
):
    f32, bf16 = jnp.float32, jnp.bfloat16
    dp = lax.axis_index("dp")
    row = lax.axis_index("row")
    col = lax.axis_index("col")
    local_rows, width = states.shape
    half = width // 2
    head_width = w_qkv.shape[2]
    hidden_width = w_fc1.shape[1]
    sub = hidden_width // 4
    span = 4 * sub
    part_rows = head_width // 4
    clip = (dp * 2 + row) * 2 + col // 2
    second = col % 2

    def quarter(s):
        return dp ^ s

    def frame(values):
        return jnp.where(
            row == 0, values, jnp.concatenate([values[:, half:], values[:, :half]], axis=1)
        )

    places = jnp.stack([dp ^ s for s in range(4)] + [col ^ j for j in range(4)]).astype(jnp.int32)
    flip = row.reshape(1).astype(jnp.int32)
    states_other = over_col(states, 1)
    small = jnp.concatenate(
        [
            fc1_bias.reshape(4, sub),
            q_bias.reshape(1, sub),
            v_bias.reshape(1, sub),
            jnp.zeros((10, sub), bf16),
        ],
        axis=0,
    )
    slab = make_slab(places, w_fc1, w_fc2, w_proj, w_qkv.transpose(1, 0, 2), small)
    unit_rows_total = half + 2 * sub + 2 * part_rows + small.shape[0]
    small_at = unit_rows_total - small.shape[0]
    two = over_col(slab, 2)
    w_qkv2 = w_qkv.reshape(half, 3 * head_width)
    w_qkv2 = tie(w_qkv2, slab)
    qkv_near = jnp.concatenate([w_qkv2, over_row(w_qkv2)], axis=0)
    vectors = jnp.stack([ln1_gain, ln1_bias, proj_bias, ln2_gain, ln2_bias, fc2_bias])
    vectors, states, teacher, loss_mask = lax.optimization_barrier(
        (vectors, states, teacher, loss_mask, slab)
    )[:4]
    vectors = jnp.concatenate([vectors, over_row(vectors)], axis=1).astype(f32)
    fc1_other, fc2_other, proj_other = over_row(w_fc1), over_row(w_fc2), over_row(w_proj)
    two = tie(two, fc1_other, fc2_other, proj_other)
    two_x, two_y = over_dp(two, 1), over_dp(two, 2)
    states_other = tie(states_other, two)

    all_clips = lengths.shape[0]
    valid_all = (
        loss_mask.reshape(all_clips, L) * (jnp.arange(L)[None, :] < lengths[:, None])
    ).astype(f32)
    valid_total = jnp.maximum(jnp.sum(valid_all), 1.0)
    first_row = ((dp * 2 + row) * 4 + col) * local_rows
    valid = lax.dynamic_slice_in_dim(valid_all.reshape(all_clips * L), first_row, local_rows)
    my_length = lax.dynamic_slice_in_dim(lengths, clip, 1)
    spot = jnp.arange(L)
    position = jnp.where(
        spot < local_rows, second * local_rows + spot, (1 - second) * local_rows + spot - local_rows
    )
    key_bias = jnp.where(position < my_length, 0.0, MASKED).astype(f32)
    key_bias = jnp.broadcast_to(key_bias[:, None], (L, 128))

    gain_one, shift_one = vectors[0], vectors[1]
    norm_one, _, _ = normalize(frame(states).astype(f32), gain_one, shift_one)
    norm_other, _, _ = normalize(frame(states_other).astype(f32), gain_one, shift_one)
    tokens_one = jnp.concatenate([norm_one.astype(bf16), norm_other.astype(bf16)], axis=0)

    zero_bias = jnp.zeros((head_width,), f32)
    score_scale = HD**-0.5
    scale = jnp.where(jnp.arange(3 * head_width) < head_width, score_scale, 1.0).astype(bf16)
    split = local_rows // QT * QT
    later = L - split
    over = local_rows - split

    def project(matrix, q_add, v_add):
        projected = jnp.dot(tokens_one, matrix, preferred_element_type=f32)
        add = jnp.concatenate([q_add.astype(f32), zero_bias, v_add.astype(f32)])
        return (projected + add[None]).astype(bf16) * scale[None]

    table = jnp.stack(
        [(dp ^ s) * 4 + (col ^ j) for s in range(4) for j in range(4)]
        + [a * 4 + col for a in range(4)]
        + [dp ^ s for s in range(4)]
        + [col ^ b for b in range(4)]
        + [row]
    ).astype(jnp.int32)
    loss_scale = all_clips * L * width / 2.0
    factor = (loss_scale * 2.0 / (valid_total * width)).reshape(1)
    valid = valid[:, None]
    packed_near = tie(project(qkv_near, q_bias, v_bias), table, factor, valid)
    cut_at = two.shape[0] // 32 * 16
    two_x, two_y = tie(two_x, packed_near), tie(two_y, packed_near)
    two_low, two_high = over_dp(two_y[:cut_at], 1), over_dp(two_x[cut_at:], 2)
    one_give = jnp.concatenate([slab[:unit_rows_total], two[:unit_rows_total]], axis=0)
    one = over_col(tie(one_give, states_other), 1)
    near_late, near_late_lse = attend(tie(packed_near, two_x, two_y, one), key_bias, split, later)
    two_low, two_high = tie(two_low, near_late), tie(two_high, near_late)
    two_all = jnp.concatenate([two, two_x, two_y, two_low, two_high], axis=0)
    two_theirs = over_row(two_all)
    near_other = over_col(near_late[over:], 1)
    one_x, one_y = over_dp(one, 1), over_dp(one, 2)
    one_other = over_row(tie(one, near_late))
    near_soon, near_soon_lse = attend(
        tie(packed_near, two_all, near_late, one), key_bias, 0, split
    )
    two_theirs = tie(two_theirs, near_soon)
    qkv_far = far_qkv(places, two_all, two_theirs, unit_rows_total, width)
    far_small = two_all[small_at : small_at + small.shape[0]]
    packed_far = project(qkv_far, far_small[4], far_small[5])
    packed_far = tie(packed_far, one, near_other)
    far_late, far_late_lse = attend(packed_far, key_bias, split, later)
    far_other = over_col(far_late[over:], 1)
    one_x, one_y = tie(one_x, far_late), tie(one_y, far_late)
    cut_at = one.shape[0] // 2
    one_low, one_high = over_dp(one_y[:cut_at], 1), over_dp(one_x[cut_at:], 2)
    one_theirs = [over_row(one_x), over_row(one_y)]
    far_soon, far_soon_lse = attend(
        tie(packed_far, one_x, one_y, far_late, one_other), key_bias, 0, split
    )
    one_low, one_high = tie(one_low, far_soon, far_other), tie(one_high, far_soon, far_other)
    one_mine = [one, one_x, one_y, one_low, one_high]
    one_theirs = [one_other, *one_theirs, over_row(one_low), over_row(one_high)]
    turned = tie(tokens_one, far_late).T
    at = unit_rows_total + small_at
    smalls = jnp.stack(
        [small, one[small_at : small_at + 16], two_all[small_at : small_at + 16], one[at : at + 16]]
    ).astype(f32)
    (
        attended_rows,
        outputs,
        hidden,
        grad_pre,
        norm_two,
        grad_low,
        mid_low,
        grad_mid,
        up_own,
        up_give,
        hidden_sum,
        sums,
    ) = middle_block(
        table,
        factor,
        states,
        teacher,
        valid,
        vectors,
        smalls,
        (
            w_fc1,
            fc1_other,
            w_fc2,
            fc2_other,
            w_proj,
            proj_other,
            two_all,
            two_theirs,
            *one_mine,
            *one_theirs,
            near_soon,
            near_late,
            near_other,
            far_soon,
            far_late,
            far_other,
        ),
    )
    up_far = over_col(up_give, 1)

    def joined(kept, taken):
        return (kept.astype(f32) + taken.astype(f32)).astype(bf16)

    give_fc2 = over_row(dot_tn(grad_low[:, half:], hidden).astype(bf16))
    give_fc1 = over_row(dot_tn(norm_two[:, half:], grad_pre).astype(bf16))
    give_proj = over_row(dot_tn(attended_rows, mid_low[:, half:]).astype(bf16))
    kept_proj = dot_tn(attended_rows, mid_low[:, :half])

    def plane_first(wide):
        keep_x, give_x, keep_y, give_y = wide
        return (keep_x, keep_y), (give_x, give_y), (over_dp(give_x, 1), over_dp(give_y, 2))

    def plane_second(keep, taken):
        shape = ((keep[0].shape[0] // 2, keep[0].shape[1]), bf16)
        keep_x, give_x, keep_y, give_y = on_chip(
            plane_sum_kernel, [shape] * 4, "plane_sum", keep[0], taken[0], keep[1], taken[1]
        )
        return (keep_x, keep_y), (give_x, give_y), (over_dp(give_x, 2), over_dp(give_y, 1))

    def cols_out(keep, taken, rows):
        blocks = on_chip(
            cols_out_kernel,
            [((rows, sub), bf16)] * 4,
            "cols_out",
            *(places, keep[0], taken[0], keep[1], taken[1]),
            tables=1,
        )
        return blocks, [over_col(blocks[j], j) for j in (1, 2, 3)]

    def all_tied(values, *others):
        return [tie(v, *others) for v in values]

    wide = wide_grads(places, grad_low, hidden, give_fc2)
    fc2_keep, fc2_give, fc2_taken = plane_first(wide)
    wide = wide_grads(
        places, tie(norm_two, *fc2_give), grad_pre, give_fc1, (kept_proj, give_proj)
    )
    fc1_keep, fc1_give, fc1_taken = plane_first(wide)

    packed_near = tie(packed_near, *fc2_give, *fc1_give)
    part_near = attend_back(packed_near, key_bias, near_soon_lse, near_soon, up_own, None, 0, 0)
    fc2_keep, fc2_give, fc2_taken = plane_second(fc2_keep, all_tied(fc2_taken, part_near[0]))

    packed_far = tie(packed_far, *fc2_give, part_near[0])
    part_far = attend_back(
        packed_far, key_bias, far_soon_lse, far_soon, up_own, None, head_width, 0
    )
    fc2_blocks, fc2_cols = cols_out(fc2_keep, all_tied(fc2_taken, part_far[0]), 2 * sub)
    fc1_keep, fc1_give, fc1_taken = plane_second(fc1_keep, all_tied(fc1_taken, part_far[0]))

    packed_near = tie(packed_near, *fc2_blocks, *fc1_give)
    grad_near, near_sums = attend_back(
        packed_near, key_bias, near_late_lse, near_late, up_own, up_far, 0, split, part_near
    )
    fc2_cols = all_tied(fc2_cols, grad_near)
    fc1_blocks, fc1_cols = cols_out(
        fc1_keep, all_tied(fc1_taken, grad_near, *fc2_cols), 2 * sub + 2 * part_rows
    )
    near_tied = tie(grad_near, *fc1_blocks)
    near_row = over_row(dot_tn(tokens_one[:, half:], near_tied).astype(bf16))
    wide_near = joined(dot_tn(tokens_one[:, :half], near_tied), near_row)
    deep = half // 4
    near_give = jnp.concatenate([cut(wide_near, quarter(s), deep) for s in (1, 3)], axis=0)
    near_taken = over_dp(near_give, 1)

    packed_far = tie(packed_far, near_give, *fc1_blocks, *fc2_cols)
    grad_far, far_sums = attend_back(
        packed_far, key_bias, far_late_lse, far_late, up_own, up_far, head_width, split, part_far
    )

    norm_own, norm_give, norm_sums = token_back(
        flip, grad_near, grad_far, qkv_near, qkv_far, states, states_other
    )
    norm_taken = over_col(norm_give, 1)
    columns, slots = grad_far.shape[1], 2 * VECTORS
    vec_keep, row_give, kept = on_chip(
        far_grads_kernel,
        [((VECTORS, half), f32), ((half + slots, columns), bf16), ((half, columns), f32)],
        "far_grads",
        *(turned, tie(grad_far, norm_give, near_taken, *fc1_cols), sums, hidden_sum, norm_sums, near_sums, far_sums),
    )
    row_taken = over_row(row_give)
    fc1_cols = all_tied(fc1_cols, row_give)
    mine_rows = fc2_blocks[0].shape[0] + fc1_blocks[0].shape[0]
    (mine,) = on_chip(
        mine_kernel,
        [((mine_rows, sub), bf16)],
        "mine",
        *(fc2_blocks[0], *fc2_cols, fc1_blocks[0], *fc1_cols),
    )
    mine_x = over_dp(mine, 1)
    near_own, far_own, vec_sum, *plane_give = on_chip(
        after_row_kernel,
        [((deep, columns), f32)] * 2
        + [((VECTORS, half), f32)]
        + [((deep + slots + (deep if s == 2 else 0), columns), bf16) for s in (1, 2, 3)],
        "after_row",
        *(places, kept, tie(row_taken, mine), vec_keep, wide_near, tie(near_taken, mine)),
        tables=1,
    )
    plane_taken = [over_dp(plane_give[s - 1], s) for s in (1, 2, 3)]
    mine_two = jnp.concatenate([mine, tie(mine_x, *plane_give)], axis=0)
    plane_taken = all_tied(plane_taken, mine_two, norm_taken)
    near_own, vec_sum, col_give, vec_give = on_chip(
        after_plane_kernel,
        [
            ((deep, columns), f32),
            ((VECTORS, half), f32),
            ((deep + slots, columns), bf16),
            ((slots, half), bf16),
        ],
        "after_plane",
        *(near_own, far_own, vec_sum, *plane_taken),
    )
    mine_y = over_dp(tie(mine_two, col_give), 2)
    col_taken = [over_col(vec_give, 1), over_col(col_give, 2), over_col(vec_give, 3)]
    norm_taken = tie(norm_taken, col_give)
    grad_states = last_norm(flip, norm_own, norm_taken, states, grad_mid, vectors)

    qkv_mine, vec_total = on_chip(
        after_cols_kernel,
        [((deep, columns), bf16), ((VECTORS, half), f32)],
        "after_cols",
        *(near_own, vec_sum, *all_tied(col_taken, grad_states)),
    )
    qkv_back = [over_dp(qkv_mine, s) for s in (1, 2, 3)]
    fc2_grad, fc1_grad, proj_grad = finish(places, [mine_two, tie(mine_y, qkv_mine)], part_rows)
    qkv_grad = finish_qkv(places, [qkv_mine, *all_tied(qkv_back, fc2_grad)]).transpose(1, 0, 2)

    fc1_bias_grad = lax.dynamic_index_in_dim(vec_total[6:14].reshape(4, 4, sub), col, 1, False)
    loss_value = jnp.sum(vec_total[16]) / (valid_total * width)
    return (
        outputs,
        loss_value,
        grad_states,
        vec_total[4],
        vec_total[5],
        qkv_grad,
        vec_total[14, :head_width],
        vec_total[14, head_width:],
        proj_grad,
        vec_total[2],
        vec_total[0],
        vec_total[1],
        fc1_grad,
        fc1_bias_grad.reshape(span),
        fc2_grad,
        vec_total[3],
    )


def solution(mesh):
    sizes = (mesh.shape["dp"], mesh.shape["row"], mesh.shape["col"])
    body = local_paired if sizes == PAIRED_MESH else local_general
    in_specs = (
        P(("dp", "row", "col"), None),
        P("row"),
        P("row"),
        P("row", None, "col"),
        P("col"),
        P("col"),
        P("col", "row"),
        P("row"),
        P("row"),
        P("row"),
        P("row", "col"),
        P("col"),
        P("col", "row"),
        P("row"),
        P(("dp", "row", "col"), None),
        P(),
        P(),
    )
    out_specs = (
        P(("dp", "row", "col"), None),
        P(),
        P(("dp", "row", "col"), None),
        P("row"),
        P("row"),
        P("row", None, "col"),
        P("col"),
        P("col"),
        P("col", "row"),
        P("row"),
        P("row"),
        P("row"),
        P("row", "col"),
        P("col"),
        P("col", "row"),
        P("row"),
    )
    return jax.shard_map(body, mesh=mesh, in_specs=in_specs, out_specs=out_specs, check_vma=False)
```

```python
import functools

import jax
import jax.numpy as jnp
from jax import lax
from jax.experimental import pallas as pl
from jax.experimental.pallas import tpu as pltpu
from jax.sharding import PartitionSpec as P

HD = 64
L = 1568


EPSILON = 1e-06
MASKED = -1e30
ROOT_HALF = 0.7071067811865476
DENSITY_FACTOR = 0.3989422804014327


def normalize(values, factor, offset):
    centered = values - jnp.mean(values, axis=-1, keepdims=True)
    spread = lax.rsqrt(jnp.mean(centered * centered, axis=-1, keepdims=True) + EPSILON)
    normal = centered * spread
    return (normal * factor + offset, normal, spread)


def norm_back(upstream, normal, spread, factor):
    inner = upstream * factor
    center_term = jnp.mean(inner, axis=-1, keepdims=True)
    slope_term = jnp.mean(inner * normal, axis=-1, keepdims=True)
    back = spread * (inner - center_term - normal * slope_term)
    return (back, jnp.sum(upstream * normal, axis=0), jnp.sum(upstream, axis=0))


def gelu_value(values):
    return values * (0.5 * (1.0 + lax.erf(values * ROOT_HALF)))


def gelu_slope(values):
    normal_cdf = 0.5 * (1.0 + lax.erf(values * ROOT_HALF))
    return normal_cdf + values * jnp.exp(-0.5 * values * values) * DENSITY_FACTOR


def masked_scores(queries, key_rows, length, score_scale):
    logits = (
        jnp.einsum("ihd,jhd->hij", queries, key_rows, preferred_element_type=jnp.float32)
        * score_scale
    )
    keep = jnp.arange(key_rows.shape[0]) < length
    return jnp.where(keep[None, None, :], logits, MASKED)


def attend_clip(packed, length, score_scale):
    half_span = packed.shape[0] // 2
    key_rows = packed[:, 1]
    value_rows = packed[:, 2]
    pieces = []
    totals = []
    for block_index in range(2):
        queries = packed[block_index * half_span : (block_index + 1) * half_span, 0]
        logits = masked_scores(queries, key_rows, length, score_scale)
        peak = jnp.max(logits, axis=-1, keepdims=True)
        total = peak + jnp.log(jnp.sum(jnp.exp(logits - peak), axis=-1, keepdims=True))
        weights = jnp.exp(logits - total).astype(jnp.bfloat16)
        pieces.append(
            jnp.einsum("hij,jhd->ihd", weights, value_rows, preferred_element_type=jnp.float32)
        )
        totals.append(total[..., 0])
    return (jnp.concatenate(pieces, 0), jnp.concatenate(totals, 1))


def attend_clip_back(packed, length, totals, upstream, score_scale):
    half_span = packed.shape[0] // 2
    key_rows = packed[:, 1]
    value_rows = packed[:, 2]
    grad_keys = jnp.zeros(key_rows.shape, jnp.float32)
    grad_values = jnp.zeros(value_rows.shape, jnp.float32)
    grad_queries = []
    for block_index in range(2):
        first = block_index * half_span
        queries = packed[first : first + half_span, 0]
        logits = masked_scores(queries, key_rows, length, score_scale)
        probs = jnp.exp(logits - totals[:, first : first + half_span][..., None])
        incoming = upstream[first : first + half_span]
        grad_values = grad_values + jnp.einsum(
            "hij,ihd->jhd", probs.astype(jnp.bfloat16), incoming, preferred_element_type=jnp.float32
        )
        grad_probs = jnp.einsum(
            "ihd,jhd->hij", incoming, value_rows, preferred_element_type=jnp.float32
        )
        grad_logits = (
            probs * (grad_probs - jnp.sum(probs * grad_probs, axis=-1, keepdims=True))
        ).astype(jnp.bfloat16)
        grad_queries.append(
            jnp.einsum("hij,jhd->ihd", grad_logits, key_rows, preferred_element_type=jnp.float32)
            * score_scale
        )
        grad_keys = (
            grad_keys
            + jnp.einsum("hij,ihd->jhd", grad_logits, queries, preferred_element_type=jnp.float32)
            * score_scale
        )
    return jnp.stack([jnp.concatenate(grad_queries, 0), grad_keys, grad_values], axis=1)


def local_general(
    states,
    ln1_gain,
    ln1_bias,
    w_qkv,
    q_bias,
    v_bias,
    w_proj,
    proj_bias,
    ln2_gain,
    ln2_bias,
    w_fc1,
    fc1_bias,
    w_fc2,
    fc2_bias,
    teacher,
    loss_mask,
    lengths,
):
    row_count = lax.axis_size("row")
    col_count = lax.axis_size("col")
    col_index = lax.axis_index("col")
    group_index = lax.axis_index("dp") * row_count + lax.axis_index("row")
    local_rows = states.shape[0]
    width = states.shape[1]
    group_rows = local_rows * col_count
    clip_count = group_rows // L
    head_width = w_qkv.shape[2]
    heads_here = head_width // HD
    hidden_width = w_fc1.shape[1]
    score_scale = HD ** (-0.5)
    vectors = jnp.stack([ln1_gain, ln1_bias, proj_bias, ln2_gain, ln2_bias, fc2_bias])
    qkv_full, proj_full, fc1_full, fc2_full, vector_full = (
        lax.all_gather(w_qkv, "row", axis=0, tiled=True),
        lax.all_gather(w_proj, "row", axis=1, tiled=True),
        lax.all_gather(w_fc1, "row", axis=0, tiled=True),
        lax.all_gather(w_fc2, "row", axis=1, tiled=True),
        lax.all_gather(vectors, "row", axis=1, tiled=True),
    )
    vector_full = vector_full.astype(jnp.float32)
    gain_one = vector_full[0]
    shift_one = vector_full[1]
    bias_proj = vector_full[2]
    gain_two = vector_full[3]
    shift_two = vector_full[4]
    bias_two = vector_full[5]
    all_clips = lengths.shape[0]
    valid_all = (
        loss_mask.reshape(all_clips, L) * (jnp.arange(L)[None, :] < lengths[:, None])
    ).astype(jnp.float32)
    valid_total = jnp.maximum(jnp.sum(valid_all), 1.0)
    first_row = (group_index * col_count + col_index) * local_rows
    valid = lax.dynamic_slice_in_dim(valid_all.reshape(all_clips * L), first_row, local_rows)
    my_lengths = lax.dynamic_slice_in_dim(lengths, group_index * clip_count, clip_count)
    inputs = states.astype(jnp.float32)
    norm_one, unit_one, spread_one = normalize(inputs, gain_one, shift_one)
    norm_one = norm_one.astype(jnp.bfloat16)
    tokens_one = lax.all_gather(norm_one, "col", axis=0, tiled=True)
    qkv_matrix = qkv_full.reshape(width, 3 * head_width)
    projected = jnp.dot(tokens_one, qkv_matrix, preferred_element_type=jnp.float32).reshape(
        group_rows, 3, head_width
    )
    bias_rows = jnp.stack(
        [
            q_bias.astype(jnp.float32),
            jnp.zeros((head_width,), jnp.float32),
            v_bias.astype(jnp.float32),
        ]
    )
    packed = (projected + bias_rows[None]).astype(jnp.bfloat16)
    clips_packed = packed.reshape(clip_count, L, 3, heads_here, HD)
    attended, totals = lax.map(
        lambda element: attend_clip(element[0], element[1], score_scale), (clips_packed, my_lengths)
    )
    attended = attended.reshape(group_rows, head_width).astype(jnp.bfloat16)
    proj_whole, qkv_whole = (
        lax.all_gather(proj_full, "col", axis=0, tiled=True),
        lax.all_gather(qkv_full, "col", axis=2, tiled=True),
    )
    attended_rows = lax.all_to_all(attended, "col", split_axis=0, concat_axis=1, tiled=True)
    middle = inputs + (
        jnp.dot(attended_rows, proj_whole, preferred_element_type=jnp.float32) + bias_proj
    )
    norm_two, unit_two, spread_two = normalize(middle, gain_two, shift_two)
    norm_two = norm_two.astype(jnp.bfloat16)
    fc1_whole, fc2_whole, fc1_bias_whole = (
        lax.all_gather(fc1_full, "col", axis=1, tiled=True),
        lax.all_gather(fc2_full, "col", axis=0, tiled=True),
        lax.all_gather(fc1_bias, "col", axis=0, tiled=True),
    )
    hidden_pre = jnp.dot(
        norm_two, fc1_whole, preferred_element_type=jnp.float32
    ) + fc1_bias_whole.astype(jnp.float32)
    hidden = gelu_value(hidden_pre).astype(jnp.bfloat16)
    outputs = middle + (jnp.dot(hidden, fc2_whole, preferred_element_type=jnp.float32) + bias_two)
    differ = outputs - teacher.astype(jnp.float32)
    numerator = jnp.sum(valid[:, None] * differ * differ)
    loss_scale = all_clips * L * width / 2.0
    grad_out = loss_scale * 2.0 / (valid_total * width) * valid[:, None] * differ
    grad_low = grad_out.astype(jnp.bfloat16)
    grad_hidden = jnp.dot(grad_low, fc2_whole.T, preferred_element_type=jnp.float32)
    grad_pre = (grad_hidden * gelu_slope(hidden_pre)).astype(jnp.bfloat16)
    wide_fc2 = jnp.dot(hidden.T, grad_low, preferred_element_type=jnp.float32)
    wide_fc1 = jnp.dot(norm_two.T, grad_pre, preferred_element_type=jnp.float32)
    fc1_grad_part, fc2_grad_part = (
        lax.psum_scatter(
            wide_fc1.astype(jnp.bfloat16), "col", scatter_dimension=1, tiled=True
        ).astype(jnp.float32),
        lax.psum_scatter(
            wide_fc2.astype(jnp.bfloat16), "col", scatter_dimension=0, tiled=True
        ).astype(jnp.float32),
    )
    fc1_bias_sum = jnp.sum(grad_pre, axis=0, dtype=jnp.float32)
    grad_norm_two = jnp.dot(grad_pre, fc1_whole.T, preferred_element_type=jnp.float32)
    back_two, gain_two_grad, shift_two_grad = norm_back(
        grad_norm_two, unit_two, spread_two, gain_two
    )
    grad_mid = grad_out + back_two
    mid_low = grad_mid.astype(jnp.bfloat16)
    wide_proj = jnp.dot(attended_rows.T, mid_low, preferred_element_type=jnp.float32)
    proj_grad_part = lax.psum_scatter(
        wide_proj.astype(jnp.bfloat16), "col", scatter_dimension=0, tiled=True
    )
    grad_attended_rows = jnp.dot(mid_low, proj_whole.T, preferred_element_type=jnp.float32).astype(
        jnp.bfloat16
    )
    grad_attended = lax.all_to_all(
        grad_attended_rows, "col", split_axis=1, concat_axis=0, tiled=True
    )
    grads_packed = lax.map(
        lambda element: attend_clip_back(
            element[0], element[1], element[2], element[3], score_scale
        ),
        (clips_packed, my_lengths, totals, grad_attended.reshape(clip_count, L, heads_here, HD)),
    )
    grads_packed = grads_packed.reshape(group_rows, 3 * head_width).astype(jnp.bfloat16)
    qkv_grad_part = jnp.dot(tokens_one.T, grads_packed, preferred_element_type=jnp.float32).reshape(
        width, 3, head_width
    )
    bias_sums = jnp.sum(grads_packed.reshape(group_rows, 3, head_width), axis=0, dtype=jnp.float32)
    grads_rows = lax.all_to_all(
        grads_packed.reshape(group_rows, 3, head_width),
        "col",
        split_axis=0,
        concat_axis=2,
        tiled=True,
    )
    grad_norm_one = jnp.dot(
        grads_rows.reshape(local_rows, 3 * width),
        qkv_whole.reshape(width, 3 * width).T,
        preferred_element_type=jnp.float32,
    )
    back_one, gain_one_grad, shift_one_grad = norm_back(
        grad_norm_one, unit_one, spread_one, gain_one
    )
    grad_states = (grad_mid + back_one).astype(jnp.bfloat16)
    proj_bias_grad = jnp.sum(mid_low, axis=0, dtype=jnp.float32)
    fc2_bias_grad = jnp.sum(grad_low, axis=0, dtype=jnp.float32)
    token_vectors = jnp.stack(
        [
            gain_one_grad,
            shift_one_grad,
            proj_bias_grad,
            gain_two_grad,
            shift_two_grad,
            fc2_bias_grad,
        ]
    )
    head_vectors = lax.dynamic_update_slice(
        jnp.zeros((2, width), jnp.float32),
        jnp.stack([bias_sums[0], bias_sums[2]]),
        (0, col_index * head_width),
    )
    token_sums, head_sums, fc1_sums, loss_sum = lax.psum(
        (token_vectors, head_vectors, fc1_bias_sum, numerator), ("dp", "row", "col")
    )
    qkv_rows, proj_cols, fc1_rows, fc2_cols = (
        lax.psum_scatter(
            qkv_grad_part.astype(jnp.bfloat16), "row", scatter_dimension=0, tiled=True
        ).astype(jnp.float32),
        lax.psum_scatter(proj_grad_part, "row", scatter_dimension=1, tiled=True).astype(
            jnp.float32
        ),
        lax.psum_scatter(
            fc1_grad_part.astype(jnp.bfloat16), "row", scatter_dimension=0, tiled=True
        ).astype(jnp.float32),
        lax.psum_scatter(
            fc2_grad_part.astype(jnp.bfloat16), "row", scatter_dimension=1, tiled=True
        ).astype(jnp.float32),
    )
    qkv_grad, proj_grad, fc1_grad, fc2_grad = (
        lax.psum(qkv_rows.astype(jnp.bfloat16), "dp").astype(jnp.float32),
        lax.psum(proj_cols.astype(jnp.bfloat16), "dp").astype(jnp.float32),
        lax.psum(fc1_rows.astype(jnp.bfloat16), "dp").astype(jnp.float32),
        lax.psum(fc2_cols.astype(jnp.bfloat16), "dp").astype(jnp.float32),
    )
    half_width = width // row_count
    token_part = lax.dynamic_slice_in_dim(
        token_sums, lax.axis_index("row") * half_width, half_width, 1
    )
    head_part = lax.dynamic_slice_in_dim(head_sums, col_index * head_width, head_width, 1)
    fc1_part = lax.dynamic_slice_in_dim(fc1_sums, col_index * hidden_width, hidden_width, 0)
    loss_value = loss_sum / (valid_total * width)
    return (
        outputs.astype(jnp.bfloat16),
        loss_value,
        grad_states,
        token_part[0],
        token_part[1],
        qkv_grad,
        head_part[0],
        head_part[1],
        proj_grad,
        token_part[2],
        token_part[3],
        token_part[4],
        fc1_grad,
        fc1_part,
        fc2_grad,
        token_part[5],
    )


PAIRED_MESH = (4, 2, 4)
GROUP = 4


def small_cost(flops):
    return pl.CostEstimate(flops=flops, bytes_accessed=0, transcendentals=0)
QT = 128


def dot_nn(a, b):
    return lax.dot_general(a, b, (((1,), (0,)), ((), ())), preferred_element_type=jnp.float32)


def dot_nt(a, b):
    return lax.dot_general(a, b, (((1,), (1,)), ((), ())), preferred_element_type=jnp.float32)


def dot_tn(a, b):
    return lax.dot_general(a, b, (((0,), (0,)), ((), ())), preferred_element_type=jnp.float32)


def head_stack(values, zero):
    lane_head = lax.broadcasted_iota(jnp.int32, values.shape, 1) // HD
    return jnp.concatenate([jnp.where(lane_head == h, values, zero) for h in range(GROUP)], axis=0)


def head_unstack(wide, count):
    return jnp.concatenate(
        [wide[h * HD : (h + 1) * HD, h * count : (h + 1) * count] for h in range(GROUP)], axis=0
    ).T


def tiles_of(rows, tile):
    full = rows // QT

    @pl.loop(0, full)
    def _(index):
        tile(pl.multiple_of(index * QT, QT), QT, index)

    if rows > full * QT:
        tile(full * QT, rows - full * QT, full)


def attend_kernel(first, packed_ref, bias_ref, out_ref, lse_ref, vt_ref):
    width = GROUP * HD
    vt_ref[...] = packed_ref[:, 2 * width : 3 * width].T

    def tile(start, count, index):
        cols = GROUP * count
        stacked = head_stack(
            packed_ref[pl.ds(first + start, count), 0:width], jnp.zeros((), jnp.bfloat16)
        )
        keys = packed_ref[:, width : 2 * width]
        bias = bias_ref[...]
        scores = dot_nt(keys, stacked) + jnp.concatenate([bias] * (cols // 128), axis=1)
        peak = jnp.max(scores, axis=0, keepdims=True)
        weights = jnp.exp(scores - peak)
        total = jnp.sum(weights, axis=0, keepdims=True)
        wide = dot_nn(vt_ref[...], weights.astype(jnp.bfloat16)) * (1.0 / total)
        out_ref[pl.ds(start, count), :] = head_unstack(wide, count).astype(jnp.bfloat16)
        lse_ref[index, :, 0:cols] = jnp.broadcast_to(peak + jnp.log(total), (8, cols))

    tiles_of(out_ref.shape[0], tile)


def attend_back_kernel(
    first, lane, last, packed_ref, bias_ref, lse_ref, att_ref, up_own_ref, up_far_ref, *refs
):
    width = GROUP * HD
    lanes = slice(lane, lane + width)
    own_rows = up_own_ref.shape[0]
    if last:
        dq_in, dk_in, dv_in, out_ref, sum_ref, kt_ref, up_ref, dk_ref, dv_ref = refs
        dk_ref[...] = dk_in[...]
        dv_ref[...] = dv_in[...]
        out_ref[0:first, 0:width] = dq_in[...]
        rows = out_ref.shape[0] - first
        up_ref[0 : own_rows - first, :] = up_own_ref[first:own_rows, lanes]
        up_ref[own_rows - first :, :] = up_far_ref[:, lanes]
    else:
        out_ref, dk_ref, dv_ref, kt_ref, up_ref = refs
        dk_ref[...] = jnp.zeros_like(dk_ref)
        dv_ref[...] = jnp.zeros_like(dv_ref)
        rows = out_ref.shape[0]
        up_ref[...] = up_own_ref[0:rows, lanes]
    kt_ref[...] = packed_ref[:, width : 2 * width].T

    def tile(start, count, index):
        cols = GROUP * count
        zero = jnp.zeros((), jnp.bfloat16)
        up = up_ref[pl.ds(start, count), :]
        stacked = head_stack(packed_ref[pl.ds(first + start, count), 0:width], zero)
        up_stacked = head_stack(up, zero)
        product = head_stack(
            up.astype(jnp.float32) * att_ref[pl.ds(start, count), :].astype(jnp.float32),
            jnp.zeros((), jnp.float32),
        )
        high = product.astype(jnp.bfloat16)
        low = (product - high.astype(jnp.float32)).astype(jnp.bfloat16)
        ones = jnp.ones((8, width), jnp.bfloat16)
        delta = (dot_nt(ones, high) + dot_nt(ones, low))[0:1]
        keys = packed_ref[:, width : 2 * width]
        values = packed_ref[:, 2 * width : 3 * width]
        bias = bias_ref[...]
        scores = dot_nt(keys, stacked) + jnp.concatenate([bias] * (cols // 128), axis=1)
        weights = jnp.exp(scores - lse_ref[index, 0:1, 0:cols])
        dv_ref[...] += dot_nn(weights.astype(jnp.bfloat16), up_stacked)
        grad = (weights * (dot_nt(values, up_stacked) - delta)).astype(jnp.bfloat16)
        dk_ref[...] += dot_nn(grad, stacked)
        wide = dot_nn(kt_ref[...], grad) * (HD**-0.5)
        at = pl.ds(first + start if last else start, count)
        out_ref[at, 0:width] = head_unstack(wide, count).astype(jnp.bfloat16)

    tiles_of(rows, tile)
    if last:
        out_ref[:, width : 2 * width] = dk_ref[...].astype(jnp.bfloat16)
        out_ref[:, 2 * width : 3 * width] = dv_ref[...].astype(jnp.bfloat16)
        for k in range(3):
            part = out_ref[:, k * width : (k + 1) * width].astype(jnp.float32)
            sum_ref[:, k * width : (k + 1) * width] = jnp.sum(part, axis=0, keepdims=True)


def attend(packed, bias, first, rows):
    tokens, width = packed.shape[0], GROUP * HD
    tiles = -(-rows // QT)
    return pl.pallas_call(
        functools.partial(attend_kernel, first),
        out_shape=(
            jax.ShapeDtypeStruct((rows, width), jnp.bfloat16),
            jax.ShapeDtypeStruct((tiles, 8, GROUP * QT), jnp.float32),
        ),
        in_specs=[pl.BlockSpec(memory_space=pltpu.VMEM)] * 2,
        out_specs=[pl.BlockSpec(memory_space=pltpu.VMEM)] * 2,
        scratch_shapes=[pltpu.VMEM((width, tokens), jnp.bfloat16)],
        compiler_params=pltpu.CompilerParams(vmem_limit_bytes=32 << 20),
        cost_estimate=pl.CostEstimate(
            flops=2 * rows * tokens * width * 4, bytes_accessed=6 << 20, transcendentals=0
        ),
        name="attend",
    )(packed, bias)


def attend_back(packed, bias, lse, att, up_own, up_far, lane, first, before=None):
    tokens, width = packed.shape[0], GROUP * HD
    rows = att.shape[0]
    total = jax.ShapeDtypeStruct((tokens, width), jnp.float32)
    vmem = pl.BlockSpec(memory_space=pltpu.VMEM)
    scratch = [pltpu.VMEM((width, tokens), jnp.bfloat16), pltpu.VMEM((rows, width), jnp.bfloat16)]
    if before is None:
        extra = ()
        out_shape = (jax.ShapeDtypeStruct((rows, width), jnp.bfloat16), total, total)
        up_far = up_own
    else:
        extra = before
        out_shape = (
            jax.ShapeDtypeStruct((tokens, 3 * width), jnp.bfloat16),
            jax.ShapeDtypeStruct((1, 3 * width), jnp.float32),
        )
        scratch += [pltpu.VMEM((tokens, width), jnp.float32)] * 2
    return pl.pallas_call(
        functools.partial(attend_back_kernel, first, lane, before is not None),
        out_shape=out_shape,
        in_specs=[vmem] * (6 + len(extra)),
        out_specs=(vmem,) * len(out_shape),
        scratch_shapes=scratch,
        compiler_params=pltpu.CompilerParams(vmem_limit_bytes=52 << 20),
        cost_estimate=pl.CostEstimate(
            flops=4 * rows * tokens * width * 4, bytes_accessed=10 << 20, transcendentals=0
        ),
        name="attend_back",
    )(packed, bias, lse, att, up_own, up_far, *extra)


FF_CHUNK = 512
ROWS = 112


def rows_of(total, body):
    @pl.loop(0, total // ROWS)
    def _(index):
        body(pl.ds(pl.multiple_of(index * ROWS, ROWS), ROWS))


def unit_rows(values):
    centered = values - jnp.mean(values, axis=-1, keepdims=True)
    spread = lax.rsqrt(jnp.mean(centered * centered, axis=-1, keepdims=True) + EPSILON)
    return centered * spread, spread


def middle_kernel(
    table_ref,
    factor_ref,
    input_ref,
    target_ref,
    valid_ref,
    vector_ref,
    small_ref,
    fc1_own,
    fc1_other,
    fc2_own,
    fc2_other,
    proj_own,
    proj_other,
    two_mine,
    two_theirs,
    *refs,
):
    one_mine, one_theirs, att_parts, refs = refs[:5], refs[5:10], refs[10:16], refs[16:]
    (
        att_hbm,
        out_hbm,
        hidden_hbm,
        pre_hbm,
        norm_hbm,
        grad_low_hbm,
        mid_low_ref,
        grad_mid_ref,
        up_own_ref,
        up_give_ref,
        hidden_sum_ref,
        sums_ref,
        fc1_v,
        fc2_v,
        proj_v,
        middle_v,
        back_v,
        out_ref,
        hidden_ref,
        pre_ref,
        norm_ref,
        grad_low_ref,
        att_ref,
        sem_one,
        sem_two,
        sem_proj,
        sem_att,
        sem_out,
    ) = refs
    stores = [
        pltpu.make_async_copy(source, target, sem_out.at[i])
        for i, (source, target) in enumerate(
            (
                (norm_ref, norm_hbm),
                (hidden_ref, hidden_hbm),
                (out_ref, out_hbm),
                (grad_low_ref, grad_low_hbm),
                (pre_ref, pre_hbm),
                (att_ref, att_hbm),
            )
        )
    ]
    f32, bf16 = jnp.float32, jnp.bfloat16
    total_rows = input_ref.shape[0]
    half = fc1_own.shape[0]
    sub = fc1_own.shape[1] // 4
    heads = proj_own.shape[0]
    part = heads // 4
    hidden_total = hidden_ref.shape[1]
    chunks = hidden_total // FF_CHUNK
    unit = half + 2 * sub + 2 * part + 16

    def fc1_copy(source, side, at):
        lanes = pl.ds(pl.multiple_of(at * sub, sub), sub)
        pltpu.make_async_copy(
            source, fc1_v.at[side * half : (side + 1) * half, lanes], sem_one.at[at // 2]
        ).start()

    def fc2_copy(source, side, i, at):
        lane = side * half + i * sub
        pltpu.make_async_copy(
            source, fc2_v.at[pl.ds(pl.multiple_of(at * sub, sub), sub), lane : lane + sub], sem_two
        ).start()

    sources = []
    for s in range(4):
        step = two_mine.shape[0] // 4
        sources.append((s, 2, two_mine, two_theirs, s * step))
        low, high = (3, 4) if s == 3 else (s, s)
        sources.append((s, 1, one_mine[low], one_theirs[low], 0))
        sources.append((s, 3, one_mine[high], one_theirs[high], 0 if s == 3 else unit))

    early_rows = att_parts[0].shape[0]
    for at in range(2):
        soon, late, other = att_parts[3 * at : 3 * at + 3]
        lanes = slice(2 * at * heads, (2 * at + 1) * heads)
        pltpu.make_async_copy(soon, att_ref.at[0:early_rows, lanes], sem_att).start()
        pltpu.make_async_copy(
            late.at[0 : total_rows - early_rows], att_ref.at[early_rows:total_rows, lanes], sem_att
        ).start()
        lanes = slice((2 * at + 1) * heads, (2 * at + 2) * heads)
        pltpu.make_async_copy(other, att_ref.at[:, lanes], sem_att).start()
    for side, ref in enumerate((proj_own, proj_other)):
        pltpu.make_async_copy(
            ref, proj_v.at[0:heads, side * half : (side + 1) * half], sem_proj
        ).start()
    for s, j, *refs, base in sources:
        rows = pl.ds(pl.multiple_of(j * heads + table_ref[20 + s] * part, part), part)
        for side in range(2):
            for i in range(2):
                low = base + half + 2 * sub + i * part
                lane = side * half + i * sub
                pltpu.make_async_copy(
                    refs[side].at[low : low + part, :], proj_v.at[rows, lane : lane + sub], sem_proj
                ).start()
    for a in range(4):
        for side, ref in enumerate((fc1_own, fc1_other)):
            fc1_copy(ref.at[:, a * sub : (a + 1) * sub], side, table_ref[16 + a])
    for s, j, *refs, base in sources:
        for side in range(2):
            fc1_copy(refs[side].at[base : base + half, :], side, table_ref[4 * s + j])
    for a in range(4):
        for side, ref in enumerate((fc2_own, fc2_other)):
            for i in range(2):
                fc2_copy(
                    ref.at[a * sub : (a + 1) * sub, i * sub : (i + 1) * sub], side, i, table_ref[16 + a]
                )
    for s, j, *refs, base in sources:
        for side in range(2):
            for i in range(2):
                low = base + half + i * sub
                fc2_copy(refs[side].at[low : low + sub, :], side, i, table_ref[4 * s + j])

    def lanes_of(i):
        return pl.ds(pl.multiple_of((table_ref[28] ^ i) * half, half), half)

    sums_ref[...] = jnp.zeros_like(sums_ref)

    pltpu.make_async_copy(att_ref, att_ref, sem_att).wait()
    stores[5].start()
    pltpu.make_async_copy(proj_v, proj_v, sem_proj).wait()
    for i in range(2):
        cols = slice(i * half, (i + 1) * half)
        middle_v[:, cols] = input_ref[:, lanes_of(i)].astype(f32) + (
            dot_nn(att_ref[...], proj_v[:, cols]) + vector_ref[2:3, cols]
        )

    @functools.partial(rows_of, total_rows)
    def _(rows):
        normal, _ = unit_rows(middle_v[rows, :])
        norm_ref[rows, :] = (normal * vector_ref[3:4, :] + vector_ref[4:5, :]).astype(bf16)

    stores[0].start()

    @pl.loop(0, chunks)
    def _(k):
        span = pl.ds(pl.multiple_of(k * FF_CHUNK, FF_CHUNK), FF_CHUNK)
        pltpu.make_async_copy(fc1_v.at[:, span], fc1_v.at[:, span], sem_one.at[k]).wait()
        a = k // 2
        bias = jnp.concatenate(
            [
                small_ref[table_ref[24 + 2 * (k % 2) + i], pl.ds(a, 1), :]
                for i in range(FF_CHUNK // sub)
            ],
            axis=1,
        )
        pre = dot_nn(norm_ref[...], fc1_v[:, span]) + bias
        cdf = 0.5 * (1.0 + lax.erf(pre * ROOT_HALF))
        hidden_ref[:, span] = (pre * cdf).astype(bf16)
        slope = cdf + pre * jnp.exp(-0.5 * pre * pre) * DENSITY_FACTOR
        pre_ref[:, span] = slope.astype(bf16)

    stores[1].start()
    pltpu.make_async_copy(fc2_v, fc2_v, sem_two).wait()
    for i in range(2):
        cols = slice(i * half, (i + 1) * half)
        total = middle_v[:, cols] + (dot_nn(hidden_ref[...], fc2_v[:, cols]) + vector_ref[5:6, cols])
        out_ref[:, lanes_of(i)] = total.astype(bf16)
        differ = total - target_ref[:, lanes_of(i)].astype(f32)
        weighted = valid_ref[...] * differ
        sums_ref[0:1, cols] = jnp.sum(weighted * differ, axis=0, keepdims=True)
        grad = factor_ref[0] * weighted
        grad_mid_ref[:, cols] = grad
        low = grad.astype(bf16)
        grad_low_ref[:, cols] = low
        sums_ref[1:2, cols] = jnp.sum(low.astype(f32), axis=0, keepdims=True)

    stores[2].start()
    stores[3].start()

    @pl.loop(0, chunks)
    def _(k):
        span = pl.ds(pl.multiple_of(k * FF_CHUNK, FF_CHUNK), FF_CHUNK)
        back = dot_nt(grad_low_ref[...], fc2_v[span, :])
        back = (back * pre_ref[:, span].astype(f32)).astype(bf16)
        pre_ref[:, span] = back
        hidden_sum_ref[0:1, span] = jnp.sum(back.astype(f32), axis=0, keepdims=True)

    stores[4].start()
    for i in range(2):
        cols = slice(i * half, (i + 1) * half)
        back_v[:, cols] = dot_nt(pre_ref[...], fc1_v[cols, :])

    @functools.partial(rows_of, total_rows)
    def _(rows):
        normal, spread = unit_rows(middle_v[rows, :])
        upstream = back_v[rows, :]
        inner = upstream * vector_ref[3:4, :]
        center = jnp.mean(inner, axis=-1, keepdims=True)
        slope = jnp.mean(inner * normal, axis=-1, keepdims=True)
        grad = grad_mid_ref[rows, :] + spread * (inner - center - normal * slope)
        grad_mid_ref[rows, :] = grad
        low = grad.astype(bf16)
        mid_low_ref[rows, :] = low
        sums_ref[2:3, :] += jnp.sum(upstream * normal, axis=0, keepdims=True)
        sums_ref[3:4, :] += jnp.sum(upstream, axis=0, keepdims=True)
        sums_ref[4:5, :] += jnp.sum(low.astype(f32), axis=0, keepdims=True)

    for j, (ref, at) in enumerate(((up_own_ref, 0), (up_give_ref, 0), (up_own_ref, 1), (up_give_ref, 1))):
        grad = dot_nt(mid_low_ref[...], proj_v[j * heads : (j + 1) * heads, :])
        ref[:, at * heads : (at + 1) * heads] = grad.astype(bf16)
    for store in stores:
        store.wait()


def middle_block(table, factor, inputs, target, valid, vectors, smalls, pieces):
    rows, width = inputs.shape
    hidden = 4 * pieces[0].shape[1]
    vmem = pl.BlockSpec(memory_space=pltpu.VMEM)
    smem = pl.BlockSpec(memory_space=pltpu.SMEM)
    anywhere = pl.BlockSpec(memory_space=pl.ANY)
    f32, bf16 = jnp.float32, jnp.bfloat16

    def result(columns, dtype):
        return jax.ShapeDtypeStruct((rows, columns), dtype)

    return pl.pallas_call(
        middle_kernel,
        out_shape=(
            result(width, bf16),
            result(width, bf16),
            result(hidden, bf16),
            result(hidden, bf16),
            result(width, bf16),
            result(width, bf16),
            result(width, bf16),
            result(width, f32),
            result(width // 2, bf16),
            result(width // 2, bf16),
            jax.ShapeDtypeStruct((1, hidden), f32),
            jax.ShapeDtypeStruct((8, width), f32),
        ),
        in_specs=[smem] * 2 + [vmem] * 5 + [anywhere] * len(pieces),
        out_specs=[anywhere] * 6 + [vmem] * 6,
        scratch_shapes=[
            pltpu.VMEM((width, hidden), bf16),
            pltpu.VMEM((hidden, width), bf16),
            pltpu.VMEM((width, width), bf16),
            pltpu.VMEM((rows, width), f32),
            pltpu.VMEM((rows, width), f32),
            pltpu.VMEM((rows, width), bf16),
            pltpu.VMEM((rows, hidden), bf16),
            pltpu.VMEM((rows, hidden), bf16),
            pltpu.VMEM((rows, width), bf16),
            pltpu.VMEM((rows, width), bf16),
            pltpu.VMEM((rows, width), bf16),
            pltpu.SemaphoreType.DMA((hidden // FF_CHUNK,)),
            pltpu.SemaphoreType.DMA,
            pltpu.SemaphoreType.DMA,
            pltpu.SemaphoreType.DMA,
            pltpu.SemaphoreType.DMA((6,)),
        ],
        compiler_params=pltpu.CompilerParams(vmem_limit_bytes=62 << 20),
        cost_estimate=pl.CostEstimate(
            flops=2 * rows * width * hidden, bytes_accessed=44 << 20, transcendentals=0
        ),
        name="middle_block",
    )(table, factor, inputs, target, valid, vectors, smalls, *pieces)


def swap(values, axis, mask, size):
    return lax.ppermute(values, axis, [(i, i ^ mask) for i in range(size)])


def over_row(values):
    return swap(values, "row", 1, 2)


def over_dp(values, mask):
    return swap(values, "dp", mask, 4)


def over_col(values, mask):
    return swap(values, "col", mask, 4)


def cut(values, index, size, axis=0):
    return lax.dynamic_slice_in_dim(values, index * size, size, axis)


def place(pieces, index_of, axis):
    size = pieces[0].shape[axis]
    shape = list(pieces[0].shape)
    shape[axis] = size * len(pieces)
    whole = jnp.zeros(shape, pieces[0].dtype)
    for s, piece in enumerate(pieces):
        whole = lax.dynamic_update_slice_in_dim(whole, piece, index_of(s) * size, axis)
    return whole


def copies(listed, sem_ref):
    for index, (source, target) in enumerate(listed):
        pltpu.make_async_copy(source, target, sem_ref.at[index]).start()
    for index, (source, target) in enumerate(listed):
        pltpu.make_async_copy(source, target, sem_ref.at[index]).wait()


def slab_kernel(places_ref, fc1_ref, fc2_ref, proj_ref, qkv_ref, small_ref, out_ref, sem_ref):
    half, sub = fc1_ref.shape[0], fc1_ref.shape[1] // 4
    part, deep = proj_ref.shape[0] // 4, half // 4
    mine = places_ref[0]
    fc2 = fc2_ref.at[pl.ds(pl.multiple_of(mine * sub, sub), sub)]
    proj = proj_ref.at[pl.ds(pl.multiple_of(mine * part, part), part)]
    listed = [(fc1_ref.at[:, pl.ds(pl.multiple_of(mine * sub, sub), sub)], half)]
    listed += [(fc2.at[:, i * sub : (i + 1) * sub], sub) for i in range(2)]
    listed += [(proj.at[:, i * sub : (i + 1) * sub], part) for i in range(2)]
    listed += [(small_ref, small_ref.shape[0])]
    rows = pl.ds(pl.multiple_of(mine * deep, deep), deep)
    listed += [(qkv_ref.at[k, rows], deep) for k in range(3)]
    pairs, at = [], 0
    for source, count in listed:
        pairs.append((source, out_ref.at[at : at + count]))
        at += count
    copies(pairs, sem_ref)


def make_slab(places, fc1, fc2, proj, qkv, small):
    half, sub = fc1.shape[0], fc1.shape[1] // 4
    rows = half + 2 * sub + proj.shape[0] // 2 + small.shape[0] + 3 * (half // 4)
    anywhere = pl.BlockSpec(memory_space=pl.ANY)
    return pl.pallas_call(
        slab_kernel,
        out_shape=jax.ShapeDtypeStruct((rows, sub), fc1.dtype),
        in_specs=[pl.BlockSpec(memory_space=pltpu.SMEM)] + [anywhere] * 5,
        out_specs=pl.BlockSpec(memory_space=pltpu.VMEM),
        scratch_shapes=[pltpu.SemaphoreType.DMA((9,))],
        cost_estimate=small_cost(100000000),
        name="make_slab",
    )(places, fc1, fc2, proj, qkv, small)


def far_qkv_kernel(base, places_ref, mine_ref, theirs_ref, out_ref, sem_ref):
    sub = mine_ref.shape[1]
    half = out_ref.shape[0] // 2
    deep, step = half // 4, mine_ref.shape[0] // 4
    pairs = []
    for side, ref in enumerate((mine_ref, theirs_ref)):
        for s in range(4):
            rows = pl.ds(pl.multiple_of(side * half + places_ref[s] * deep, deep), deep)
            for k in range(3):
                at = s * step + base + k * deep
                pairs.append((ref.at[at : at + deep], out_ref.at[rows, k * sub : (k + 1) * sub]))
    copies(pairs, sem_ref)


def far_qkv(places, mine, theirs, base, width):
    anywhere = pl.BlockSpec(memory_space=pl.ANY)
    return pl.pallas_call(
        functools.partial(far_qkv_kernel, base),
        out_shape=jax.ShapeDtypeStruct((width, 3 * mine.shape[1]), mine.dtype),
        in_specs=[pl.BlockSpec(memory_space=pltpu.SMEM)] + [anywhere] * 2,
        out_specs=pl.BlockSpec(memory_space=pltpu.VMEM),
        scratch_shapes=[pltpu.SemaphoreType.DMA((24,))],
        cost_estimate=small_cost(100000000),
        name="far_qkv",
    )(places, mine, theirs)


VECTORS = 32


def put_split(ref, at, values):
    high = values.astype(jnp.bfloat16)
    low = (values - high.astype(jnp.float32)).astype(jnp.bfloat16)
    columns = values.shape[1]
    ref[at : at + VECTORS, 0:columns] = high
    ref[at + VECTORS : at + 2 * VECTORS, 0:columns] = low
    rest = ref.shape[1] - columns
    if rest:
        ref[at : at + 2 * VECTORS, columns:] = jnp.zeros((2 * VECTORS, rest), jnp.bfloat16)


def get_split(ref, at, columns):
    high = ref[at : at + VECTORS, 0:columns].astype(jnp.float32)
    return high + ref[at + VECTORS : at + 2 * VECTORS, 0:columns].astype(jnp.float32)


def framed(ref, rows, flip, half):
    return jnp.concatenate(
        [ref[rows, pl.ds(pl.multiple_of((flip ^ i) * half, half), half)] for i in range(2)], axis=1
    ).astype(jnp.float32)


def token_back_kernel(
    flip_ref, near_ref, far_ref, w_near, w_far, own_states, other_states, own_ref, give_ref, sums_ref, other_v
):
    rows_all, half = own_ref.shape[0], own_ref.shape[1] // 2
    sums_ref[...] = jnp.zeros_like(sums_ref)
    for start, out_ref in ((rows_all, other_v), (0, own_ref)):
        rows = slice(start, start + rows_all)
        out_ref[...] = dot_nt(near_ref[rows, :], w_near[...]) + dot_nt(far_ref[rows, :], w_far[...])
    for out_ref, states in ((other_v, other_states), (own_ref, own_states)):

        @functools.partial(rows_of, rows_all)
        def _(rows, out_ref=out_ref, states=states):
            normal, _ = unit_rows(framed(states, rows, flip_ref[0], half))
            upstream = out_ref[rows, :]
            sums_ref[0:1, :] += jnp.sum(upstream * normal, axis=0, keepdims=True)
            sums_ref[1:2, :] += jnp.sum(upstream, axis=0, keepdims=True)
            if out_ref is other_v:
                give_ref[rows, :] = upstream.astype(jnp.bfloat16)


def token_back(flip, near, far, w_near, w_far, own_states, other_states):
    rows, width = own_states.shape
    vmem = pl.BlockSpec(memory_space=pltpu.VMEM)
    return pl.pallas_call(
        token_back_kernel,
        out_shape=(
            jax.ShapeDtypeStruct((rows, width), jnp.float32),
            jax.ShapeDtypeStruct((rows, width), jnp.bfloat16),
            jax.ShapeDtypeStruct((2, width), jnp.float32),
        ),
        in_specs=[pl.BlockSpec(memory_space=pltpu.SMEM)] + [vmem] * 6,
        out_specs=(vmem,) * 3,
        scratch_shapes=[pltpu.VMEM((rows, width), jnp.float32)],
        compiler_params=pltpu.CompilerParams(vmem_limit_bytes=40 << 20),
        cost_estimate=small_cost(100000000),
        name="token_back",
    )(flip, near, far, w_near, w_far, own_states, other_states)


def last_kernel(flip_ref, own_ref, taken_ref, states_ref, mid_ref, vector_ref, out_ref):
    half = own_ref.shape[1] // 2
    upstream = own_ref[...] + taken_ref[...].astype(jnp.float32)
    everything = slice(0, own_ref.shape[0])
    normal, spread = unit_rows(framed(states_ref, everything, flip_ref[0], half))
    inner = upstream * vector_ref[0:1, :]
    center = jnp.mean(inner, axis=-1, keepdims=True)
    slope = jnp.mean(inner * normal, axis=-1, keepdims=True)
    back = mid_ref[...] + spread * (inner - center - normal * slope)
    for i in range(2):
        lanes = pl.ds(pl.multiple_of((flip_ref[0] ^ i) * half, half), half)
        out_ref[:, lanes] = back[:, i * half : (i + 1) * half].astype(jnp.bfloat16)


def last_norm(flip, own, taken, states, mid, vectors):
    rows, width = own.shape
    block = pl.BlockSpec((ROWS, width), lambda i: (i, 0))
    whole = pl.BlockSpec(vectors.shape, lambda i: (0, 0))
    return pl.pallas_call(
        last_kernel,
        grid=(rows // ROWS,),
        out_shape=jax.ShapeDtypeStruct((rows, width), jnp.bfloat16),
        in_specs=[pl.BlockSpec(memory_space=pltpu.SMEM)] + [block] * 4 + [whole],
        out_specs=block,
        cost_estimate=small_cost(500000000),
        name="last_norm",
    )(flip, own, taken, states, mid, vectors)


def far_grads_kernel(
    turned_ref, grad_ref, sums_ref, hidden_ref, near_ref, far_ref, keep_ref, out_ref, kept_ref
):
    half = keep_ref.shape[1]
    width = near_ref.shape[1] // 3
    shared = [hidden_ref[0:1, i * half : (i + 1) * half] for i in range(8)]
    for ref in (near_ref, far_ref):
        shared.append(jnp.concatenate([ref[0:1, 0:width], ref[0:1, 2 * width :]], axis=1))
    shared.append(sums_ref[0:1, 0:half] + sums_ref[0:1, half:])
    blank = jnp.zeros((VECTORS - 6 - len(shared), half), jnp.float32)

    def rows(lanes):
        split = [sums_ref[i : i + 1, lanes] for i in (2, 3, 4, 1)]
        split += [jnp.zeros((2, half), jnp.float32)]
        return jnp.concatenate(split + shared + [blank], axis=0)

    keep_ref[...] = rows(slice(0, half))
    put_split(out_ref, half, rows(slice(half, 2 * half)))
    out_ref[0:half, :] = dot_nn(turned_ref[half:, :], grad_ref[...]).astype(jnp.bfloat16)
    kept_ref[...] = dot_nn(turned_ref[0:half, :], grad_ref[...])


def after_row_kernel(
    places_ref,
    kept_ref,
    taken_ref,
    keep_ref,
    norm_ref,
    near_ref,
    near_taken,
    near_own_ref,
    far_own_ref,
    sum_ref,
    *outs,
):
    deep = far_own_ref.shape[0]
    half = keep_ref.shape[1]
    vectors = keep_ref[...] + get_split(taken_ref, 4 * deep, half)
    vectors = jnp.concatenate(
        [vectors[0:4], norm_ref[:, 0:half], vectors[6:17], norm_ref[:, half:], vectors[19:]], axis=0
    )
    sum_ref[...] = vectors
    for s in range(4):
        rows = pl.ds(pl.multiple_of(places_ref[s] * deep, deep), deep)
        far = kept_ref[rows, :] + taken_ref[rows, :].astype(jnp.float32)
        if s == 0:
            far_own_ref[...] = far
        else:
            outs[s - 1][0:deep, :] = far.astype(jnp.bfloat16)
            put_split(outs[s - 1], deep, vectors)
        if s % 2 == 0:
            at = slice(s // 2 * deep, (s // 2 + 1) * deep)
            near = near_ref[rows, :].astype(jnp.float32) + near_taken[at, :].astype(jnp.float32)
            if s == 0:
                near_own_ref[...] = near
            else:
                outs[s - 1][deep + 2 * VECTORS :, :] = near.astype(jnp.bfloat16)


def after_plane_kernel(near_ref, far_ref, sum_ref, *refs):
    takes, (keep_ref, vector_ref, give_ref, small_ref) = refs[:3], refs[3:]
    deep = far_ref.shape[0]
    vectors, far = sum_ref[...], far_ref[...]
    keep_ref[...] = near_ref[...] + takes[1][deep + 2 * VECTORS :, :].astype(jnp.float32)
    for take in takes:
        vectors = vectors + get_split(take, deep, vectors.shape[1])
        far = far + take[0:deep, :].astype(jnp.float32)
    vector_ref[...] = vectors
    give_ref[0:deep, :] = far.astype(jnp.bfloat16)
    put_split(give_ref, deep, vectors)
    put_split(small_ref, 0, vectors)


def after_cols_kernel(keep_ref, vector_ref, one_ref, two_ref, three_ref, out_ref, total_ref):
    deep = keep_ref.shape[0]
    out_ref[...] = (keep_ref[...] + two_ref[0:deep, :].astype(jnp.float32)).astype(jnp.bfloat16)
    columns = vector_ref.shape[1]
    far = get_split(two_ref, deep, columns)
    total = vector_ref[...] + far
    total = total + get_split(one_ref, 0, columns) + get_split(three_ref, 0, columns)
    total_ref[...] = total
    total_ref[14:15, :] = vector_ref[14:15, :] + far[15:16, :]


def on_chip(kernel, shapes, name, *args, tables=0):
    vmem = pl.BlockSpec(memory_space=pltpu.VMEM)
    return pl.pallas_call(
        kernel,
        out_shape=tuple(jax.ShapeDtypeStruct(*s) for s in shapes),
        in_specs=[pl.BlockSpec(memory_space=pltpu.SMEM)] * tables + [vmem] * (len(args) - tables),
        out_specs=(vmem,) * len(shapes),
        cost_estimate=small_cost(100000000),
        name=name,
    )(*args)


def wide_kernel(with_proj, places_ref, small_ref, big_ref, taken_ref, *refs):
    if with_proj:
        proj_kept, proj_taken, *refs = refs
    *outs, turned_v = refs
    half, sub = turned_v.shape[0], turned_v.shape[0] // 2
    span = big_ref.shape[1] // 4
    part = 256 // 4 if not with_proj else proj_kept.shape[0] // 16
    turned_v[...] = small_ref[:, 0:half].T
    for s in range(4):
        lanes = pl.ds(pl.multiple_of(places_ref[s] * span, span), span)
        block = dot_nn(turned_v[...], big_ref[:, lanes]) + taken_ref[:, lanes].astype(jnp.float32)
        block = block.astype(jnp.bfloat16)
        for side, (go, slot) in enumerate(((s % 2, s // 2), (s // 2, s % 2))):
            out = outs[2 * side + go]
            rows = slice(slot * sub, (slot + 1) * sub)
            out[rows, 0:span] = block[side * sub : (side + 1) * sub]
            if with_proj:
                at = side * sub
                for j in range(4):
                    start = pl.multiple_of(4 * j * part + places_ref[s] * part, part)
                    piece = proj_kept[pl.ds(start, part), at : at + sub] + proj_taken[
                        pl.ds(start, part), at : at + sub
                    ].astype(jnp.float32)
                    low = slot * sub + j * part
                    out[low : low + part, span:] = piece.astype(jnp.bfloat16)


def wide_grads(places, small, big, taken, proj=()):
    half = small.shape[1] // 2
    columns = big.shape[1] // 4 + (half // 2 if proj else 0)
    vmem = pl.BlockSpec(memory_space=pltpu.VMEM)
    return pl.pallas_call(
        functools.partial(wide_kernel, bool(proj)),
        out_shape=(jax.ShapeDtypeStruct((half, columns), jnp.bfloat16),) * 4,
        in_specs=[pl.BlockSpec(memory_space=pltpu.SMEM)] + [vmem] * (3 + len(proj)),
        out_specs=(vmem,) * 4,
        scratch_shapes=[pltpu.VMEM((half, small.shape[0]), jnp.bfloat16)],
        compiler_params=pltpu.CompilerParams(vmem_limit_bytes=44 << 20),
        cost_estimate=small_cost(3000000000),
        name="wide_grads",
    )(places, small, big, taken, *proj)


def plane_sum_kernel(*refs):
    sub = refs[4].shape[0]
    for side in range(2):
        kept, taken = refs[2 * side : 2 * side + 2]
        for slot in range(2):
            rows = slice(slot * sub, (slot + 1) * sub)
            total = kept[rows, :].astype(jnp.float32) + taken[rows, :].astype(jnp.float32)
            refs[4 + 2 * side + slot][...] = total.astype(jnp.bfloat16)


def cols_out_kernel(places_ref, *refs):
    outs = refs[4:]
    sub = refs[0].shape[0]
    columns = refs[0].shape[1]
    part = (outs[0].shape[0] - 2 * sub) // 2
    for side in range(2):
        kept, taken = refs[2 * side : 2 * side + 2]
        for j in range(4):
            lanes = pl.ds(pl.multiple_of(places_ref[4 + j] * sub, sub), sub)
            total = kept[:, lanes].astype(jnp.float32) + taken[:, lanes].astype(jnp.float32)
            outs[j][side * sub : (side + 1) * sub, :] = total.astype(jnp.bfloat16)
            if part:
                rows = slice(j * part, (j + 1) * part)
                total = kept[rows, columns - sub :].astype(jnp.float32)
                total = total + taken[rows, columns - sub :].astype(jnp.float32)
                low = 2 * sub + side * part
                outs[j][low : low + part, :] = total.astype(jnp.bfloat16)


def mine_kernel(*refs):
    out_ref, at = refs[8], 0
    for group in (refs[0:4], refs[4:8]):
        total = group[0][...].astype(jnp.float32)
        for ref in group[1:]:
            total = total + ref[...].astype(jnp.float32)
        out_ref[at : at + total.shape[0], :] = total.astype(jnp.bfloat16)
        at += total.shape[0]


def finish_kernel(part_rows, places_ref, *refs):
    pieces, (fc2_ref, fc1_ref, proj_ref) = refs[:2], refs[2:]
    half, sub = fc1_ref.shape[0], pieces[0].shape[1]
    for s in range(4):
        piece, base = pieces[s // 2], (s % 2) * (pieces[0].shape[0] // 2)
        at = places_ref[s]
        rows = pl.ds(pl.multiple_of(at * sub, sub), sub)
        fc2_ref[rows, :] = piece[base : base + half, :].astype(jnp.float32).T
        fc1_ref[:, rows] = piece[base + half : base + 2 * half, :].astype(jnp.float32)
        rows = pl.ds(pl.multiple_of(at * part_rows, part_rows), part_rows)
        for i in range(2):
            low = base + 2 * half + i * part_rows
            proj_ref[rows, i * sub : (i + 1) * sub] = piece[low : low + part_rows, :].astype(jnp.float32)


def finish_qkv_kernel(places_ref, *refs):
    out_ref = refs[4]
    deep, width = refs[0].shape[0], out_ref.shape[2]
    for s in range(4):
        rows = pl.ds(pl.multiple_of(places_ref[s] * deep, deep), deep)
        for k in range(3):
            out_ref[k, rows, :] = refs[s][:, k * width : (k + 1) * width].astype(jnp.float32)


def finish(places, pieces, part_rows):
    rows, sub = pieces[0].shape
    half = (rows // 2 - 2 * part_rows) // 2
    vmem = pl.BlockSpec(memory_space=pltpu.VMEM)
    return pl.pallas_call(
        functools.partial(finish_kernel, part_rows),
        out_shape=(
            jax.ShapeDtypeStruct((4 * sub, half), jnp.float32),
            jax.ShapeDtypeStruct((half, 4 * sub), jnp.float32),
            jax.ShapeDtypeStruct((4 * part_rows, half), jnp.float32),
        ),
        in_specs=[pl.BlockSpec(memory_space=pltpu.SMEM)] + [vmem] * 2,
        out_specs=[vmem] * 3,
        cost_estimate=small_cost(100000000),
        name="finish",
    )(places, *pieces)


def finish_qkv(places, pieces):
    deep, width = pieces[0].shape
    vmem = pl.BlockSpec(memory_space=pltpu.VMEM)
    return pl.pallas_call(
        finish_qkv_kernel,
        out_shape=jax.ShapeDtypeStruct((3, 4 * deep, width // 3), jnp.float32),
        in_specs=[pl.BlockSpec(memory_space=pltpu.SMEM)] + [vmem] * 4,
        out_specs=vmem,
        cost_estimate=small_cost(100000000),
        name="finish_qkv",
    )(places, *pieces)


def tie(value, *others):
    return lax.optimization_barrier((value, *others))[0]


def add_up(own, taken):
    total = own.astype(jnp.float32)
    for piece in taken:
        total = total + piece.astype(jnp.float32)
    return total


def local_paired(
    states,
    ln1_gain,
    ln1_bias,
    w_qkv,
    q_bias,
    v_bias,
    w_proj,
    proj_bias,
    ln2_gain,
    ln2_bias,
    w_fc1,
    fc1_bias,
    w_fc2,
    fc2_bias,
    teacher,
    loss_mask,
    lengths,
):
    f32, bf16 = jnp.float32, jnp.bfloat16
    dp = lax.axis_index("dp")
    row = lax.axis_index("row")
    col = lax.axis_index("col")
    local_rows, width = states.shape
    half = width // 2
    head_width = w_qkv.shape[2]
    hidden_width = w_fc1.shape[1]
    sub = hidden_width // 4
    span = 4 * sub
    part_rows = head_width // 4
    clip = (dp * 2 + row) * 2 + col // 2
    second = col % 2

    def quarter(s):
        return dp ^ s

    def frame(values):
        return jnp.where(
            row == 0, values, jnp.concatenate([values[:, half:], values[:, :half]], axis=1)
        )

    places = jnp.stack([dp ^ s for s in range(4)] + [col ^ j for j in range(4)]).astype(jnp.int32)
    flip = row.reshape(1).astype(jnp.int32)
    states_other = over_col(states, 1)
    small = jnp.concatenate(
        [
            fc1_bias.reshape(4, sub),
            q_bias.reshape(1, sub),
            v_bias.reshape(1, sub),
            jnp.zeros((10, sub), bf16),
        ],
        axis=0,
    )
    slab = make_slab(places, w_fc1, w_fc2, w_proj, w_qkv.transpose(1, 0, 2), small)
    unit_rows_total = half + 2 * sub + 2 * part_rows + small.shape[0]
    small_at = unit_rows_total - small.shape[0]
    two = over_col(slab, 2)
    w_qkv2 = w_qkv.reshape(half, 3 * head_width)
    w_qkv2 = tie(w_qkv2, slab)
    qkv_near = jnp.concatenate([w_qkv2, over_row(w_qkv2)], axis=0)
    vectors = jnp.stack([ln1_gain, ln1_bias, proj_bias, ln2_gain, ln2_bias, fc2_bias])
    vectors, states, teacher, loss_mask = lax.optimization_barrier(
        (vectors, states, teacher, loss_mask, slab)
    )[:4]
    vectors = jnp.concatenate([vectors, over_row(vectors)], axis=1).astype(f32)
    fc1_other, fc2_other, proj_other = over_row(w_fc1), over_row(w_fc2), over_row(w_proj)
    two = tie(two, fc1_other, fc2_other, proj_other)
    two_x, two_y = over_dp(two, 1), over_dp(two, 2)
    states_other = tie(states_other, two)

    all_clips = lengths.shape[0]
    valid_all = (
        loss_mask.reshape(all_clips, L) * (jnp.arange(L)[None, :] < lengths[:, None])
    ).astype(f32)
    valid_total = jnp.maximum(jnp.sum(valid_all), 1.0)
    first_row = ((dp * 2 + row) * 4 + col) * local_rows
    valid = lax.dynamic_slice_in_dim(valid_all.reshape(all_clips * L), first_row, local_rows)
    my_length = lax.dynamic_slice_in_dim(lengths, clip, 1)
    spot = jnp.arange(L)
    position = jnp.where(
        spot < local_rows, second * local_rows + spot, (1 - second) * local_rows + spot - local_rows
    )
    key_bias = jnp.where(position < my_length, 0.0, MASKED).astype(f32)
    key_bias = jnp.broadcast_to(key_bias[:, None], (L, 128))

    gain_one, shift_one = vectors[0], vectors[1]
    norm_one, _, _ = normalize(frame(states).astype(f32), gain_one, shift_one)
    norm_other, _, _ = normalize(frame(states_other).astype(f32), gain_one, shift_one)
    tokens_one = jnp.concatenate([norm_one.astype(bf16), norm_other.astype(bf16)], axis=0)

    zero_bias = jnp.zeros((head_width,), f32)
    score_scale = HD**-0.5
    scale = jnp.where(jnp.arange(3 * head_width) < head_width, score_scale, 1.0).astype(bf16)
    split = local_rows // QT * QT
    later = L - split
    over = local_rows - split

    def project(matrix, q_add, v_add):
        projected = jnp.dot(tokens_one, matrix, preferred_element_type=f32)
        add = jnp.concatenate([q_add.astype(f32), zero_bias, v_add.astype(f32)])
        return (projected + add[None]).astype(bf16) * scale[None]

    table = jnp.stack(
        [(dp ^ s) * 4 + (col ^ j) for s in range(4) for j in range(4)]
        + [a * 4 + col for a in range(4)]
        + [dp ^ s for s in range(4)]
        + [col ^ b for b in range(4)]
        + [row]
    ).astype(jnp.int32)
    loss_scale = all_clips * L * width / 2.0
    factor = (loss_scale * 2.0 / (valid_total * width)).reshape(1)
    valid = valid[:, None]
    packed_near = tie(project(qkv_near, q_bias, v_bias), table, factor, valid)
    cut_at = two.shape[0] // 32 * 16
    two_x, two_y = tie(two_x, packed_near), tie(two_y, packed_near)
    two_low, two_high = over_dp(two_y[:cut_at], 1), over_dp(two_x[cut_at:], 2)
    one_give = jnp.concatenate([slab[:unit_rows_total], two[:unit_rows_total]], axis=0)
    one = over_col(tie(one_give, states_other), 1)
    near_late, near_late_lse = attend(tie(packed_near, two_x, two_y, one), key_bias, split, later)
    two_low, two_high = tie(two_low, near_late), tie(two_high, near_late)
    two_all = jnp.concatenate([two, two_x, two_y, two_low, two_high], axis=0)
    two_theirs = over_row(two_all)
    near_other = over_col(near_late[over:], 1)
    one_x, one_y = over_dp(one, 1), over_dp(one, 2)
    one_other = over_row(tie(one, near_late))
    near_soon, near_soon_lse = attend(
        tie(packed_near, two_all, near_late, one), key_bias, 0, split
    )
    two_theirs = tie(two_theirs, near_soon)
    qkv_far = far_qkv(places, two_all, two_theirs, unit_rows_total, width)
    far_small = two_all[small_at : small_at + small.shape[0]]
    packed_far = project(qkv_far, far_small[4], far_small[5])
    packed_far = tie(packed_far, one, near_other)
    far_late, far_late_lse = attend(packed_far, key_bias, split, later)
    far_other = over_col(far_late[over:], 1)
    one_x, one_y = tie(one_x, far_late), tie(one_y, far_late)
    cut_at = one.shape[0] // 2
    one_low, one_high = over_dp(one_y[:cut_at], 1), over_dp(one_x[cut_at:], 2)
    one_theirs = [over_row(one_x), over_row(one_y)]
    far_soon, far_soon_lse = attend(
        tie(packed_far, one_x, one_y, far_late, one_other), key_bias, 0, split
    )
    one_low, one_high = tie(one_low, far_soon, far_other), tie(one_high, far_soon, far_other)
    one_mine = [one, one_x, one_y, one_low, one_high]
    one_theirs = [one_other, *one_theirs, over_row(one_low), over_row(one_high)]
    turned = tie(tokens_one, far_late).T
    at = unit_rows_total + small_at
    smalls = jnp.stack(
        [small, one[small_at : small_at + 16], two_all[small_at : small_at + 16], one[at : at + 16]]
    ).astype(f32)
    (
        attended_rows,
        outputs,
        hidden,
        grad_pre,
        norm_two,
        grad_low,
        mid_low,
        grad_mid,
        up_own,
        up_give,
        hidden_sum,
        sums,
    ) = middle_block(
        table,
        factor,
        states,
        teacher,
        valid,
        vectors,
        smalls,
        (
            w_fc1,
            fc1_other,
            w_fc2,
            fc2_other,
            w_proj,
            proj_other,
            two_all,
            two_theirs,
            *one_mine,
            *one_theirs,
            near_soon,
            near_late,
            near_other,
            far_soon,
            far_late,
            far_other,
        ),
    )
    up_far = over_col(up_give, 1)

    def joined(kept, taken):
        return (kept.astype(f32) + taken.astype(f32)).astype(bf16)

    give_fc2 = over_row(dot_tn(grad_low[:, half:], hidden).astype(bf16))
    give_fc1 = over_row(dot_tn(norm_two[:, half:], grad_pre).astype(bf16))
    give_proj = over_row(dot_tn(attended_rows, mid_low[:, half:]).astype(bf16))
    kept_proj = dot_tn(attended_rows, mid_low[:, :half])

    def plane_first(wide):
        keep_x, give_x, keep_y, give_y = wide
        return (keep_x, keep_y), (give_x, give_y), (over_dp(give_x, 1), over_dp(give_y, 2))

    def plane_second(keep, taken):
        shape = ((keep[0].shape[0] // 2, keep[0].shape[1]), bf16)
        keep_x, give_x, keep_y, give_y = on_chip(
            plane_sum_kernel, [shape] * 4, "plane_sum", keep[0], taken[0], keep[1], taken[1]
        )
        return (keep_x, keep_y), (give_x, give_y), (over_dp(give_x, 2), over_dp(give_y, 1))

    def cols_out(keep, taken, rows):
        blocks = on_chip(
            cols_out_kernel,
            [((rows, sub), bf16)] * 4,
            "cols_out",
            *(places, keep[0], taken[0], keep[1], taken[1]),
            tables=1,
        )
        return blocks, [over_col(blocks[j], j) for j in (1, 2, 3)]

    def all_tied(values, *others):
        return [tie(v, *others) for v in values]

    wide = wide_grads(places, grad_low, hidden, give_fc2)
    fc2_keep, fc2_give, fc2_taken = plane_first(wide)
    wide = wide_grads(
        places, tie(norm_two, *fc2_give), grad_pre, give_fc1, (kept_proj, give_proj)
    )
    fc1_keep, fc1_give, fc1_taken = plane_first(wide)

    packed_near = tie(packed_near, *fc2_give, *fc1_give)
    part_near = attend_back(packed_near, key_bias, near_soon_lse, near_soon, up_own, None, 0, 0)
    fc2_keep, fc2_give, fc2_taken = plane_second(fc2_keep, all_tied(fc2_taken, part_near[0]))

    packed_far = tie(packed_far, *fc2_give, part_near[0])
    part_far = attend_back(
        packed_far, key_bias, far_soon_lse, far_soon, up_own, None, head_width, 0
    )
    fc2_blocks, fc2_cols = cols_out(fc2_keep, all_tied(fc2_taken, part_far[0]), 2 * sub)
    fc1_keep, fc1_give, fc1_taken = plane_second(fc1_keep, all_tied(fc1_taken, part_far[0]))

    packed_near = tie(packed_near, *fc2_blocks, *fc1_give)
    grad_near, near_sums = attend_back(
        packed_near, key_bias, near_late_lse, near_late, up_own, up_far, 0, split, part_near
    )
    fc2_cols = all_tied(fc2_cols, grad_near)
    fc1_blocks, fc1_cols = cols_out(
        fc1_keep, all_tied(fc1_taken, grad_near, *fc2_cols), 2 * sub + 2 * part_rows
    )
    near_tied = tie(grad_near, *fc1_blocks)
    near_row = over_row(dot_tn(tokens_one[:, half:], near_tied).astype(bf16))
    wide_near = joined(dot_tn(tokens_one[:, :half], near_tied), near_row)
    deep = half // 4
    near_give = jnp.concatenate([cut(wide_near, quarter(s), deep) for s in (1, 3)], axis=0)
    near_taken = over_dp(near_give, 1)

    packed_far = tie(packed_far, near_give, *fc1_blocks, *fc2_cols)
    grad_far, far_sums = attend_back(
        packed_far, key_bias, far_late_lse, far_late, up_own, up_far, head_width, split, part_far
    )

    columns, slots = grad_far.shape[1], 2 * VECTORS
    vec_keep, row_give, kept = on_chip(
        far_grads_kernel,
        [((VECTORS, half), f32), ((half + slots, columns), bf16), ((half, columns), f32)],
        "far_grads",
        *(turned, tie(grad_far, near_taken, *fc1_cols), sums, hidden_sum, near_sums, far_sums),
    )
    row_taken = over_row(row_give)
    mine_rows = fc2_blocks[0].shape[0] + fc1_blocks[0].shape[0]
    (mine,) = on_chip(
        mine_kernel,
        [((mine_rows, sub), bf16)],
        "mine",
        *(fc2_blocks[0], *fc2_cols, fc1_blocks[0], *all_tied(fc1_cols, row_give)),
    )
    mine_x = over_dp(mine, 1)
    norm_own, norm_give, norm_sums = token_back(
        flip, grad_near, tie(grad_far, mine), qkv_near, qkv_far, states, states_other
    )
    norm_give = tie(norm_give, row_taken, mine_x)
    norm_taken = over_col(norm_give, 1)
    near_own, far_own, vec_sum, *plane_give = on_chip(
        after_row_kernel,
        [((deep, columns), f32)] * 2
        + [((VECTORS, half), f32)]
        + [((deep + slots + (deep if s == 2 else 0), columns), bf16) for s in (1, 2, 3)],
        "after_row",
        *(places, kept, tie(row_taken, norm_give), vec_keep, norm_sums, wide_near, near_taken),
        tables=1,
    )
    plane_taken = [over_dp(plane_give[s - 1], s) for s in (1, 2, 3)]
    mine_two = jnp.concatenate([mine, tie(mine_x, *plane_give)], axis=0)
    plane_taken = all_tied(plane_taken, mine_two, norm_taken)
    near_own, vec_sum, col_give, vec_give = on_chip(
        after_plane_kernel,
        [
            ((deep, columns), f32),
            ((VECTORS, half), f32),
            ((deep + slots, columns), bf16),
            ((slots, half), bf16),
        ],
        "after_plane",
        *(near_own, far_own, vec_sum, *plane_taken),
    )
    mine_y = over_dp(tie(mine_two, col_give), 2)
    col_taken = [over_col(vec_give, 1), over_col(col_give, 2), over_col(vec_give, 3)]
    norm_taken = tie(norm_taken, col_give)
    grad_states = last_norm(flip, norm_own, norm_taken, states, grad_mid, vectors)

    qkv_mine, vec_total = on_chip(
        after_cols_kernel,
        [((deep, columns), bf16), ((VECTORS, half), f32)],
        "after_cols",
        *(near_own, vec_sum, *all_tied(col_taken, grad_states)),
    )
    qkv_back = [over_dp(qkv_mine, s) for s in (1, 2, 3)]
    norm_total = vec_total[4:6] + over_row(vec_total[17:19])
    fc2_grad, fc1_grad, proj_grad = finish(places, [mine_two, tie(mine_y, qkv_mine)], part_rows)
    qkv_grad = finish_qkv(places, [qkv_mine, *all_tied(qkv_back, fc2_grad)]).transpose(1, 0, 2)

    fc1_bias_grad = lax.dynamic_index_in_dim(vec_total[6:14].reshape(4, 4, sub), col, 1, False)
    loss_value = jnp.sum(vec_total[16]) / (valid_total * width)
    return (
        outputs,
        loss_value,
        grad_states,
        norm_total[0],
        norm_total[1],
        qkv_grad,
        vec_total[14, :head_width],
        vec_total[14, head_width:],
        proj_grad,
        vec_total[2],
        vec_total[0],
        vec_total[1],
        fc1_grad,
        fc1_bias_grad.reshape(span),
        fc2_grad,
        vec_total[3],
    )


def solution(mesh):
    sizes = (mesh.shape["dp"], mesh.shape["row"], mesh.shape["col"])
    body = local_paired if sizes == PAIRED_MESH else local_general
    in_specs = (
        P(("dp", "row", "col"), None),
        P("row"),
        P("row"),
        P("row", None, "col"),
        P("col"),
        P("col"),
        P("col", "row"),
        P("row"),
        P("row"),
        P("row"),
        P("row", "col"),
        P("col"),
        P("col", "row"),
        P("row"),
        P(("dp", "row", "col"), None),
        P(),
        P(),
    )
    out_specs = (
        P(("dp", "row", "col"), None),
        P(),
        P(("dp", "row", "col"), None),
        P("row"),
        P("row"),
        P("row", None, "col"),
        P("col"),
        P("col"),
        P("col", "row"),
        P("row"),
        P("row"),
        P("row"),
        P("row", "col"),
        P("col"),
        P("col", "row"),
        P("row"),
    )
    return jax.shard_map(body, mesh=mesh, in_specs=in_specs, out_specs=out_specs, check_vma=False)
```

```python
import functools

import jax
import jax.numpy as jnp
from jax import lax
from jax.experimental import pallas as pl
from jax.experimental.pallas import tpu as pltpu
from jax.sharding import PartitionSpec as P

HD = 64
L = 1568


EPSILON = 1e-06
MASKED = -1e30
ROOT_HALF = 0.7071067811865476
DENSITY_FACTOR = 0.3989422804014327


def normalize(values, factor, offset):
    centered = values - jnp.mean(values, axis=-1, keepdims=True)
    spread = lax.rsqrt(jnp.mean(centered * centered, axis=-1, keepdims=True) + EPSILON)
    normal = centered * spread
    return (normal * factor + offset, normal, spread)


def norm_back(upstream, normal, spread, factor):
    inner = upstream * factor
    center_term = jnp.mean(inner, axis=-1, keepdims=True)
    slope_term = jnp.mean(inner * normal, axis=-1, keepdims=True)
    back = spread * (inner - center_term - normal * slope_term)
    return (back, jnp.sum(upstream * normal, axis=0), jnp.sum(upstream, axis=0))


def gelu_value(values):
    return values * (0.5 * (1.0 + lax.erf(values * ROOT_HALF)))


def gelu_slope(values):
    normal_cdf = 0.5 * (1.0 + lax.erf(values * ROOT_HALF))
    return normal_cdf + values * jnp.exp(-0.5 * values * values) * DENSITY_FACTOR


def masked_scores(queries, key_rows, length, score_scale):
    logits = (
        jnp.einsum("ihd,jhd->hij", queries, key_rows, preferred_element_type=jnp.float32)
        * score_scale
    )
    keep = jnp.arange(key_rows.shape[0]) < length
    return jnp.where(keep[None, None, :], logits, MASKED)


def attend_clip(packed, length, score_scale):
    half_span = packed.shape[0] // 2
    key_rows = packed[:, 1]
    value_rows = packed[:, 2]
    pieces = []
    totals = []
    for block_index in range(2):
        queries = packed[block_index * half_span : (block_index + 1) * half_span, 0]
        logits = masked_scores(queries, key_rows, length, score_scale)
        peak = jnp.max(logits, axis=-1, keepdims=True)
        total = peak + jnp.log(jnp.sum(jnp.exp(logits - peak), axis=-1, keepdims=True))
        weights = jnp.exp(logits - total).astype(jnp.bfloat16)
        pieces.append(
            jnp.einsum("hij,jhd->ihd", weights, value_rows, preferred_element_type=jnp.float32)
        )
        totals.append(total[..., 0])
    return (jnp.concatenate(pieces, 0), jnp.concatenate(totals, 1))


def attend_clip_back(packed, length, totals, upstream, score_scale):
    half_span = packed.shape[0] // 2
    key_rows = packed[:, 1]
    value_rows = packed[:, 2]
    grad_keys = jnp.zeros(key_rows.shape, jnp.float32)
    grad_values = jnp.zeros(value_rows.shape, jnp.float32)
    grad_queries = []
    for block_index in range(2):
        first = block_index * half_span
        queries = packed[first : first + half_span, 0]
        logits = masked_scores(queries, key_rows, length, score_scale)
        probs = jnp.exp(logits - totals[:, first : first + half_span][..., None])
        incoming = upstream[first : first + half_span]
        grad_values = grad_values + jnp.einsum(
            "hij,ihd->jhd", probs.astype(jnp.bfloat16), incoming, preferred_element_type=jnp.float32
        )
        grad_probs = jnp.einsum(
            "ihd,jhd->hij", incoming, value_rows, preferred_element_type=jnp.float32
        )
        grad_logits = (
            probs * (grad_probs - jnp.sum(probs * grad_probs, axis=-1, keepdims=True))
        ).astype(jnp.bfloat16)
        grad_queries.append(
            jnp.einsum("hij,jhd->ihd", grad_logits, key_rows, preferred_element_type=jnp.float32)
            * score_scale
        )
        grad_keys = (
            grad_keys
            + jnp.einsum("hij,ihd->jhd", grad_logits, queries, preferred_element_type=jnp.float32)
            * score_scale
        )
    return jnp.stack([jnp.concatenate(grad_queries, 0), grad_keys, grad_values], axis=1)


def local_general(
    states,
    ln1_gain,
    ln1_bias,
    w_qkv,
    q_bias,
    v_bias,
    w_proj,
    proj_bias,
    ln2_gain,
    ln2_bias,
    w_fc1,
    fc1_bias,
    w_fc2,
    fc2_bias,
    teacher,
    loss_mask,
    lengths,
):
    row_count = lax.axis_size("row")
    col_count = lax.axis_size("col")
    col_index = lax.axis_index("col")
    group_index = lax.axis_index("dp") * row_count + lax.axis_index("row")
    local_rows = states.shape[0]
    width = states.shape[1]
    group_rows = local_rows * col_count
    clip_count = group_rows // L
    head_width = w_qkv.shape[2]
    heads_here = head_width // HD
    hidden_width = w_fc1.shape[1]
    score_scale = HD ** (-0.5)
    vectors = jnp.stack([ln1_gain, ln1_bias, proj_bias, ln2_gain, ln2_bias, fc2_bias])
    qkv_full, proj_full, fc1_full, fc2_full, vector_full = (
        lax.all_gather(w_qkv, "row", axis=0, tiled=True),
        lax.all_gather(w_proj, "row", axis=1, tiled=True),
        lax.all_gather(w_fc1, "row", axis=0, tiled=True),
        lax.all_gather(w_fc2, "row", axis=1, tiled=True),
        lax.all_gather(vectors, "row", axis=1, tiled=True),
    )
    vector_full = vector_full.astype(jnp.float32)
    gain_one = vector_full[0]
    shift_one = vector_full[1]
    bias_proj = vector_full[2]
    gain_two = vector_full[3]
    shift_two = vector_full[4]
    bias_two = vector_full[5]
    all_clips = lengths.shape[0]
    valid_all = (
        loss_mask.reshape(all_clips, L) * (jnp.arange(L)[None, :] < lengths[:, None])
    ).astype(jnp.float32)
    valid_total = jnp.maximum(jnp.sum(valid_all), 1.0)
    first_row = (group_index * col_count + col_index) * local_rows
    valid = lax.dynamic_slice_in_dim(valid_all.reshape(all_clips * L), first_row, local_rows)
    my_lengths = lax.dynamic_slice_in_dim(lengths, group_index * clip_count, clip_count)
    inputs = states.astype(jnp.float32)
    norm_one, unit_one, spread_one = normalize(inputs, gain_one, shift_one)
    norm_one = norm_one.astype(jnp.bfloat16)
    tokens_one = lax.all_gather(norm_one, "col", axis=0, tiled=True)
    qkv_matrix = qkv_full.reshape(width, 3 * head_width)
    projected = jnp.dot(tokens_one, qkv_matrix, preferred_element_type=jnp.float32).reshape(
        group_rows, 3, head_width
    )
    bias_rows = jnp.stack(
        [
            q_bias.astype(jnp.float32),
            jnp.zeros((head_width,), jnp.float32),
            v_bias.astype(jnp.float32),
        ]
    )
    packed = (projected + bias_rows[None]).astype(jnp.bfloat16)
    clips_packed = packed.reshape(clip_count, L, 3, heads_here, HD)
    attended, totals = lax.map(
        lambda element: attend_clip(element[0], element[1], score_scale), (clips_packed, my_lengths)
    )
    attended = attended.reshape(group_rows, head_width).astype(jnp.bfloat16)
    proj_whole, qkv_whole = (
        lax.all_gather(proj_full, "col", axis=0, tiled=True),
        lax.all_gather(qkv_full, "col", axis=2, tiled=True),
    )
    attended_rows = lax.all_to_all(attended, "col", split_axis=0, concat_axis=1, tiled=True)
    middle = inputs + (
        jnp.dot(attended_rows, proj_whole, preferred_element_type=jnp.float32) + bias_proj
    )
    norm_two, unit_two, spread_two = normalize(middle, gain_two, shift_two)
    norm_two = norm_two.astype(jnp.bfloat16)
    fc1_whole, fc2_whole, fc1_bias_whole = (
        lax.all_gather(fc1_full, "col", axis=1, tiled=True),
        lax.all_gather(fc2_full, "col", axis=0, tiled=True),
        lax.all_gather(fc1_bias, "col", axis=0, tiled=True),
    )
    hidden_pre = jnp.dot(
        norm_two, fc1_whole, preferred_element_type=jnp.float32
    ) + fc1_bias_whole.astype(jnp.float32)
    hidden = gelu_value(hidden_pre).astype(jnp.bfloat16)
    outputs = middle + (jnp.dot(hidden, fc2_whole, preferred_element_type=jnp.float32) + bias_two)
    differ = outputs - teacher.astype(jnp.float32)
    numerator = jnp.sum(valid[:, None] * differ * differ)
    loss_scale = all_clips * L * width / 2.0
    grad_out = loss_scale * 2.0 / (valid_total * width) * valid[:, None] * differ
    grad_low = grad_out.astype(jnp.bfloat16)
    grad_hidden = jnp.dot(grad_low, fc2_whole.T, preferred_element_type=jnp.float32)
    grad_pre = (grad_hidden * gelu_slope(hidden_pre)).astype(jnp.bfloat16)
    wide_fc2 = jnp.dot(hidden.T, grad_low, preferred_element_type=jnp.float32)
    wide_fc1 = jnp.dot(norm_two.T, grad_pre, preferred_element_type=jnp.float32)
    fc1_grad_part, fc2_grad_part = (
        lax.psum_scatter(
            wide_fc1.astype(jnp.bfloat16), "col", scatter_dimension=1, tiled=True
        ).astype(jnp.float32),
        lax.psum_scatter(
            wide_fc2.astype(jnp.bfloat16), "col", scatter_dimension=0, tiled=True
        ).astype(jnp.float32),
    )
    fc1_bias_sum = jnp.sum(grad_pre, axis=0, dtype=jnp.float32)
    grad_norm_two = jnp.dot(grad_pre, fc1_whole.T, preferred_element_type=jnp.float32)
    back_two, gain_two_grad, shift_two_grad = norm_back(
        grad_norm_two, unit_two, spread_two, gain_two
    )
    grad_mid = grad_out + back_two
    mid_low = grad_mid.astype(jnp.bfloat16)
    wide_proj = jnp.dot(attended_rows.T, mid_low, preferred_element_type=jnp.float32)
    proj_grad_part = lax.psum_scatter(
        wide_proj.astype(jnp.bfloat16), "col", scatter_dimension=0, tiled=True
    )
    grad_attended_rows = jnp.dot(mid_low, proj_whole.T, preferred_element_type=jnp.float32).astype(
        jnp.bfloat16
    )
    grad_attended = lax.all_to_all(
        grad_attended_rows, "col", split_axis=1, concat_axis=0, tiled=True
    )
    grads_packed = lax.map(
        lambda element: attend_clip_back(
            element[0], element[1], element[2], element[3], score_scale
        ),
        (clips_packed, my_lengths, totals, grad_attended.reshape(clip_count, L, heads_here, HD)),
    )
    grads_packed = grads_packed.reshape(group_rows, 3 * head_width).astype(jnp.bfloat16)
    qkv_grad_part = jnp.dot(tokens_one.T, grads_packed, preferred_element_type=jnp.float32).reshape(
        width, 3, head_width
    )
    bias_sums = jnp.sum(grads_packed.reshape(group_rows, 3, head_width), axis=0, dtype=jnp.float32)
    grads_rows = lax.all_to_all(
        grads_packed.reshape(group_rows, 3, head_width),
        "col",
        split_axis=0,
        concat_axis=2,
        tiled=True,
    )
    grad_norm_one = jnp.dot(
        grads_rows.reshape(local_rows, 3 * width),
        qkv_whole.reshape(width, 3 * width).T,
        preferred_element_type=jnp.float32,
    )
    back_one, gain_one_grad, shift_one_grad = norm_back(
        grad_norm_one, unit_one, spread_one, gain_one
    )
    grad_states = (grad_mid + back_one).astype(jnp.bfloat16)
    proj_bias_grad = jnp.sum(mid_low, axis=0, dtype=jnp.float32)
    fc2_bias_grad = jnp.sum(grad_low, axis=0, dtype=jnp.float32)
    token_vectors = jnp.stack(
        [
            gain_one_grad,
            shift_one_grad,
            proj_bias_grad,
            gain_two_grad,
            shift_two_grad,
            fc2_bias_grad,
        ]
    )
    head_vectors = lax.dynamic_update_slice(
        jnp.zeros((2, width), jnp.float32),
        jnp.stack([bias_sums[0], bias_sums[2]]),
        (0, col_index * head_width),
    )
    token_sums, head_sums, fc1_sums, loss_sum = lax.psum(
        (token_vectors, head_vectors, fc1_bias_sum, numerator), ("dp", "row", "col")
    )
    qkv_rows, proj_cols, fc1_rows, fc2_cols = (
        lax.psum_scatter(
            qkv_grad_part.astype(jnp.bfloat16), "row", scatter_dimension=0, tiled=True
        ).astype(jnp.float32),
        lax.psum_scatter(proj_grad_part, "row", scatter_dimension=1, tiled=True).astype(
            jnp.float32
        ),
        lax.psum_scatter(
            fc1_grad_part.astype(jnp.bfloat16), "row", scatter_dimension=0, tiled=True
        ).astype(jnp.float32),
        lax.psum_scatter(
            fc2_grad_part.astype(jnp.bfloat16), "row", scatter_dimension=1, tiled=True
        ).astype(jnp.float32),
    )
    qkv_grad, proj_grad, fc1_grad, fc2_grad = (
        lax.psum(qkv_rows.astype(jnp.bfloat16), "dp").astype(jnp.float32),
        lax.psum(proj_cols.astype(jnp.bfloat16), "dp").astype(jnp.float32),
        lax.psum(fc1_rows.astype(jnp.bfloat16), "dp").astype(jnp.float32),
        lax.psum(fc2_cols.astype(jnp.bfloat16), "dp").astype(jnp.float32),
    )
    half_width = width // row_count
    token_part = lax.dynamic_slice_in_dim(
        token_sums, lax.axis_index("row") * half_width, half_width, 1
    )
    head_part = lax.dynamic_slice_in_dim(head_sums, col_index * head_width, head_width, 1)
    fc1_part = lax.dynamic_slice_in_dim(fc1_sums, col_index * hidden_width, hidden_width, 0)
    loss_value = loss_sum / (valid_total * width)
    return (
        outputs.astype(jnp.bfloat16),
        loss_value,
        grad_states,
        token_part[0],
        token_part[1],
        qkv_grad,
        head_part[0],
        head_part[1],
        proj_grad,
        token_part[2],
        token_part[3],
        token_part[4],
        fc1_grad,
        fc1_part,
        fc2_grad,
        token_part[5],
    )


PAIRED_MESH = (4, 2, 4)
GROUP = 4


def small_cost(flops):
    return pl.CostEstimate(flops=flops, bytes_accessed=0, transcendentals=0)
QT = 128


def dot_nn(a, b):
    return lax.dot_general(a, b, (((1,), (0,)), ((), ())), preferred_element_type=jnp.float32)


def dot_nt(a, b):
    return lax.dot_general(a, b, (((1,), (1,)), ((), ())), preferred_element_type=jnp.float32)


def dot_tn(a, b):
    return lax.dot_general(a, b, (((0,), (0,)), ((), ())), preferred_element_type=jnp.float32)


def head_stack(values, zero):
    lane_head = lax.broadcasted_iota(jnp.int32, values.shape, 1) // HD
    return jnp.concatenate([jnp.where(lane_head == h, values, zero) for h in range(GROUP)], axis=0)


def head_unstack(wide, count):
    return jnp.concatenate(
        [wide[h * HD : (h + 1) * HD, h * count : (h + 1) * count] for h in range(GROUP)], axis=0
    ).T


def tiles_of(rows, tile):
    full = rows // QT

    @pl.loop(0, full)
    def _(index):
        tile(pl.multiple_of(index * QT, QT), QT, index)

    if rows > full * QT:
        tile(full * QT, rows - full * QT, full)


def attend_kernel(first, packed_ref, bias_ref, out_ref, lse_ref, vt_ref):
    width = GROUP * HD
    vt_ref[...] = packed_ref[:, 2 * width : 3 * width].T

    def tile(start, count, index):
        cols = GROUP * count
        stacked = head_stack(
            packed_ref[pl.ds(first + start, count), 0:width], jnp.zeros((), jnp.bfloat16)
        )
        keys = packed_ref[:, width : 2 * width]
        bias = bias_ref[...]
        scores = dot_nt(keys, stacked) + jnp.concatenate([bias] * (cols // 128), axis=1)
        peak = jnp.max(scores, axis=0, keepdims=True)
        weights = jnp.exp(scores - peak)
        total = jnp.sum(weights, axis=0, keepdims=True)
        wide = dot_nn(vt_ref[...], weights.astype(jnp.bfloat16)) * (1.0 / total)
        out_ref[pl.ds(start, count), :] = head_unstack(wide, count).astype(jnp.bfloat16)
        lse_ref[index, :, 0:cols] = jnp.broadcast_to(peak + jnp.log(total), (8, cols))

    tiles_of(out_ref.shape[0], tile)


def attend_back_kernel(
    first, lane, last, packed_ref, bias_ref, lse_ref, att_ref, up_own_ref, up_far_ref, *refs
):
    width = GROUP * HD
    lanes = slice(lane, lane + width)
    own_rows = up_own_ref.shape[0]
    if last:
        dq_in, dk_in, dv_in, out_ref, sum_ref, kt_ref, up_ref, dk_ref, dv_ref = refs
        dk_ref[...] = dk_in[...]
        dv_ref[...] = dv_in[...]
        out_ref[0:first, 0:width] = dq_in[...]
        rows = out_ref.shape[0] - first
        up_ref[0 : own_rows - first, :] = up_own_ref[first:own_rows, lanes]
        up_ref[own_rows - first :, :] = up_far_ref[:, lanes]
    else:
        out_ref, dk_ref, dv_ref, kt_ref, up_ref = refs
        dk_ref[...] = jnp.zeros_like(dk_ref)
        dv_ref[...] = jnp.zeros_like(dv_ref)
        rows = out_ref.shape[0]
        up_ref[...] = up_own_ref[0:rows, lanes]
    kt_ref[...] = packed_ref[:, width : 2 * width].T

    def tile(start, count, index):
        cols = GROUP * count
        zero = jnp.zeros((), jnp.bfloat16)
        up = up_ref[pl.ds(start, count), :]
        stacked = head_stack(packed_ref[pl.ds(first + start, count), 0:width], zero)
        up_stacked = head_stack(up, zero)
        product = head_stack(
            up.astype(jnp.float32) * att_ref[pl.ds(start, count), :].astype(jnp.float32),
            jnp.zeros((), jnp.float32),
        )
        high = product.astype(jnp.bfloat16)
        low = (product - high.astype(jnp.float32)).astype(jnp.bfloat16)
        ones = jnp.ones((8, width), jnp.bfloat16)
        delta = (dot_nt(ones, high) + dot_nt(ones, low))[0:1]
        keys = packed_ref[:, width : 2 * width]
        values = packed_ref[:, 2 * width : 3 * width]
        bias = bias_ref[...]
        scores = dot_nt(keys, stacked) + jnp.concatenate([bias] * (cols // 128), axis=1)
        weights = jnp.exp(scores - lse_ref[index, 0:1, 0:cols])
        dv_ref[...] += dot_nn(weights.astype(jnp.bfloat16), up_stacked)
        grad = (weights * (dot_nt(values, up_stacked) - delta)).astype(jnp.bfloat16)
        dk_ref[...] += dot_nn(grad, stacked)
        wide = dot_nn(kt_ref[...], grad) * (HD**-0.5)
        at = pl.ds(first + start if last else start, count)
        out_ref[at, 0:width] = head_unstack(wide, count).astype(jnp.bfloat16)

    tiles_of(rows, tile)
    if last:
        out_ref[:, width : 2 * width] = dk_ref[...].astype(jnp.bfloat16)
        out_ref[:, 2 * width : 3 * width] = dv_ref[...].astype(jnp.bfloat16)
        for k in range(3):
            part = out_ref[:, k * width : (k + 1) * width].astype(jnp.float32)
            sum_ref[:, k * width : (k + 1) * width] = jnp.sum(part, axis=0, keepdims=True)


def attend(packed, bias, first, rows):
    tokens, width = packed.shape[0], GROUP * HD
    tiles = -(-rows // QT)
    return pl.pallas_call(
        functools.partial(attend_kernel, first),
        out_shape=(
            jax.ShapeDtypeStruct((rows, width), jnp.bfloat16),
            jax.ShapeDtypeStruct((tiles, 8, GROUP * QT), jnp.float32),
        ),
        in_specs=[pl.BlockSpec(memory_space=pltpu.VMEM)] * 2,
        out_specs=[pl.BlockSpec(memory_space=pltpu.VMEM)] * 2,
        scratch_shapes=[pltpu.VMEM((width, tokens), jnp.bfloat16)],
        compiler_params=pltpu.CompilerParams(vmem_limit_bytes=32 << 20),
        cost_estimate=pl.CostEstimate(
            flops=2 * rows * tokens * width * 4, bytes_accessed=6 << 20, transcendentals=0
        ),
        name="attend",
    )(packed, bias)


def attend_back(packed, bias, lse, att, up_own, up_far, lane, first, before=None):
    tokens, width = packed.shape[0], GROUP * HD
    rows = att.shape[0]
    total = jax.ShapeDtypeStruct((tokens, width), jnp.float32)
    vmem = pl.BlockSpec(memory_space=pltpu.VMEM)
    scratch = [pltpu.VMEM((width, tokens), jnp.bfloat16), pltpu.VMEM((rows, width), jnp.bfloat16)]
    if before is None:
        extra = ()
        out_shape = (jax.ShapeDtypeStruct((rows, width), jnp.bfloat16), total, total)
        up_far = up_own
    else:
        extra = before
        out_shape = (
            jax.ShapeDtypeStruct((tokens, 3 * width), jnp.bfloat16),
            jax.ShapeDtypeStruct((1, 3 * width), jnp.float32),
        )
        scratch += [pltpu.VMEM((tokens, width), jnp.float32)] * 2
    return pl.pallas_call(
        functools.partial(attend_back_kernel, first, lane, before is not None),
        out_shape=out_shape,
        in_specs=[vmem] * (6 + len(extra)),
        out_specs=(vmem,) * len(out_shape),
        scratch_shapes=scratch,
        compiler_params=pltpu.CompilerParams(vmem_limit_bytes=52 << 20),
        cost_estimate=pl.CostEstimate(
            flops=4 * rows * tokens * width * 4, bytes_accessed=10 << 20, transcendentals=0
        ),
        name="attend_back",
    )(packed, bias, lse, att, up_own, up_far, *extra)


FF_CHUNK = 512
ROWS = 112


def rows_of(total, body):
    @pl.loop(0, total // ROWS)
    def _(index):
        body(pl.ds(pl.multiple_of(index * ROWS, ROWS), ROWS))


def unit_rows(values):
    centered = values - jnp.mean(values, axis=-1, keepdims=True)
    spread = lax.rsqrt(jnp.mean(centered * centered, axis=-1, keepdims=True) + EPSILON)
    return centered * spread, spread


def middle_kernel(
    table_ref,
    factor_ref,
    input_ref,
    target_ref,
    valid_ref,
    vector_ref,
    small_ref,
    fc1_own,
    fc1_other,
    fc2_own,
    fc2_other,
    proj_own,
    proj_other,
    two_mine,
    two_theirs,
    *refs,
):
    one_mine, one_theirs, att_parts, refs = refs[:5], refs[5:10], refs[10:16], refs[16:]
    (
        att_hbm,
        out_hbm,
        hidden_hbm,
        pre_hbm,
        norm_hbm,
        grad_low_hbm,
        mid_low_ref,
        grad_mid_ref,
        up_own_ref,
        up_give_ref,
        hidden_sum_ref,
        sums_ref,
        fc1_v,
        fc2_v,
        proj_v,
        middle_v,
        back_v,
        out_ref,
        hidden_ref,
        pre_ref,
        norm_ref,
        grad_low_ref,
        att_ref,
        sem_one,
        sem_two,
        sem_proj,
        sem_att,
        sem_out,
    ) = refs
    stores = [
        pltpu.make_async_copy(source, target, sem_out.at[i])
        for i, (source, target) in enumerate(
            (
                (norm_ref, norm_hbm),
                (hidden_ref, hidden_hbm),
                (out_ref, out_hbm),
                (grad_low_ref, grad_low_hbm),
                (pre_ref, pre_hbm),
                (att_ref, att_hbm),
            )
        )
    ]
    f32, bf16 = jnp.float32, jnp.bfloat16
    total_rows = input_ref.shape[0]
    half = fc1_own.shape[0]
    sub = fc1_own.shape[1] // 4
    heads = proj_own.shape[0]
    part = heads // 4
    hidden_total = hidden_ref.shape[1]
    chunks = hidden_total // FF_CHUNK
    unit = half + 2 * sub + 2 * part + 16

    def fc1_copy(source, side, at):
        lanes = pl.ds(pl.multiple_of(at * sub, sub), sub)
        pltpu.make_async_copy(
            source, fc1_v.at[side * half : (side + 1) * half, lanes], sem_one.at[at // 2]
        ).start()

    def fc2_copy(source, side, i, at):
        lane = side * half + i * sub
        pltpu.make_async_copy(
            source, fc2_v.at[pl.ds(pl.multiple_of(at * sub, sub), sub), lane : lane + sub], sem_two
        ).start()

    sources = []
    for s in range(4):
        step = two_mine.shape[0] // 4
        sources.append((s, 2, two_mine, two_theirs, s * step))
        low, high = (3, 4) if s == 3 else (s, s)
        sources.append((s, 1, one_mine[low], one_theirs[low], 0))
        sources.append((s, 3, one_mine[high], one_theirs[high], 0 if s == 3 else unit))

    early_rows = att_parts[0].shape[0]
    for at in range(2):
        soon, late, other = att_parts[3 * at : 3 * at + 3]
        lanes = slice(2 * at * heads, (2 * at + 1) * heads)
        pltpu.make_async_copy(soon, att_ref.at[0:early_rows, lanes], sem_att).start()
        pltpu.make_async_copy(
            late.at[0 : total_rows - early_rows], att_ref.at[early_rows:total_rows, lanes], sem_att
        ).start()
        lanes = slice((2 * at + 1) * heads, (2 * at + 2) * heads)
        pltpu.make_async_copy(other, att_ref.at[:, lanes], sem_att).start()
    for side, ref in enumerate((proj_own, proj_other)):
        pltpu.make_async_copy(
            ref, proj_v.at[0:heads, side * half : (side + 1) * half], sem_proj
        ).start()
    for s, j, *refs, base in sources:
        rows = pl.ds(pl.multiple_of(j * heads + table_ref[20 + s] * part, part), part)
        for side in range(2):
            for i in range(2):
                low = base + half + 2 * sub + i * part
                lane = side * half + i * sub
                pltpu.make_async_copy(
                    refs[side].at[low : low + part, :], proj_v.at[rows, lane : lane + sub], sem_proj
                ).start()
    for a in range(4):
        for side, ref in enumerate((fc1_own, fc1_other)):
            fc1_copy(ref.at[:, a * sub : (a + 1) * sub], side, table_ref[16 + a])
    for s, j, *refs, base in sources:
        for side in range(2):
            fc1_copy(refs[side].at[base : base + half, :], side, table_ref[4 * s + j])
    for a in range(4):
        for side, ref in enumerate((fc2_own, fc2_other)):
            for i in range(2):
                fc2_copy(
                    ref.at[a * sub : (a + 1) * sub, i * sub : (i + 1) * sub], side, i, table_ref[16 + a]
                )
    for s, j, *refs, base in sources:
        for side in range(2):
            for i in range(2):
                low = base + half + i * sub
                fc2_copy(refs[side].at[low : low + sub, :], side, i, table_ref[4 * s + j])

    def lanes_of(i):
        return pl.ds(pl.multiple_of((table_ref[28] ^ i) * half, half), half)

    sums_ref[...] = jnp.zeros_like(sums_ref)

    pltpu.make_async_copy(att_ref, att_ref, sem_att).wait()
    stores[5].start()
    pltpu.make_async_copy(proj_v, proj_v, sem_proj).wait()
    for i in range(2):
        cols = slice(i * half, (i + 1) * half)
        middle_v[:, cols] = input_ref[:, lanes_of(i)].astype(f32) + (
            dot_nn(att_ref[...], proj_v[:, cols]) + vector_ref[2:3, cols]
        )

    @functools.partial(rows_of, total_rows)
    def _(rows):
        normal, _ = unit_rows(middle_v[rows, :])
        norm_ref[rows, :] = (normal * vector_ref[3:4, :] + vector_ref[4:5, :]).astype(bf16)

    stores[0].start()

    @pl.loop(0, chunks)
    def _(k):
        span = pl.ds(pl.multiple_of(k * FF_CHUNK, FF_CHUNK), FF_CHUNK)
        pltpu.make_async_copy(fc1_v.at[:, span], fc1_v.at[:, span], sem_one.at[k]).wait()
        a = k // 2
        bias = jnp.concatenate(
            [
                small_ref[table_ref[24 + 2 * (k % 2) + i], pl.ds(a, 1), :]
                for i in range(FF_CHUNK // sub)
            ],
            axis=1,
        )
        pre = dot_nn(norm_ref[...], fc1_v[:, span]) + bias
        cdf = 0.5 * (1.0 + lax.erf(pre * ROOT_HALF))
        hidden_ref[:, span] = (pre * cdf).astype(bf16)
        slope = cdf + pre * jnp.exp(-0.5 * pre * pre) * DENSITY_FACTOR
        pre_ref[:, span] = slope.astype(bf16)

    stores[1].start()
    pltpu.make_async_copy(fc2_v, fc2_v, sem_two).wait()
    for i in range(2):
        cols = slice(i * half, (i + 1) * half)
        total = middle_v[:, cols] + (dot_nn(hidden_ref[...], fc2_v[:, cols]) + vector_ref[5:6, cols])
        out_ref[:, lanes_of(i)] = total.astype(bf16)
        differ = total - target_ref[:, lanes_of(i)].astype(f32)
        weighted = valid_ref[...] * differ
        sums_ref[0:1, cols] = jnp.sum(weighted * differ, axis=0, keepdims=True)
        grad = factor_ref[0] * weighted
        grad_mid_ref[:, cols] = grad
        low = grad.astype(bf16)
        grad_low_ref[:, cols] = low
        sums_ref[1:2, cols] = jnp.sum(low.astype(f32), axis=0, keepdims=True)

    stores[2].start()
    stores[3].start()

    @pl.loop(0, chunks)
    def _(k):
        span = pl.ds(pl.multiple_of(k * FF_CHUNK, FF_CHUNK), FF_CHUNK)
        back = dot_nt(grad_low_ref[...], fc2_v[span, :])
        back = (back * pre_ref[:, span].astype(f32)).astype(bf16)
        pre_ref[:, span] = back
        hidden_sum_ref[0:1, span] = jnp.sum(back.astype(f32), axis=0, keepdims=True)

    stores[4].start()
    for i in range(2):
        cols = slice(i * half, (i + 1) * half)
        back_v[:, cols] = dot_nt(pre_ref[...], fc1_v[cols, :])

    @functools.partial(rows_of, total_rows)
    def _(rows):
        normal, spread = unit_rows(middle_v[rows, :])
        upstream = back_v[rows, :]
        inner = upstream * vector_ref[3:4, :]
        center = jnp.mean(inner, axis=-1, keepdims=True)
        slope = jnp.mean(inner * normal, axis=-1, keepdims=True)
        grad = grad_mid_ref[rows, :] + spread * (inner - center - normal * slope)
        grad_mid_ref[rows, :] = grad
        low = grad.astype(bf16)
        mid_low_ref[rows, :] = low
        sums_ref[2:3, :] += jnp.sum(upstream * normal, axis=0, keepdims=True)
        sums_ref[3:4, :] += jnp.sum(upstream, axis=0, keepdims=True)
        sums_ref[4:5, :] += jnp.sum(low.astype(f32), axis=0, keepdims=True)

    for j, (ref, at) in enumerate(((up_own_ref, 0), (up_give_ref, 0), (up_own_ref, 1), (up_give_ref, 1))):
        grad = dot_nt(mid_low_ref[...], proj_v[j * heads : (j + 1) * heads, :])
        ref[:, at * heads : (at + 1) * heads] = grad.astype(bf16)
    for store in stores:
        store.wait()


def middle_block(table, factor, inputs, target, valid, vectors, smalls, pieces):
    rows, width = inputs.shape
    hidden = 4 * pieces[0].shape[1]
    vmem = pl.BlockSpec(memory_space=pltpu.VMEM)
    smem = pl.BlockSpec(memory_space=pltpu.SMEM)
    anywhere = pl.BlockSpec(memory_space=pl.ANY)
    f32, bf16 = jnp.float32, jnp.bfloat16

    def result(columns, dtype):
        return jax.ShapeDtypeStruct((rows, columns), dtype)

    return pl.pallas_call(
        middle_kernel,
        out_shape=(
            result(width, bf16),
            result(width, bf16),
            result(hidden, bf16),
            result(hidden, bf16),
            result(width, bf16),
            result(width, bf16),
            result(width, bf16),
            result(width, f32),
            result(width // 2, bf16),
            result(width // 2, bf16),
            jax.ShapeDtypeStruct((1, hidden), f32),
            jax.ShapeDtypeStruct((8, width), f32),
        ),
        in_specs=[smem] * 2 + [vmem] * 5 + [anywhere] * len(pieces),
        out_specs=[anywhere] * 6 + [vmem] * 6,
        scratch_shapes=[
            pltpu.VMEM((width, hidden), bf16),
            pltpu.VMEM((hidden, width), bf16),
            pltpu.VMEM((width, width), bf16),
            pltpu.VMEM((rows, width), f32),
            pltpu.VMEM((rows, width), f32),
            pltpu.VMEM((rows, width), bf16),
            pltpu.VMEM((rows, hidden), bf16),
            pltpu.VMEM((rows, hidden), bf16),
            pltpu.VMEM((rows, width), bf16),
            pltpu.VMEM((rows, width), bf16),
            pltpu.VMEM((rows, width), bf16),
            pltpu.SemaphoreType.DMA((hidden // FF_CHUNK,)),
            pltpu.SemaphoreType.DMA,
            pltpu.SemaphoreType.DMA,
            pltpu.SemaphoreType.DMA,
            pltpu.SemaphoreType.DMA((6,)),
        ],
        compiler_params=pltpu.CompilerParams(vmem_limit_bytes=62 << 20),
        cost_estimate=pl.CostEstimate(
            flops=2 * rows * width * hidden, bytes_accessed=44 << 20, transcendentals=0
        ),
        name="middle_block",
    )(table, factor, inputs, target, valid, vectors, smalls, *pieces)


def swap(values, axis, mask, size):
    return lax.ppermute(values, axis, [(i, i ^ mask) for i in range(size)])


def over_row(values):
    return swap(values, "row", 1, 2)


def over_dp(values, mask):
    return swap(values, "dp", mask, 4)


def over_col(values, mask):
    return swap(values, "col", mask, 4)


def cut(values, index, size, axis=0):
    return lax.dynamic_slice_in_dim(values, index * size, size, axis)


def place(pieces, index_of, axis):
    size = pieces[0].shape[axis]
    shape = list(pieces[0].shape)
    shape[axis] = size * len(pieces)
    whole = jnp.zeros(shape, pieces[0].dtype)
    for s, piece in enumerate(pieces):
        whole = lax.dynamic_update_slice_in_dim(whole, piece, index_of(s) * size, axis)
    return whole


def copies(listed, sem_ref):
    for index, (source, target) in enumerate(listed):
        pltpu.make_async_copy(source, target, sem_ref.at[index]).start()
    for index, (source, target) in enumerate(listed):
        pltpu.make_async_copy(source, target, sem_ref.at[index]).wait()


def slab_kernel(places_ref, fc1_ref, fc2_ref, proj_ref, qkv_ref, small_ref, out_ref, sem_ref):
    half, sub = fc1_ref.shape[0], fc1_ref.shape[1] // 4
    part, deep = proj_ref.shape[0] // 4, half // 4
    mine = places_ref[0]
    fc2 = fc2_ref.at[pl.ds(pl.multiple_of(mine * sub, sub), sub)]
    proj = proj_ref.at[pl.ds(pl.multiple_of(mine * part, part), part)]
    listed = [(fc1_ref.at[:, pl.ds(pl.multiple_of(mine * sub, sub), sub)], half)]
    listed += [(fc2.at[:, i * sub : (i + 1) * sub], sub) for i in range(2)]
    listed += [(proj.at[:, i * sub : (i + 1) * sub], part) for i in range(2)]
    listed += [(small_ref, small_ref.shape[0])]
    rows = pl.ds(pl.multiple_of(mine * deep, deep), deep)
    listed += [(qkv_ref.at[k, rows], deep) for k in range(3)]
    pairs, at = [], 0
    for source, count in listed:
        pairs.append((source, out_ref.at[at : at + count]))
        at += count
    copies(pairs, sem_ref)


def make_slab(places, fc1, fc2, proj, qkv, small):
    half, sub = fc1.shape[0], fc1.shape[1] // 4
    rows = half + 2 * sub + proj.shape[0] // 2 + small.shape[0] + 3 * (half // 4)
    anywhere = pl.BlockSpec(memory_space=pl.ANY)
    return pl.pallas_call(
        slab_kernel,
        out_shape=jax.ShapeDtypeStruct((rows, sub), fc1.dtype),
        in_specs=[pl.BlockSpec(memory_space=pltpu.SMEM)] + [anywhere] * 5,
        out_specs=pl.BlockSpec(memory_space=pltpu.VMEM),
        scratch_shapes=[pltpu.SemaphoreType.DMA((9,))],
        cost_estimate=small_cost(100000000),
        name="make_slab",
    )(places, fc1, fc2, proj, qkv, small)


def far_qkv_kernel(base, places_ref, mine_ref, theirs_ref, out_ref, sem_ref):
    sub = mine_ref.shape[1]
    half = out_ref.shape[0] // 2
    deep, step = half // 4, mine_ref.shape[0] // 4
    pairs = []
    for side, ref in enumerate((mine_ref, theirs_ref)):
        for s in range(4):
            rows = pl.ds(pl.multiple_of(side * half + places_ref[s] * deep, deep), deep)
            for k in range(3):
                at = s * step + base + k * deep
                pairs.append((ref.at[at : at + deep], out_ref.at[rows, k * sub : (k + 1) * sub]))
    copies(pairs, sem_ref)


def far_qkv(places, mine, theirs, base, width):
    anywhere = pl.BlockSpec(memory_space=pl.ANY)
    return pl.pallas_call(
        functools.partial(far_qkv_kernel, base),
        out_shape=jax.ShapeDtypeStruct((width, 3 * mine.shape[1]), mine.dtype),
        in_specs=[pl.BlockSpec(memory_space=pltpu.SMEM)] + [anywhere] * 2,
        out_specs=pl.BlockSpec(memory_space=pltpu.VMEM),
        scratch_shapes=[pltpu.SemaphoreType.DMA((24,))],
        cost_estimate=small_cost(100000000),
        name="far_qkv",
    )(places, mine, theirs)


VECTORS = 32


def put_split(ref, at, values):
    high = values.astype(jnp.bfloat16)
    low = (values - high.astype(jnp.float32)).astype(jnp.bfloat16)
    columns = values.shape[1]
    ref[at : at + VECTORS, 0:columns] = high
    ref[at + VECTORS : at + 2 * VECTORS, 0:columns] = low
    rest = ref.shape[1] - columns
    if rest:
        ref[at : at + 2 * VECTORS, columns:] = jnp.zeros((2 * VECTORS, rest), jnp.bfloat16)


def get_split(ref, at, columns):
    high = ref[at : at + VECTORS, 0:columns].astype(jnp.float32)
    return high + ref[at + VECTORS : at + 2 * VECTORS, 0:columns].astype(jnp.float32)


def framed(ref, rows, flip, half):
    return jnp.concatenate(
        [ref[rows, pl.ds(pl.multiple_of((flip ^ i) * half, half), half)] for i in range(2)], axis=1
    ).astype(jnp.float32)


def token_back_kernel(
    flip_ref, near_ref, far_ref, w_near, w_far, own_states, other_states, own_ref, give_ref, sums_ref, other_v
):
    rows_all, half = own_ref.shape[0], own_ref.shape[1] // 2
    sums_ref[...] = jnp.zeros_like(sums_ref)
    for start, out_ref in ((rows_all, other_v), (0, own_ref)):
        rows = slice(start, start + rows_all)
        out_ref[...] = dot_nt(near_ref[rows, :], w_near[...]) + dot_nt(far_ref[rows, :], w_far[...])
    for out_ref, states in ((other_v, other_states), (own_ref, own_states)):

        @functools.partial(rows_of, rows_all)
        def _(rows, out_ref=out_ref, states=states):
            normal, _ = unit_rows(framed(states, rows, flip_ref[0], half))
            upstream = out_ref[rows, :]
            sums_ref[0:1, :] += jnp.sum(upstream * normal, axis=0, keepdims=True)
            sums_ref[1:2, :] += jnp.sum(upstream, axis=0, keepdims=True)
            if out_ref is other_v:
                give_ref[rows, :] = upstream.astype(jnp.bfloat16)


def token_back(flip, near, far, w_near, w_far, own_states, other_states):
    rows, width = own_states.shape
    vmem = pl.BlockSpec(memory_space=pltpu.VMEM)
    return pl.pallas_call(
        token_back_kernel,
        out_shape=(
            jax.ShapeDtypeStruct((rows, width), jnp.float32),
            jax.ShapeDtypeStruct((rows, width), jnp.bfloat16),
            jax.ShapeDtypeStruct((2, width), jnp.float32),
        ),
        in_specs=[pl.BlockSpec(memory_space=pltpu.SMEM)] + [vmem] * 6,
        out_specs=(vmem,) * 3,
        scratch_shapes=[pltpu.VMEM((rows, width), jnp.float32)],
        compiler_params=pltpu.CompilerParams(vmem_limit_bytes=40 << 20),
        cost_estimate=small_cost(100000000),
        name="token_back",
    )(flip, near, far, w_near, w_far, own_states, other_states)


def last_kernel(flip_ref, own_ref, taken_ref, states_ref, mid_ref, vector_ref, out_ref):
    half = own_ref.shape[1] // 2
    upstream = own_ref[...] + taken_ref[...].astype(jnp.float32)
    everything = slice(0, own_ref.shape[0])
    normal, spread = unit_rows(framed(states_ref, everything, flip_ref[0], half))
    inner = upstream * vector_ref[0:1, :]
    center = jnp.mean(inner, axis=-1, keepdims=True)
    slope = jnp.mean(inner * normal, axis=-1, keepdims=True)
    back = mid_ref[...] + spread * (inner - center - normal * slope)
    for i in range(2):
        lanes = pl.ds(pl.multiple_of((flip_ref[0] ^ i) * half, half), half)
        out_ref[:, lanes] = back[:, i * half : (i + 1) * half].astype(jnp.bfloat16)


def last_norm(flip, own, taken, states, mid, vectors):
    rows, width = own.shape
    block = pl.BlockSpec((ROWS, width), lambda i: (i, 0))
    whole = pl.BlockSpec(vectors.shape, lambda i: (0, 0))
    return pl.pallas_call(
        last_kernel,
        grid=(rows // ROWS,),
        out_shape=jax.ShapeDtypeStruct((rows, width), jnp.bfloat16),
        in_specs=[pl.BlockSpec(memory_space=pltpu.SMEM)] + [block] * 4 + [whole],
        out_specs=block,
        cost_estimate=small_cost(500000000),
        name="last_norm",
    )(flip, own, taken, states, mid, vectors)


def far_grads_kernel(
    turned_ref, grad_ref, sums_ref, hidden_ref, near_ref, far_ref, keep_ref, out_ref, kept_ref
):
    half = keep_ref.shape[1]
    width = near_ref.shape[1] // 3
    shared = [hidden_ref[0:1, i * half : (i + 1) * half] for i in range(8)]
    for ref in (near_ref, far_ref):
        shared.append(jnp.concatenate([ref[0:1, 0:width], ref[0:1, 2 * width :]], axis=1))
    shared.append(sums_ref[0:1, 0:half] + sums_ref[0:1, half:])
    blank = jnp.zeros((VECTORS - 6 - len(shared), half), jnp.float32)

    def rows(lanes):
        split = [sums_ref[i : i + 1, lanes] for i in (2, 3, 4, 1)]
        split += [jnp.zeros((2, half), jnp.float32)]
        return jnp.concatenate(split + shared + [blank], axis=0)

    keep_ref[...] = rows(slice(0, half))
    put_split(out_ref, half, rows(slice(half, 2 * half)))
    out_ref[0:half, :] = dot_nn(turned_ref[half:, :], grad_ref[...]).astype(jnp.bfloat16)
    kept_ref[...] = dot_nn(turned_ref[0:half, :], grad_ref[...])


def after_row_kernel(
    places_ref,
    kept_ref,
    taken_ref,
    keep_ref,
    norm_ref,
    near_ref,
    near_taken,
    near_own_ref,
    far_own_ref,
    sum_ref,
    *outs,
):
    deep = far_own_ref.shape[0]
    half = keep_ref.shape[1]
    vectors = keep_ref[...] + get_split(taken_ref, 4 * deep, half)
    vectors = jnp.concatenate(
        [vectors[0:4], norm_ref[:, 0:half], vectors[6:17], norm_ref[:, half:], vectors[19:]], axis=0
    )
    sum_ref[...] = vectors
    for s in range(4):
        rows = pl.ds(pl.multiple_of(places_ref[s] * deep, deep), deep)
        far = kept_ref[rows, :] + taken_ref[rows, :].astype(jnp.float32)
        if s == 0:
            far_own_ref[...] = far
        else:
            outs[s - 1][0:deep, :] = far.astype(jnp.bfloat16)
            put_split(outs[s - 1], deep, vectors)
        if s % 2 == 0:
            at = slice(s // 2 * deep, (s // 2 + 1) * deep)
            near = near_ref[rows, :].astype(jnp.float32) + near_taken[at, :].astype(jnp.float32)
            if s == 0:
                near_own_ref[...] = near
            else:
                outs[s - 1][deep + 2 * VECTORS :, :] = near.astype(jnp.bfloat16)


def after_plane_kernel(near_ref, far_ref, sum_ref, *refs):
    takes, (keep_ref, vector_ref, give_ref, small_ref) = refs[:3], refs[3:]
    deep = far_ref.shape[0]
    vectors, far = sum_ref[...], far_ref[...]
    keep_ref[...] = near_ref[...] + takes[1][deep + 2 * VECTORS :, :].astype(jnp.float32)
    for take in takes:
        vectors = vectors + get_split(take, deep, vectors.shape[1])
        far = far + take[0:deep, :].astype(jnp.float32)
    vector_ref[...] = vectors
    give_ref[0:deep, :] = far.astype(jnp.bfloat16)
    put_split(give_ref, deep, vectors)
    put_split(small_ref, 0, vectors)


def after_cols_kernel(keep_ref, vector_ref, one_ref, two_ref, three_ref, out_ref, total_ref):
    deep = keep_ref.shape[0]
    out_ref[...] = (keep_ref[...] + two_ref[0:deep, :].astype(jnp.float32)).astype(jnp.bfloat16)
    columns = vector_ref.shape[1]
    far = get_split(two_ref, deep, columns)
    total = vector_ref[...] + far
    total = total + get_split(one_ref, 0, columns) + get_split(three_ref, 0, columns)
    total_ref[...] = total
    total_ref[14:15, :] = vector_ref[14:15, :] + far[15:16, :]


def on_chip(kernel, shapes, name, *args, tables=0):
    vmem = pl.BlockSpec(memory_space=pltpu.VMEM)
    return pl.pallas_call(
        kernel,
        out_shape=tuple(jax.ShapeDtypeStruct(*s) for s in shapes),
        in_specs=[pl.BlockSpec(memory_space=pltpu.SMEM)] * tables + [vmem] * (len(args) - tables),
        out_specs=(vmem,) * len(shapes),
        cost_estimate=small_cost(100000000),
        name=name,
    )(*args)


def wide_kernel(with_proj, places_ref, small_ref, big_ref, taken_ref, *refs):
    if with_proj:
        proj_kept, proj_taken, *refs = refs
    *outs, turned_v = refs
    half, sub = turned_v.shape[0], turned_v.shape[0] // 2
    span = big_ref.shape[1] // 4
    part = 256 // 4 if not with_proj else proj_kept.shape[0] // 16
    turned_v[...] = small_ref[:, 0:half].T
    for s in range(4):
        lanes = pl.ds(pl.multiple_of(places_ref[s] * span, span), span)
        block = dot_nn(turned_v[...], big_ref[:, lanes]) + taken_ref[:, lanes].astype(jnp.float32)
        block = block.astype(jnp.bfloat16)
        for side, (go, slot) in enumerate(((s % 2, s // 2), (s // 2, s % 2))):
            out = outs[2 * side + go]
            rows = slice(slot * sub, (slot + 1) * sub)
            out[rows, 0:span] = block[side * sub : (side + 1) * sub]
            if with_proj:
                at = side * sub
                for j in range(4):
                    start = pl.multiple_of(4 * j * part + places_ref[s] * part, part)
                    piece = proj_kept[pl.ds(start, part), at : at + sub] + proj_taken[
                        pl.ds(start, part), at : at + sub
                    ].astype(jnp.float32)
                    low = slot * sub + j * part
                    out[low : low + part, span:] = piece.astype(jnp.bfloat16)


def wide_grads(places, small, big, taken, proj=()):
    half = small.shape[1] // 2
    columns = big.shape[1] // 4 + (half // 2 if proj else 0)
    vmem = pl.BlockSpec(memory_space=pltpu.VMEM)
    return pl.pallas_call(
        functools.partial(wide_kernel, bool(proj)),
        out_shape=(jax.ShapeDtypeStruct((half, columns), jnp.bfloat16),) * 4,
        in_specs=[pl.BlockSpec(memory_space=pltpu.SMEM)] + [vmem] * (3 + len(proj)),
        out_specs=(vmem,) * 4,
        scratch_shapes=[pltpu.VMEM((half, small.shape[0]), jnp.bfloat16)],
        compiler_params=pltpu.CompilerParams(vmem_limit_bytes=44 << 20),
        cost_estimate=small_cost(3000000000),
        name="wide_grads",
    )(places, small, big, taken, *proj)


def plane_sum_kernel(*refs):
    sub = refs[4].shape[0]
    for side in range(2):
        kept, taken = refs[2 * side : 2 * side + 2]
        for slot in range(2):
            rows = slice(slot * sub, (slot + 1) * sub)
            total = kept[rows, :].astype(jnp.float32) + taken[rows, :].astype(jnp.float32)
            refs[4 + 2 * side + slot][...] = total.astype(jnp.bfloat16)


def cols_out_kernel(places_ref, *refs):
    outs = refs[4:]
    sub = refs[0].shape[0]
    columns = refs[0].shape[1]
    part = (outs[0].shape[0] - 2 * sub) // 2
    for side in range(2):
        kept, taken = refs[2 * side : 2 * side + 2]
        for j in range(4):
            lanes = pl.ds(pl.multiple_of(places_ref[4 + j] * sub, sub), sub)
            total = kept[:, lanes].astype(jnp.float32) + taken[:, lanes].astype(jnp.float32)
            outs[j][side * sub : (side + 1) * sub, :] = total.astype(jnp.bfloat16)
            if part:
                rows = slice(j * part, (j + 1) * part)
                total = kept[rows, columns - sub :].astype(jnp.float32)
                total = total + taken[rows, columns - sub :].astype(jnp.float32)
                low = 2 * sub + side * part
                outs[j][low : low + part, :] = total.astype(jnp.bfloat16)


def mine_kernel(*refs):
    out_ref, at = refs[8], 0
    for group in (refs[0:4], refs[4:8]):
        total = group[0][...].astype(jnp.float32)
        for ref in group[1:]:
            total = total + ref[...].astype(jnp.float32)
        out_ref[at : at + total.shape[0], :] = total.astype(jnp.bfloat16)
        at += total.shape[0]


def finish_kernel(part_rows, places_ref, *refs):
    pieces, (fc2_ref, fc1_ref, proj_ref) = refs[:2], refs[2:]
    half, sub = fc1_ref.shape[0], pieces[0].shape[1]
    for s in range(4):
        piece, base = pieces[s // 2], (s % 2) * (pieces[0].shape[0] // 2)
        at = places_ref[s]
        rows = pl.ds(pl.multiple_of(at * sub, sub), sub)
        fc2_ref[rows, :] = piece[base : base + half, :].astype(jnp.float32).T
        fc1_ref[:, rows] = piece[base + half : base + 2 * half, :].astype(jnp.float32)
        rows = pl.ds(pl.multiple_of(at * part_rows, part_rows), part_rows)
        for i in range(2):
            low = base + 2 * half + i * part_rows
            proj_ref[rows, i * sub : (i + 1) * sub] = piece[low : low + part_rows, :].astype(jnp.float32)


def finish_qkv_kernel(places_ref, *refs):
    out_ref = refs[4]
    deep, width = refs[0].shape[0], out_ref.shape[2]
    for s in range(4):
        rows = pl.ds(pl.multiple_of(places_ref[s] * deep, deep), deep)
        for k in range(3):
            out_ref[k, rows, :] = refs[s][:, k * width : (k + 1) * width].astype(jnp.float32)


def finish(places, pieces, part_rows):
    rows, sub = pieces[0].shape
    half = (rows // 2 - 2 * part_rows) // 2
    vmem = pl.BlockSpec(memory_space=pltpu.VMEM)
    return pl.pallas_call(
        functools.partial(finish_kernel, part_rows),
        out_shape=(
            jax.ShapeDtypeStruct((4 * sub, half), jnp.float32),
            jax.ShapeDtypeStruct((half, 4 * sub), jnp.float32),
            jax.ShapeDtypeStruct((4 * part_rows, half), jnp.float32),
        ),
        in_specs=[pl.BlockSpec(memory_space=pltpu.SMEM)] + [vmem] * 2,
        out_specs=[vmem] * 3,
        cost_estimate=small_cost(100000000),
        name="finish",
    )(places, *pieces)


def finish_qkv(places, pieces):
    deep, width = pieces[0].shape
    vmem = pl.BlockSpec(memory_space=pltpu.VMEM)
    return pl.pallas_call(
        finish_qkv_kernel,
        out_shape=jax.ShapeDtypeStruct((3, 4 * deep, width // 3), jnp.float32),
        in_specs=[pl.BlockSpec(memory_space=pltpu.SMEM)] + [vmem] * 4,
        out_specs=vmem,
        cost_estimate=small_cost(100000000),
        name="finish_qkv",
    )(places, *pieces)


def tie(value, *others):
    return lax.optimization_barrier((value, *others))[0]


def add_up(own, taken):
    total = own.astype(jnp.float32)
    for piece in taken:
        total = total + piece.astype(jnp.float32)
    return total


def local_paired(
    states,
    ln1_gain,
    ln1_bias,
    w_qkv,
    q_bias,
    v_bias,
    w_proj,
    proj_bias,
    ln2_gain,
    ln2_bias,
    w_fc1,
    fc1_bias,
    w_fc2,
    fc2_bias,
    teacher,
    loss_mask,
    lengths,
):
    f32, bf16 = jnp.float32, jnp.bfloat16
    dp = lax.axis_index("dp")
    row = lax.axis_index("row")
    col = lax.axis_index("col")
    local_rows, width = states.shape
    half = width // 2
    head_width = w_qkv.shape[2]
    hidden_width = w_fc1.shape[1]
    sub = hidden_width // 4
    span = 4 * sub
    part_rows = head_width // 4
    clip = (dp * 2 + row) * 2 + col // 2
    second = col % 2

    def quarter(s):
        return dp ^ s

    def frame(values):
        return jnp.where(
            row == 0, values, jnp.concatenate([values[:, half:], values[:, :half]], axis=1)
        )

    places = jnp.stack([dp ^ s for s in range(4)] + [col ^ j for j in range(4)]).astype(jnp.int32)
    flip = row.reshape(1).astype(jnp.int32)
    states_other = over_col(states, 1)
    small = jnp.concatenate(
        [
            fc1_bias.reshape(4, sub),
            q_bias.reshape(1, sub),
            v_bias.reshape(1, sub),
            jnp.zeros((10, sub), bf16),
        ],
        axis=0,
    )
    slab = make_slab(places, w_fc1, w_fc2, w_proj, w_qkv.transpose(1, 0, 2), small)
    unit_rows_total = half + 2 * sub + 2 * part_rows + small.shape[0]
    small_at = unit_rows_total - small.shape[0]
    two = over_col(slab, 2)
    w_qkv2 = w_qkv.reshape(half, 3 * head_width)
    w_qkv2 = tie(w_qkv2, slab)
    qkv_near = jnp.concatenate([w_qkv2, over_row(w_qkv2)], axis=0)
    vectors = jnp.stack([ln1_gain, ln1_bias, proj_bias, ln2_gain, ln2_bias, fc2_bias])
    vectors, states, teacher, loss_mask = lax.optimization_barrier(
        (vectors, states, teacher, loss_mask, slab)
    )[:4]
    vectors = jnp.concatenate([vectors, over_row(vectors)], axis=1).astype(f32)
    fc1_other, fc2_other, proj_other = over_row(w_fc1), over_row(w_fc2), over_row(w_proj)
    two = tie(two, fc1_other, fc2_other, proj_other)
    two_x, two_y = over_dp(two, 1), over_dp(two, 2)
    states_other = tie(states_other, two)

    all_clips = lengths.shape[0]
    valid_all = (
        loss_mask.reshape(all_clips, L) * (jnp.arange(L)[None, :] < lengths[:, None])
    ).astype(f32)
    valid_total = jnp.maximum(jnp.sum(valid_all), 1.0)
    first_row = ((dp * 2 + row) * 4 + col) * local_rows
    valid = lax.dynamic_slice_in_dim(valid_all.reshape(all_clips * L), first_row, local_rows)
    my_length = lax.dynamic_slice_in_dim(lengths, clip, 1)
    spot = jnp.arange(L)
    position = jnp.where(
        spot < local_rows, second * local_rows + spot, (1 - second) * local_rows + spot - local_rows
    )
    key_bias = jnp.where(position < my_length, 0.0, MASKED).astype(f32)
    key_bias = jnp.broadcast_to(key_bias[:, None], (L, 128))

    gain_one, shift_one = vectors[0], vectors[1]
    norm_one, _, _ = normalize(frame(states).astype(f32), gain_one, shift_one)
    norm_other, _, _ = normalize(frame(states_other).astype(f32), gain_one, shift_one)
    tokens_one = jnp.concatenate([norm_one.astype(bf16), norm_other.astype(bf16)], axis=0)

    zero_bias = jnp.zeros((head_width,), f32)
    score_scale = HD**-0.5
    scale = jnp.where(jnp.arange(3 * head_width) < head_width, score_scale, 1.0).astype(bf16)
    split = local_rows // QT * QT
    later = L - split
    over = local_rows - split

    def project(matrix, q_add, v_add):
        projected = jnp.dot(tokens_one, matrix, preferred_element_type=f32)
        add = jnp.concatenate([q_add.astype(f32), zero_bias, v_add.astype(f32)])
        return (projected + add[None]).astype(bf16) * scale[None]

    table = jnp.stack(
        [(dp ^ s) * 4 + (col ^ j) for s in range(4) for j in range(4)]
        + [a * 4 + col for a in range(4)]
        + [dp ^ s for s in range(4)]
        + [col ^ b for b in range(4)]
        + [row]
    ).astype(jnp.int32)
    loss_scale = all_clips * L * width / 2.0
    factor = (loss_scale * 2.0 / (valid_total * width)).reshape(1)
    valid = valid[:, None]
    packed_near = tie(project(qkv_near, q_bias, v_bias), table, factor, valid)
    cut_at = two.shape[0] // 32 * 16
    two_x, two_y = tie(two_x, packed_near), tie(two_y, packed_near)
    two_low, two_high = over_dp(two_y[:cut_at], 1), over_dp(two_x[cut_at:], 2)
    one_give = jnp.concatenate([slab[:unit_rows_total], two[:unit_rows_total]], axis=0)
    one = over_col(tie(one_give, states_other), 1)
    near_late, near_late_lse = attend(tie(packed_near, two_x, two_y, one), key_bias, split, later)
    two_low, two_high = tie(two_low, near_late), tie(two_high, near_late)
    two_all = jnp.concatenate([two, two_x, two_y, two_low, two_high], axis=0)
    two_theirs = over_row(two_all)
    near_other = over_col(near_late[over:], 1)
    one_x, one_y = over_dp(one, 1), over_dp(one, 2)
    one_other = over_row(tie(one, near_late))
    near_soon, near_soon_lse = attend(
        tie(packed_near, two_all, near_late, one), key_bias, 0, split
    )
    two_theirs = tie(two_theirs, near_soon)
    qkv_far = far_qkv(places, two_all, two_theirs, unit_rows_total, width)
    far_small = two_all[small_at : small_at + small.shape[0]]
    packed_far = project(qkv_far, far_small[4], far_small[5])
    packed_far = tie(packed_far, one, near_other)
    far_late, far_late_lse = attend(packed_far, key_bias, split, later)
    far_other = over_col(far_late[over:], 1)
    one_x, one_y = tie(one_x, far_late), tie(one_y, far_late)
    cut_at = one.shape[0] // 2
    one_low, one_high = over_dp(one_y[:cut_at], 1), over_dp(one_x[cut_at:], 2)
    one_theirs = [over_row(one_x), over_row(one_y)]
    far_soon, far_soon_lse = attend(
        tie(packed_far, one_x, one_y, far_late, one_other), key_bias, 0, split
    )
    one_low, one_high = tie(one_low, far_soon, far_other), tie(one_high, far_soon, far_other)
    one_mine = [one, one_x, one_y, one_low, one_high]
    one_theirs = [one_other, *one_theirs, over_row(one_low), over_row(one_high)]
    turned = tie(tokens_one, far_late).T
    at = unit_rows_total + small_at
    smalls = jnp.stack(
        [small, one[small_at : small_at + 16], two_all[small_at : small_at + 16], one[at : at + 16]]
    ).astype(f32)
    (
        attended_rows,
        outputs,
        hidden,
        grad_pre,
        norm_two,
        grad_low,
        mid_low,
        grad_mid,
        up_own,
        up_give,
        hidden_sum,
        sums,
    ) = middle_block(
        table,
        factor,
        states,
        teacher,
        valid,
        vectors,
        smalls,
        (
            w_fc1,
            fc1_other,
            w_fc2,
            fc2_other,
            w_proj,
            proj_other,
            two_all,
            two_theirs,
            *one_mine,
            *one_theirs,
            near_soon,
            near_late,
            near_other,
            far_soon,
            far_late,
            far_other,
        ),
    )
    up_far = over_col(up_give, 1)

    def joined(kept, taken):
        return (kept.astype(f32) + taken.astype(f32)).astype(bf16)

    give_fc2 = over_row(dot_tn(grad_low[:, half:], hidden).astype(bf16))
    give_fc1 = over_row(dot_tn(norm_two[:, half:], grad_pre).astype(bf16))
    give_proj = over_row(dot_tn(attended_rows, mid_low[:, half:]).astype(bf16))
    kept_proj = dot_tn(attended_rows, mid_low[:, :half])

    def plane_first(wide):
        keep_x, give_x, keep_y, give_y = wide
        return (keep_x, keep_y), (give_x, give_y), (over_dp(give_x, 1), over_dp(give_y, 2))

    def plane_second(keep, taken):
        shape = ((keep[0].shape[0] // 2, keep[0].shape[1]), bf16)
        keep_x, give_x, keep_y, give_y = on_chip(
            plane_sum_kernel, [shape] * 4, "plane_sum", keep[0], taken[0], keep[1], taken[1]
        )
        return (keep_x, keep_y), (give_x, give_y), (over_dp(give_x, 2), over_dp(give_y, 1))

    def cols_out(keep, taken, rows):
        blocks = on_chip(
            cols_out_kernel,
            [((rows, sub), bf16)] * 4,
            "cols_out",
            *(places, keep[0], taken[0], keep[1], taken[1]),
            tables=1,
        )
        return blocks, [over_col(blocks[j], j) for j in (1, 2, 3)]

    def all_tied(values, *others):
        return [tie(v, *others) for v in values]

    wide = wide_grads(places, grad_low, hidden, give_fc2)
    fc2_keep, fc2_give, fc2_taken = plane_first(wide)
    wide = wide_grads(
        places, tie(norm_two, *fc2_give), grad_pre, give_fc1, (kept_proj, give_proj)
    )
    fc1_keep, fc1_give, fc1_taken = plane_first(wide)

    packed_near = tie(packed_near, *fc2_give, *fc1_give)
    part_near = attend_back(packed_near, key_bias, near_soon_lse, near_soon, up_own, None, 0, 0)
    fc2_keep, fc2_give, fc2_taken = plane_second(fc2_keep, all_tied(fc2_taken, part_near[0]))

    packed_far = tie(packed_far, *fc2_give, part_near[0])
    part_far = attend_back(
        packed_far, key_bias, far_soon_lse, far_soon, up_own, None, head_width, 0
    )
    fc2_blocks, fc2_cols = cols_out(fc2_keep, all_tied(fc2_taken, part_far[0]), 2 * sub)
    fc1_keep, fc1_give, fc1_taken = plane_second(fc1_keep, all_tied(fc1_taken, part_far[0]))

    packed_near = tie(packed_near, *fc2_blocks, *fc1_give)
    grad_near, near_sums = attend_back(
        packed_near, key_bias, near_late_lse, near_late, up_own, up_far, 0, split, part_near
    )
    fc2_cols = all_tied(fc2_cols, grad_near)
    fc1_blocks, fc1_cols = cols_out(
        fc1_keep, all_tied(fc1_taken, grad_near, *fc2_cols), 2 * sub + 2 * part_rows
    )
    near_tied = tie(grad_near, *fc1_blocks)
    near_row = over_row(dot_tn(tokens_one[:, half:], near_tied).astype(bf16))
    wide_near = joined(dot_tn(tokens_one[:, :half], near_tied), near_row)
    deep = half // 4
    near_give = jnp.concatenate([cut(wide_near, quarter(s), deep) for s in (1, 3)], axis=0)
    near_taken = over_dp(near_give, 1)

    packed_far = tie(packed_far, near_give, *fc1_blocks, *fc2_cols)
    grad_far, far_sums = attend_back(
        packed_far, key_bias, far_late_lse, far_late, up_own, up_far, head_width, split, part_far
    )

    columns, slots = grad_far.shape[1], 2 * VECTORS
    vec_keep, row_give, kept = on_chip(
        far_grads_kernel,
        [((VECTORS, half), f32), ((half + slots, columns), bf16), ((half, columns), f32)],
        "far_grads",
        *(turned, tie(grad_far, near_taken, *fc1_cols), sums, hidden_sum, near_sums, far_sums),
    )
    row_taken = over_row(row_give)
    mine_rows = fc2_blocks[0].shape[0] + fc1_blocks[0].shape[0]
    (mine,) = on_chip(
        mine_kernel,
        [((mine_rows, sub), bf16)],
        "mine",
        *(fc2_blocks[0], *fc2_cols, fc1_blocks[0], *all_tied(fc1_cols, row_give)),
    )
    mine_x = over_dp(mine, 1)
    norm_own, norm_give, norm_sums = token_back(
        flip, grad_near, tie(grad_far, mine), qkv_near, qkv_far, states, states_other
    )
    norm_give = tie(norm_give, row_taken, mine_x)
    norm_taken = over_col(norm_give, 1)
    near_own, far_own, vec_sum, *plane_give = on_chip(
        after_row_kernel,
        [((deep, columns), f32)] * 2
        + [((VECTORS, half), f32)]
        + [((deep + slots + (deep if s == 2 else 0), columns), bf16) for s in (1, 2, 3)],
        "after_row",
        *(places, kept, tie(row_taken, norm_give), vec_keep, norm_sums, wide_near, near_taken),
        tables=1,
    )
    plane_taken = [over_dp(plane_give[s - 1], s) for s in (1, 2, 3)]
    mine_two = jnp.concatenate([mine, tie(mine_x, *plane_give)], axis=0)
    plane_taken = all_tied(plane_taken, mine_two)
    near_own, vec_sum, col_give, vec_give = on_chip(
        after_plane_kernel,
        [
            ((deep, columns), f32),
            ((VECTORS, half), f32),
            ((deep + slots, columns), bf16),
            ((slots, half), bf16),
        ],
        "after_plane",
        *(near_own, far_own, vec_sum, *plane_taken),
    )
    mine_y = over_dp(tie(mine_two, col_give), 2)
    col_taken = [over_col(vec_give, 1), over_col(col_give, 2), over_col(vec_give, 3)]
    qkv_mine, vec_total = on_chip(
        after_cols_kernel,
        [((deep, columns), bf16), ((VECTORS, half), f32)],
        "after_cols",
        *(near_own, vec_sum, *col_taken),
    )
    qkv_back = [over_dp(qkv_mine, s) for s in (1, 2, 3)]
    norm_total = vec_total[4:6] + over_row(vec_total[17:19])
    grad_states = last_norm(flip, norm_own, tie(norm_taken, qkv_mine), states, grad_mid, vectors)
    fc2_grad, fc1_grad, proj_grad = finish(places, [mine_two, tie(mine_y, grad_states)], part_rows)
    qkv_grad = finish_qkv(places, [qkv_mine, *all_tied(qkv_back, fc2_grad)]).transpose(1, 0, 2)

    fc1_bias_grad = lax.dynamic_index_in_dim(vec_total[6:14].reshape(4, 4, sub), col, 1, False)
    loss_value = jnp.sum(vec_total[16]) / (valid_total * width)
    return (
        outputs,
        loss_value,
        grad_states,
        norm_total[0],
        norm_total[1],
        qkv_grad,
        vec_total[14, :head_width],
        vec_total[14, head_width:],
        proj_grad,
        vec_total[2],
        vec_total[0],
        vec_total[1],
        fc1_grad,
        fc1_bias_grad.reshape(span),
        fc2_grad,
        vec_total[3],
    )


def solution(mesh):
    sizes = (mesh.shape["dp"], mesh.shape["row"], mesh.shape["col"])
    body = local_paired if sizes == PAIRED_MESH else local_general
    in_specs = (
        P(("dp", "row", "col"), None),
        P("row"),
        P("row"),
        P("row", None, "col"),
        P("col"),
        P("col"),
        P("col", "row"),
        P("row"),
        P("row"),
        P("row"),
        P("row", "col"),
        P("col"),
        P("col", "row"),
        P("row"),
        P(("dp", "row", "col"), None),
        P(),
        P(),
    )
    out_specs = (
        P(("dp", "row", "col"), None),
        P(),
        P(("dp", "row", "col"), None),
        P("row"),
        P("row"),
        P("row", None, "col"),
        P("col"),
        P("col"),
        P("col", "row"),
        P("row"),
        P("row"),
        P("row"),
        P("row", "col"),
        P("col"),
        P("col", "row"),
        P("row"),
    )
    return jax.shard_map(body, mesh=mesh, in_specs=in_specs, out_specs=out_specs, check_vma=False)
```

```python
import functools

import jax
import jax.numpy as jnp
from jax import lax
from jax.experimental import pallas as pl
from jax.experimental.pallas import tpu as pltpu
from jax.sharding import PartitionSpec as P

HD = 64
L = 1568


EPSILON = 1e-06
MASKED = -1e30
ROOT_HALF = 0.7071067811865476
DENSITY_FACTOR = 0.3989422804014327


def normalize(values, factor, offset):
    centered = values - jnp.mean(values, axis=-1, keepdims=True)
    spread = lax.rsqrt(jnp.mean(centered * centered, axis=-1, keepdims=True) + EPSILON)
    normal = centered * spread
    return (normal * factor + offset, normal, spread)


def norm_back(upstream, normal, spread, factor):
    inner = upstream * factor
    center_term = jnp.mean(inner, axis=-1, keepdims=True)
    slope_term = jnp.mean(inner * normal, axis=-1, keepdims=True)
    back = spread * (inner - center_term - normal * slope_term)
    return (back, jnp.sum(upstream * normal, axis=0), jnp.sum(upstream, axis=0))


def gelu_value(values):
    return values * (0.5 * (1.0 + lax.erf(values * ROOT_HALF)))


def gelu_slope(values):
    normal_cdf = 0.5 * (1.0 + lax.erf(values * ROOT_HALF))
    return normal_cdf + values * jnp.exp(-0.5 * values * values) * DENSITY_FACTOR


def masked_scores(queries, key_rows, length, score_scale):
    logits = (
        jnp.einsum("ihd,jhd->hij", queries, key_rows, preferred_element_type=jnp.float32)
        * score_scale
    )
    keep = jnp.arange(key_rows.shape[0]) < length
    return jnp.where(keep[None, None, :], logits, MASKED)


def attend_clip(packed, length, score_scale):
    half_span = packed.shape[0] // 2
    key_rows = packed[:, 1]
    value_rows = packed[:, 2]
    pieces = []
    totals = []
    for block_index in range(2):
        queries = packed[block_index * half_span : (block_index + 1) * half_span, 0]
        logits = masked_scores(queries, key_rows, length, score_scale)
        peak = jnp.max(logits, axis=-1, keepdims=True)
        total = peak + jnp.log(jnp.sum(jnp.exp(logits - peak), axis=-1, keepdims=True))
        weights = jnp.exp(logits - total).astype(jnp.bfloat16)
        pieces.append(
            jnp.einsum("hij,jhd->ihd", weights, value_rows, preferred_element_type=jnp.float32)
        )
        totals.append(total[..., 0])
    return (jnp.concatenate(pieces, 0), jnp.concatenate(totals, 1))


def attend_clip_back(packed, length, totals, upstream, score_scale):
    half_span = packed.shape[0] // 2
    key_rows = packed[:, 1]
    value_rows = packed[:, 2]
    grad_keys = jnp.zeros(key_rows.shape, jnp.float32)
    grad_values = jnp.zeros(value_rows.shape, jnp.float32)
    grad_queries = []
    for block_index in range(2):
        first = block_index * half_span
        queries = packed[first : first + half_span, 0]
        logits = masked_scores(queries, key_rows, length, score_scale)
        probs = jnp.exp(logits - totals[:, first : first + half_span][..., None])
        incoming = upstream[first : first + half_span]
        grad_values = grad_values + jnp.einsum(
            "hij,ihd->jhd", probs.astype(jnp.bfloat16), incoming, preferred_element_type=jnp.float32
        )
        grad_probs = jnp.einsum(
            "ihd,jhd->hij", incoming, value_rows, preferred_element_type=jnp.float32
        )
        grad_logits = (
            probs * (grad_probs - jnp.sum(probs * grad_probs, axis=-1, keepdims=True))
        ).astype(jnp.bfloat16)
        grad_queries.append(
            jnp.einsum("hij,jhd->ihd", grad_logits, key_rows, preferred_element_type=jnp.float32)
            * score_scale
        )
        grad_keys = (
            grad_keys
            + jnp.einsum("hij,ihd->jhd", grad_logits, queries, preferred_element_type=jnp.float32)
            * score_scale
        )
    return jnp.stack([jnp.concatenate(grad_queries, 0), grad_keys, grad_values], axis=1)


def local_general(
    states,
    ln1_gain,
    ln1_bias,
    w_qkv,
    q_bias,
    v_bias,
    w_proj,
    proj_bias,
    ln2_gain,
    ln2_bias,
    w_fc1,
    fc1_bias,
    w_fc2,
    fc2_bias,
    teacher,
    loss_mask,
    lengths,
):
    row_count = lax.axis_size("row")
    col_count = lax.axis_size("col")
    col_index = lax.axis_index("col")
    group_index = lax.axis_index("dp") * row_count + lax.axis_index("row")
    local_rows = states.shape[0]
    width = states.shape[1]
    group_rows = local_rows * col_count
    clip_count = group_rows // L
    head_width = w_qkv.shape[2]
    heads_here = head_width // HD
    hidden_width = w_fc1.shape[1]
    score_scale = HD ** (-0.5)
    vectors = jnp.stack([ln1_gain, ln1_bias, proj_bias, ln2_gain, ln2_bias, fc2_bias])
    qkv_full, proj_full, fc1_full, fc2_full, vector_full = (
        lax.all_gather(w_qkv, "row", axis=0, tiled=True),
        lax.all_gather(w_proj, "row", axis=1, tiled=True),
        lax.all_gather(w_fc1, "row", axis=0, tiled=True),
        lax.all_gather(w_fc2, "row", axis=1, tiled=True),
        lax.all_gather(vectors, "row", axis=1, tiled=True),
    )
    vector_full = vector_full.astype(jnp.float32)
    gain_one = vector_full[0]
    shift_one = vector_full[1]
    bias_proj = vector_full[2]
    gain_two = vector_full[3]
    shift_two = vector_full[4]
    bias_two = vector_full[5]
    all_clips = lengths.shape[0]
    valid_all = (
        loss_mask.reshape(all_clips, L) * (jnp.arange(L)[None, :] < lengths[:, None])
    ).astype(jnp.float32)
    valid_total = jnp.maximum(jnp.sum(valid_all), 1.0)
    first_row = (group_index * col_count + col_index) * local_rows
    valid = lax.dynamic_slice_in_dim(valid_all.reshape(all_clips * L), first_row, local_rows)
    my_lengths = lax.dynamic_slice_in_dim(lengths, group_index * clip_count, clip_count)
    inputs = states.astype(jnp.float32)
    norm_one, unit_one, spread_one = normalize(inputs, gain_one, shift_one)
    norm_one = norm_one.astype(jnp.bfloat16)
    tokens_one = lax.all_gather(norm_one, "col", axis=0, tiled=True)
    qkv_matrix = qkv_full.reshape(width, 3 * head_width)
    projected = jnp.dot(tokens_one, qkv_matrix, preferred_element_type=jnp.float32).reshape(
        group_rows, 3, head_width
    )
    bias_rows = jnp.stack(
        [
            q_bias.astype(jnp.float32),
            jnp.zeros((head_width,), jnp.float32),
            v_bias.astype(jnp.float32),
        ]
    )
    packed = (projected + bias_rows[None]).astype(jnp.bfloat16)
    clips_packed = packed.reshape(clip_count, L, 3, heads_here, HD)
    attended, totals = lax.map(
        lambda element: attend_clip(element[0], element[1], score_scale), (clips_packed, my_lengths)
    )
    attended = attended.reshape(group_rows, head_width).astype(jnp.bfloat16)
    proj_whole, qkv_whole = (
        lax.all_gather(proj_full, "col", axis=0, tiled=True),
        lax.all_gather(qkv_full, "col", axis=2, tiled=True),
    )
    attended_rows = lax.all_to_all(attended, "col", split_axis=0, concat_axis=1, tiled=True)
    middle = inputs + (
        jnp.dot(attended_rows, proj_whole, preferred_element_type=jnp.float32) + bias_proj
    )
    norm_two, unit_two, spread_two = normalize(middle, gain_two, shift_two)
    norm_two = norm_two.astype(jnp.bfloat16)
    fc1_whole, fc2_whole, fc1_bias_whole = (
        lax.all_gather(fc1_full, "col", axis=1, tiled=True),
        lax.all_gather(fc2_full, "col", axis=0, tiled=True),
        lax.all_gather(fc1_bias, "col", axis=0, tiled=True),
    )
    hidden_pre = jnp.dot(
        norm_two, fc1_whole, preferred_element_type=jnp.float32
    ) + fc1_bias_whole.astype(jnp.float32)
    hidden = gelu_value(hidden_pre).astype(jnp.bfloat16)
    outputs = middle + (jnp.dot(hidden, fc2_whole, preferred_element_type=jnp.float32) + bias_two)
    differ = outputs - teacher.astype(jnp.float32)
    numerator = jnp.sum(valid[:, None] * differ * differ)
    loss_scale = all_clips * L * width / 2.0
    grad_out = loss_scale * 2.0 / (valid_total * width) * valid[:, None] * differ
    grad_low = grad_out.astype(jnp.bfloat16)
    grad_hidden = jnp.dot(grad_low, fc2_whole.T, preferred_element_type=jnp.float32)
    grad_pre = (grad_hidden * gelu_slope(hidden_pre)).astype(jnp.bfloat16)
    wide_fc2 = jnp.dot(hidden.T, grad_low, preferred_element_type=jnp.float32)
    wide_fc1 = jnp.dot(norm_two.T, grad_pre, preferred_element_type=jnp.float32)
    fc1_grad_part, fc2_grad_part = (
        lax.psum_scatter(
            wide_fc1.astype(jnp.bfloat16), "col", scatter_dimension=1, tiled=True
        ).astype(jnp.float32),
        lax.psum_scatter(
            wide_fc2.astype(jnp.bfloat16), "col", scatter_dimension=0, tiled=True
        ).astype(jnp.float32),
    )
    fc1_bias_sum = jnp.sum(grad_pre, axis=0, dtype=jnp.float32)
    grad_norm_two = jnp.dot(grad_pre, fc1_whole.T, preferred_element_type=jnp.float32)
    back_two, gain_two_grad, shift_two_grad = norm_back(
        grad_norm_two, unit_two, spread_two, gain_two
    )
    grad_mid = grad_out + back_two
    mid_low = grad_mid.astype(jnp.bfloat16)
    wide_proj = jnp.dot(attended_rows.T, mid_low, preferred_element_type=jnp.float32)
    proj_grad_part = lax.psum_scatter(
        wide_proj.astype(jnp.bfloat16), "col", scatter_dimension=0, tiled=True
    )
    grad_attended_rows = jnp.dot(mid_low, proj_whole.T, preferred_element_type=jnp.float32).astype(
        jnp.bfloat16
    )
    grad_attended = lax.all_to_all(
        grad_attended_rows, "col", split_axis=1, concat_axis=0, tiled=True
    )
    grads_packed = lax.map(
        lambda element: attend_clip_back(
            element[0], element[1], element[2], element[3], score_scale
        ),
        (clips_packed, my_lengths, totals, grad_attended.reshape(clip_count, L, heads_here, HD)),
    )
    grads_packed = grads_packed.reshape(group_rows, 3 * head_width).astype(jnp.bfloat16)
    qkv_grad_part = jnp.dot(tokens_one.T, grads_packed, preferred_element_type=jnp.float32).reshape(
        width, 3, head_width
    )
    bias_sums = jnp.sum(grads_packed.reshape(group_rows, 3, head_width), axis=0, dtype=jnp.float32)
    grads_rows = lax.all_to_all(
        grads_packed.reshape(group_rows, 3, head_width),
        "col",
        split_axis=0,
        concat_axis=2,
        tiled=True,
    )
    grad_norm_one = jnp.dot(
        grads_rows.reshape(local_rows, 3 * width),
        qkv_whole.reshape(width, 3 * width).T,
        preferred_element_type=jnp.float32,
    )
    back_one, gain_one_grad, shift_one_grad = norm_back(
        grad_norm_one, unit_one, spread_one, gain_one
    )
    grad_states = (grad_mid + back_one).astype(jnp.bfloat16)
    proj_bias_grad = jnp.sum(mid_low, axis=0, dtype=jnp.float32)
    fc2_bias_grad = jnp.sum(grad_low, axis=0, dtype=jnp.float32)
    token_vectors = jnp.stack(
        [
            gain_one_grad,
            shift_one_grad,
            proj_bias_grad,
            gain_two_grad,
            shift_two_grad,
            fc2_bias_grad,
        ]
    )
    head_vectors = lax.dynamic_update_slice(
        jnp.zeros((2, width), jnp.float32),
        jnp.stack([bias_sums[0], bias_sums[2]]),
        (0, col_index * head_width),
    )
    token_sums, head_sums, fc1_sums, loss_sum = lax.psum(
        (token_vectors, head_vectors, fc1_bias_sum, numerator), ("dp", "row", "col")
    )
    qkv_rows, proj_cols, fc1_rows, fc2_cols = (
        lax.psum_scatter(
            qkv_grad_part.astype(jnp.bfloat16), "row", scatter_dimension=0, tiled=True
        ).astype(jnp.float32),
        lax.psum_scatter(proj_grad_part, "row", scatter_dimension=1, tiled=True).astype(
            jnp.float32
        ),
        lax.psum_scatter(
            fc1_grad_part.astype(jnp.bfloat16), "row", scatter_dimension=0, tiled=True
        ).astype(jnp.float32),
        lax.psum_scatter(
            fc2_grad_part.astype(jnp.bfloat16), "row", scatter_dimension=1, tiled=True
        ).astype(jnp.float32),
    )
    qkv_grad, proj_grad, fc1_grad, fc2_grad = (
        lax.psum(qkv_rows.astype(jnp.bfloat16), "dp").astype(jnp.float32),
        lax.psum(proj_cols.astype(jnp.bfloat16), "dp").astype(jnp.float32),
        lax.psum(fc1_rows.astype(jnp.bfloat16), "dp").astype(jnp.float32),
        lax.psum(fc2_cols.astype(jnp.bfloat16), "dp").astype(jnp.float32),
    )
    half_width = width // row_count
    token_part = lax.dynamic_slice_in_dim(
        token_sums, lax.axis_index("row") * half_width, half_width, 1
    )
    head_part = lax.dynamic_slice_in_dim(head_sums, col_index * head_width, head_width, 1)
    fc1_part = lax.dynamic_slice_in_dim(fc1_sums, col_index * hidden_width, hidden_width, 0)
    loss_value = loss_sum / (valid_total * width)
    return (
        outputs.astype(jnp.bfloat16),
        loss_value,
        grad_states,
        token_part[0],
        token_part[1],
        qkv_grad,
        head_part[0],
        head_part[1],
        proj_grad,
        token_part[2],
        token_part[3],
        token_part[4],
        fc1_grad,
        fc1_part,
        fc2_grad,
        token_part[5],
    )


PAIRED_MESH = (4, 2, 4)
GROUP = 4


def small_cost(flops):
    return pl.CostEstimate(flops=flops, bytes_accessed=0, transcendentals=0)
QT = 128


def dot_nn(a, b):
    return lax.dot_general(a, b, (((1,), (0,)), ((), ())), preferred_element_type=jnp.float32)


def dot_nt(a, b):
    return lax.dot_general(a, b, (((1,), (1,)), ((), ())), preferred_element_type=jnp.float32)


def dot_tn(a, b):
    return lax.dot_general(a, b, (((0,), (0,)), ((), ())), preferred_element_type=jnp.float32)


def head_stack(values, zero):
    lane_head = lax.broadcasted_iota(jnp.int32, values.shape, 1) // HD
    return jnp.concatenate([jnp.where(lane_head == h, values, zero) for h in range(GROUP)], axis=0)


def head_unstack(wide, count):
    return jnp.concatenate(
        [wide[h * HD : (h + 1) * HD, h * count : (h + 1) * count] for h in range(GROUP)], axis=0
    ).T


def tiles_of(rows, tile):
    full = rows // QT

    @pl.loop(0, full)
    def _(index):
        tile(pl.multiple_of(index * QT, QT), QT, index)

    if rows > full * QT:
        tile(full * QT, rows - full * QT, full)


def attend_kernel(first, packed_ref, bias_ref, out_ref, lse_ref, vt_ref):
    width = GROUP * HD
    vt_ref[...] = packed_ref[:, 2 * width : 3 * width].T

    def tile(start, count, index):
        cols = GROUP * count
        stacked = head_stack(
            packed_ref[pl.ds(first + start, count), 0:width], jnp.zeros((), jnp.bfloat16)
        )
        keys = packed_ref[:, width : 2 * width]
        bias = bias_ref[...]
        scores = dot_nt(keys, stacked) + jnp.concatenate([bias] * (cols // 128), axis=1)
        peak = jnp.max(scores, axis=0, keepdims=True)
        weights = jnp.exp(scores - peak)
        total = jnp.sum(weights, axis=0, keepdims=True)
        wide = dot_nn(vt_ref[...], weights.astype(jnp.bfloat16)) * (1.0 / total)
        out_ref[pl.ds(start, count), :] = head_unstack(wide, count).astype(jnp.bfloat16)
        lse_ref[index, :, 0:cols] = jnp.broadcast_to(peak + jnp.log(total), (8, cols))

    tiles_of(out_ref.shape[0], tile)


def attend_back_kernel(
    first, lane, last, packed_ref, bias_ref, lse_ref, att_ref, up_own_ref, up_far_ref, *refs
):
    width = GROUP * HD
    lanes = slice(lane, lane + width)
    own_rows = up_own_ref.shape[0]
    if last:
        dq_in, dk_in, dv_in, out_ref, sum_ref, kt_ref, up_ref, dk_ref, dv_ref = refs
        dk_ref[...] = dk_in[...]
        dv_ref[...] = dv_in[...]
        out_ref[0:first, 0:width] = dq_in[...]
        rows = out_ref.shape[0] - first
        up_ref[0 : own_rows - first, :] = up_own_ref[first:own_rows, lanes]
        up_ref[own_rows - first :, :] = up_far_ref[:, lanes]
    else:
        out_ref, dk_ref, dv_ref, kt_ref, up_ref = refs
        dk_ref[...] = jnp.zeros_like(dk_ref)
        dv_ref[...] = jnp.zeros_like(dv_ref)
        rows = out_ref.shape[0]
        up_ref[...] = up_own_ref[0:rows, lanes]
    kt_ref[...] = packed_ref[:, width : 2 * width].T

    def tile(start, count, index):
        cols = GROUP * count
        zero = jnp.zeros((), jnp.bfloat16)
        up = up_ref[pl.ds(start, count), :]
        stacked = head_stack(packed_ref[pl.ds(first + start, count), 0:width], zero)
        up_stacked = head_stack(up, zero)
        product = head_stack(
            up.astype(jnp.float32) * att_ref[pl.ds(start, count), :].astype(jnp.float32),
            jnp.zeros((), jnp.float32),
        )
        high = product.astype(jnp.bfloat16)
        low = (product - high.astype(jnp.float32)).astype(jnp.bfloat16)
        ones = jnp.ones((8, width), jnp.bfloat16)
        delta = (dot_nt(ones, high) + dot_nt(ones, low))[0:1]
        keys = packed_ref[:, width : 2 * width]
        values = packed_ref[:, 2 * width : 3 * width]
        bias = bias_ref[...]
        scores = dot_nt(keys, stacked) + jnp.concatenate([bias] * (cols // 128), axis=1)
        weights = jnp.exp(scores - lse_ref[index, 0:1, 0:cols])
        dv_ref[...] += dot_nn(weights.astype(jnp.bfloat16), up_stacked)
        grad = (weights * (dot_nt(values, up_stacked) - delta)).astype(jnp.bfloat16)
        dk_ref[...] += dot_nn(grad, stacked)
        wide = dot_nn(kt_ref[...], grad) * (HD**-0.5)
        at = pl.ds(first + start if last else start, count)
        out_ref[at, 0:width] = head_unstack(wide, count).astype(jnp.bfloat16)

    tiles_of(rows, tile)
    if last:
        out_ref[:, width : 2 * width] = dk_ref[...].astype(jnp.bfloat16)
        out_ref[:, 2 * width : 3 * width] = dv_ref[...].astype(jnp.bfloat16)
        for k in range(3):
            part = out_ref[:, k * width : (k + 1) * width].astype(jnp.float32)
            sum_ref[:, k * width : (k + 1) * width] = jnp.sum(part, axis=0, keepdims=True)


def attend(packed, bias, first, rows):
    tokens, width = packed.shape[0], GROUP * HD
    tiles = -(-rows // QT)
    return pl.pallas_call(
        functools.partial(attend_kernel, first),
        out_shape=(
            jax.ShapeDtypeStruct((rows, width), jnp.bfloat16),
            jax.ShapeDtypeStruct((tiles, 8, GROUP * QT), jnp.float32),
        ),
        in_specs=[pl.BlockSpec(memory_space=pltpu.VMEM)] * 2,
        out_specs=[pl.BlockSpec(memory_space=pltpu.VMEM)] * 2,
        scratch_shapes=[pltpu.VMEM((width, tokens), jnp.bfloat16)],
        compiler_params=pltpu.CompilerParams(vmem_limit_bytes=32 << 20),
        cost_estimate=pl.CostEstimate(
            flops=2 * rows * tokens * width * 4, bytes_accessed=6 << 20, transcendentals=0
        ),
        name="attend",
    )(packed, bias)


def attend_back(packed, bias, lse, att, up_own, up_far, lane, first, before=None):
    tokens, width = packed.shape[0], GROUP * HD
    rows = att.shape[0]
    total = jax.ShapeDtypeStruct((tokens, width), jnp.float32)
    vmem = pl.BlockSpec(memory_space=pltpu.VMEM)
    scratch = [pltpu.VMEM((width, tokens), jnp.bfloat16), pltpu.VMEM((rows, width), jnp.bfloat16)]
    if before is None:
        extra = ()
        out_shape = (jax.ShapeDtypeStruct((rows, width), jnp.bfloat16), total, total)
        up_far = up_own
    else:
        extra = before
        out_shape = (
            jax.ShapeDtypeStruct((tokens, 3 * width), jnp.bfloat16),
            jax.ShapeDtypeStruct((1, 3 * width), jnp.float32),
        )
        scratch += [pltpu.VMEM((tokens, width), jnp.float32)] * 2
    return pl.pallas_call(
        functools.partial(attend_back_kernel, first, lane, before is not None),
        out_shape=out_shape,
        in_specs=[vmem] * (6 + len(extra)),
        out_specs=(vmem,) * len(out_shape),
        scratch_shapes=scratch,
        compiler_params=pltpu.CompilerParams(vmem_limit_bytes=52 << 20),
        cost_estimate=pl.CostEstimate(
            flops=4 * rows * tokens * width * 4, bytes_accessed=10 << 20, transcendentals=0
        ),
        name="attend_back",
    )(packed, bias, lse, att, up_own, up_far, *extra)


FF_CHUNK = 512
ROWS = 112


def rows_of(total, body):
    @pl.loop(0, total // ROWS)
    def _(index):
        body(pl.ds(pl.multiple_of(index * ROWS, ROWS), ROWS))


def unit_rows(values):
    centered = values - jnp.mean(values, axis=-1, keepdims=True)
    spread = lax.rsqrt(jnp.mean(centered * centered, axis=-1, keepdims=True) + EPSILON)
    return centered * spread, spread


def middle_kernel(
    table_ref,
    factor_ref,
    input_ref,
    target_ref,
    valid_ref,
    vector_ref,
    small_ref,
    fc1_own,
    fc1_other,
    fc2_own,
    fc2_other,
    proj_own,
    proj_other,
    two_mine,
    two_theirs,
    *refs,
):
    one_mine, one_theirs, att_parts, refs = refs[:5], refs[5:10], refs[10:16], refs[16:]
    (
        att_hbm,
        out_hbm,
        hidden_hbm,
        pre_hbm,
        norm_hbm,
        grad_low_hbm,
        mid_low_ref,
        grad_mid_ref,
        up_own_ref,
        up_give_ref,
        hidden_sum_ref,
        sums_ref,
        fc1_v,
        fc2_v,
        proj_v,
        middle_v,
        back_v,
        out_ref,
        hidden_ref,
        pre_ref,
        norm_ref,
        grad_low_ref,
        att_ref,
        sem_one,
        sem_two,
        sem_proj,
        sem_att,
        sem_out,
    ) = refs
    stores = [
        pltpu.make_async_copy(source, target, sem_out.at[i])
        for i, (source, target) in enumerate(
            (
                (norm_ref, norm_hbm),
                (hidden_ref, hidden_hbm),
                (out_ref, out_hbm),
                (grad_low_ref, grad_low_hbm),
                (pre_ref, pre_hbm),
                (att_ref, att_hbm),
            )
        )
    ]
    f32, bf16 = jnp.float32, jnp.bfloat16
    total_rows = input_ref.shape[0]
    half = fc1_own.shape[0]
    sub = fc1_own.shape[1] // 4
    heads = proj_own.shape[0]
    part = heads // 4
    hidden_total = hidden_ref.shape[1]
    chunks = hidden_total // FF_CHUNK
    unit = half + 2 * sub + 2 * part + 16

    def fc1_copy(source, side, at):
        lanes = pl.ds(pl.multiple_of(at * sub, sub), sub)
        pltpu.make_async_copy(
            source, fc1_v.at[side * half : (side + 1) * half, lanes], sem_one.at[at // 2]
        ).start()

    def fc2_copy(source, side, i, at):
        lane = side * half + i * sub
        pltpu.make_async_copy(
            source, fc2_v.at[pl.ds(pl.multiple_of(at * sub, sub), sub), lane : lane + sub], sem_two
        ).start()

    sources = []
    for s in range(4):
        step = two_mine.shape[0] // 4
        sources.append((s, 2, two_mine, two_theirs, s * step))
        low, high = (3, 4) if s == 3 else (s, s)
        sources.append((s, 1, one_mine[low], one_theirs[low], 0))
        sources.append((s, 3, one_mine[high], one_theirs[high], 0 if s == 3 else unit))

    early_rows = att_parts[0].shape[0]
    for at in range(2):
        soon, late, other = att_parts[3 * at : 3 * at + 3]
        lanes = slice(2 * at * heads, (2 * at + 1) * heads)
        pltpu.make_async_copy(soon, att_ref.at[0:early_rows, lanes], sem_att).start()
        pltpu.make_async_copy(
            late.at[0 : total_rows - early_rows], att_ref.at[early_rows:total_rows, lanes], sem_att
        ).start()
        lanes = slice((2 * at + 1) * heads, (2 * at + 2) * heads)
        pltpu.make_async_copy(other, att_ref.at[:, lanes], sem_att).start()
    for side, ref in enumerate((proj_own, proj_other)):
        pltpu.make_async_copy(
            ref, proj_v.at[0:heads, side * half : (side + 1) * half], sem_proj
        ).start()
    for s, j, *refs, base in sources:
        rows = pl.ds(pl.multiple_of(j * heads + table_ref[20 + s] * part, part), part)
        for side in range(2):
            for i in range(2):
                low = base + half + 2 * sub + i * part
                lane = side * half + i * sub
                pltpu.make_async_copy(
                    refs[side].at[low : low + part, :], proj_v.at[rows, lane : lane + sub], sem_proj
                ).start()
    for a in range(4):
        for side, ref in enumerate((fc1_own, fc1_other)):
            fc1_copy(ref.at[:, a * sub : (a + 1) * sub], side, table_ref[16 + a])
    for s, j, *refs, base in sources:
        for side in range(2):
            fc1_copy(refs[side].at[base : base + half, :], side, table_ref[4 * s + j])
    for a in range(4):
        for side, ref in enumerate((fc2_own, fc2_other)):
            for i in range(2):
                fc2_copy(
                    ref.at[a * sub : (a + 1) * sub, i * sub : (i + 1) * sub], side, i, table_ref[16 + a]
                )
    for s, j, *refs, base in sources:
        for side in range(2):
            for i in range(2):
                low = base + half + i * sub
                fc2_copy(refs[side].at[low : low + sub, :], side, i, table_ref[4 * s + j])

    def lanes_of(i):
        return pl.ds(pl.multiple_of((table_ref[28] ^ i) * half, half), half)

    sums_ref[...] = jnp.zeros_like(sums_ref)

    pltpu.make_async_copy(att_ref, att_ref, sem_att).wait()
    stores[5].start()
    pltpu.make_async_copy(proj_v, proj_v, sem_proj).wait()
    for i in range(2):
        cols = slice(i * half, (i + 1) * half)
        middle_v[:, cols] = input_ref[:, lanes_of(i)].astype(f32) + (
            dot_nn(att_ref[...], proj_v[:, cols]) + vector_ref[2:3, cols]
        )

    @functools.partial(rows_of, total_rows)
    def _(rows):
        normal, _ = unit_rows(middle_v[rows, :])
        norm_ref[rows, :] = (normal * vector_ref[3:4, :] + vector_ref[4:5, :]).astype(bf16)

    stores[0].start()

    @pl.loop(0, chunks)
    def _(k):
        span = pl.ds(pl.multiple_of(k * FF_CHUNK, FF_CHUNK), FF_CHUNK)
        pltpu.make_async_copy(fc1_v.at[:, span], fc1_v.at[:, span], sem_one.at[k]).wait()
        a = k // 2
        bias = jnp.concatenate(
            [
                small_ref[table_ref[24 + 2 * (k % 2) + i], pl.ds(a, 1), :]
                for i in range(FF_CHUNK // sub)
            ],
            axis=1,
        )
        pre = dot_nn(norm_ref[...], fc1_v[:, span]) + bias
        cdf = 0.5 * (1.0 + lax.erf(pre * ROOT_HALF))
        hidden_ref[:, span] = (pre * cdf).astype(bf16)
        slope = cdf + pre * jnp.exp(-0.5 * pre * pre) * DENSITY_FACTOR
        pre_ref[:, span] = slope.astype(bf16)

    stores[1].start()
    pltpu.make_async_copy(fc2_v, fc2_v, sem_two).wait()
    for i in range(2):
        cols = slice(i * half, (i + 1) * half)
        total = middle_v[:, cols] + (dot_nn(hidden_ref[...], fc2_v[:, cols]) + vector_ref[5:6, cols])
        out_ref[:, lanes_of(i)] = total.astype(bf16)
        differ = total - target_ref[:, lanes_of(i)].astype(f32)
        weighted = valid_ref[...] * differ
        sums_ref[0:1, cols] = jnp.sum(weighted * differ, axis=0, keepdims=True)
        grad = factor_ref[0] * weighted
        grad_mid_ref[:, cols] = grad
        low = grad.astype(bf16)
        grad_low_ref[:, cols] = low
        sums_ref[1:2, cols] = jnp.sum(low.astype(f32), axis=0, keepdims=True)

    stores[2].start()
    stores[3].start()

    @pl.loop(0, chunks)
    def _(k):
        span = pl.ds(pl.multiple_of(k * FF_CHUNK, FF_CHUNK), FF_CHUNK)
        back = dot_nt(grad_low_ref[...], fc2_v[span, :])
        back = (back * pre_ref[:, span].astype(f32)).astype(bf16)
        pre_ref[:, span] = back
        hidden_sum_ref[0:1, span] = jnp.sum(back.astype(f32), axis=0, keepdims=True)

    stores[4].start()
    for i in range(2):
        cols = slice(i * half, (i + 1) * half)
        back_v[:, cols] = dot_nt(pre_ref[...], fc1_v[cols, :])

    @functools.partial(rows_of, total_rows)
    def _(rows):
        normal, spread = unit_rows(middle_v[rows, :])
        upstream = back_v[rows, :]
        inner = upstream * vector_ref[3:4, :]
        center = jnp.mean(inner, axis=-1, keepdims=True)
        slope = jnp.mean(inner * normal, axis=-1, keepdims=True)
        grad = grad_mid_ref[rows, :] + spread * (inner - center - normal * slope)
        grad_mid_ref[rows, :] = grad
        low = grad.astype(bf16)
        mid_low_ref[rows, :] = low
        sums_ref[2:3, :] += jnp.sum(upstream * normal, axis=0, keepdims=True)
        sums_ref[3:4, :] += jnp.sum(upstream, axis=0, keepdims=True)
        sums_ref[4:5, :] += jnp.sum(low.astype(f32), axis=0, keepdims=True)

    for j, (ref, at) in enumerate(((up_own_ref, 0), (up_give_ref, 0), (up_own_ref, 1), (up_give_ref, 1))):
        grad = dot_nt(mid_low_ref[...], proj_v[j * heads : (j + 1) * heads, :])
        ref[:, at * heads : (at + 1) * heads] = grad.astype(bf16)
    for store in stores:
        store.wait()


def middle_block(table, factor, inputs, target, valid, vectors, smalls, pieces):
    rows, width = inputs.shape
    hidden = 4 * pieces[0].shape[1]
    vmem = pl.BlockSpec(memory_space=pltpu.VMEM)
    smem = pl.BlockSpec(memory_space=pltpu.SMEM)
    anywhere = pl.BlockSpec(memory_space=pl.ANY)
    f32, bf16 = jnp.float32, jnp.bfloat16

    def result(columns, dtype):
        return jax.ShapeDtypeStruct((rows, columns), dtype)

    return pl.pallas_call(
        middle_kernel,
        out_shape=(
            result(width, bf16),
            result(width, bf16),
            result(hidden, bf16),
            result(hidden, bf16),
            result(width, bf16),
            result(width, bf16),
            result(width, bf16),
            result(width, f32),
            result(width // 2, bf16),
            result(width // 2, bf16),
            jax.ShapeDtypeStruct((1, hidden), f32),
            jax.ShapeDtypeStruct((8, width), f32),
        ),
        in_specs=[smem] * 2 + [vmem] * 5 + [anywhere] * len(pieces),
        out_specs=[anywhere] * 6 + [vmem] * 6,
        scratch_shapes=[
            pltpu.VMEM((width, hidden), bf16),
            pltpu.VMEM((hidden, width), bf16),
            pltpu.VMEM((width, width), bf16),
            pltpu.VMEM((rows, width), f32),
            pltpu.VMEM((rows, width), f32),
            pltpu.VMEM((rows, width), bf16),
            pltpu.VMEM((rows, hidden), bf16),
            pltpu.VMEM((rows, hidden), bf16),
            pltpu.VMEM((rows, width), bf16),
            pltpu.VMEM((rows, width), bf16),
            pltpu.VMEM((rows, width), bf16),
            pltpu.SemaphoreType.DMA((hidden // FF_CHUNK,)),
            pltpu.SemaphoreType.DMA,
            pltpu.SemaphoreType.DMA,
            pltpu.SemaphoreType.DMA,
            pltpu.SemaphoreType.DMA((6,)),
        ],
        compiler_params=pltpu.CompilerParams(vmem_limit_bytes=62 << 20),
        cost_estimate=pl.CostEstimate(
            flops=2 * rows * width * hidden, bytes_accessed=44 << 20, transcendentals=0
        ),
        name="middle_block",
    )(table, factor, inputs, target, valid, vectors, smalls, *pieces)


def swap(values, axis, mask, size):
    return lax.ppermute(values, axis, [(i, i ^ mask) for i in range(size)])


def over_row(values):
    return swap(values, "row", 1, 2)


def over_dp(values, mask):
    return swap(values, "dp", mask, 4)


def over_col(values, mask):
    return swap(values, "col", mask, 4)


def cut(values, index, size, axis=0):
    return lax.dynamic_slice_in_dim(values, index * size, size, axis)


def place(pieces, index_of, axis):
    size = pieces[0].shape[axis]
    shape = list(pieces[0].shape)
    shape[axis] = size * len(pieces)
    whole = jnp.zeros(shape, pieces[0].dtype)
    for s, piece in enumerate(pieces):
        whole = lax.dynamic_update_slice_in_dim(whole, piece, index_of(s) * size, axis)
    return whole


def copies(listed, sem_ref):
    for index, (source, target) in enumerate(listed):
        pltpu.make_async_copy(source, target, sem_ref.at[index]).start()
    for index, (source, target) in enumerate(listed):
        pltpu.make_async_copy(source, target, sem_ref.at[index]).wait()


def slab_kernel(places_ref, fc1_ref, fc2_ref, proj_ref, qkv_ref, small_ref, out_ref, sem_ref):
    half, sub = fc1_ref.shape[0], fc1_ref.shape[1] // 4
    part, deep = proj_ref.shape[0] // 4, half // 4
    mine = places_ref[0]
    fc2 = fc2_ref.at[pl.ds(pl.multiple_of(mine * sub, sub), sub)]
    proj = proj_ref.at[pl.ds(pl.multiple_of(mine * part, part), part)]
    listed = [(fc1_ref.at[:, pl.ds(pl.multiple_of(mine * sub, sub), sub)], half)]
    listed += [(fc2.at[:, i * sub : (i + 1) * sub], sub) for i in range(2)]
    listed += [(proj.at[:, i * sub : (i + 1) * sub], part) for i in range(2)]
    listed += [(small_ref, small_ref.shape[0])]
    rows = pl.ds(pl.multiple_of(mine * deep, deep), deep)
    listed += [(qkv_ref.at[k, rows], deep) for k in range(3)]
    pairs, at = [], 0
    for source, count in listed:
        pairs.append((source, out_ref.at[at : at + count]))
        at += count
    copies(pairs, sem_ref)


def make_slab(places, fc1, fc2, proj, qkv, small):
    half, sub = fc1.shape[0], fc1.shape[1] // 4
    rows = half + 2 * sub + proj.shape[0] // 2 + small.shape[0] + 3 * (half // 4)
    anywhere = pl.BlockSpec(memory_space=pl.ANY)
    return pl.pallas_call(
        slab_kernel,
        out_shape=jax.ShapeDtypeStruct((rows, sub), fc1.dtype),
        in_specs=[pl.BlockSpec(memory_space=pltpu.SMEM)] + [anywhere] * 5,
        out_specs=pl.BlockSpec(memory_space=pltpu.VMEM),
        scratch_shapes=[pltpu.SemaphoreType.DMA((9,))],
        cost_estimate=small_cost(100000000),
        name="make_slab",
    )(places, fc1, fc2, proj, qkv, small)


def far_qkv_kernel(base, places_ref, mine_ref, theirs_ref, out_ref, sem_ref):
    sub = mine_ref.shape[1]
    half = out_ref.shape[0] // 2
    deep, step = half // 4, mine_ref.shape[0] // 4
    pairs = []
    for side, ref in enumerate((mine_ref, theirs_ref)):
        for s in range(4):
            rows = pl.ds(pl.multiple_of(side * half + places_ref[s] * deep, deep), deep)
            for k in range(3):
                at = s * step + base + k * deep
                pairs.append((ref.at[at : at + deep], out_ref.at[rows, k * sub : (k + 1) * sub]))
    copies(pairs, sem_ref)


def far_qkv(places, mine, theirs, base, width):
    anywhere = pl.BlockSpec(memory_space=pl.ANY)
    return pl.pallas_call(
        functools.partial(far_qkv_kernel, base),
        out_shape=jax.ShapeDtypeStruct((width, 3 * mine.shape[1]), mine.dtype),
        in_specs=[pl.BlockSpec(memory_space=pltpu.SMEM)] + [anywhere] * 2,
        out_specs=pl.BlockSpec(memory_space=pltpu.VMEM),
        scratch_shapes=[pltpu.SemaphoreType.DMA((24,))],
        cost_estimate=small_cost(100000000),
        name="far_qkv",
    )(places, mine, theirs)


def first_norm_kernel(flip_ref, states_ref, vector_ref, *refs):
    out_ref = refs[-1]
    rows_all, width = states_ref.shape
    start = out_ref.shape[0] - rows_all
    if start:
        out_ref[0:start, :] = refs[0][...]

    @pl.loop(0, rows_all // ROWS)
    def _(index):
        rows = pl.ds(pl.multiple_of(index * ROWS, ROWS), ROWS)
        normal, _ = unit_rows(framed(states_ref, rows, flip_ref[0], width // 2))
        values = (normal * vector_ref[0:1, :] + vector_ref[1:2, :]).astype(jnp.bfloat16)
        out_ref[pl.ds(pl.multiple_of(start + index * ROWS, 16), ROWS), :] = values


def first_norm(flip, states, vectors, *before):
    vmem = pl.BlockSpec(memory_space=pltpu.VMEM)
    rows = states.shape[0] + sum(b.shape[0] for b in before)
    return pl.pallas_call(
        first_norm_kernel,
        out_shape=jax.ShapeDtypeStruct((rows, states.shape[1]), jnp.bfloat16),
        in_specs=[pl.BlockSpec(memory_space=pltpu.SMEM)] + [vmem] * (2 + len(before)),
        out_specs=vmem,
        cost_estimate=small_cost(100000000),
        name="first_norm",
    )(flip, states, vectors, *before)


VECTORS = 32


def put_split(ref, at, values):
    high = values.astype(jnp.bfloat16)
    low = (values - high.astype(jnp.float32)).astype(jnp.bfloat16)
    columns = values.shape[1]
    ref[at : at + VECTORS, 0:columns] = high
    ref[at + VECTORS : at + 2 * VECTORS, 0:columns] = low
    rest = ref.shape[1] - columns
    if rest:
        ref[at : at + 2 * VECTORS, columns:] = jnp.zeros((2 * VECTORS, rest), jnp.bfloat16)


def get_split(ref, at, columns):
    high = ref[at : at + VECTORS, 0:columns].astype(jnp.float32)
    return high + ref[at + VECTORS : at + 2 * VECTORS, 0:columns].astype(jnp.float32)


def framed(ref, rows, flip, half):
    return jnp.concatenate(
        [ref[rows, pl.ds(pl.multiple_of((flip ^ i) * half, half), half)] for i in range(2)], axis=1
    ).astype(jnp.float32)


def token_back_kernel(
    flip_ref, near_ref, far_ref, w_near, w_far, own_states, other_states, own_ref, give_ref, sums_ref, other_v
):
    rows_all, half = own_ref.shape[0], own_ref.shape[1] // 2
    sums_ref[...] = jnp.zeros_like(sums_ref)
    for start, out_ref in ((rows_all, other_v), (0, own_ref)):
        rows = slice(start, start + rows_all)
        out_ref[...] = dot_nt(near_ref[rows, :], w_near[...]) + dot_nt(far_ref[rows, :], w_far[...])
    for out_ref, states in ((other_v, other_states), (own_ref, own_states)):

        @functools.partial(rows_of, rows_all)
        def _(rows, out_ref=out_ref, states=states):
            normal, _ = unit_rows(framed(states, rows, flip_ref[0], half))
            upstream = out_ref[rows, :]
            sums_ref[0:1, :] += jnp.sum(upstream * normal, axis=0, keepdims=True)
            sums_ref[1:2, :] += jnp.sum(upstream, axis=0, keepdims=True)
            if out_ref is other_v:
                give_ref[rows, :] = upstream.astype(jnp.bfloat16)


def token_back(flip, near, far, w_near, w_far, own_states, other_states):
    rows, width = own_states.shape
    vmem = pl.BlockSpec(memory_space=pltpu.VMEM)
    return pl.pallas_call(
        token_back_kernel,
        out_shape=(
            jax.ShapeDtypeStruct((rows, width), jnp.float32),
            jax.ShapeDtypeStruct((rows, width), jnp.bfloat16),
            jax.ShapeDtypeStruct((2, width), jnp.float32),
        ),
        in_specs=[pl.BlockSpec(memory_space=pltpu.SMEM)] + [vmem] * 6,
        out_specs=(vmem,) * 3,
        scratch_shapes=[pltpu.VMEM((rows, width), jnp.float32)],
        compiler_params=pltpu.CompilerParams(vmem_limit_bytes=40 << 20),
        cost_estimate=small_cost(100000000),
        name="token_back",
    )(flip, near, far, w_near, w_far, own_states, other_states)


def last_kernel(flip_ref, own_ref, taken_ref, states_ref, mid_ref, vector_ref, out_ref):
    half = own_ref.shape[1] // 2
    upstream = own_ref[...] + taken_ref[...].astype(jnp.float32)
    everything = slice(0, own_ref.shape[0])
    normal, spread = unit_rows(framed(states_ref, everything, flip_ref[0], half))
    inner = upstream * vector_ref[0:1, :]
    center = jnp.mean(inner, axis=-1, keepdims=True)
    slope = jnp.mean(inner * normal, axis=-1, keepdims=True)
    back = mid_ref[...] + spread * (inner - center - normal * slope)
    for i in range(2):
        lanes = pl.ds(pl.multiple_of((flip_ref[0] ^ i) * half, half), half)
        out_ref[:, lanes] = back[:, i * half : (i + 1) * half].astype(jnp.bfloat16)


def last_norm(flip, own, taken, states, mid, vectors):
    rows, width = own.shape
    block = pl.BlockSpec((ROWS, width), lambda i: (i, 0))
    whole = pl.BlockSpec(vectors.shape, lambda i: (0, 0))
    return pl.pallas_call(
        last_kernel,
        grid=(rows // ROWS,),
        out_shape=jax.ShapeDtypeStruct((rows, width), jnp.bfloat16),
        in_specs=[pl.BlockSpec(memory_space=pltpu.SMEM)] + [block] * 4 + [whole],
        out_specs=block,
        cost_estimate=small_cost(500000000),
        name="last_norm",
    )(flip, own, taken, states, mid, vectors)


def far_grads_kernel(
    turned_ref, grad_ref, sums_ref, hidden_ref, norm_ref, near_ref, far_ref, keep_ref, out_ref, kept_ref
):
    half = keep_ref.shape[1]
    width = near_ref.shape[1] // 3
    shared = [hidden_ref[0:1, i * half : (i + 1) * half] for i in range(8)]
    for ref in (near_ref, far_ref):
        shared.append(jnp.concatenate([ref[0:1, 0:width], ref[0:1, 2 * width :]], axis=1))
    shared.append(sums_ref[0:1, 0:half] + sums_ref[0:1, half:])
    blank = jnp.zeros((VECTORS - 6 - len(shared), half), jnp.float32)

    def rows(lanes):
        split = [sums_ref[i : i + 1, lanes] for i in (2, 3, 4, 1)]
        split += [norm_ref[i : i + 1, lanes] for i in range(2)]
        return jnp.concatenate(split + shared + [blank], axis=0)

    keep_ref[...] = rows(slice(0, half))
    put_split(out_ref, half, rows(slice(half, 2 * half)))
    out_ref[0:half, :] = dot_nn(turned_ref[half:, :], grad_ref[...]).astype(jnp.bfloat16)
    kept_ref[...] = dot_nn(turned_ref[0:half, :], grad_ref[...])


def after_row_kernel(
    places_ref, kept_ref, taken_ref, keep_ref, near_ref, near_taken, near_own_ref, far_own_ref, sum_ref, *outs
):
    deep = far_own_ref.shape[0]
    vectors = keep_ref[...] + get_split(taken_ref, 4 * deep, keep_ref.shape[1])
    sum_ref[...] = vectors
    for s in range(4):
        rows = pl.ds(pl.multiple_of(places_ref[s] * deep, deep), deep)
        far = kept_ref[rows, :] + taken_ref[rows, :].astype(jnp.float32)
        if s == 0:
            far_own_ref[...] = far
        else:
            outs[s - 1][0:deep, :] = far.astype(jnp.bfloat16)
            put_split(outs[s - 1], deep, vectors)
        if s % 2 == 0:
            at = slice(s // 2 * deep, (s // 2 + 1) * deep)
            near = near_ref[rows, :].astype(jnp.float32) + near_taken[at, :].astype(jnp.float32)
            if s == 0:
                near_own_ref[...] = near
            else:
                outs[s - 1][deep + 2 * VECTORS :, :] = near.astype(jnp.bfloat16)


def after_plane_kernel(near_ref, far_ref, sum_ref, *refs):
    takes, (keep_ref, vector_ref, give_ref, small_ref) = refs[:3], refs[3:]
    deep = far_ref.shape[0]
    vectors, far = sum_ref[...], far_ref[...]
    keep_ref[...] = near_ref[...] + takes[1][deep + 2 * VECTORS :, :].astype(jnp.float32)
    for take in takes:
        vectors = vectors + get_split(take, deep, vectors.shape[1])
        far = far + take[0:deep, :].astype(jnp.float32)
    vector_ref[...] = vectors
    give_ref[0:deep, :] = far.astype(jnp.bfloat16)
    put_split(give_ref, deep, vectors)
    put_split(small_ref, 0, vectors)


def after_cols_kernel(keep_ref, vector_ref, one_ref, two_ref, three_ref, out_ref, total_ref):
    deep = keep_ref.shape[0]
    out_ref[...] = (keep_ref[...] + two_ref[0:deep, :].astype(jnp.float32)).astype(jnp.bfloat16)
    columns = vector_ref.shape[1]
    far = get_split(two_ref, deep, columns)
    total = vector_ref[...] + far
    total = total + get_split(one_ref, 0, columns) + get_split(three_ref, 0, columns)
    total_ref[...] = total
    total_ref[14:15, :] = vector_ref[14:15, :] + far[15:16, :]


def on_chip(kernel, shapes, name, *args, tables=0):
    vmem = pl.BlockSpec(memory_space=pltpu.VMEM)
    return pl.pallas_call(
        kernel,
        out_shape=tuple(jax.ShapeDtypeStruct(*s) for s in shapes),
        in_specs=[pl.BlockSpec(memory_space=pltpu.SMEM)] * tables + [vmem] * (len(args) - tables),
        out_specs=(vmem,) * len(shapes),
        cost_estimate=small_cost(100000000),
        name=name,
    )(*args)


def wide_kernel(with_proj, places_ref, small_ref, big_ref, taken_ref, *refs):
    if with_proj:
        proj_kept, proj_taken, *refs = refs
    *outs, turned_v = refs
    half, sub = turned_v.shape[0], turned_v.shape[0] // 2
    span = big_ref.shape[1] // 4
    part = 256 // 4 if not with_proj else proj_kept.shape[0] // 16
    turned_v[...] = small_ref[:, 0:half].T
    for s in range(4):
        lanes = pl.ds(pl.multiple_of(places_ref[s] * span, span), span)
        block = dot_nn(turned_v[...], big_ref[:, lanes]) + taken_ref[:, lanes].astype(jnp.float32)
        block = block.astype(jnp.bfloat16)
        for side, (go, slot) in enumerate(((s % 2, s // 2), (s // 2, s % 2))):
            out = outs[2 * side + go]
            rows = slice(slot * sub, (slot + 1) * sub)
            out[rows, 0:span] = block[side * sub : (side + 1) * sub]
            if with_proj:
                at = side * sub
                for j in range(4):
                    start = pl.multiple_of(4 * j * part + places_ref[s] * part, part)
                    piece = proj_kept[pl.ds(start, part), at : at + sub] + proj_taken[
                        pl.ds(start, part), at : at + sub
                    ].astype(jnp.float32)
                    low = slot * sub + j * part
                    out[low : low + part, span:] = piece.astype(jnp.bfloat16)


def wide_grads(places, small, big, taken, proj=()):
    half = small.shape[1] // 2
    columns = big.shape[1] // 4 + (half // 2 if proj else 0)
    vmem = pl.BlockSpec(memory_space=pltpu.VMEM)
    return pl.pallas_call(
        functools.partial(wide_kernel, bool(proj)),
        out_shape=(jax.ShapeDtypeStruct((half, columns), jnp.bfloat16),) * 4,
        in_specs=[pl.BlockSpec(memory_space=pltpu.SMEM)] + [vmem] * (3 + len(proj)),
        out_specs=(vmem,) * 4,
        scratch_shapes=[pltpu.VMEM((half, small.shape[0]), jnp.bfloat16)],
        compiler_params=pltpu.CompilerParams(vmem_limit_bytes=44 << 20),
        cost_estimate=small_cost(3000000000),
        name="wide_grads",
    )(places, small, big, taken, *proj)


def plane_sum_kernel(*refs):
    sub = refs[4].shape[0]
    for side in range(2):
        kept, taken = refs[2 * side : 2 * side + 2]
        for slot in range(2):
            rows = slice(slot * sub, (slot + 1) * sub)
            total = kept[rows, :].astype(jnp.float32) + taken[rows, :].astype(jnp.float32)
            refs[4 + 2 * side + slot][...] = total.astype(jnp.bfloat16)


def cols_out_kernel(places_ref, *refs):
    outs = refs[4:]
    sub = refs[0].shape[0]
    columns = refs[0].shape[1]
    part = (outs[0].shape[0] - 2 * sub) // 2
    for side in range(2):
        kept, taken = refs[2 * side : 2 * side + 2]
        for j in range(4):
            lanes = pl.ds(pl.multiple_of(places_ref[4 + j] * sub, sub), sub)
            total = kept[:, lanes].astype(jnp.float32) + taken[:, lanes].astype(jnp.float32)
            outs[j][side * sub : (side + 1) * sub, :] = total.astype(jnp.bfloat16)
            if part:
                rows = slice(j * part, (j + 1) * part)
                total = kept[rows, columns - sub :].astype(jnp.float32)
                total = total + taken[rows, columns - sub :].astype(jnp.float32)
                low = 2 * sub + side * part
                outs[j][low : low + part, :] = total.astype(jnp.bfloat16)


def mine_kernel(*refs):
    out_ref, at = refs[8], 0
    for group in (refs[0:4], refs[4:8]):
        total = group[0][...].astype(jnp.float32)
        for ref in group[1:]:
            total = total + ref[...].astype(jnp.float32)
        out_ref[at : at + total.shape[0], :] = total.astype(jnp.bfloat16)
        at += total.shape[0]


def finish_kernel(part_rows, places_ref, *refs):
    pieces, (fc2_ref, fc1_ref, proj_ref) = refs[:2], refs[2:]
    half, sub = fc1_ref.shape[0], pieces[0].shape[1]
    for s in range(4):
        piece, base = pieces[s // 2], (s % 2) * (pieces[0].shape[0] // 2)
        at = places_ref[s]
        rows = pl.ds(pl.multiple_of(at * sub, sub), sub)
        fc2_ref[rows, :] = piece[base : base + half, :].astype(jnp.float32).T
        fc1_ref[:, rows] = piece[base + half : base + 2 * half, :].astype(jnp.float32)
        rows = pl.ds(pl.multiple_of(at * part_rows, part_rows), part_rows)
        for i in range(2):
            low = base + 2 * half + i * part_rows
            proj_ref[rows, i * sub : (i + 1) * sub] = piece[low : low + part_rows, :].astype(jnp.float32)


def finish_qkv_kernel(places_ref, *refs):
    out_ref = refs[4]
    deep, width = refs[0].shape[0], out_ref.shape[2]
    for s in range(4):
        rows = pl.ds(pl.multiple_of(places_ref[s] * deep, deep), deep)
        for k in range(3):
            out_ref[k, rows, :] = refs[s][:, k * width : (k + 1) * width].astype(jnp.float32)


def finish(places, pieces, part_rows):
    rows, sub = pieces[0].shape
    half = (rows // 2 - 2 * part_rows) // 2
    vmem = pl.BlockSpec(memory_space=pltpu.VMEM)
    return pl.pallas_call(
        functools.partial(finish_kernel, part_rows),
        out_shape=(
            jax.ShapeDtypeStruct((4 * sub, half), jnp.float32),
            jax.ShapeDtypeStruct((half, 4 * sub), jnp.float32),
            jax.ShapeDtypeStruct((4 * part_rows, half), jnp.float32),
        ),
        in_specs=[pl.BlockSpec(memory_space=pltpu.SMEM)] + [vmem] * 2,
        out_specs=[vmem] * 3,
        cost_estimate=small_cost(100000000),
        name="finish",
    )(places, *pieces)


def finish_qkv(places, pieces):
    deep, width = pieces[0].shape
    vmem = pl.BlockSpec(memory_space=pltpu.VMEM)
    return pl.pallas_call(
        finish_qkv_kernel,
        out_shape=jax.ShapeDtypeStruct((3, 4 * deep, width // 3), jnp.float32),
        in_specs=[pl.BlockSpec(memory_space=pltpu.SMEM)] + [vmem] * 4,
        out_specs=vmem,
        cost_estimate=small_cost(100000000),
        name="finish_qkv",
    )(places, *pieces)


def tie(value, *others):
    return lax.optimization_barrier((value, *others))[0]


def add_up(own, taken):
    total = own.astype(jnp.float32)
    for piece in taken:
        total = total + piece.astype(jnp.float32)
    return total


def local_paired(
    states,
    ln1_gain,
    ln1_bias,
    w_qkv,
    q_bias,
    v_bias,
    w_proj,
    proj_bias,
    ln2_gain,
    ln2_bias,
    w_fc1,
    fc1_bias,
    w_fc2,
    fc2_bias,
    teacher,
    loss_mask,
    lengths,
):
    f32, bf16 = jnp.float32, jnp.bfloat16
    dp = lax.axis_index("dp")
    row = lax.axis_index("row")
    col = lax.axis_index("col")
    local_rows, width = states.shape
    half = width // 2
    head_width = w_qkv.shape[2]
    hidden_width = w_fc1.shape[1]
    sub = hidden_width // 4
    span = 4 * sub
    part_rows = head_width // 4
    clip = (dp * 2 + row) * 2 + col // 2
    second = col % 2

    def quarter(s):
        return dp ^ s

    def frame(values):
        return jnp.where(
            row == 0, values, jnp.concatenate([values[:, half:], values[:, :half]], axis=1)
        )

    places = jnp.stack([dp ^ s for s in range(4)] + [col ^ j for j in range(4)]).astype(jnp.int32)
    flip = row.reshape(1).astype(jnp.int32)
    states_other = over_col(states, 1)
    small = jnp.concatenate(
        [
            fc1_bias.reshape(4, sub),
            q_bias.reshape(1, sub),
            v_bias.reshape(1, sub),
            jnp.zeros((10, sub), bf16),
        ],
        axis=0,
    )
    slab = make_slab(places, w_fc1, w_fc2, w_proj, w_qkv.transpose(1, 0, 2), small)
    unit_rows_total = half + 2 * sub + 2 * part_rows + small.shape[0]
    small_at = unit_rows_total - small.shape[0]
    two = over_col(slab, 2)
    w_qkv2 = w_qkv.reshape(half, 3 * head_width)
    w_qkv2 = tie(w_qkv2, slab)
    qkv_near = jnp.concatenate([w_qkv2, over_row(w_qkv2)], axis=0)
    vectors = jnp.stack([ln1_gain, ln1_bias, proj_bias, ln2_gain, ln2_bias, fc2_bias])
    vectors, states, teacher, loss_mask = lax.optimization_barrier(
        (vectors, states, teacher, loss_mask, slab)
    )[:4]
    vectors = jnp.concatenate([vectors, over_row(vectors)], axis=1).astype(f32)
    fc1_other, fc2_other, proj_other = over_row(w_fc1), over_row(w_fc2), over_row(w_proj)
    two = tie(two, fc1_other, fc2_other, proj_other)
    two_x, two_y = over_dp(two, 1), over_dp(two, 2)
    states_other = tie(states_other, two)

    all_clips = lengths.shape[0]
    valid_all = (
        loss_mask.reshape(all_clips, L) * (jnp.arange(L)[None, :] < lengths[:, None])
    ).astype(f32)
    valid_total = jnp.maximum(jnp.sum(valid_all), 1.0)
    first_row = ((dp * 2 + row) * 4 + col) * local_rows
    valid = lax.dynamic_slice_in_dim(valid_all.reshape(all_clips * L), first_row, local_rows)
    my_length = lax.dynamic_slice_in_dim(lengths, clip, 1)
    spot = jnp.arange(L)
    position = jnp.where(
        spot < local_rows, second * local_rows + spot, (1 - second) * local_rows + spot - local_rows
    )
    key_bias = jnp.where(position < my_length, 0.0, MASKED).astype(f32)
    key_bias = jnp.broadcast_to(key_bias[:, None], (L, 128))

    norm_one = first_norm(flip, states, vectors)
    tokens_one = first_norm(flip, states_other, vectors, tie(norm_one, two))

    zero_bias = jnp.zeros((head_width,), f32)
    score_scale = HD**-0.5
    scale = jnp.where(jnp.arange(3 * head_width) < head_width, score_scale, 1.0).astype(bf16)
    split = local_rows // QT * QT
    later = L - split
    over = local_rows - split

    def project(matrix, q_add, v_add):
        projected = jnp.dot(tokens_one, matrix, preferred_element_type=f32)
        add = jnp.concatenate([q_add.astype(f32), zero_bias, v_add.astype(f32)])
        return (projected + add[None]).astype(bf16) * scale[None]

    table = jnp.stack(
        [(dp ^ s) * 4 + (col ^ j) for s in range(4) for j in range(4)]
        + [a * 4 + col for a in range(4)]
        + [dp ^ s for s in range(4)]
        + [col ^ b for b in range(4)]
        + [row]
    ).astype(jnp.int32)
    loss_scale = all_clips * L * width / 2.0
    factor = (loss_scale * 2.0 / (valid_total * width)).reshape(1)
    valid = valid[:, None]
    packed_near = tie(project(qkv_near, q_bias, v_bias), table, factor, valid)
    cut_at = two.shape[0] // 32 * 16
    two_x, two_y = tie(two_x, packed_near), tie(two_y, packed_near)
    two_low, two_high = over_dp(two_y[:cut_at], 1), over_dp(two_x[cut_at:], 2)
    one_give = jnp.concatenate([slab[:unit_rows_total], two[:unit_rows_total]], axis=0)
    one = over_col(tie(one_give, states_other), 1)
    turned = lax.optimization_barrier((tokens_one.T, packed_near))[0]
    near_late, near_late_lse = attend(
        tie(packed_near, two_x, two_y, one, turned), key_bias, split, later
    )
    two_low, two_high = tie(two_low, near_late), tie(two_high, near_late)
    two_all = jnp.concatenate([two, two_x, two_y, two_low, two_high], axis=0)
    two_theirs = over_row(two_all)
    near_other = over_col(near_late[over:], 1)
    one_x, one_y = over_dp(one, 1), over_dp(one, 2)
    one_other = over_row(tie(one, near_late))
    near_soon, near_soon_lse = attend(
        tie(packed_near, two_all, near_late, one), key_bias, 0, split
    )
    two_theirs = tie(two_theirs, near_soon, near_other)
    qkv_far = far_qkv(places, two_all, two_theirs, unit_rows_total, width)
    far_small = two_all[small_at : small_at + small.shape[0]]
    packed_far = project(qkv_far, far_small[4], far_small[5])
    packed_far = tie(packed_far, one, near_other)
    far_late, far_late_lse = attend(packed_far, key_bias, split, later)
    far_other = over_col(far_late[over:], 1)
    one_x, one_y = tie(one_x, far_late), tie(one_y, far_late)
    cut_at = one.shape[0] // 2
    one_low, one_high = over_dp(one_y[:cut_at], 1), over_dp(one_x[cut_at:], 2)
    one_theirs = [over_row(one_x), over_row(one_y)]
    far_soon, far_soon_lse = attend(
        tie(packed_far, one_x, one_y, far_late, one_other), key_bias, 0, split
    )
    one_low, one_high = tie(one_low, far_soon, far_other), tie(one_high, far_soon, far_other)
    one_mine = [one, one_x, one_y, one_low, one_high]
    one_theirs = [one_other, *one_theirs, over_row(one_low), over_row(one_high)]
    at = unit_rows_total + small_at
    smalls = jnp.stack(
        [small, one[small_at : small_at + 16], two_all[small_at : small_at + 16], one[at : at + 16]]
    ).astype(f32)
    (
        attended_rows,
        outputs,
        hidden,
        grad_pre,
        norm_two,
        grad_low,
        mid_low,
        grad_mid,
        up_own,
        up_give,
        hidden_sum,
        sums,
    ) = middle_block(
        table,
        factor,
        states,
        teacher,
        valid,
        vectors,
        smalls,
        (
            w_fc1,
            fc1_other,
            w_fc2,
            fc2_other,
            w_proj,
            proj_other,
            two_all,
            two_theirs,
            *one_mine,
            *one_theirs,
            near_soon,
            near_late,
            near_other,
            far_soon,
            far_late,
            far_other,
        ),
    )
    up_far = over_col(up_give, 1)

    def joined(kept, taken):
        return (kept.astype(f32) + taken.astype(f32)).astype(bf16)

    give_fc2 = over_row(dot_tn(grad_low[:, half:], hidden).astype(bf16))
    give_fc1 = over_row(dot_tn(norm_two[:, half:], grad_pre).astype(bf16))
    give_proj = over_row(dot_tn(attended_rows, mid_low[:, half:]).astype(bf16))
    kept_proj = dot_tn(attended_rows, mid_low[:, :half])

    def plane_first(wide):
        keep_x, give_x, keep_y, give_y = wide
        return (keep_x, keep_y), (give_x, give_y), (over_dp(give_x, 1), over_dp(give_y, 2))

    def plane_second(keep, taken):
        shape = ((keep[0].shape[0] // 2, keep[0].shape[1]), bf16)
        keep_x, give_x, keep_y, give_y = on_chip(
            plane_sum_kernel, [shape] * 4, "plane_sum", keep[0], taken[0], keep[1], taken[1]
        )
        return (keep_x, keep_y), (give_x, give_y), (over_dp(give_x, 2), over_dp(give_y, 1))

    def cols_out(keep, taken, rows):
        blocks = on_chip(
            cols_out_kernel,
            [((rows, sub), bf16)] * 4,
            "cols_out",
            *(places, keep[0], taken[0], keep[1], taken[1]),
            tables=1,
        )
        return blocks, [over_col(blocks[j], j) for j in (1, 2, 3)]

    def all_tied(values, *others):
        return [tie(v, *others) for v in values]

    wide = wide_grads(places, grad_low, hidden, give_fc2)
    fc2_keep, fc2_give, fc2_taken = plane_first(wide)
    wide = wide_grads(
        places, tie(norm_two, *fc2_give), grad_pre, give_fc1, (kept_proj, give_proj)
    )
    fc1_keep, fc1_give, fc1_taken = plane_first(wide)

    packed_near = tie(packed_near, *fc2_give, *fc1_give)
    part_near = attend_back(packed_near, key_bias, near_soon_lse, near_soon, up_own, None, 0, 0)
    fc2_keep, fc2_give, fc2_taken = plane_second(fc2_keep, all_tied(fc2_taken, part_near[0]))

    packed_far = tie(packed_far, *fc2_give, part_near[0])
    part_far = attend_back(
        packed_far, key_bias, far_soon_lse, far_soon, up_own, None, head_width, 0
    )
    fc2_blocks, fc2_cols = cols_out(fc2_keep, all_tied(fc2_taken, part_far[0]), 2 * sub)
    fc1_keep, fc1_give, fc1_taken = plane_second(fc1_keep, all_tied(fc1_taken, part_far[0]))

    packed_near = tie(packed_near, *fc2_blocks, *fc1_give)
    grad_near, near_sums = attend_back(
        packed_near, key_bias, near_late_lse, near_late, up_own, up_far, 0, split, part_near
    )
    fc2_cols = all_tied(fc2_cols, grad_near)
    fc1_blocks, fc1_cols = cols_out(
        fc1_keep, all_tied(fc1_taken, grad_near, *fc2_cols), 2 * sub + 2 * part_rows
    )
    near_tied = tie(grad_near, *fc1_blocks)
    near_row = over_row(dot_tn(tokens_one[:, half:], near_tied).astype(bf16))
    wide_near = joined(dot_tn(tokens_one[:, :half], near_tied), near_row)
    deep = half // 4
    near_give = jnp.concatenate([cut(wide_near, quarter(s), deep) for s in (1, 3)], axis=0)
    near_taken = over_dp(near_give, 1)

    packed_far = tie(packed_far, near_give, *fc1_blocks, *fc2_cols)
    grad_far, far_sums = attend_back(
        packed_far, key_bias, far_late_lse, far_late, up_own, up_far, head_width, split, part_far
    )

    norm_own, norm_give, norm_sums = token_back(
        flip, grad_near, grad_far, qkv_near, qkv_far, states, states_other
    )
    norm_taken = over_col(norm_give, 1)
    columns, slots = grad_far.shape[1], 2 * VECTORS
    vec_keep, row_give, kept = on_chip(
        far_grads_kernel,
        [((VECTORS, half), f32), ((half + slots, columns), bf16), ((half, columns), f32)],
        "far_grads",
        *(turned, tie(grad_far, norm_give, near_taken, *fc1_cols), sums, hidden_sum, norm_sums, near_sums, far_sums),
    )
    row_taken = over_row(row_give)
    fc1_cols = all_tied(fc1_cols, row_give)
    mine_rows = fc2_blocks[0].shape[0] + fc1_blocks[0].shape[0]
    (mine,) = on_chip(
        mine_kernel,
        [((mine_rows, sub), bf16)],
        "mine",
        *(fc2_blocks[0], *fc2_cols, fc1_blocks[0], *fc1_cols),
    )
    mine_x = over_dp(mine, 1)
    near_own, far_own, vec_sum, *plane_give = on_chip(
        after_row_kernel,
        [((deep, columns), f32)] * 2
        + [((VECTORS, half), f32)]
        + [((deep + slots + (deep if s == 2 else 0), columns), bf16) for s in (1, 2, 3)],
        "after_row",
        *(places, kept, tie(row_taken, mine), vec_keep, wide_near, tie(near_taken, mine)),
        tables=1,
    )
    plane_taken = [over_dp(plane_give[s - 1], s) for s in (1, 2, 3)]
    mine_two = jnp.concatenate([mine, tie(mine_x, *plane_give)], axis=0)
    plane_taken = all_tied(plane_taken, mine_two, norm_taken)
    near_own, vec_sum, col_give, vec_give = on_chip(
        after_plane_kernel,
        [
            ((deep, columns), f32),
            ((VECTORS, half), f32),
            ((deep + slots, columns), bf16),
            ((slots, half), bf16),
        ],
        "after_plane",
        *(near_own, far_own, vec_sum, *plane_taken),
    )
    mine_y = over_dp(tie(mine_two, col_give), 2)
    col_taken = [over_col(vec_give, 1), over_col(col_give, 2), over_col(vec_give, 3)]
    norm_taken = tie(norm_taken, col_give)
    grad_states = last_norm(flip, norm_own, norm_taken, states, grad_mid, vectors)

    qkv_mine, vec_total = on_chip(
        after_cols_kernel,
        [((deep, columns), bf16), ((VECTORS, half), f32)],
        "after_cols",
        *(near_own, vec_sum, *all_tied(col_taken, grad_states)),
    )
    qkv_back = [over_dp(qkv_mine, s) for s in (1, 2, 3)]
    fc2_grad, fc1_grad, proj_grad = finish(places, [mine_two, tie(mine_y, qkv_mine)], part_rows)
    qkv_grad = finish_qkv(places, [qkv_mine, *all_tied(qkv_back, fc2_grad)]).transpose(1, 0, 2)

    fc1_bias_grad = lax.dynamic_index_in_dim(vec_total[6:14].reshape(4, 4, sub), col, 1, False)
    loss_value = jnp.sum(vec_total[16]) / (valid_total * width)
    return (
        outputs,
        loss_value,
        grad_states,
        vec_total[4],
        vec_total[5],
        qkv_grad,
        vec_total[14, :head_width],
        vec_total[14, head_width:],
        proj_grad,
        vec_total[2],
        vec_total[0],
        vec_total[1],
        fc1_grad,
        fc1_bias_grad.reshape(span),
        fc2_grad,
        vec_total[3],
    )


def solution(mesh):
    sizes = (mesh.shape["dp"], mesh.shape["row"], mesh.shape["col"])
    body = local_paired if sizes == PAIRED_MESH else local_general
    in_specs = (
        P(("dp", "row", "col"), None),
        P("row"),
        P("row"),
        P("row", None, "col"),
        P("col"),
        P("col"),
        P("col", "row"),
        P("row"),
        P("row"),
        P("row"),
        P("row", "col"),
        P("col"),
        P("col", "row"),
        P("row"),
        P(("dp", "row", "col"), None),
        P(),
        P(),
    )
    out_specs = (
        P(("dp", "row", "col"), None),
        P(),
        P(("dp", "row", "col"), None),
        P("row"),
        P("row"),
        P("row", None, "col"),
        P("col"),
        P("col"),
        P("col", "row"),
        P("row"),
        P("row"),
        P("row"),
        P("row", "col"),
        P("col"),
        P("col", "row"),
        P("row"),
    )
    return jax.shard_map(body, mesh=mesh, in_specs=in_specs, out_specs=out_specs, check_vma=False)
```

```python
import functools

import jax
import jax.numpy as jnp
from jax import lax
from jax.experimental import pallas as pl
from jax.experimental.pallas import tpu as pltpu
from jax.sharding import PartitionSpec as P

HD = 64
L = 1568


EPSILON = 1e-06
MASKED = -1e30
ROOT_HALF = 0.7071067811865476
DENSITY_FACTOR = 0.3989422804014327


def normalize(values, factor, offset):
    centered = values - jnp.mean(values, axis=-1, keepdims=True)
    spread = lax.rsqrt(jnp.mean(centered * centered, axis=-1, keepdims=True) + EPSILON)
    normal = centered * spread
    return (normal * factor + offset, normal, spread)


def norm_back(upstream, normal, spread, factor):
    inner = upstream * factor
    center_term = jnp.mean(inner, axis=-1, keepdims=True)
    slope_term = jnp.mean(inner * normal, axis=-1, keepdims=True)
    back = spread * (inner - center_term - normal * slope_term)
    return (back, jnp.sum(upstream * normal, axis=0), jnp.sum(upstream, axis=0))


def gelu_value(values):
    return values * (0.5 * (1.0 + lax.erf(values * ROOT_HALF)))


def gelu_slope(values):
    normal_cdf = 0.5 * (1.0 + lax.erf(values * ROOT_HALF))
    return normal_cdf + values * jnp.exp(-0.5 * values * values) * DENSITY_FACTOR


def masked_scores(queries, key_rows, length, score_scale):
    logits = (
        jnp.einsum("ihd,jhd->hij", queries, key_rows, preferred_element_type=jnp.float32)
        * score_scale
    )
    keep = jnp.arange(key_rows.shape[0]) < length
    return jnp.where(keep[None, None, :], logits, MASKED)


def attend_clip(packed, length, score_scale):
    half_span = packed.shape[0] // 2
    key_rows = packed[:, 1]
    value_rows = packed[:, 2]
    pieces = []
    totals = []
    for block_index in range(2):
        queries = packed[block_index * half_span : (block_index + 1) * half_span, 0]
        logits = masked_scores(queries, key_rows, length, score_scale)
        peak = jnp.max(logits, axis=-1, keepdims=True)
        total = peak + jnp.log(jnp.sum(jnp.exp(logits - peak), axis=-1, keepdims=True))
        weights = jnp.exp(logits - total).astype(jnp.bfloat16)
        pieces.append(
            jnp.einsum("hij,jhd->ihd", weights, value_rows, preferred_element_type=jnp.float32)
        )
        totals.append(total[..., 0])
    return (jnp.concatenate(pieces, 0), jnp.concatenate(totals, 1))


def attend_clip_back(packed, length, totals, upstream, score_scale):
    half_span = packed.shape[0] // 2
    key_rows = packed[:, 1]
    value_rows = packed[:, 2]
    grad_keys = jnp.zeros(key_rows.shape, jnp.float32)
    grad_values = jnp.zeros(value_rows.shape, jnp.float32)
    grad_queries = []
    for block_index in range(2):
        first = block_index * half_span
        queries = packed[first : first + half_span, 0]
        logits = masked_scores(queries, key_rows, length, score_scale)
        probs = jnp.exp(logits - totals[:, first : first + half_span][..., None])
        incoming = upstream[first : first + half_span]
        grad_values = grad_values + jnp.einsum(
            "hij,ihd->jhd", probs.astype(jnp.bfloat16), incoming, preferred_element_type=jnp.float32
        )
        grad_probs = jnp.einsum(
            "ihd,jhd->hij", incoming, value_rows, preferred_element_type=jnp.float32
        )
        grad_logits = (
            probs * (grad_probs - jnp.sum(probs * grad_probs, axis=-1, keepdims=True))
        ).astype(jnp.bfloat16)
        grad_queries.append(
            jnp.einsum("hij,jhd->ihd", grad_logits, key_rows, preferred_element_type=jnp.float32)
            * score_scale
        )
        grad_keys = (
            grad_keys
            + jnp.einsum("hij,ihd->jhd", grad_logits, queries, preferred_element_type=jnp.float32)
            * score_scale
        )
    return jnp.stack([jnp.concatenate(grad_queries, 0), grad_keys, grad_values], axis=1)


def local_general(
    states,
    ln1_gain,
    ln1_bias,
    w_qkv,
    q_bias,
    v_bias,
    w_proj,
    proj_bias,
    ln2_gain,
    ln2_bias,
    w_fc1,
    fc1_bias,
    w_fc2,
    fc2_bias,
    teacher,
    loss_mask,
    lengths,
):
    row_count = lax.axis_size("row")
    col_count = lax.axis_size("col")
    col_index = lax.axis_index("col")
    group_index = lax.axis_index("dp") * row_count + lax.axis_index("row")
    local_rows = states.shape[0]
    width = states.shape[1]
    group_rows = local_rows * col_count
    clip_count = group_rows // L
    head_width = w_qkv.shape[2]
    heads_here = head_width // HD
    hidden_width = w_fc1.shape[1]
    score_scale = HD ** (-0.5)
    vectors = jnp.stack([ln1_gain, ln1_bias, proj_bias, ln2_gain, ln2_bias, fc2_bias])
    qkv_full, proj_full, fc1_full, fc2_full, vector_full = (
        lax.all_gather(w_qkv, "row", axis=0, tiled=True),
        lax.all_gather(w_proj, "row", axis=1, tiled=True),
        lax.all_gather(w_fc1, "row", axis=0, tiled=True),
        lax.all_gather(w_fc2, "row", axis=1, tiled=True),
        lax.all_gather(vectors, "row", axis=1, tiled=True),
    )
    vector_full = vector_full.astype(jnp.float32)
    gain_one = vector_full[0]
    shift_one = vector_full[1]
    bias_proj = vector_full[2]
    gain_two = vector_full[3]
    shift_two = vector_full[4]
    bias_two = vector_full[5]
    all_clips = lengths.shape[0]
    valid_all = (
        loss_mask.reshape(all_clips, L) * (jnp.arange(L)[None, :] < lengths[:, None])
    ).astype(jnp.float32)
    valid_total = jnp.maximum(jnp.sum(valid_all), 1.0)
    first_row = (group_index * col_count + col_index) * local_rows
    valid = lax.dynamic_slice_in_dim(valid_all.reshape(all_clips * L), first_row, local_rows)
    my_lengths = lax.dynamic_slice_in_dim(lengths, group_index * clip_count, clip_count)
    inputs = states.astype(jnp.float32)
    norm_one, unit_one, spread_one = normalize(inputs, gain_one, shift_one)
    norm_one = norm_one.astype(jnp.bfloat16)
    tokens_one = lax.all_gather(norm_one, "col", axis=0, tiled=True)
    qkv_matrix = qkv_full.reshape(width, 3 * head_width)
    projected = jnp.dot(tokens_one, qkv_matrix, preferred_element_type=jnp.float32).reshape(
        group_rows, 3, head_width
    )
    bias_rows = jnp.stack(
        [
            q_bias.astype(jnp.float32),
            jnp.zeros((head_width,), jnp.float32),
            v_bias.astype(jnp.float32),
        ]
    )
    packed = (projected + bias_rows[None]).astype(jnp.bfloat16)
    clips_packed = packed.reshape(clip_count, L, 3, heads_here, HD)
    attended, totals = lax.map(
        lambda element: attend_clip(element[0], element[1], score_scale), (clips_packed, my_lengths)
    )
    attended = attended.reshape(group_rows, head_width).astype(jnp.bfloat16)
    proj_whole, qkv_whole = (
        lax.all_gather(proj_full, "col", axis=0, tiled=True),
        lax.all_gather(qkv_full, "col", axis=2, tiled=True),
    )
    attended_rows = lax.all_to_all(attended, "col", split_axis=0, concat_axis=1, tiled=True)
    middle = inputs + (
        jnp.dot(attended_rows, proj_whole, preferred_element_type=jnp.float32) + bias_proj
    )
    norm_two, unit_two, spread_two = normalize(middle, gain_two, shift_two)
    norm_two = norm_two.astype(jnp.bfloat16)
    fc1_whole, fc2_whole, fc1_bias_whole = (
        lax.all_gather(fc1_full, "col", axis=1, tiled=True),
        lax.all_gather(fc2_full, "col", axis=0, tiled=True),
        lax.all_gather(fc1_bias, "col", axis=0, tiled=True),
    )
    hidden_pre = jnp.dot(
        norm_two, fc1_whole, preferred_element_type=jnp.float32
    ) + fc1_bias_whole.astype(jnp.float32)
    hidden = gelu_value(hidden_pre).astype(jnp.bfloat16)
    outputs = middle + (jnp.dot(hidden, fc2_whole, preferred_element_type=jnp.float32) + bias_two)
    differ = outputs - teacher.astype(jnp.float32)
    numerator = jnp.sum(valid[:, None] * differ * differ)
    loss_scale = all_clips * L * width / 2.0
    grad_out = loss_scale * 2.0 / (valid_total * width) * valid[:, None] * differ
    grad_low = grad_out.astype(jnp.bfloat16)
    grad_hidden = jnp.dot(grad_low, fc2_whole.T, preferred_element_type=jnp.float32)
    grad_pre = (grad_hidden * gelu_slope(hidden_pre)).astype(jnp.bfloat16)
    wide_fc2 = jnp.dot(hidden.T, grad_low, preferred_element_type=jnp.float32)
    wide_fc1 = jnp.dot(norm_two.T, grad_pre, preferred_element_type=jnp.float32)
    fc1_grad_part, fc2_grad_part = (
        lax.psum_scatter(
            wide_fc1.astype(jnp.bfloat16), "col", scatter_dimension=1, tiled=True
        ).astype(jnp.float32),
        lax.psum_scatter(
            wide_fc2.astype(jnp.bfloat16), "col", scatter_dimension=0, tiled=True
        ).astype(jnp.float32),
    )
    fc1_bias_sum = jnp.sum(grad_pre, axis=0, dtype=jnp.float32)
    grad_norm_two = jnp.dot(grad_pre, fc1_whole.T, preferred_element_type=jnp.float32)
    back_two, gain_two_grad, shift_two_grad = norm_back(
        grad_norm_two, unit_two, spread_two, gain_two
    )
    grad_mid = grad_out + back_two
    mid_low = grad_mid.astype(jnp.bfloat16)
    wide_proj = jnp.dot(attended_rows.T, mid_low, preferred_element_type=jnp.float32)
    proj_grad_part = lax.psum_scatter(
        wide_proj.astype(jnp.bfloat16), "col", scatter_dimension=0, tiled=True
    )
    grad_attended_rows = jnp.dot(mid_low, proj_whole.T, preferred_element_type=jnp.float32).astype(
        jnp.bfloat16
    )
    grad_attended = lax.all_to_all(
        grad_attended_rows, "col", split_axis=1, concat_axis=0, tiled=True
    )
    grads_packed = lax.map(
        lambda element: attend_clip_back(
            element[0], element[1], element[2], element[3], score_scale
        ),
        (clips_packed, my_lengths, totals, grad_attended.reshape(clip_count, L, heads_here, HD)),
    )
    grads_packed = grads_packed.reshape(group_rows, 3 * head_width).astype(jnp.bfloat16)
    qkv_grad_part = jnp.dot(tokens_one.T, grads_packed, preferred_element_type=jnp.float32).reshape(
        width, 3, head_width
    )
    bias_sums = jnp.sum(grads_packed.reshape(group_rows, 3, head_width), axis=0, dtype=jnp.float32)
    grads_rows = lax.all_to_all(
        grads_packed.reshape(group_rows, 3, head_width),
        "col",
        split_axis=0,
        concat_axis=2,
        tiled=True,
    )
    grad_norm_one = jnp.dot(
        grads_rows.reshape(local_rows, 3 * width),
        qkv_whole.reshape(width, 3 * width).T,
        preferred_element_type=jnp.float32,
    )
    back_one, gain_one_grad, shift_one_grad = norm_back(
        grad_norm_one, unit_one, spread_one, gain_one
    )
    grad_states = (grad_mid + back_one).astype(jnp.bfloat16)
    proj_bias_grad = jnp.sum(mid_low, axis=0, dtype=jnp.float32)
    fc2_bias_grad = jnp.sum(grad_low, axis=0, dtype=jnp.float32)
    token_vectors = jnp.stack(
        [
            gain_one_grad,
            shift_one_grad,
            proj_bias_grad,
            gain_two_grad,
            shift_two_grad,
            fc2_bias_grad,
        ]
    )
    head_vectors = lax.dynamic_update_slice(
        jnp.zeros((2, width), jnp.float32),
        jnp.stack([bias_sums[0], bias_sums[2]]),
        (0, col_index * head_width),
    )
    token_sums, head_sums, fc1_sums, loss_sum = lax.psum(
        (token_vectors, head_vectors, fc1_bias_sum, numerator), ("dp", "row", "col")
    )
    qkv_rows, proj_cols, fc1_rows, fc2_cols = (
        lax.psum_scatter(
            qkv_grad_part.astype(jnp.bfloat16), "row", scatter_dimension=0, tiled=True
        ).astype(jnp.float32),
        lax.psum_scatter(proj_grad_part, "row", scatter_dimension=1, tiled=True).astype(
            jnp.float32
        ),
        lax.psum_scatter(
            fc1_grad_part.astype(jnp.bfloat16), "row", scatter_dimension=0, tiled=True
        ).astype(jnp.float32),
        lax.psum_scatter(
            fc2_grad_part.astype(jnp.bfloat16), "row", scatter_dimension=1, tiled=True
        ).astype(jnp.float32),
    )
    qkv_grad, proj_grad, fc1_grad, fc2_grad = (
        lax.psum(qkv_rows.astype(jnp.bfloat16), "dp").astype(jnp.float32),
        lax.psum(proj_cols.astype(jnp.bfloat16), "dp").astype(jnp.float32),
        lax.psum(fc1_rows.astype(jnp.bfloat16), "dp").astype(jnp.float32),
        lax.psum(fc2_cols.astype(jnp.bfloat16), "dp").astype(jnp.float32),
    )
    half_width = width // row_count
    token_part = lax.dynamic_slice_in_dim(
        token_sums, lax.axis_index("row") * half_width, half_width, 1
    )
    head_part = lax.dynamic_slice_in_dim(head_sums, col_index * head_width, head_width, 1)
    fc1_part = lax.dynamic_slice_in_dim(fc1_sums, col_index * hidden_width, hidden_width, 0)
    loss_value = loss_sum / (valid_total * width)
    return (
        outputs.astype(jnp.bfloat16),
        loss_value,
        grad_states,
        token_part[0],
        token_part[1],
        qkv_grad,
        head_part[0],
        head_part[1],
        proj_grad,
        token_part[2],
        token_part[3],
        token_part[4],
        fc1_grad,
        fc1_part,
        fc2_grad,
        token_part[5],
    )


PAIRED_MESH = (4, 2, 4)
GROUP = 4


def small_cost(flops):
    return pl.CostEstimate(flops=flops, bytes_accessed=0, transcendentals=0)
QT = 128


def dot_nn(a, b):
    return lax.dot_general(a, b, (((1,), (0,)), ((), ())), preferred_element_type=jnp.float32)


def dot_nt(a, b):
    return lax.dot_general(a, b, (((1,), (1,)), ((), ())), preferred_element_type=jnp.float32)


def dot_tn(a, b):
    return lax.dot_general(a, b, (((0,), (0,)), ((), ())), preferred_element_type=jnp.float32)


def head_stack(values, zero):
    lane_head = lax.broadcasted_iota(jnp.int32, values.shape, 1) // HD
    return jnp.concatenate([jnp.where(lane_head == h, values, zero) for h in range(GROUP)], axis=0)


def head_unstack(wide, count):
    return jnp.concatenate(
        [wide[h * HD : (h + 1) * HD, h * count : (h + 1) * count] for h in range(GROUP)], axis=0
    ).T


def tiles_of(rows, tile):
    full = rows // QT

    @pl.loop(0, full)
    def _(index):
        tile(pl.multiple_of(index * QT, QT), QT, index)

    if rows > full * QT:
        tile(full * QT, rows - full * QT, full)


def attend_kernel(first, packed_ref, bias_ref, out_ref, lse_ref, vt_ref):
    width = GROUP * HD
    vt_ref[...] = packed_ref[:, 2 * width : 3 * width].T

    def tile(start, count, index):
        cols = GROUP * count
        stacked = head_stack(
            packed_ref[pl.ds(first + start, count), 0:width], jnp.zeros((), jnp.bfloat16)
        )
        half = packed_ref.shape[0] // 2

        def scores_of(at):
            bias = jnp.concatenate([bias_ref[at : at + half, :]] * (cols // 128), axis=1)
            return dot_nt(packed_ref[at : at + half, width : 2 * width], stacked) + bias

        scores, later = scores_of(0), scores_of(half)
        first_peak = jnp.max(scores, axis=0, keepdims=True)
        weights = jnp.exp(scores - first_peak)
        total = jnp.sum(weights, axis=0, keepdims=True)
        wide = dot_nn(vt_ref[:, 0:half], weights.astype(jnp.bfloat16))
        peak = jnp.maximum(first_peak, jnp.max(later, axis=0, keepdims=True))
        weights = jnp.exp(later - peak)
        scale = jnp.exp(first_peak - peak)
        total = total * scale + jnp.sum(weights, axis=0, keepdims=True)
        wide = wide * scale + dot_nn(vt_ref[:, half:], weights.astype(jnp.bfloat16))
        wide = wide * (1.0 / total)
        out_ref[pl.ds(start, count), :] = head_unstack(wide, count).astype(jnp.bfloat16)
        lse_ref[index, :, 0:cols] = jnp.broadcast_to(peak + jnp.log(total), (8, cols))

    tiles_of(out_ref.shape[0], tile)


def attend_back_kernel(
    first, lane, last, packed_ref, bias_ref, lse_ref, att_ref, up_own_ref, up_far_ref, *refs
):
    width = GROUP * HD
    lanes = slice(lane, lane + width)
    own_rows = up_own_ref.shape[0]
    if last:
        dq_in, dk_in, dv_in, out_ref, sum_ref, kt_ref, up_ref, ds_ref, dk_ref, dv_ref = refs
        dk_ref[...] = dk_in[...]
        dv_ref[...] = dv_in[...]
        out_ref[0:first, 0:width] = dq_in[...]
        rows = out_ref.shape[0] - first
        up_ref[0 : own_rows - first, :] = up_own_ref[first:own_rows, lanes]
        up_ref[own_rows - first :, :] = up_far_ref[:, lanes]
    else:
        out_ref, dk_ref, dv_ref, kt_ref, up_ref, ds_ref = refs
        dk_ref[...] = jnp.zeros_like(dk_ref)
        dv_ref[...] = jnp.zeros_like(dv_ref)
        rows = out_ref.shape[0]
        up_ref[...] = up_own_ref[0:rows, lanes]
    kt_ref[...] = packed_ref[:, width : 2 * width].T

    def tile(start, count, index):
        cols = GROUP * count
        zero = jnp.zeros((), jnp.bfloat16)
        up = up_ref[pl.ds(start, count), :]
        stacked = head_stack(packed_ref[pl.ds(first + start, count), 0:width], zero)
        up_stacked = head_stack(up, zero)
        product = head_stack(
            up.astype(jnp.float32) * att_ref[pl.ds(start, count), :].astype(jnp.float32),
            jnp.zeros((), jnp.float32),
        )
        high = product.astype(jnp.bfloat16)
        low = (product - high.astype(jnp.float32)).astype(jnp.bfloat16)
        ones = jnp.ones((8, width), jnp.bfloat16)
        delta = (dot_nt(ones, high) + dot_nt(ones, low))[0:1]
        half = packed_ref.shape[0] // 2

        def products(at):
            bias = jnp.concatenate([bias_ref[at : at + half, :]] * (cols // 128), axis=1)
            scores = dot_nt(packed_ref[at : at + half, width : 2 * width], stacked) + bias
            return scores, dot_nt(packed_ref[at : at + half, 2 * width : 3 * width], up_stacked)

        following = products(0)
        for at in (0, half):
            scores, slopes = following
            if not at:
                following = products(half)
            rows_here = slice(at, at + half)
            weights = jnp.exp(scores - lse_ref[index, 0:1, 0:cols])
            dv_ref[rows_here, :] += dot_nn(weights.astype(jnp.bfloat16), up_stacked)
            grad = (weights * (slopes - delta)).astype(jnp.bfloat16)
            ds_ref[rows_here, 0:cols] = grad
            dk_ref[rows_here, :] += dot_nn(grad, stacked)
        wide = dot_nn(kt_ref[...], ds_ref[:, 0:cols]) * (HD**-0.5)
        at = pl.ds(first + start if last else start, count)
        out_ref[at, 0:width] = head_unstack(wide, count).astype(jnp.bfloat16)

    tiles_of(rows, tile)
    if last:
        out_ref[:, width : 2 * width] = dk_ref[...].astype(jnp.bfloat16)
        out_ref[:, 2 * width : 3 * width] = dv_ref[...].astype(jnp.bfloat16)
        for k in range(3):
            part = out_ref[:, k * width : (k + 1) * width].astype(jnp.float32)
            sum_ref[:, k * width : (k + 1) * width] = jnp.sum(part, axis=0, keepdims=True)


def attend(packed, bias, first, rows):
    tokens, width = packed.shape[0], GROUP * HD
    tiles = -(-rows // QT)
    return pl.pallas_call(
        functools.partial(attend_kernel, first),
        out_shape=(
            jax.ShapeDtypeStruct((rows, width), jnp.bfloat16),
            jax.ShapeDtypeStruct((tiles, 8, GROUP * QT), jnp.float32),
        ),
        in_specs=[pl.BlockSpec(memory_space=pltpu.VMEM)] * 2,
        out_specs=[pl.BlockSpec(memory_space=pltpu.VMEM)] * 2,
        scratch_shapes=[pltpu.VMEM((width, tokens), jnp.bfloat16)],
        compiler_params=pltpu.CompilerParams(vmem_limit_bytes=32 << 20),
        cost_estimate=pl.CostEstimate(
            flops=2 * rows * tokens * width * 4, bytes_accessed=6 << 20, transcendentals=0
        ),
        name="attend",
    )(packed, bias)


def attend_back(packed, bias, lse, att, up_own, up_far, lane, first, before=None):
    tokens, width = packed.shape[0], GROUP * HD
    rows = att.shape[0]
    total = jax.ShapeDtypeStruct((tokens, width), jnp.float32)
    vmem = pl.BlockSpec(memory_space=pltpu.VMEM)
    scratch = [
        pltpu.VMEM((width, tokens), jnp.bfloat16),
        pltpu.VMEM((rows, width), jnp.bfloat16),
        pltpu.VMEM((tokens, GROUP * QT), jnp.bfloat16),
    ]
    if before is None:
        extra = ()
        out_shape = (jax.ShapeDtypeStruct((rows, width), jnp.bfloat16), total, total)
        up_far = up_own
    else:
        extra = before
        out_shape = (
            jax.ShapeDtypeStruct((tokens, 3 * width), jnp.bfloat16),
            jax.ShapeDtypeStruct((1, 3 * width), jnp.float32),
        )
        scratch += [pltpu.VMEM((tokens, width), jnp.float32)] * 2
    return pl.pallas_call(
        functools.partial(attend_back_kernel, first, lane, before is not None),
        out_shape=out_shape,
        in_specs=[vmem] * (6 + len(extra)),
        out_specs=(vmem,) * len(out_shape),
        scratch_shapes=scratch,
        compiler_params=pltpu.CompilerParams(vmem_limit_bytes=52 << 20),
        cost_estimate=pl.CostEstimate(
            flops=4 * rows * tokens * width * 4, bytes_accessed=10 << 20, transcendentals=0
        ),
        name="attend_back",
    )(packed, bias, lse, att, up_own, up_far, *extra)


FF_CHUNK = 512
ROWS = 112


def rows_of(total, body):
    @pl.loop(0, total // ROWS)
    def _(index):
        body(pl.ds(pl.multiple_of(index * ROWS, ROWS), ROWS))


def unit_rows(values):
    centered = values - jnp.mean(values, axis=-1, keepdims=True)
    spread = lax.rsqrt(jnp.mean(centered * centered, axis=-1, keepdims=True) + EPSILON)
    return centered * spread, spread


def middle_kernel(
    table_ref,
    factor_ref,
    input_ref,
    target_ref,
    valid_ref,
    vector_ref,
    small_ref,
    fc1_own,
    fc1_other,
    fc2_own,
    fc2_other,
    proj_own,
    proj_other,
    two_mine,
    two_theirs,
    *refs,
):
    one_mine, one_theirs, att_parts, refs = refs[:5], refs[5:10], refs[10:16], refs[16:]
    (
        att_hbm,
        out_hbm,
        hidden_hbm,
        pre_hbm,
        norm_hbm,
        grad_low_hbm,
        mid_low_ref,
        grad_mid_ref,
        up_own_ref,
        up_give_ref,
        hidden_sum_ref,
        sums_ref,
        fc1_v,
        fc2_v,
        proj_v,
        middle_v,
        back_v,
        out_ref,
        hidden_ref,
        pre_ref,
        norm_ref,
        grad_low_ref,
        att_ref,
        sem_one,
        sem_two,
        sem_proj,
        sem_att,
        sem_out,
    ) = refs
    stores = [
        pltpu.make_async_copy(source, target, sem_out.at[i])
        for i, (source, target) in enumerate(
            (
                (norm_ref, norm_hbm),
                (hidden_ref, hidden_hbm),
                (out_ref, out_hbm),
                (grad_low_ref, grad_low_hbm),
                (pre_ref, pre_hbm),
                (att_ref, att_hbm),
            )
        )
    ]
    f32, bf16 = jnp.float32, jnp.bfloat16
    total_rows = input_ref.shape[0]
    half = fc1_own.shape[0]
    sub = fc1_own.shape[1] // 4
    heads = proj_own.shape[0]
    part = heads // 4
    hidden_total = hidden_ref.shape[1]
    chunks = hidden_total // FF_CHUNK
    unit = half + 2 * sub + 2 * part + 16

    def fc1_copy(source, side, at):
        lanes = pl.ds(pl.multiple_of(at * sub, sub), sub)
        pltpu.make_async_copy(
            source, fc1_v.at[side * half : (side + 1) * half, lanes], sem_one.at[at // 2]
        ).start()

    def fc2_copy(source, side, i, at):
        lane = side * half + i * sub
        pltpu.make_async_copy(
            source, fc2_v.at[pl.ds(pl.multiple_of(at * sub, sub), sub), lane : lane + sub], sem_two
        ).start()

    sources = []
    for s in range(4):
        step = two_mine.shape[0] // 4
        sources.append((s, 2, two_mine, two_theirs, s * step))
        low, high = (3, 4) if s == 3 else (s, s)
        sources.append((s, 1, one_mine[low], one_theirs[low], 0))
        sources.append((s, 3, one_mine[high], one_theirs[high], 0 if s == 3 else unit))

    early_rows = att_parts[0].shape[0]
    for at in range(2):
        soon, late, other = att_parts[3 * at : 3 * at + 3]
        lanes = slice(2 * at * heads, (2 * at + 1) * heads)
        pltpu.make_async_copy(soon, att_ref.at[0:early_rows, lanes], sem_att).start()
        pltpu.make_async_copy(
            late.at[0 : total_rows - early_rows], att_ref.at[early_rows:total_rows, lanes], sem_att
        ).start()
        lanes = slice((2 * at + 1) * heads, (2 * at + 2) * heads)
        pltpu.make_async_copy(other, att_ref.at[:, lanes], sem_att).start()
    for side, ref in enumerate((proj_own, proj_other)):
        pltpu.make_async_copy(
            ref, proj_v.at[0:heads, side * half : (side + 1) * half], sem_proj
        ).start()
    for s, j, *refs, base in sources:
        rows = pl.ds(pl.multiple_of(j * heads + table_ref[20 + s] * part, part), part)
        for side in range(2):
            for i in range(2):
                low = base + half + 2 * sub + i * part
                lane = side * half + i * sub
                pltpu.make_async_copy(
                    refs[side].at[low : low + part, :], proj_v.at[rows, lane : lane + sub], sem_proj
                ).start()
    for a in range(4):
        for side, ref in enumerate((fc1_own, fc1_other)):
            fc1_copy(ref.at[:, a * sub : (a + 1) * sub], side, table_ref[16 + a])
    for s, j, *refs, base in sources:
        for side in range(2):
            fc1_copy(refs[side].at[base : base + half, :], side, table_ref[4 * s + j])
    for a in range(4):
        for side, ref in enumerate((fc2_own, fc2_other)):
            for i in range(2):
                fc2_copy(
                    ref.at[a * sub : (a + 1) * sub, i * sub : (i + 1) * sub], side, i, table_ref[16 + a]
                )
    for s, j, *refs, base in sources:
        for side in range(2):
            for i in range(2):
                low = base + half + i * sub
                fc2_copy(refs[side].at[low : low + sub, :], side, i, table_ref[4 * s + j])

    def lanes_of(i):
        return pl.ds(pl.multiple_of((table_ref[28] ^ i) * half, half), half)

    sums_ref[...] = jnp.zeros_like(sums_ref)

    pltpu.make_async_copy(att_ref, att_ref, sem_att).wait()
    stores[5].start()
    pltpu.make_async_copy(proj_v, proj_v, sem_proj).wait()
    for i in range(2):
        cols = slice(i * half, (i + 1) * half)
        middle_v[:, cols] = input_ref[:, lanes_of(i)].astype(f32) + (
            dot_nn(att_ref[...], proj_v[:, cols]) + vector_ref[2:3, cols]
        )

    @functools.partial(rows_of, total_rows)
    def _(rows):
        normal, _ = unit_rows(middle_v[rows, :])
        norm_ref[rows, :] = (normal * vector_ref[3:4, :] + vector_ref[4:5, :]).astype(bf16)

    stores[0].start()

    @pl.loop(0, chunks)
    def _(k):
        span = pl.ds(pl.multiple_of(k * FF_CHUNK, FF_CHUNK), FF_CHUNK)
        pltpu.make_async_copy(fc1_v.at[:, span], fc1_v.at[:, span], sem_one.at[k]).wait()
        a = k // 2
        bias = jnp.concatenate(
            [
                small_ref[table_ref[24 + 2 * (k % 2) + i], pl.ds(a, 1), :]
                for i in range(FF_CHUNK // sub)
            ],
            axis=1,
        )
        pre = dot_nn(norm_ref[...], fc1_v[:, span]) + bias
        cdf = 0.5 * (1.0 + lax.erf(pre * ROOT_HALF))
        hidden_ref[:, span] = (pre * cdf).astype(bf16)
        slope = cdf + pre * jnp.exp(-0.5 * pre * pre) * DENSITY_FACTOR
        pre_ref[:, span] = slope.astype(bf16)

    stores[1].start()
    pltpu.make_async_copy(fc2_v, fc2_v, sem_two).wait()
    for i in range(2):
        cols = slice(i * half, (i + 1) * half)
        total = middle_v[:, cols] + (dot_nn(hidden_ref[...], fc2_v[:, cols]) + vector_ref[5:6, cols])
        out_ref[:, lanes_of(i)] = total.astype(bf16)
        differ = total - target_ref[:, lanes_of(i)].astype(f32)
        weighted = valid_ref[...] * differ
        sums_ref[0:1, cols] = jnp.sum(weighted * differ, axis=0, keepdims=True)
        grad = factor_ref[0] * weighted
        grad_mid_ref[:, cols] = grad
        low = grad.astype(bf16)
        grad_low_ref[:, cols] = low
        sums_ref[1:2, cols] = jnp.sum(low.astype(f32), axis=0, keepdims=True)

    stores[2].start()
    stores[3].start()

    @pl.loop(0, chunks)
    def _(k):
        span = pl.ds(pl.multiple_of(k * FF_CHUNK, FF_CHUNK), FF_CHUNK)
        back = dot_nt(grad_low_ref[...], fc2_v[span, :])
        back = (back * pre_ref[:, span].astype(f32)).astype(bf16)
        pre_ref[:, span] = back
        hidden_sum_ref[0:1, span] = jnp.sum(back.astype(f32), axis=0, keepdims=True)

    stores[4].start()
    for i in range(2):
        cols = slice(i * half, (i + 1) * half)
        back_v[:, cols] = dot_nt(pre_ref[...], fc1_v[cols, :])

    @functools.partial(rows_of, total_rows)
    def _(rows):
        normal, spread = unit_rows(middle_v[rows, :])
        upstream = back_v[rows, :]
        inner = upstream * vector_ref[3:4, :]
        center = jnp.mean(inner, axis=-1, keepdims=True)
        slope = jnp.mean(inner * normal, axis=-1, keepdims=True)
        grad = grad_mid_ref[rows, :] + spread * (inner - center - normal * slope)
        grad_mid_ref[rows, :] = grad
        low = grad.astype(bf16)
        mid_low_ref[rows, :] = low
        sums_ref[2:3, :] += jnp.sum(upstream * normal, axis=0, keepdims=True)
        sums_ref[3:4, :] += jnp.sum(upstream, axis=0, keepdims=True)
        sums_ref[4:5, :] += jnp.sum(low.astype(f32), axis=0, keepdims=True)

    for j, (ref, at) in enumerate(((up_own_ref, 0), (up_give_ref, 0), (up_own_ref, 1), (up_give_ref, 1))):
        grad = dot_nt(mid_low_ref[...], proj_v[j * heads : (j + 1) * heads, :])
        ref[:, at * heads : (at + 1) * heads] = grad.astype(bf16)
    for store in stores:
        store.wait()


def middle_block(table, factor, inputs, target, valid, vectors, smalls, pieces):
    rows, width = inputs.shape
    hidden = 4 * pieces[0].shape[1]
    vmem = pl.BlockSpec(memory_space=pltpu.VMEM)
    smem = pl.BlockSpec(memory_space=pltpu.SMEM)
    anywhere = pl.BlockSpec(memory_space=pl.ANY)
    f32, bf16 = jnp.float32, jnp.bfloat16

    def result(columns, dtype):
        return jax.ShapeDtypeStruct((rows, columns), dtype)

    return pl.pallas_call(
        middle_kernel,
        out_shape=(
            result(width, bf16),
            result(width, bf16),
            result(hidden, bf16),
            result(hidden, bf16),
            result(width, bf16),
            result(width, bf16),
            result(width, bf16),
            result(width, f32),
            result(width // 2, bf16),
            result(width // 2, bf16),
            jax.ShapeDtypeStruct((1, hidden), f32),
            jax.ShapeDtypeStruct((8, width), f32),
        ),
        in_specs=[smem] * 2 + [vmem] * 5 + [anywhere] * len(pieces),
        out_specs=[anywhere] * 6 + [vmem] * 6,
        scratch_shapes=[
            pltpu.VMEM((width, hidden), bf16),
            pltpu.VMEM((hidden, width), bf16),
            pltpu.VMEM((width, width), bf16),
            pltpu.VMEM((rows, width), f32),
            pltpu.VMEM((rows, width), f32),
            pltpu.VMEM((rows, width), bf16),
            pltpu.VMEM((rows, hidden), bf16),
            pltpu.VMEM((rows, hidden), bf16),
            pltpu.VMEM((rows, width), bf16),
            pltpu.VMEM((rows, width), bf16),
            pltpu.VMEM((rows, width), bf16),
            pltpu.SemaphoreType.DMA((hidden // FF_CHUNK,)),
            pltpu.SemaphoreType.DMA,
            pltpu.SemaphoreType.DMA,
            pltpu.SemaphoreType.DMA,
            pltpu.SemaphoreType.DMA((6,)),
        ],
        compiler_params=pltpu.CompilerParams(vmem_limit_bytes=62 << 20),
        cost_estimate=pl.CostEstimate(
            flops=2 * rows * width * hidden, bytes_accessed=44 << 20, transcendentals=0
        ),
        name="middle_block",
    )(table, factor, inputs, target, valid, vectors, smalls, *pieces)


def swap(values, axis, mask, size):
    return lax.ppermute(values, axis, [(i, i ^ mask) for i in range(size)])


def over_row(values):
    return swap(values, "row", 1, 2)


def over_dp(values, mask):
    return swap(values, "dp", mask, 4)


def over_col(values, mask):
    return swap(values, "col", mask, 4)


def cut(values, index, size, axis=0):
    return lax.dynamic_slice_in_dim(values, index * size, size, axis)


def place(pieces, index_of, axis):
    size = pieces[0].shape[axis]
    shape = list(pieces[0].shape)
    shape[axis] = size * len(pieces)
    whole = jnp.zeros(shape, pieces[0].dtype)
    for s, piece in enumerate(pieces):
        whole = lax.dynamic_update_slice_in_dim(whole, piece, index_of(s) * size, axis)
    return whole


def copies(listed, sem_ref):
    for index, (source, target) in enumerate(listed):
        pltpu.make_async_copy(source, target, sem_ref.at[index]).start()
    for index, (source, target) in enumerate(listed):
        pltpu.make_async_copy(source, target, sem_ref.at[index]).wait()


def slab_kernel(places_ref, fc1_ref, fc2_ref, proj_ref, qkv_ref, small_ref, out_ref, sem_ref):
    half, sub = fc1_ref.shape[0], fc1_ref.shape[1] // 4
    part, deep = proj_ref.shape[0] // 4, half // 4
    mine = places_ref[0]
    fc2 = fc2_ref.at[pl.ds(pl.multiple_of(mine * sub, sub), sub)]
    proj = proj_ref.at[pl.ds(pl.multiple_of(mine * part, part), part)]
    listed = [(fc1_ref.at[:, pl.ds(pl.multiple_of(mine * sub, sub), sub)], half)]
    listed += [(fc2.at[:, i * sub : (i + 1) * sub], sub) for i in range(2)]
    listed += [(proj.at[:, i * sub : (i + 1) * sub], part) for i in range(2)]
    listed += [(small_ref, small_ref.shape[0])]
    rows = pl.ds(pl.multiple_of(mine * deep, deep), deep)
    listed += [(qkv_ref.at[k, rows], deep) for k in range(3)]
    pairs, at = [], 0
    for source, count in listed:
        pairs.append((source, out_ref.at[at : at + count]))
        at += count
    copies(pairs, sem_ref)


def make_slab(places, fc1, fc2, proj, qkv, small):
    half, sub = fc1.shape[0], fc1.shape[1] // 4
    rows = half + 2 * sub + proj.shape[0] // 2 + small.shape[0] + 3 * (half // 4)
    anywhere = pl.BlockSpec(memory_space=pl.ANY)
    return pl.pallas_call(
        slab_kernel,
        out_shape=jax.ShapeDtypeStruct((rows, sub), fc1.dtype),
        in_specs=[pl.BlockSpec(memory_space=pltpu.SMEM)] + [anywhere] * 5,
        out_specs=pl.BlockSpec(memory_space=pltpu.VMEM),
        scratch_shapes=[pltpu.SemaphoreType.DMA((9,))],
        cost_estimate=small_cost(100000000),
        name="make_slab",
    )(places, fc1, fc2, proj, qkv, small)


def far_qkv_kernel(base, places_ref, mine_ref, theirs_ref, out_ref, sem_ref):
    sub = mine_ref.shape[1]
    half = out_ref.shape[0] // 2
    deep, step = half // 4, mine_ref.shape[0] // 4
    pairs = []
    for side, ref in enumerate((mine_ref, theirs_ref)):
        for s in range(4):
            rows = pl.ds(pl.multiple_of(side * half + places_ref[s] * deep, deep), deep)
            for k in range(3):
                at = s * step + base + k * deep
                pairs.append((ref.at[at : at + deep], out_ref.at[rows, k * sub : (k + 1) * sub]))
    copies(pairs, sem_ref)


def far_qkv(places, mine, theirs, base, width):
    anywhere = pl.BlockSpec(memory_space=pl.ANY)
    return pl.pallas_call(
        functools.partial(far_qkv_kernel, base),
        out_shape=jax.ShapeDtypeStruct((width, 3 * mine.shape[1]), mine.dtype),
        in_specs=[pl.BlockSpec(memory_space=pltpu.SMEM)] + [anywhere] * 2,
        out_specs=pl.BlockSpec(memory_space=pltpu.VMEM),
        scratch_shapes=[pltpu.SemaphoreType.DMA((24,))],
        cost_estimate=small_cost(100000000),
        name="far_qkv",
    )(places, mine, theirs)


def first_norm_kernel(flip_ref, states_ref, vector_ref, *refs):
    out_ref = refs[-1]
    rows_all, width = states_ref.shape
    start = out_ref.shape[0] - rows_all
    if start:
        out_ref[0:start, :] = refs[0][...]

    @pl.loop(0, rows_all // ROWS)
    def _(index):
        rows = pl.ds(pl.multiple_of(index * ROWS, ROWS), ROWS)
        normal, _ = unit_rows(framed(states_ref, rows, flip_ref[0], width // 2))
        values = (normal * vector_ref[0:1, :] + vector_ref[1:2, :]).astype(jnp.bfloat16)
        out_ref[pl.ds(pl.multiple_of(start + index * ROWS, 16), ROWS), :] = values


def first_norm(flip, states, vectors, *before):
    vmem = pl.BlockSpec(memory_space=pltpu.VMEM)
    rows = states.shape[0] + sum(b.shape[0] for b in before)
    return pl.pallas_call(
        first_norm_kernel,
        out_shape=jax.ShapeDtypeStruct((rows, states.shape[1]), jnp.bfloat16),
        in_specs=[pl.BlockSpec(memory_space=pltpu.SMEM)] + [vmem] * (2 + len(before)),
        out_specs=vmem,
        cost_estimate=small_cost(100000000),
        name="first_norm",
    )(flip, states, vectors, *before)


VECTORS = 32


def put_split(ref, at, values):
    high = values.astype(jnp.bfloat16)
    low = (values - high.astype(jnp.float32)).astype(jnp.bfloat16)
    columns = values.shape[1]
    ref[at : at + VECTORS, 0:columns] = high
    ref[at + VECTORS : at + 2 * VECTORS, 0:columns] = low
    rest = ref.shape[1] - columns
    if rest:
        ref[at : at + 2 * VECTORS, columns:] = jnp.zeros((2 * VECTORS, rest), jnp.bfloat16)


def get_split(ref, at, columns):
    high = ref[at : at + VECTORS, 0:columns].astype(jnp.float32)
    return high + ref[at + VECTORS : at + 2 * VECTORS, 0:columns].astype(jnp.float32)


def framed(ref, rows, flip, half):
    return jnp.concatenate(
        [ref[rows, pl.ds(pl.multiple_of((flip ^ i) * half, half), half)] for i in range(2)], axis=1
    ).astype(jnp.float32)


def token_back_kernel(
    flip_ref, near_ref, far_ref, w_near, w_far, own_states, other_states, own_ref, give_ref, sums_ref, other_v
):
    rows_all, half = own_ref.shape[0], own_ref.shape[1] // 2
    sums_ref[...] = jnp.zeros_like(sums_ref)
    for start, out_ref in ((rows_all, other_v), (0, own_ref)):
        rows = slice(start, start + rows_all)
        out_ref[...] = dot_nt(near_ref[rows, :], w_near[...]) + dot_nt(far_ref[rows, :], w_far[...])
    for out_ref, states in ((other_v, other_states), (own_ref, own_states)):

        @functools.partial(rows_of, rows_all)
        def _(rows, out_ref=out_ref, states=states):
            normal, _ = unit_rows(framed(states, rows, flip_ref[0], half))
            upstream = out_ref[rows, :]
            sums_ref[0:1, :] += jnp.sum(upstream * normal, axis=0, keepdims=True)
            sums_ref[1:2, :] += jnp.sum(upstream, axis=0, keepdims=True)
            if out_ref is other_v:
                give_ref[rows, :] = upstream.astype(jnp.bfloat16)


def token_back(flip, near, far, w_near, w_far, own_states, other_states):
    rows, width = own_states.shape
    vmem = pl.BlockSpec(memory_space=pltpu.VMEM)
    return pl.pallas_call(
        token_back_kernel,
        out_shape=(
            jax.ShapeDtypeStruct((rows, width), jnp.float32),
            jax.ShapeDtypeStruct((rows, width), jnp.bfloat16),
            jax.ShapeDtypeStruct((2, width), jnp.float32),
        ),
        in_specs=[pl.BlockSpec(memory_space=pltpu.SMEM)] + [vmem] * 6,
        out_specs=(vmem,) * 3,
        scratch_shapes=[pltpu.VMEM((rows, width), jnp.float32)],
        compiler_params=pltpu.CompilerParams(vmem_limit_bytes=40 << 20),
        cost_estimate=small_cost(100000000),
        name="token_back",
    )(flip, near, far, w_near, w_far, own_states, other_states)


def last_kernel(flip_ref, own_ref, taken_ref, states_ref, mid_ref, vector_ref, out_ref):
    half = own_ref.shape[1] // 2
    upstream = own_ref[...] + taken_ref[...].astype(jnp.float32)
    everything = slice(0, own_ref.shape[0])
    normal, spread = unit_rows(framed(states_ref, everything, flip_ref[0], half))
    inner = upstream * vector_ref[0:1, :]
    center = jnp.mean(inner, axis=-1, keepdims=True)
    slope = jnp.mean(inner * normal, axis=-1, keepdims=True)
    back = mid_ref[...] + spread * (inner - center - normal * slope)
    for i in range(2):
        lanes = pl.ds(pl.multiple_of((flip_ref[0] ^ i) * half, half), half)
        out_ref[:, lanes] = back[:, i * half : (i + 1) * half].astype(jnp.bfloat16)


def last_norm(flip, own, taken, states, mid, vectors):
    rows, width = own.shape
    block = pl.BlockSpec((ROWS, width), lambda i: (i, 0))
    whole = pl.BlockSpec(vectors.shape, lambda i: (0, 0))
    return pl.pallas_call(
        last_kernel,
        grid=(rows // ROWS,),
        out_shape=jax.ShapeDtypeStruct((rows, width), jnp.bfloat16),
        in_specs=[pl.BlockSpec(memory_space=pltpu.SMEM)] + [block] * 4 + [whole],
        out_specs=block,
        cost_estimate=small_cost(500000000),
        name="last_norm",
    )(flip, own, taken, states, mid, vectors)


def far_grads_kernel(
    turned_ref, grad_ref, sums_ref, hidden_ref, norm_ref, near_ref, far_ref, keep_ref, out_ref, kept_ref
):
    half = keep_ref.shape[1]
    width = near_ref.shape[1] // 3
    shared = [hidden_ref[0:1, i * half : (i + 1) * half] for i in range(8)]
    for ref in (near_ref, far_ref):
        shared.append(jnp.concatenate([ref[0:1, 0:width], ref[0:1, 2 * width :]], axis=1))
    shared.append(sums_ref[0:1, 0:half] + sums_ref[0:1, half:])
    blank = jnp.zeros((VECTORS - 6 - len(shared), half), jnp.float32)

    def rows(lanes):
        split = [sums_ref[i : i + 1, lanes] for i in (2, 3, 4, 1)]
        split += [norm_ref[i : i + 1, lanes] for i in range(2)]
        return jnp.concatenate(split + shared + [blank], axis=0)

    keep_ref[...] = rows(slice(0, half))
    put_split(out_ref, half, rows(slice(half, 2 * half)))
    out_ref[0:half, :] = dot_nn(turned_ref[half:, :], grad_ref[...]).astype(jnp.bfloat16)
    kept_ref[...] = dot_nn(turned_ref[0:half, :], grad_ref[...])


def after_row_kernel(
    places_ref, kept_ref, taken_ref, keep_ref, near_ref, near_taken, near_own_ref, far_own_ref, sum_ref, *outs
):
    deep = far_own_ref.shape[0]
    vectors = keep_ref[...] + get_split(taken_ref, 4 * deep, keep_ref.shape[1])
    sum_ref[...] = vectors
    for s in range(4):
        rows = pl.ds(pl.multiple_of(places_ref[s] * deep, deep), deep)
        far = kept_ref[rows, :] + taken_ref[rows, :].astype(jnp.float32)
        if s == 0:
            far_own_ref[...] = far
        else:
            outs[s - 1][0:deep, :] = far.astype(jnp.bfloat16)
            put_split(outs[s - 1], deep, vectors)
        if s % 2 == 0:
            at = slice(s // 2 * deep, (s // 2 + 1) * deep)
            near = near_ref[rows, :].astype(jnp.float32) + near_taken[at, :].astype(jnp.float32)
            if s == 0:
                near_own_ref[...] = near
            else:
                outs[s - 1][deep + 2 * VECTORS :, :] = near.astype(jnp.bfloat16)


def after_plane_kernel(near_ref, far_ref, sum_ref, *refs):
    takes, (keep_ref, vector_ref, give_ref, small_ref) = refs[:3], refs[3:]
    deep = far_ref.shape[0]
    vectors, far = sum_ref[...], far_ref[...]
    keep_ref[...] = near_ref[...] + takes[1][deep + 2 * VECTORS :, :].astype(jnp.float32)
    for take in takes:
        vectors = vectors + get_split(take, deep, vectors.shape[1])
        far = far + take[0:deep, :].astype(jnp.float32)
    vector_ref[...] = vectors
    give_ref[0:deep, :] = far.astype(jnp.bfloat16)
    put_split(give_ref, deep, vectors)
    put_split(small_ref, 0, vectors)


def after_cols_kernel(keep_ref, vector_ref, one_ref, two_ref, three_ref, out_ref, total_ref):
    deep = keep_ref.shape[0]
    out_ref[...] = (keep_ref[...] + two_ref[0:deep, :].astype(jnp.float32)).astype(jnp.bfloat16)
    columns = vector_ref.shape[1]
    far = get_split(two_ref, deep, columns)
    total = vector_ref[...] + far
    total = total + get_split(one_ref, 0, columns) + get_split(three_ref, 0, columns)
    total_ref[...] = total
    total_ref[14:15, :] = vector_ref[14:15, :] + far[15:16, :]


def on_chip(kernel, shapes, name, *args, tables=0):
    vmem = pl.BlockSpec(memory_space=pltpu.VMEM)
    return pl.pallas_call(
        kernel,
        out_shape=tuple(jax.ShapeDtypeStruct(*s) for s in shapes),
        in_specs=[pl.BlockSpec(memory_space=pltpu.SMEM)] * tables + [vmem] * (len(args) - tables),
        out_specs=(vmem,) * len(shapes),
        cost_estimate=small_cost(100000000),
        name=name,
    )(*args)


def wide_kernel(with_proj, places_ref, small_ref, big_ref, taken_ref, *refs):
    if with_proj:
        proj_kept, proj_taken, *refs = refs
    *outs, turned_v = refs
    half, sub = turned_v.shape[0], turned_v.shape[0] // 2
    span = big_ref.shape[1] // 4
    part = 256 // 4 if not with_proj else proj_kept.shape[0] // 16
    turned_v[...] = small_ref[:, 0:half].T
    for s in range(4):
        lanes = pl.ds(pl.multiple_of(places_ref[s] * span, span), span)
        block = dot_nn(turned_v[...], big_ref[:, lanes]) + taken_ref[:, lanes].astype(jnp.float32)
        block = block.astype(jnp.bfloat16)
        for side, (go, slot) in enumerate(((s % 2, s // 2), (s // 2, s % 2))):
            out = outs[2 * side + go]
            rows = slice(slot * sub, (slot + 1) * sub)
            out[rows, 0:span] = block[side * sub : (side + 1) * sub]
            if with_proj:
                at = side * sub
                for j in range(4):
                    start = pl.multiple_of(4 * j * part + places_ref[s] * part, part)
                    piece = proj_kept[pl.ds(start, part), at : at + sub] + proj_taken[
                        pl.ds(start, part), at : at + sub
                    ].astype(jnp.float32)
                    low = slot * sub + j * part
                    out[low : low + part, span:] = piece.astype(jnp.bfloat16)


def wide_grads(places, small, big, taken, proj=()):
    half = small.shape[1] // 2
    columns = big.shape[1] // 4 + (half // 2 if proj else 0)
    vmem = pl.BlockSpec(memory_space=pltpu.VMEM)
    return pl.pallas_call(
        functools.partial(wide_kernel, bool(proj)),
        out_shape=(jax.ShapeDtypeStruct((half, columns), jnp.bfloat16),) * 4,
        in_specs=[pl.BlockSpec(memory_space=pltpu.SMEM)] + [vmem] * (3 + len(proj)),
        out_specs=(vmem,) * 4,
        scratch_shapes=[pltpu.VMEM((half, small.shape[0]), jnp.bfloat16)],
        compiler_params=pltpu.CompilerParams(vmem_limit_bytes=44 << 20),
        cost_estimate=small_cost(3000000000),
        name="wide_grads",
    )(places, small, big, taken, *proj)


def plane_sum_kernel(*refs):
    sub = refs[4].shape[0]
    for side in range(2):
        kept, taken = refs[2 * side : 2 * side + 2]
        for slot in range(2):
            rows = slice(slot * sub, (slot + 1) * sub)
            total = kept[rows, :].astype(jnp.float32) + taken[rows, :].astype(jnp.float32)
            refs[4 + 2 * side + slot][...] = total.astype(jnp.bfloat16)


def cols_out_kernel(places_ref, *refs):
    outs = refs[4:]
    sub = refs[0].shape[0]
    columns = refs[0].shape[1]
    part = (outs[0].shape[0] - 2 * sub) // 2
    for side in range(2):
        kept, taken = refs[2 * side : 2 * side + 2]
        for j in range(4):
            lanes = pl.ds(pl.multiple_of(places_ref[4 + j] * sub, sub), sub)
            total = kept[:, lanes].astype(jnp.float32) + taken[:, lanes].astype(jnp.float32)
            outs[j][side * sub : (side + 1) * sub, :] = total.astype(jnp.bfloat16)
            if part:
                rows = slice(j * part, (j + 1) * part)
                total = kept[rows, columns - sub :].astype(jnp.float32)
                total = total + taken[rows, columns - sub :].astype(jnp.float32)
                low = 2 * sub + side * part
                outs[j][low : low + part, :] = total.astype(jnp.bfloat16)


def mine_kernel(*refs):
    out_ref, at = refs[8], 0
    for group in (refs[0:4], refs[4:8]):
        total = group[0][...].astype(jnp.float32)
        for ref in group[1:]:
            total = total + ref[...].astype(jnp.float32)
        out_ref[at : at + total.shape[0], :] = total.astype(jnp.bfloat16)
        at += total.shape[0]


def finish_kernel(part_rows, places_ref, *refs):
    pieces, (fc2_ref, fc1_ref, proj_ref) = refs[:2], refs[2:]
    half, sub = fc1_ref.shape[0], pieces[0].shape[1]
    for s in range(4):
        piece, base = pieces[s // 2], (s % 2) * (pieces[0].shape[0] // 2)
        at = places_ref[s]
        rows = pl.ds(pl.multiple_of(at * sub, sub), sub)
        fc2_ref[rows, :] = piece[base : base + half, :].astype(jnp.float32).T
        fc1_ref[:, rows] = piece[base + half : base + 2 * half, :].astype(jnp.float32)
        rows = pl.ds(pl.multiple_of(at * part_rows, part_rows), part_rows)
        for i in range(2):
            low = base + 2 * half + i * part_rows
            proj_ref[rows, i * sub : (i + 1) * sub] = piece[low : low + part_rows, :].astype(jnp.float32)


def finish_qkv_kernel(places_ref, *refs):
    out_ref = refs[4]
    deep, width = refs[0].shape[0], out_ref.shape[2]
    for s in range(4):
        rows = pl.ds(pl.multiple_of(places_ref[s] * deep, deep), deep)
        for k in range(3):
            out_ref[k, rows, :] = refs[s][:, k * width : (k + 1) * width].astype(jnp.float32)


def finish(places, pieces, part_rows):
    rows, sub = pieces[0].shape
    half = (rows // 2 - 2 * part_rows) // 2
    vmem = pl.BlockSpec(memory_space=pltpu.VMEM)
    return pl.pallas_call(
        functools.partial(finish_kernel, part_rows),
        out_shape=(
            jax.ShapeDtypeStruct((4 * sub, half), jnp.float32),
            jax.ShapeDtypeStruct((half, 4 * sub), jnp.float32),
            jax.ShapeDtypeStruct((4 * part_rows, half), jnp.float32),
        ),
        in_specs=[pl.BlockSpec(memory_space=pltpu.SMEM)] + [vmem] * 2,
        out_specs=[vmem] * 3,
        cost_estimate=small_cost(100000000),
        name="finish",
    )(places, *pieces)


def finish_qkv(places, pieces):
    deep, width = pieces[0].shape
    vmem = pl.BlockSpec(memory_space=pltpu.VMEM)
    return pl.pallas_call(
        finish_qkv_kernel,
        out_shape=jax.ShapeDtypeStruct((3, 4 * deep, width // 3), jnp.float32),
        in_specs=[pl.BlockSpec(memory_space=pltpu.SMEM)] + [vmem] * 4,
        out_specs=vmem,
        cost_estimate=small_cost(100000000),
        name="finish_qkv",
    )(places, *pieces)


def tie(value, *others):
    return lax.optimization_barrier((value, *others))[0]


def add_up(own, taken):
    total = own.astype(jnp.float32)
    for piece in taken:
        total = total + piece.astype(jnp.float32)
    return total


def local_paired(
    states,
    ln1_gain,
    ln1_bias,
    w_qkv,
    q_bias,
    v_bias,
    w_proj,
    proj_bias,
    ln2_gain,
    ln2_bias,
    w_fc1,
    fc1_bias,
    w_fc2,
    fc2_bias,
    teacher,
    loss_mask,
    lengths,
):
    f32, bf16 = jnp.float32, jnp.bfloat16
    dp = lax.axis_index("dp")
    row = lax.axis_index("row")
    col = lax.axis_index("col")
    local_rows, width = states.shape
    half = width // 2
    head_width = w_qkv.shape[2]
    hidden_width = w_fc1.shape[1]
    sub = hidden_width // 4
    span = 4 * sub
    part_rows = head_width // 4
    clip = (dp * 2 + row) * 2 + col // 2
    second = col % 2

    def quarter(s):
        return dp ^ s

    def frame(values):
        return jnp.where(
            row == 0, values, jnp.concatenate([values[:, half:], values[:, :half]], axis=1)
        )

    places = jnp.stack([dp ^ s for s in range(4)] + [col ^ j for j in range(4)]).astype(jnp.int32)
    flip = row.reshape(1).astype(jnp.int32)
    states_other = over_col(states, 1)
    small = jnp.concatenate(
        [
            fc1_bias.reshape(4, sub),
            q_bias.reshape(1, sub),
            v_bias.reshape(1, sub),
            jnp.zeros((10, sub), bf16),
        ],
        axis=0,
    )
    slab = make_slab(places, w_fc1, w_fc2, w_proj, w_qkv.transpose(1, 0, 2), small)
    unit_rows_total = half + 2 * sub + 2 * part_rows + small.shape[0]
    small_at = unit_rows_total - small.shape[0]
    two = over_col(slab, 2)
    w_qkv2 = w_qkv.reshape(half, 3 * head_width)
    w_qkv2 = tie(w_qkv2, slab)
    qkv_near = jnp.concatenate([w_qkv2, over_row(w_qkv2)], axis=0)
    vectors = jnp.stack([ln1_gain, ln1_bias, proj_bias, ln2_gain, ln2_bias, fc2_bias])
    vectors, states, teacher, loss_mask = lax.optimization_barrier(
        (vectors, states, teacher, loss_mask, slab)
    )[:4]
    vectors = jnp.concatenate([vectors, over_row(vectors)], axis=1).astype(f32)
    fc1_other, fc2_other, proj_other = over_row(w_fc1), over_row(w_fc2), over_row(w_proj)
    two = tie(two, fc1_other, fc2_other, proj_other)
    two_x, two_y = over_dp(two, 1), over_dp(two, 2)
    states_other = tie(states_other, two)

    all_clips = lengths.shape[0]
    valid_all = (
        loss_mask.reshape(all_clips, L) * (jnp.arange(L)[None, :] < lengths[:, None])
    ).astype(f32)
    valid_total = jnp.maximum(jnp.sum(valid_all), 1.0)
    first_row = ((dp * 2 + row) * 4 + col) * local_rows
    valid = lax.dynamic_slice_in_dim(valid_all.reshape(all_clips * L), first_row, local_rows)
    my_length = lax.dynamic_slice_in_dim(lengths, clip, 1)
    spot = jnp.arange(L)
    position = jnp.where(
        spot < local_rows, second * local_rows + spot, (1 - second) * local_rows + spot - local_rows
    )
    key_bias = jnp.where(position < my_length, 0.0, MASKED).astype(f32)
    key_bias = jnp.broadcast_to(key_bias[:, None], (L, 128))

    norm_one = first_norm(flip, states, vectors)
    tokens_one = first_norm(flip, states_other, vectors, tie(norm_one, two))

    zero_bias = jnp.zeros((head_width,), f32)
    score_scale = HD**-0.5
    scale = jnp.where(jnp.arange(3 * head_width) < head_width, score_scale, 1.0).astype(bf16)
    split = local_rows // QT * QT
    later = L - split
    over = local_rows - split

    def project(matrix, q_add, v_add):
        projected = jnp.dot(tokens_one, matrix, preferred_element_type=f32)
        add = jnp.concatenate([q_add.astype(f32), zero_bias, v_add.astype(f32)])
        return (projected + add[None]).astype(bf16) * scale[None]

    table = jnp.stack(
        [(dp ^ s) * 4 + (col ^ j) for s in range(4) for j in range(4)]
        + [a * 4 + col for a in range(4)]
        + [dp ^ s for s in range(4)]
        + [col ^ b for b in range(4)]
        + [row]
    ).astype(jnp.int32)
    loss_scale = all_clips * L * width / 2.0
    factor = (loss_scale * 2.0 / (valid_total * width)).reshape(1)
    valid = valid[:, None]
    packed_near = tie(project(qkv_near, q_bias, v_bias), table, factor, valid)
    cut_at = two.shape[0] // 32 * 16
    two_x, two_y = tie(two_x, packed_near), tie(two_y, packed_near)
    two_low, two_high = over_dp(two_y[:cut_at], 1), over_dp(two_x[cut_at:], 2)
    one_give = jnp.concatenate([slab[:unit_rows_total], two[:unit_rows_total]], axis=0)
    one = over_col(tie(one_give, states_other), 1)
    turned = lax.optimization_barrier((tokens_one.T, packed_near))[0]
    near_late, near_late_lse = attend(
        tie(packed_near, two_x, two_y, one, turned), key_bias, split, later
    )
    two_low, two_high = tie(two_low, near_late), tie(two_high, near_late)
    two_all = jnp.concatenate([two, two_x, two_y, two_low, two_high], axis=0)
    two_theirs = over_row(two_all)
    near_other = over_col(near_late[over:], 1)
    one_x, one_y = over_dp(one, 1), over_dp(one, 2)
    one_other = over_row(tie(one, near_late))
    near_soon, near_soon_lse = attend(
        tie(packed_near, two_all, near_late, one), key_bias, 0, split
    )
    two_theirs = tie(two_theirs, near_soon, near_other)
    qkv_far = far_qkv(places, two_all, two_theirs, unit_rows_total, width)
    far_small = two_all[small_at : small_at + small.shape[0]]
    packed_far = project(qkv_far, far_small[4], far_small[5])
    packed_far = tie(packed_far, one, near_other)
    far_late, far_late_lse = attend(packed_far, key_bias, split, later)
    far_other = over_col(far_late[over:], 1)
    one_x, one_y = tie(one_x, far_late), tie(one_y, far_late)
    cut_at = one.shape[0] // 2
    one_low, one_high = over_dp(one_y[:cut_at], 1), over_dp(one_x[cut_at:], 2)
    one_theirs = [over_row(one_x), over_row(one_y)]
    far_soon, far_soon_lse = attend(
        tie(packed_far, one_x, one_y, far_late, one_other), key_bias, 0, split
    )
    one_low, one_high = tie(one_low, far_soon, far_other), tie(one_high, far_soon, far_other)
    one_mine = [one, one_x, one_y, one_low, one_high]
    one_theirs = [one_other, *one_theirs, over_row(one_low), over_row(one_high)]
    at = unit_rows_total + small_at
    smalls = jnp.stack(
        [small, one[small_at : small_at + 16], two_all[small_at : small_at + 16], one[at : at + 16]]
    ).astype(f32)
    (
        attended_rows,
        outputs,
        hidden,
        grad_pre,
        norm_two,
        grad_low,
        mid_low,
        grad_mid,
        up_own,
        up_give,
        hidden_sum,
        sums,
    ) = middle_block(
        table,
        factor,
        states,
        teacher,
        valid,
        vectors,
        smalls,
        (
            w_fc1,
            fc1_other,
            w_fc2,
            fc2_other,
            w_proj,
            proj_other,
            two_all,
            two_theirs,
            *one_mine,
            *one_theirs,
            near_soon,
            near_late,
            near_other,
            far_soon,
            far_late,
            far_other,
        ),
    )
    up_far = over_col(up_give, 1)

    def joined(kept, taken):
        return (kept.astype(f32) + taken.astype(f32)).astype(bf16)

    give_fc2 = over_row(dot_tn(grad_low[:, half:], hidden).astype(bf16))
    give_fc1 = over_row(dot_tn(norm_two[:, half:], grad_pre).astype(bf16))
    give_proj = over_row(dot_tn(attended_rows, mid_low[:, half:]).astype(bf16))
    kept_proj = dot_tn(attended_rows, mid_low[:, :half])

    def plane_first(wide):
        keep_x, give_x, keep_y, give_y = wide
        return (keep_x, keep_y), (give_x, give_y), (over_dp(give_x, 1), over_dp(give_y, 2))

    def plane_second(keep, taken):
        shape = ((keep[0].shape[0] // 2, keep[0].shape[1]), bf16)
        keep_x, give_x, keep_y, give_y = on_chip(
            plane_sum_kernel, [shape] * 4, "plane_sum", keep[0], taken[0], keep[1], taken[1]
        )
        return (keep_x, keep_y), (give_x, give_y), (over_dp(give_x, 2), over_dp(give_y, 1))

    def cols_out(keep, taken, rows):
        blocks = on_chip(
            cols_out_kernel,
            [((rows, sub), bf16)] * 4,
            "cols_out",
            *(places, keep[0], taken[0], keep[1], taken[1]),
            tables=1,
        )
        return blocks, [over_col(blocks[j], j) for j in (1, 2, 3)]

    def all_tied(values, *others):
        return [tie(v, *others) for v in values]

    wide = wide_grads(places, grad_low, hidden, give_fc2)
    fc2_keep, fc2_give, fc2_taken = plane_first(wide)
    wide = wide_grads(
        places, tie(norm_two, *fc2_give), grad_pre, give_fc1, (kept_proj, give_proj)
    )
    fc1_keep, fc1_give, fc1_taken = plane_first(wide)

    packed_near = tie(packed_near, *fc2_give, *fc1_give)
    part_near = attend_back(packed_near, key_bias, near_soon_lse, near_soon, up_own, None, 0, 0)
    fc2_keep, fc2_give, fc2_taken = plane_second(fc2_keep, all_tied(fc2_taken, part_near[0]))

    packed_far = tie(packed_far, *fc2_give, part_near[0])
    part_far = attend_back(
        packed_far, key_bias, far_soon_lse, far_soon, up_own, None, head_width, 0
    )
    fc2_blocks, fc2_cols = cols_out(fc2_keep, all_tied(fc2_taken, part_far[0]), 2 * sub)
    fc1_keep, fc1_give, fc1_taken = plane_second(fc1_keep, all_tied(fc1_taken, part_far[0]))

    packed_near = tie(packed_near, *fc2_blocks, *fc1_give)
    grad_near, near_sums = attend_back(
        packed_near, key_bias, near_late_lse, near_late, up_own, up_far, 0, split, part_near
    )
    fc2_cols = all_tied(fc2_cols, grad_near)
    fc1_blocks, fc1_cols = cols_out(
        fc1_keep, all_tied(fc1_taken, grad_near, *fc2_cols), 2 * sub + 2 * part_rows
    )
    near_tied = tie(grad_near, *fc1_blocks)
    near_row = over_row(dot_tn(tokens_one[:, half:], near_tied).astype(bf16))
    wide_near = joined(dot_tn(tokens_one[:, :half], near_tied), near_row)
    deep = half // 4
    near_give = jnp.concatenate([cut(wide_near, quarter(s), deep) for s in (1, 3)], axis=0)
    near_taken = over_dp(near_give, 1)

    packed_far = tie(packed_far, near_give, *fc1_blocks, *fc2_cols)
    grad_far, far_sums = attend_back(
        packed_far, key_bias, far_late_lse, far_late, up_own, up_far, head_width, split, part_far
    )

    norm_own, norm_give, norm_sums = token_back(
        flip, grad_near, grad_far, qkv_near, qkv_far, states, states_other
    )
    norm_taken = over_col(norm_give, 1)
    columns, slots = grad_far.shape[1], 2 * VECTORS
    vec_keep, row_give, kept = on_chip(
        far_grads_kernel,
        [((VECTORS, half), f32), ((half + slots, columns), bf16), ((half, columns), f32)],
        "far_grads",
        *(turned, tie(grad_far, norm_give, near_taken, *fc1_cols), sums, hidden_sum, norm_sums, near_sums, far_sums),
    )
    row_taken = over_row(row_give)
    fc1_cols = all_tied(fc1_cols, row_give)
    mine_rows = fc2_blocks[0].shape[0] + fc1_blocks[0].shape[0]
    (mine,) = on_chip(
        mine_kernel,
        [((mine_rows, sub), bf16)],
        "mine",
        *(fc2_blocks[0], *fc2_cols, fc1_blocks[0], *fc1_cols),
    )
    mine_x = over_dp(mine, 1)
    near_own, far_own, vec_sum, *plane_give = on_chip(
        after_row_kernel,
        [((deep, columns), f32)] * 2
        + [((VECTORS, half), f32)]
        + [((deep + slots + (deep if s == 2 else 0), columns), bf16) for s in (1, 2, 3)],
        "after_row",
        *(places, kept, tie(row_taken, mine), vec_keep, wide_near, tie(near_taken, mine)),
        tables=1,
    )
    plane_taken = [over_dp(plane_give[s - 1], s) for s in (1, 2, 3)]
    mine_two = jnp.concatenate([mine, tie(mine_x, *plane_give)], axis=0)
    plane_taken = all_tied(plane_taken, mine_two, norm_taken)
    near_own, vec_sum, col_give, vec_give = on_chip(
        after_plane_kernel,
        [
            ((deep, columns), f32),
            ((VECTORS, half), f32),
            ((deep + slots, columns), bf16),
            ((slots, half), bf16),
        ],
        "after_plane",
        *(near_own, far_own, vec_sum, *plane_taken),
    )
    mine_y = over_dp(tie(mine_two, col_give), 2)
    col_taken = [over_col(vec_give, 1), over_col(col_give, 2), over_col(vec_give, 3)]
    norm_taken = tie(norm_taken, col_give)
    grad_states = last_norm(flip, norm_own, norm_taken, states, grad_mid, vectors)

    qkv_mine, vec_total = on_chip(
        after_cols_kernel,
        [((deep, columns), bf16), ((VECTORS, half), f32)],
        "after_cols",
        *(near_own, vec_sum, *all_tied(col_taken, grad_states)),
    )
    qkv_back = [over_dp(qkv_mine, s) for s in (1, 2, 3)]
    fc2_grad, fc1_grad, proj_grad = finish(places, [mine_two, tie(mine_y, qkv_mine)], part_rows)
    qkv_grad = finish_qkv(places, [qkv_mine, *all_tied(qkv_back, fc2_grad)]).transpose(1, 0, 2)

    fc1_bias_grad = lax.dynamic_index_in_dim(vec_total[6:14].reshape(4, 4, sub), col, 1, False)
    loss_value = jnp.sum(vec_total[16]) / (valid_total * width)
    return (
        outputs,
        loss_value,
        grad_states,
        vec_total[4],
        vec_total[5],
        qkv_grad,
        vec_total[14, :head_width],
        vec_total[14, head_width:],
        proj_grad,
        vec_total[2],
        vec_total[0],
        vec_total[1],
        fc1_grad,
        fc1_bias_grad.reshape(span),
        fc2_grad,
        vec_total[3],
    )


def solution(mesh):
    sizes = (mesh.shape["dp"], mesh.shape["row"], mesh.shape["col"])
    body = local_paired if sizes == PAIRED_MESH else local_general
    in_specs = (
        P(("dp", "row", "col"), None),
        P("row"),
        P("row"),
        P("row", None, "col"),
        P("col"),
        P("col"),
        P("col", "row"),
        P("row"),
        P("row"),
        P("row"),
        P("row", "col"),
        P("col"),
        P("col", "row"),
        P("row"),
        P(("dp", "row", "col"), None),
        P(),
        P(),
    )
    out_specs = (
        P(("dp", "row", "col"), None),
        P(),
        P(("dp", "row", "col"), None),
        P("row"),
        P("row"),
        P("row", None, "col"),
        P("col"),
        P("col"),
        P("col", "row"),
        P("row"),
        P("row"),
        P("row"),
        P("row", "col"),
        P("col"),
        P("col", "row"),
        P("row"),
    )
    return jax.shard_map(body, mesh=mesh, in_specs=in_specs, out_specs=out_specs, check_vma=False)
```

```python
import functools

import jax
import jax.numpy as jnp
from jax import lax
from jax.experimental import pallas as pl
from jax.experimental.pallas import tpu as pltpu
from jax.sharding import PartitionSpec as P

HD = 64
L = 1568


EPSILON = 1e-06
MASKED = -1e30
ROOT_HALF = 0.7071067811865476
DENSITY_FACTOR = 0.3989422804014327


def normalize(values, factor, offset):
    centered = values - jnp.mean(values, axis=-1, keepdims=True)
    spread = lax.rsqrt(jnp.mean(centered * centered, axis=-1, keepdims=True) + EPSILON)
    normal = centered * spread
    return (normal * factor + offset, normal, spread)


def norm_back(upstream, normal, spread, factor):
    inner = upstream * factor
    center_term = jnp.mean(inner, axis=-1, keepdims=True)
    slope_term = jnp.mean(inner * normal, axis=-1, keepdims=True)
    back = spread * (inner - center_term - normal * slope_term)
    return (back, jnp.sum(upstream * normal, axis=0), jnp.sum(upstream, axis=0))


def gelu_value(values):
    return values * (0.5 * (1.0 + lax.erf(values * ROOT_HALF)))


def gelu_slope(values):
    normal_cdf = 0.5 * (1.0 + lax.erf(values * ROOT_HALF))
    return normal_cdf + values * jnp.exp(-0.5 * values * values) * DENSITY_FACTOR


def masked_scores(queries, key_rows, length, score_scale):
    logits = (
        jnp.einsum("ihd,jhd->hij", queries, key_rows, preferred_element_type=jnp.float32)
        * score_scale
    )
    keep = jnp.arange(key_rows.shape[0]) < length
    return jnp.where(keep[None, None, :], logits, MASKED)


def attend_clip(packed, length, score_scale):
    half_span = packed.shape[0] // 2
    key_rows = packed[:, 1]
    value_rows = packed[:, 2]
    pieces = []
    totals = []
    for block_index in range(2):
        queries = packed[block_index * half_span : (block_index + 1) * half_span, 0]
        logits = masked_scores(queries, key_rows, length, score_scale)
        peak = jnp.max(logits, axis=-1, keepdims=True)
        total = peak + jnp.log(jnp.sum(jnp.exp(logits - peak), axis=-1, keepdims=True))
        weights = jnp.exp(logits - total).astype(jnp.bfloat16)
        pieces.append(
            jnp.einsum("hij,jhd->ihd", weights, value_rows, preferred_element_type=jnp.float32)
        )
        totals.append(total[..., 0])
    return (jnp.concatenate(pieces, 0), jnp.concatenate(totals, 1))


def attend_clip_back(packed, length, totals, upstream, score_scale):
    half_span = packed.shape[0] // 2
    key_rows = packed[:, 1]
    value_rows = packed[:, 2]
    grad_keys = jnp.zeros(key_rows.shape, jnp.float32)
    grad_values = jnp.zeros(value_rows.shape, jnp.float32)
    grad_queries = []
    for block_index in range(2):
        first = block_index * half_span
        queries = packed[first : first + half_span, 0]
        logits = masked_scores(queries, key_rows, length, score_scale)
        probs = jnp.exp(logits - totals[:, first : first + half_span][..., None])
        incoming = upstream[first : first + half_span]
        grad_values = grad_values + jnp.einsum(
            "hij,ihd->jhd", probs.astype(jnp.bfloat16), incoming, preferred_element_type=jnp.float32
        )
        grad_probs = jnp.einsum(
            "ihd,jhd->hij", incoming, value_rows, preferred_element_type=jnp.float32
        )
        grad_logits = (
            probs * (grad_probs - jnp.sum(probs * grad_probs, axis=-1, keepdims=True))
        ).astype(jnp.bfloat16)
        grad_queries.append(
            jnp.einsum("hij,jhd->ihd", grad_logits, key_rows, preferred_element_type=jnp.float32)
            * score_scale
        )
        grad_keys = (
            grad_keys
            + jnp.einsum("hij,ihd->jhd", grad_logits, queries, preferred_element_type=jnp.float32)
            * score_scale
        )
    return jnp.stack([jnp.concatenate(grad_queries, 0), grad_keys, grad_values], axis=1)


def local_general(
    states,
    ln1_gain,
    ln1_bias,
    w_qkv,
    q_bias,
    v_bias,
    w_proj,
    proj_bias,
    ln2_gain,
    ln2_bias,
    w_fc1,
    fc1_bias,
    w_fc2,
    fc2_bias,
    teacher,
    loss_mask,
    lengths,
):
    row_count = lax.axis_size("row")
    col_count = lax.axis_size("col")
    col_index = lax.axis_index("col")
    group_index = lax.axis_index("dp") * row_count + lax.axis_index("row")
    local_rows = states.shape[0]
    width = states.shape[1]
    group_rows = local_rows * col_count
    clip_count = group_rows // L
    head_width = w_qkv.shape[2]
    heads_here = head_width // HD
    hidden_width = w_fc1.shape[1]
    score_scale = HD ** (-0.5)
    vectors = jnp.stack([ln1_gain, ln1_bias, proj_bias, ln2_gain, ln2_bias, fc2_bias])
    qkv_full, proj_full, fc1_full, fc2_full, vector_full = (
        lax.all_gather(w_qkv, "row", axis=0, tiled=True),
        lax.all_gather(w_proj, "row", axis=1, tiled=True),
        lax.all_gather(w_fc1, "row", axis=0, tiled=True),
        lax.all_gather(w_fc2, "row", axis=1, tiled=True),
        lax.all_gather(vectors, "row", axis=1, tiled=True),
    )
    vector_full = vector_full.astype(jnp.float32)
    gain_one = vector_full[0]
    shift_one = vector_full[1]
    bias_proj = vector_full[2]
    gain_two = vector_full[3]
    shift_two = vector_full[4]
    bias_two = vector_full[5]
    all_clips = lengths.shape[0]
    valid_all = (
        loss_mask.reshape(all_clips, L) * (jnp.arange(L)[None, :] < lengths[:, None])
    ).astype(jnp.float32)
    valid_total = jnp.maximum(jnp.sum(valid_all), 1.0)
    first_row = (group_index * col_count + col_index) * local_rows
    valid = lax.dynamic_slice_in_dim(valid_all.reshape(all_clips * L), first_row, local_rows)
    my_lengths = lax.dynamic_slice_in_dim(lengths, group_index * clip_count, clip_count)
    inputs = states.astype(jnp.float32)
    norm_one, unit_one, spread_one = normalize(inputs, gain_one, shift_one)
    norm_one = norm_one.astype(jnp.bfloat16)
    tokens_one = lax.all_gather(norm_one, "col", axis=0, tiled=True)
    qkv_matrix = qkv_full.reshape(width, 3 * head_width)
    projected = jnp.dot(tokens_one, qkv_matrix, preferred_element_type=jnp.float32).reshape(
        group_rows, 3, head_width
    )
    bias_rows = jnp.stack(
        [
            q_bias.astype(jnp.float32),
            jnp.zeros((head_width,), jnp.float32),
            v_bias.astype(jnp.float32),
        ]
    )
    packed = (projected + bias_rows[None]).astype(jnp.bfloat16)
    clips_packed = packed.reshape(clip_count, L, 3, heads_here, HD)
    attended, totals = lax.map(
        lambda element: attend_clip(element[0], element[1], score_scale), (clips_packed, my_lengths)
    )
    attended = attended.reshape(group_rows, head_width).astype(jnp.bfloat16)
    proj_whole, qkv_whole = (
        lax.all_gather(proj_full, "col", axis=0, tiled=True),
        lax.all_gather(qkv_full, "col", axis=2, tiled=True),
    )
    attended_rows = lax.all_to_all(attended, "col", split_axis=0, concat_axis=1, tiled=True)
    middle = inputs + (
        jnp.dot(attended_rows, proj_whole, preferred_element_type=jnp.float32) + bias_proj
    )
    norm_two, unit_two, spread_two = normalize(middle, gain_two, shift_two)
    norm_two = norm_two.astype(jnp.bfloat16)
    fc1_whole, fc2_whole, fc1_bias_whole = (
        lax.all_gather(fc1_full, "col", axis=1, tiled=True),
        lax.all_gather(fc2_full, "col", axis=0, tiled=True),
        lax.all_gather(fc1_bias, "col", axis=0, tiled=True),
    )
    hidden_pre = jnp.dot(
        norm_two, fc1_whole, preferred_element_type=jnp.float32
    ) + fc1_bias_whole.astype(jnp.float32)
    hidden = gelu_value(hidden_pre).astype(jnp.bfloat16)
    outputs = middle + (jnp.dot(hidden, fc2_whole, preferred_element_type=jnp.float32) + bias_two)
    differ = outputs - teacher.astype(jnp.float32)
    numerator = jnp.sum(valid[:, None] * differ * differ)
    loss_scale = all_clips * L * width / 2.0
    grad_out = loss_scale * 2.0 / (valid_total * width) * valid[:, None] * differ
    grad_low = grad_out.astype(jnp.bfloat16)
    grad_hidden = jnp.dot(grad_low, fc2_whole.T, preferred_element_type=jnp.float32)
    grad_pre = (grad_hidden * gelu_slope(hidden_pre)).astype(jnp.bfloat16)
    wide_fc2 = jnp.dot(hidden.T, grad_low, preferred_element_type=jnp.float32)
    wide_fc1 = jnp.dot(norm_two.T, grad_pre, preferred_element_type=jnp.float32)
    fc1_grad_part, fc2_grad_part = (
        lax.psum_scatter(
            wide_fc1.astype(jnp.bfloat16), "col", scatter_dimension=1, tiled=True
        ).astype(jnp.float32),
        lax.psum_scatter(
            wide_fc2.astype(jnp.bfloat16), "col", scatter_dimension=0, tiled=True
        ).astype(jnp.float32),
    )
    fc1_bias_sum = jnp.sum(grad_pre, axis=0, dtype=jnp.float32)
    grad_norm_two = jnp.dot(grad_pre, fc1_whole.T, preferred_element_type=jnp.float32)
    back_two, gain_two_grad, shift_two_grad = norm_back(
        grad_norm_two, unit_two, spread_two, gain_two
    )
    grad_mid = grad_out + back_two
    mid_low = grad_mid.astype(jnp.bfloat16)
    wide_proj = jnp.dot(attended_rows.T, mid_low, preferred_element_type=jnp.float32)
    proj_grad_part = lax.psum_scatter(
        wide_proj.astype(jnp.bfloat16), "col", scatter_dimension=0, tiled=True
    )
    grad_attended_rows = jnp.dot(mid_low, proj_whole.T, preferred_element_type=jnp.float32).astype(
        jnp.bfloat16
    )
    grad_attended = lax.all_to_all(
        grad_attended_rows, "col", split_axis=1, concat_axis=0, tiled=True
    )
    grads_packed = lax.map(
        lambda element: attend_clip_back(
            element[0], element[1], element[2], element[3], score_scale
        ),
        (clips_packed, my_lengths, totals, grad_attended.reshape(clip_count, L, heads_here, HD)),
    )
    grads_packed = grads_packed.reshape(group_rows, 3 * head_width).astype(jnp.bfloat16)
    qkv_grad_part = jnp.dot(tokens_one.T, grads_packed, preferred_element_type=jnp.float32).reshape(
        width, 3, head_width
    )
    bias_sums = jnp.sum(grads_packed.reshape(group_rows, 3, head_width), axis=0, dtype=jnp.float32)
    grads_rows = lax.all_to_all(
        grads_packed.reshape(group_rows, 3, head_width),
        "col",
        split_axis=0,
        concat_axis=2,
        tiled=True,
    )
    grad_norm_one = jnp.dot(
        grads_rows.reshape(local_rows, 3 * width),
        qkv_whole.reshape(width, 3 * width).T,
        preferred_element_type=jnp.float32,
    )
    back_one, gain_one_grad, shift_one_grad = norm_back(
        grad_norm_one, unit_one, spread_one, gain_one
    )
    grad_states = (grad_mid + back_one).astype(jnp.bfloat16)
    proj_bias_grad = jnp.sum(mid_low, axis=0, dtype=jnp.float32)
    fc2_bias_grad = jnp.sum(grad_low, axis=0, dtype=jnp.float32)
    token_vectors = jnp.stack(
        [
            gain_one_grad,
            shift_one_grad,
            proj_bias_grad,
            gain_two_grad,
            shift_two_grad,
            fc2_bias_grad,
        ]
    )
    head_vectors = lax.dynamic_update_slice(
        jnp.zeros((2, width), jnp.float32),
        jnp.stack([bias_sums[0], bias_sums[2]]),
        (0, col_index * head_width),
    )
    token_sums, head_sums, fc1_sums, loss_sum = lax.psum(
        (token_vectors, head_vectors, fc1_bias_sum, numerator), ("dp", "row", "col")
    )
    qkv_rows, proj_cols, fc1_rows, fc2_cols = (
        lax.psum_scatter(
            qkv_grad_part.astype(jnp.bfloat16), "row", scatter_dimension=0, tiled=True
        ).astype(jnp.float32),
        lax.psum_scatter(proj_grad_part, "row", scatter_dimension=1, tiled=True).astype(
            jnp.float32
        ),
        lax.psum_scatter(
            fc1_grad_part.astype(jnp.bfloat16), "row", scatter_dimension=0, tiled=True
        ).astype(jnp.float32),
        lax.psum_scatter(
            fc2_grad_part.astype(jnp.bfloat16), "row", scatter_dimension=1, tiled=True
        ).astype(jnp.float32),
    )
    qkv_grad, proj_grad, fc1_grad, fc2_grad = (
        lax.psum(qkv_rows.astype(jnp.bfloat16), "dp").astype(jnp.float32),
        lax.psum(proj_cols.astype(jnp.bfloat16), "dp").astype(jnp.float32),
        lax.psum(fc1_rows.astype(jnp.bfloat16), "dp").astype(jnp.float32),
        lax.psum(fc2_cols.astype(jnp.bfloat16), "dp").astype(jnp.float32),
    )
    half_width = width // row_count
    token_part = lax.dynamic_slice_in_dim(
        token_sums, lax.axis_index("row") * half_width, half_width, 1
    )
    head_part = lax.dynamic_slice_in_dim(head_sums, col_index * head_width, head_width, 1)
    fc1_part = lax.dynamic_slice_in_dim(fc1_sums, col_index * hidden_width, hidden_width, 0)
    loss_value = loss_sum / (valid_total * width)
    return (
        outputs.astype(jnp.bfloat16),
        loss_value,
        grad_states,
        token_part[0],
        token_part[1],
        qkv_grad,
        head_part[0],
        head_part[1],
        proj_grad,
        token_part[2],
        token_part[3],
        token_part[4],
        fc1_grad,
        fc1_part,
        fc2_grad,
        token_part[5],
    )


PAIRED_MESH = (4, 2, 4)
GROUP = 4


def small_cost(flops):
    return pl.CostEstimate(flops=flops, bytes_accessed=0, transcendentals=0)
QT = 128


def dot_nn(a, b):
    return lax.dot_general(a, b, (((1,), (0,)), ((), ())), preferred_element_type=jnp.float32)


def dot_nt(a, b):
    return lax.dot_general(a, b, (((1,), (1,)), ((), ())), preferred_element_type=jnp.float32)


def dot_tn(a, b):
    return lax.dot_general(a, b, (((0,), (0,)), ((), ())), preferred_element_type=jnp.float32)


def head_stack(values, zero):
    lane_head = lax.broadcasted_iota(jnp.int32, values.shape, 1) // HD
    return jnp.concatenate([jnp.where(lane_head == h, values, zero) for h in range(GROUP)], axis=0)


def head_unstack(wide, count):
    return jnp.concatenate(
        [wide[h * HD : (h + 1) * HD, h * count : (h + 1) * count] for h in range(GROUP)], axis=0
    ).T


def tiles_of(rows, tile):
    full = rows // QT

    @pl.loop(0, full)
    def _(index):
        tile(pl.multiple_of(index * QT, QT), QT, index)

    if rows > full * QT:
        tile(full * QT, rows - full * QT, full)


def attend_kernel(first, packed_ref, bias_ref, out_ref, lse_ref, vt_ref):
    width = GROUP * HD
    vt_ref[...] = packed_ref[:, 2 * width : 3 * width].T

    def tile(start, count, index):
        cols = GROUP * count
        stacked = head_stack(
            packed_ref[pl.ds(first + start, count), 0:width], jnp.zeros((), jnp.bfloat16)
        )
        half = packed_ref.shape[0] // 2

        def scores_of(at):
            bias = jnp.concatenate([bias_ref[at : at + half, :]] * (cols // 128), axis=1)
            return dot_nt(packed_ref[at : at + half, width : 2 * width], stacked) + bias

        scores, later = scores_of(0), scores_of(half)
        first_peak = jnp.max(scores, axis=0, keepdims=True)
        weights = jnp.exp(scores - first_peak)
        total = jnp.sum(weights, axis=0, keepdims=True)
        wide = dot_nn(vt_ref[:, 0:half], weights.astype(jnp.bfloat16))
        peak = jnp.maximum(first_peak, jnp.max(later, axis=0, keepdims=True))
        weights = jnp.exp(later - peak)
        scale = jnp.exp(first_peak - peak)
        total = total * scale + jnp.sum(weights, axis=0, keepdims=True)
        wide = wide * scale + dot_nn(vt_ref[:, half:], weights.astype(jnp.bfloat16))
        wide = wide * (1.0 / total)
        out_ref[pl.ds(start, count), :] = head_unstack(wide, count).astype(jnp.bfloat16)
        lse_ref[index, :, 0:cols] = jnp.broadcast_to(peak + jnp.log(total), (8, cols))

    tiles_of(out_ref.shape[0], tile)


def attend_back_kernel(
    first, lane, last, packed_ref, bias_ref, lse_ref, att_ref, up_own_ref, up_far_ref, *refs
):
    width = GROUP * HD
    lanes = slice(lane, lane + width)
    own_rows = up_own_ref.shape[0]
    if last:
        dq_in, dk_in, dv_in, out_ref, sum_ref, kt_ref, up_ref, ds_ref, dk_ref, dv_ref = refs
        dk_ref[...] = dk_in[...]
        dv_ref[...] = dv_in[...]
        out_ref[0:first, 0:width] = dq_in[...]
        rows = out_ref.shape[0] - first
        up_ref[0 : own_rows - first, :] = up_own_ref[first:own_rows, lanes]
        up_ref[own_rows - first :, :] = up_far_ref[:, lanes]
    else:
        out_ref, dk_ref, dv_ref, kt_ref, up_ref, ds_ref = refs
        dk_ref[...] = jnp.zeros_like(dk_ref)
        dv_ref[...] = jnp.zeros_like(dv_ref)
        rows = out_ref.shape[0]
        up_ref[...] = up_own_ref[0:rows, lanes]
    kt_ref[...] = packed_ref[:, width : 2 * width].T

    def tile(start, count, index):
        cols = GROUP * count
        zero = jnp.zeros((), jnp.bfloat16)
        up = up_ref[pl.ds(start, count), :]
        stacked = head_stack(packed_ref[pl.ds(first + start, count), 0:width], zero)
        up_stacked = head_stack(up, zero)
        product = head_stack(
            up.astype(jnp.float32) * att_ref[pl.ds(start, count), :].astype(jnp.float32),
            jnp.zeros((), jnp.float32),
        )
        high = product.astype(jnp.bfloat16)
        low = (product - high.astype(jnp.float32)).astype(jnp.bfloat16)
        ones = jnp.ones((8, width), jnp.bfloat16)
        delta = (dot_nt(ones, high) + dot_nt(ones, low))[0:1]
        half = packed_ref.shape[0] // 2

        def products(at):
            bias = jnp.concatenate([bias_ref[at : at + half, :]] * (cols // 128), axis=1)
            scores = dot_nt(packed_ref[at : at + half, width : 2 * width], stacked) + bias
            return scores, dot_nt(packed_ref[at : at + half, 2 * width : 3 * width], up_stacked)

        following = products(0)
        for at in (0, half):
            scores, slopes = following
            if not at:
                following = products(half)
            rows_here = slice(at, at + half)
            weights = jnp.exp(scores - lse_ref[index, 0:1, 0:cols])
            dv_ref[rows_here, :] += dot_nn(weights.astype(jnp.bfloat16), up_stacked)
            grad = (weights * (slopes - delta)).astype(jnp.bfloat16)
            ds_ref[rows_here, 0:cols] = grad
            dk_ref[rows_here, :] += dot_nn(grad, stacked)
        wide = dot_nn(kt_ref[...], ds_ref[:, 0:cols]) * (HD**-0.5)
        at = pl.ds(first + start if last else start, count)
        out_ref[at, 0:width] = head_unstack(wide, count).astype(jnp.bfloat16)

    tiles_of(rows, tile)
    if last:
        out_ref[:, width : 2 * width] = dk_ref[...].astype(jnp.bfloat16)
        out_ref[:, 2 * width : 3 * width] = dv_ref[...].astype(jnp.bfloat16)
        for k in range(3):
            part = out_ref[:, k * width : (k + 1) * width].astype(jnp.float32)
            sum_ref[:, k * width : (k + 1) * width] = jnp.sum(part, axis=0, keepdims=True)


def attend(packed, bias, first, rows):
    tokens, width = packed.shape[0], GROUP * HD
    tiles = -(-rows // QT)
    return pl.pallas_call(
        functools.partial(attend_kernel, first),
        out_shape=(
            jax.ShapeDtypeStruct((rows, width), jnp.bfloat16),
            jax.ShapeDtypeStruct((tiles, 8, GROUP * QT), jnp.float32),
        ),
        in_specs=[pl.BlockSpec(memory_space=pltpu.VMEM)] * 2,
        out_specs=[pl.BlockSpec(memory_space=pltpu.VMEM)] * 2,
        scratch_shapes=[pltpu.VMEM((width, tokens), jnp.bfloat16)],
        compiler_params=pltpu.CompilerParams(vmem_limit_bytes=32 << 20),
        cost_estimate=pl.CostEstimate(
            flops=2 * rows * tokens * width * 4, bytes_accessed=6 << 20, transcendentals=0
        ),
        name="attend",
    )(packed, bias)


def attend_back(packed, bias, lse, att, up_own, up_far, lane, first, before=None):
    tokens, width = packed.shape[0], GROUP * HD
    rows = att.shape[0]
    total = jax.ShapeDtypeStruct((tokens, width), jnp.float32)
    vmem = pl.BlockSpec(memory_space=pltpu.VMEM)
    scratch = [
        pltpu.VMEM((width, tokens), jnp.bfloat16),
        pltpu.VMEM((rows, width), jnp.bfloat16),
        pltpu.VMEM((tokens, GROUP * QT), jnp.bfloat16),
    ]
    if before is None:
        extra = ()
        out_shape = (jax.ShapeDtypeStruct((rows, width), jnp.bfloat16), total, total)
        up_far = up_own
    else:
        extra = before
        out_shape = (
            jax.ShapeDtypeStruct((tokens, 3 * width), jnp.bfloat16),
            jax.ShapeDtypeStruct((1, 3 * width), jnp.float32),
        )
        scratch += [pltpu.VMEM((tokens, width), jnp.float32)] * 2
    return pl.pallas_call(
        functools.partial(attend_back_kernel, first, lane, before is not None),
        out_shape=out_shape,
        in_specs=[vmem] * (6 + len(extra)),
        out_specs=(vmem,) * len(out_shape),
        scratch_shapes=scratch,
        compiler_params=pltpu.CompilerParams(vmem_limit_bytes=52 << 20),
        cost_estimate=pl.CostEstimate(
            flops=4 * rows * tokens * width * 4, bytes_accessed=10 << 20, transcendentals=0
        ),
        name="attend_back",
    )(packed, bias, lse, att, up_own, up_far, *extra)


FF_CHUNK = 512
ROWS = 112


def rows_of(total, body):
    @pl.loop(0, total // ROWS)
    def _(index):
        body(pl.ds(pl.multiple_of(index * ROWS, ROWS), ROWS))


def unit_rows(values):
    centered = values - jnp.mean(values, axis=-1, keepdims=True)
    spread = lax.rsqrt(jnp.mean(centered * centered, axis=-1, keepdims=True) + EPSILON)
    return centered * spread, spread


def middle_kernel(
    table_ref,
    factor_ref,
    input_ref,
    target_ref,
    valid_ref,
    vector_ref,
    small_ref,
    fc1_own,
    fc1_other,
    fc2_own,
    fc2_other,
    proj_own,
    proj_other,
    two_mine,
    two_theirs,
    *refs,
):
    one_mine, one_theirs, att_parts, refs = refs[:5], refs[5:10], refs[10:16], refs[16:]
    (
        att_hbm,
        out_hbm,
        hidden_hbm,
        pre_hbm,
        norm_hbm,
        grad_low_hbm,
        mid_low_ref,
        grad_mid_ref,
        up_own_ref,
        up_give_ref,
        hidden_sum_ref,
        sums_ref,
        fc1_v,
        fc2_v,
        proj_v,
        middle_v,
        back_v,
        out_ref,
        hidden_ref,
        pre_ref,
        norm_ref,
        grad_low_ref,
        att_ref,
        sem_one,
        sem_two,
        sem_proj,
        sem_att,
        sem_out,
    ) = refs
    stores = [
        pltpu.make_async_copy(source, target, sem_out.at[i])
        for i, (source, target) in enumerate(
            (
                (norm_ref, norm_hbm),
                (hidden_ref, hidden_hbm),
                (out_ref, out_hbm),
                (grad_low_ref, grad_low_hbm),
                (pre_ref, pre_hbm),
                (att_ref, att_hbm),
            )
        )
    ]
    f32, bf16 = jnp.float32, jnp.bfloat16
    total_rows = input_ref.shape[0]
    half = fc1_own.shape[0]
    sub = fc1_own.shape[1] // 4
    heads = proj_own.shape[0]
    part = heads // 4
    hidden_total = hidden_ref.shape[1]
    chunks = hidden_total // FF_CHUNK
    unit = half + 2 * sub + 2 * part + 16

    def fc1_copy(source, side, at):
        lanes = pl.ds(pl.multiple_of(at * sub, sub), sub)
        pltpu.make_async_copy(
            source, fc1_v.at[side * half : (side + 1) * half, lanes], sem_one.at[at // 2]
        ).start()

    def fc2_copy(source, side, i, at):
        lane = side * half + i * sub
        pltpu.make_async_copy(
            source, fc2_v.at[pl.ds(pl.multiple_of(at * sub, sub), sub), lane : lane + sub], sem_two
        ).start()

    sources = []
    for s in range(4):
        step = two_mine.shape[0] // 4
        sources.append((s, 2, two_mine, two_theirs, s * step))
        low, high = (3, 4) if s == 3 else (s, s)
        sources.append((s, 1, one_mine[low], one_theirs[low], 0))
        sources.append((s, 3, one_mine[high], one_theirs[high], 0 if s == 3 else unit))

    early_rows = att_parts[0].shape[0]
    for at in range(2):
        soon, late, other = att_parts[3 * at : 3 * at + 3]
        lanes = slice(2 * at * heads, (2 * at + 1) * heads)
        pltpu.make_async_copy(soon, att_ref.at[0:early_rows, lanes], sem_att).start()
        pltpu.make_async_copy(
            late.at[0 : total_rows - early_rows], att_ref.at[early_rows:total_rows, lanes], sem_att
        ).start()
        lanes = slice((2 * at + 1) * heads, (2 * at + 2) * heads)
        pltpu.make_async_copy(other, att_ref.at[:, lanes], sem_att).start()
    for side, ref in enumerate((proj_own, proj_other)):
        pltpu.make_async_copy(
            ref, proj_v.at[0:heads, side * half : (side + 1) * half], sem_proj
        ).start()
    for s, j, *refs, base in sources:
        rows = pl.ds(pl.multiple_of(j * heads + table_ref[20 + s] * part, part), part)
        for side in range(2):
            for i in range(2):
                low = base + half + 2 * sub + i * part
                lane = side * half + i * sub
                pltpu.make_async_copy(
                    refs[side].at[low : low + part, :], proj_v.at[rows, lane : lane + sub], sem_proj
                ).start()
    for a in range(4):
        for side, ref in enumerate((fc1_own, fc1_other)):
            fc1_copy(ref.at[:, a * sub : (a + 1) * sub], side, table_ref[16 + a])
    for s, j, *refs, base in sources:
        for side in range(2):
            fc1_copy(refs[side].at[base : base + half, :], side, table_ref[4 * s + j])
    for a in range(4):
        for side, ref in enumerate((fc2_own, fc2_other)):
            for i in range(2):
                fc2_copy(
                    ref.at[a * sub : (a + 1) * sub, i * sub : (i + 1) * sub], side, i, table_ref[16 + a]
                )
    for s, j, *refs, base in sources:
        for side in range(2):
            for i in range(2):
                low = base + half + i * sub
                fc2_copy(refs[side].at[low : low + sub, :], side, i, table_ref[4 * s + j])

    def lanes_of(i):
        return pl.ds(pl.multiple_of((table_ref[28] ^ i) * half, half), half)

    sums_ref[...] = jnp.zeros_like(sums_ref)

    pltpu.make_async_copy(att_ref, att_ref, sem_att).wait()
    stores[5].start()
    pltpu.make_async_copy(proj_v, proj_v, sem_proj).wait()
    for i in range(2):
        cols = slice(i * half, (i + 1) * half)
        middle_v[:, cols] = input_ref[:, lanes_of(i)].astype(f32) + (
            dot_nn(att_ref[...], proj_v[:, cols]) + vector_ref[2:3, cols]
        )

    @functools.partial(rows_of, total_rows)
    def _(rows):
        normal, _ = unit_rows(middle_v[rows, :])
        norm_ref[rows, :] = (normal * vector_ref[3:4, :] + vector_ref[4:5, :]).astype(bf16)

    stores[0].start()

    @pl.loop(0, chunks)
    def _(k):
        span = pl.ds(pl.multiple_of(k * FF_CHUNK, FF_CHUNK), FF_CHUNK)
        pltpu.make_async_copy(fc1_v.at[:, span], fc1_v.at[:, span], sem_one.at[k]).wait()
        a = k // 2
        bias = jnp.concatenate(
            [
                small_ref[table_ref[24 + 2 * (k % 2) + i], pl.ds(a, 1), :]
                for i in range(FF_CHUNK // sub)
            ],
            axis=1,
        )
        pre = dot_nn(norm_ref[...], fc1_v[:, span]) + bias
        cdf = 0.5 * (1.0 + lax.erf(pre * ROOT_HALF))
        hidden_ref[:, span] = (pre * cdf).astype(bf16)
        slope = cdf + pre * jnp.exp(-0.5 * pre * pre) * DENSITY_FACTOR
        pre_ref[:, span] = slope.astype(bf16)

    stores[1].start()
    pltpu.make_async_copy(fc2_v, fc2_v, sem_two).wait()
    for i in range(2):
        cols = slice(i * half, (i + 1) * half)
        total = middle_v[:, cols] + (dot_nn(hidden_ref[...], fc2_v[:, cols]) + vector_ref[5:6, cols])
        out_ref[:, lanes_of(i)] = total.astype(bf16)
        differ = total - target_ref[:, lanes_of(i)].astype(f32)
        weighted = valid_ref[...] * differ
        sums_ref[0:1, cols] = jnp.sum(weighted * differ, axis=0, keepdims=True)
        grad = factor_ref[0] * weighted
        grad_mid_ref[:, cols] = grad
        low = grad.astype(bf16)
        grad_low_ref[:, cols] = low
        sums_ref[1:2, cols] = jnp.sum(low.astype(f32), axis=0, keepdims=True)

    stores[2].start()
    stores[3].start()

    @pl.loop(0, chunks)
    def _(k):
        span = pl.ds(pl.multiple_of(k * FF_CHUNK, FF_CHUNK), FF_CHUNK)
        back = dot_nt(grad_low_ref[...], fc2_v[span, :])
        back = (back * pre_ref[:, span].astype(f32)).astype(bf16)
        pre_ref[:, span] = back
        hidden_sum_ref[0:1, span] = jnp.sum(back.astype(f32), axis=0, keepdims=True)

    stores[4].start()
    for i in range(2):
        cols = slice(i * half, (i + 1) * half)
        back_v[:, cols] = dot_nt(pre_ref[...], fc1_v[cols, :])

    @functools.partial(rows_of, total_rows)
    def _(rows):
        normal, spread = unit_rows(middle_v[rows, :])
        upstream = back_v[rows, :]
        inner = upstream * vector_ref[3:4, :]
        center = jnp.mean(inner, axis=-1, keepdims=True)
        slope = jnp.mean(inner * normal, axis=-1, keepdims=True)
        grad = grad_mid_ref[rows, :] + spread * (inner - center - normal * slope)
        grad_mid_ref[rows, :] = grad
        low = grad.astype(bf16)
        mid_low_ref[rows, :] = low
        sums_ref[2:3, :] += jnp.sum(upstream * normal, axis=0, keepdims=True)
        sums_ref[3:4, :] += jnp.sum(upstream, axis=0, keepdims=True)
        sums_ref[4:5, :] += jnp.sum(low.astype(f32), axis=0, keepdims=True)

    for j, (ref, at) in enumerate(((up_own_ref, 0), (up_give_ref, 0), (up_own_ref, 1), (up_give_ref, 1))):
        grad = dot_nt(mid_low_ref[...], proj_v[j * heads : (j + 1) * heads, :])
        ref[:, at * heads : (at + 1) * heads] = grad.astype(bf16)
    for store in stores:
        store.wait()


def middle_block(table, factor, inputs, target, valid, vectors, smalls, pieces):
    rows, width = inputs.shape
    hidden = 4 * pieces[0].shape[1]
    vmem = pl.BlockSpec(memory_space=pltpu.VMEM)
    smem = pl.BlockSpec(memory_space=pltpu.SMEM)
    anywhere = pl.BlockSpec(memory_space=pl.ANY)
    f32, bf16 = jnp.float32, jnp.bfloat16

    def result(columns, dtype):
        return jax.ShapeDtypeStruct((rows, columns), dtype)

    return pl.pallas_call(
        middle_kernel,
        out_shape=(
            result(width, bf16),
            result(width, bf16),
            result(hidden, bf16),
            result(hidden, bf16),
            result(width, bf16),
            result(width, bf16),
            result(width, bf16),
            result(width, f32),
            result(width // 2, bf16),
            result(width // 2, bf16),
            jax.ShapeDtypeStruct((1, hidden), f32),
            jax.ShapeDtypeStruct((8, width), f32),
        ),
        in_specs=[smem] * 2 + [vmem] * 5 + [anywhere] * len(pieces),
        out_specs=[anywhere] * 6 + [vmem] * 6,
        scratch_shapes=[
            pltpu.VMEM((width, hidden), bf16),
            pltpu.VMEM((hidden, width), bf16),
            pltpu.VMEM((width, width), bf16),
            pltpu.VMEM((rows, width), f32),
            pltpu.VMEM((rows, width), f32),
            pltpu.VMEM((rows, width), bf16),
            pltpu.VMEM((rows, hidden), bf16),
            pltpu.VMEM((rows, hidden), bf16),
            pltpu.VMEM((rows, width), bf16),
            pltpu.VMEM((rows, width), bf16),
            pltpu.VMEM((rows, width), bf16),
            pltpu.SemaphoreType.DMA((hidden // FF_CHUNK,)),
            pltpu.SemaphoreType.DMA,
            pltpu.SemaphoreType.DMA,
            pltpu.SemaphoreType.DMA,
            pltpu.SemaphoreType.DMA((6,)),
        ],
        compiler_params=pltpu.CompilerParams(vmem_limit_bytes=62 << 20),
        cost_estimate=pl.CostEstimate(
            flops=2 * rows * width * hidden, bytes_accessed=44 << 20, transcendentals=0
        ),
        name="middle_block",
    )(table, factor, inputs, target, valid, vectors, smalls, *pieces)


def swap(values, axis, mask, size):
    return lax.ppermute(values, axis, [(i, i ^ mask) for i in range(size)])


def over_row(values):
    return swap(values, "row", 1, 2)


def over_dp(values, mask):
    return swap(values, "dp", mask, 4)


def over_col(values, mask):
    return swap(values, "col", mask, 4)


def cut(values, index, size, axis=0):
    return lax.dynamic_slice_in_dim(values, index * size, size, axis)


def place(pieces, index_of, axis):
    size = pieces[0].shape[axis]
    shape = list(pieces[0].shape)
    shape[axis] = size * len(pieces)
    whole = jnp.zeros(shape, pieces[0].dtype)
    for s, piece in enumerate(pieces):
        whole = lax.dynamic_update_slice_in_dim(whole, piece, index_of(s) * size, axis)
    return whole


def copies(listed, sem_ref):
    for index, (source, target) in enumerate(listed):
        pltpu.make_async_copy(source, target, sem_ref.at[index]).start()
    for index, (source, target) in enumerate(listed):
        pltpu.make_async_copy(source, target, sem_ref.at[index]).wait()


def slab_kernel(places_ref, fc1_ref, fc2_ref, proj_ref, qkv_ref, small_ref, out_ref, sem_ref):
    half, sub = fc1_ref.shape[0], fc1_ref.shape[1] // 4
    part, deep = proj_ref.shape[0] // 4, half // 4
    mine = places_ref[0]
    fc2 = fc2_ref.at[pl.ds(pl.multiple_of(mine * sub, sub), sub)]
    proj = proj_ref.at[pl.ds(pl.multiple_of(mine * part, part), part)]
    listed = [(fc1_ref.at[:, pl.ds(pl.multiple_of(mine * sub, sub), sub)], half)]
    listed += [(fc2.at[:, i * sub : (i + 1) * sub], sub) for i in range(2)]
    listed += [(proj.at[:, i * sub : (i + 1) * sub], part) for i in range(2)]
    listed += [(small_ref, small_ref.shape[0])]
    rows = pl.ds(pl.multiple_of(mine * deep, deep), deep)
    listed += [(qkv_ref.at[k, rows], deep) for k in range(3)]
    pairs, at = [], 0
    for source, count in listed:
        pairs.append((source, out_ref.at[at : at + count]))
        at += count
    copies(pairs, sem_ref)


def make_slab(places, fc1, fc2, proj, qkv, small):
    half, sub = fc1.shape[0], fc1.shape[1] // 4
    rows = half + 2 * sub + proj.shape[0] // 2 + small.shape[0] + 3 * (half // 4)
    anywhere = pl.BlockSpec(memory_space=pl.ANY)
    return pl.pallas_call(
        slab_kernel,
        out_shape=jax.ShapeDtypeStruct((rows, sub), fc1.dtype),
        in_specs=[pl.BlockSpec(memory_space=pltpu.SMEM)] + [anywhere] * 5,
        out_specs=pl.BlockSpec(memory_space=pltpu.VMEM),
        scratch_shapes=[pltpu.SemaphoreType.DMA((9,))],
        cost_estimate=small_cost(100000000),
        name="make_slab",
    )(places, fc1, fc2, proj, qkv, small)


def far_qkv_kernel(base, places_ref, mine_ref, theirs_ref, out_ref, sem_ref):
    sub = mine_ref.shape[1]
    half = out_ref.shape[0] // 2
    deep, step = half // 4, mine_ref.shape[0] // 4
    pairs = []
    for side, ref in enumerate((mine_ref, theirs_ref)):
        for s in range(4):
            rows = pl.ds(pl.multiple_of(side * half + places_ref[s] * deep, deep), deep)
            for k in range(3):
                at = s * step + base + k * deep
                pairs.append((ref.at[at : at + deep], out_ref.at[rows, k * sub : (k + 1) * sub]))
    copies(pairs, sem_ref)


def far_qkv(places, mine, theirs, base, width):
    anywhere = pl.BlockSpec(memory_space=pl.ANY)
    return pl.pallas_call(
        functools.partial(far_qkv_kernel, base),
        out_shape=jax.ShapeDtypeStruct((width, 3 * mine.shape[1]), mine.dtype),
        in_specs=[pl.BlockSpec(memory_space=pltpu.SMEM)] + [anywhere] * 2,
        out_specs=pl.BlockSpec(memory_space=pltpu.VMEM),
        scratch_shapes=[pltpu.SemaphoreType.DMA((24,))],
        cost_estimate=small_cost(100000000),
        name="far_qkv",
    )(places, mine, theirs)


def first_norm_kernel(flip_ref, states_ref, vector_ref, *refs):
    out_ref = refs[-1]
    rows_all, width = states_ref.shape
    start = out_ref.shape[0] - rows_all
    if start:
        out_ref[0:start, :] = refs[0][...]

    @pl.loop(0, rows_all // ROWS)
    def _(index):
        rows = pl.ds(pl.multiple_of(index * ROWS, ROWS), ROWS)
        normal, _ = unit_rows(framed(states_ref, rows, flip_ref[0], width // 2))
        values = (normal * vector_ref[0:1, :] + vector_ref[1:2, :]).astype(jnp.bfloat16)
        out_ref[pl.ds(pl.multiple_of(start + index * ROWS, 16), ROWS), :] = values


def first_norm(flip, states, vectors, *before):
    vmem = pl.BlockSpec(memory_space=pltpu.VMEM)
    rows = states.shape[0] + sum(b.shape[0] for b in before)
    return pl.pallas_call(
        first_norm_kernel,
        out_shape=jax.ShapeDtypeStruct((rows, states.shape[1]), jnp.bfloat16),
        in_specs=[pl.BlockSpec(memory_space=pltpu.SMEM)] + [vmem] * (2 + len(before)),
        out_specs=vmem,
        cost_estimate=small_cost(100000000),
        name="first_norm",
    )(flip, states, vectors, *before)


VECTORS = 32


def put_split(ref, at, values):
    high = values.astype(jnp.bfloat16)
    low = (values - high.astype(jnp.float32)).astype(jnp.bfloat16)
    columns = values.shape[1]
    ref[at : at + VECTORS, 0:columns] = high
    ref[at + VECTORS : at + 2 * VECTORS, 0:columns] = low
    rest = ref.shape[1] - columns
    if rest:
        ref[at : at + 2 * VECTORS, columns:] = jnp.zeros((2 * VECTORS, rest), jnp.bfloat16)


def get_split(ref, at, columns):
    high = ref[at : at + VECTORS, 0:columns].astype(jnp.float32)
    return high + ref[at + VECTORS : at + 2 * VECTORS, 0:columns].astype(jnp.float32)


def framed(ref, rows, flip, half):
    return jnp.concatenate(
        [ref[rows, pl.ds(pl.multiple_of((flip ^ i) * half, half), half)] for i in range(2)], axis=1
    ).astype(jnp.float32)


def token_back_kernel(
    flip_ref, near_ref, far_ref, w_near, w_far, own_states, other_states, own_ref, give_ref, sums_ref, other_v
):
    rows_all, half = own_ref.shape[0], own_ref.shape[1] // 2
    sums_ref[...] = jnp.zeros_like(sums_ref)
    for start, out_ref in ((rows_all, other_v), (0, own_ref)):
        rows = slice(start, start + rows_all)
        out_ref[...] = dot_nt(near_ref[rows, :], w_near[...]) + dot_nt(far_ref[rows, :], w_far[...])
    for out_ref, states in ((other_v, other_states), (own_ref, own_states)):

        @functools.partial(rows_of, rows_all)
        def _(rows, out_ref=out_ref, states=states):
            normal, _ = unit_rows(framed(states, rows, flip_ref[0], half))
            upstream = out_ref[rows, :]
            sums_ref[0:1, :] += jnp.sum(upstream * normal, axis=0, keepdims=True)
            sums_ref[1:2, :] += jnp.sum(upstream, axis=0, keepdims=True)
            if out_ref is other_v:
                give_ref[rows, :] = upstream.astype(jnp.bfloat16)


def token_back(flip, near, far, w_near, w_far, own_states, other_states):
    rows, width = own_states.shape
    vmem = pl.BlockSpec(memory_space=pltpu.VMEM)
    return pl.pallas_call(
        token_back_kernel,
        out_shape=(
            jax.ShapeDtypeStruct((rows, width), jnp.float32),
            jax.ShapeDtypeStruct((rows, width), jnp.bfloat16),
            jax.ShapeDtypeStruct((2, width), jnp.float32),
        ),
        in_specs=[pl.BlockSpec(memory_space=pltpu.SMEM)] + [vmem] * 6,
        out_specs=(vmem,) * 3,
        scratch_shapes=[pltpu.VMEM((rows, width), jnp.float32)],
        compiler_params=pltpu.CompilerParams(vmem_limit_bytes=40 << 20),
        cost_estimate=small_cost(100000000),
        name="token_back",
    )(flip, near, far, w_near, w_far, own_states, other_states)


def last_kernel(flip_ref, own_ref, taken_ref, states_ref, mid_ref, vector_ref, out_ref):
    half = own_ref.shape[1] // 2
    upstream = own_ref[...] + taken_ref[...].astype(jnp.float32)
    everything = slice(0, own_ref.shape[0])
    normal, spread = unit_rows(framed(states_ref, everything, flip_ref[0], half))
    inner = upstream * vector_ref[0:1, :]
    center = jnp.mean(inner, axis=-1, keepdims=True)
    slope = jnp.mean(inner * normal, axis=-1, keepdims=True)
    back = mid_ref[...] + spread * (inner - center - normal * slope)
    for i in range(2):
        lanes = pl.ds(pl.multiple_of((flip_ref[0] ^ i) * half, half), half)
        out_ref[:, lanes] = back[:, i * half : (i + 1) * half].astype(jnp.bfloat16)


def last_norm(flip, own, taken, states, mid, vectors):
    rows, width = own.shape
    block = pl.BlockSpec((ROWS, width), lambda i: (i, 0))
    whole = pl.BlockSpec(vectors.shape, lambda i: (0, 0))
    return pl.pallas_call(
        last_kernel,
        grid=(rows // ROWS,),
        out_shape=jax.ShapeDtypeStruct((rows, width), jnp.bfloat16),
        in_specs=[pl.BlockSpec(memory_space=pltpu.SMEM)] + [block] * 4 + [whole],
        out_specs=block,
        cost_estimate=small_cost(500000000),
        name="last_norm",
    )(flip, own, taken, states, mid, vectors)


def far_grads_kernel(
    turned_ref, grad_ref, sums_ref, hidden_ref, norm_ref, near_ref, far_ref, keep_ref, out_ref, kept_ref
):
    half = keep_ref.shape[1]
    width = near_ref.shape[1] // 3
    shared = [hidden_ref[0:1, i * half : (i + 1) * half] for i in range(8)]
    for ref in (near_ref, far_ref):
        shared.append(jnp.concatenate([ref[0:1, 0:width], ref[0:1, 2 * width :]], axis=1))
    shared.append(sums_ref[0:1, 0:half] + sums_ref[0:1, half:])
    blank = jnp.zeros((VECTORS - 6 - len(shared), half), jnp.float32)

    def rows(lanes):
        split = [sums_ref[i : i + 1, lanes] for i in (2, 3, 4, 1)]
        split += [norm_ref[i : i + 1, lanes] for i in range(2)]
        return jnp.concatenate(split + shared + [blank], axis=0)

    keep_ref[...] = rows(slice(0, half))
    put_split(out_ref, half, rows(slice(half, 2 * half)))
    out_ref[0:half, :] = dot_nn(turned_ref[half:, :], grad_ref[...]).astype(jnp.bfloat16)
    kept_ref[...] = dot_nn(turned_ref[0:half, :], grad_ref[...])


def after_row_kernel(
    places_ref, kept_ref, taken_ref, keep_ref, near_ref, near_taken, near_own_ref, far_own_ref, sum_ref, *outs
):
    deep = far_own_ref.shape[0]
    vectors = keep_ref[...] + get_split(taken_ref, 4 * deep, keep_ref.shape[1])
    sum_ref[...] = vectors
    for s in range(4):
        rows = pl.ds(pl.multiple_of(places_ref[s] * deep, deep), deep)
        far = kept_ref[rows, :] + taken_ref[rows, :].astype(jnp.float32)
        if s == 0:
            far_own_ref[...] = far
        else:
            outs[s - 1][0:deep, :] = far.astype(jnp.bfloat16)
            put_split(outs[s - 1], deep, vectors)
        if s % 2 == 0:
            at = slice(s // 2 * deep, (s // 2 + 1) * deep)
            near = near_ref[rows, :].astype(jnp.float32) + near_taken[at, :].astype(jnp.float32)
            if s == 0:
                near_own_ref[...] = near
            else:
                outs[s - 1][deep + 2 * VECTORS :, :] = near.astype(jnp.bfloat16)


def after_plane_kernel(near_ref, far_ref, sum_ref, *refs):
    takes, (keep_ref, vector_ref, give_ref, small_ref) = refs[:3], refs[3:]
    deep = far_ref.shape[0]
    vectors, far = sum_ref[...], far_ref[...]
    keep_ref[...] = near_ref[...] + takes[1][deep + 2 * VECTORS :, :].astype(jnp.float32)
    for take in takes:
        vectors = vectors + get_split(take, deep, vectors.shape[1])
        far = far + take[0:deep, :].astype(jnp.float32)
    vector_ref[...] = vectors
    give_ref[0:deep, :] = far.astype(jnp.bfloat16)
    put_split(give_ref, deep, vectors)
    put_split(small_ref, 0, vectors)


def after_cols_kernel(keep_ref, vector_ref, one_ref, two_ref, three_ref, out_ref, total_ref):
    deep = keep_ref.shape[0]
    out_ref[...] = (keep_ref[...] + two_ref[0:deep, :].astype(jnp.float32)).astype(jnp.bfloat16)
    columns = vector_ref.shape[1]
    far = get_split(two_ref, deep, columns)
    total = vector_ref[...] + far
    total = total + get_split(one_ref, 0, columns) + get_split(three_ref, 0, columns)
    total_ref[...] = total
    total_ref[14:15, :] = vector_ref[14:15, :] + far[15:16, :]


def on_chip(kernel, shapes, name, *args, tables=0):
    vmem = pl.BlockSpec(memory_space=pltpu.VMEM)
    return pl.pallas_call(
        kernel,
        out_shape=tuple(jax.ShapeDtypeStruct(*s) for s in shapes),
        in_specs=[pl.BlockSpec(memory_space=pltpu.SMEM)] * tables + [vmem] * (len(args) - tables),
        out_specs=(vmem,) * len(shapes),
        cost_estimate=small_cost(100000000),
        name=name,
    )(*args)


def wide_kernel(with_proj, places_ref, small_ref, big_ref, taken_ref, *refs):
    if with_proj:
        proj_kept, proj_taken, *refs = refs
    *outs, turned_v = refs
    half, sub = turned_v.shape[0], turned_v.shape[0] // 2
    span = big_ref.shape[1] // 4
    part = 256 // 4 if not with_proj else proj_kept.shape[0] // 16
    turned_v[...] = small_ref[:, 0:half].T
    for s in range(4):
        lanes = pl.ds(pl.multiple_of(places_ref[s] * span, span), span)
        block = dot_nn(turned_v[...], big_ref[:, lanes]) + taken_ref[:, lanes].astype(jnp.float32)
        block = block.astype(jnp.bfloat16)
        for side, (go, slot) in enumerate(((s % 2, s // 2), (s // 2, s % 2))):
            out = outs[2 * side + go]
            rows = slice(slot * sub, (slot + 1) * sub)
            out[rows, 0:span] = block[side * sub : (side + 1) * sub]
            if with_proj:
                at = side * sub
                for j in range(4):
                    start = pl.multiple_of(4 * j * part + places_ref[s] * part, part)
                    piece = proj_kept[pl.ds(start, part), at : at + sub] + proj_taken[
                        pl.ds(start, part), at : at + sub
                    ].astype(jnp.float32)
                    low = slot * sub + j * part
                    out[low : low + part, span:] = piece.astype(jnp.bfloat16)


def wide_grads(places, small, big, taken, proj=()):
    half = small.shape[1] // 2
    columns = big.shape[1] // 4 + (half // 2 if proj else 0)
    vmem = pl.BlockSpec(memory_space=pltpu.VMEM)
    return pl.pallas_call(
        functools.partial(wide_kernel, bool(proj)),
        out_shape=(jax.ShapeDtypeStruct((half, columns), jnp.bfloat16),) * 4,
        in_specs=[pl.BlockSpec(memory_space=pltpu.SMEM)] + [vmem] * (3 + len(proj)),
        out_specs=(vmem,) * 4,
        scratch_shapes=[pltpu.VMEM((half, small.shape[0]), jnp.bfloat16)],
        compiler_params=pltpu.CompilerParams(vmem_limit_bytes=44 << 20),
        cost_estimate=small_cost(3000000000),
        name="wide_grads",
    )(places, small, big, taken, *proj)


def plane_sum_kernel(*refs):
    sub = refs[4].shape[0]
    for side in range(2):
        kept, taken = refs[2 * side : 2 * side + 2]
        for slot in range(2):
            rows = slice(slot * sub, (slot + 1) * sub)
            total = kept[rows, :].astype(jnp.float32) + taken[rows, :].astype(jnp.float32)
            refs[4 + 2 * side + slot][...] = total.astype(jnp.bfloat16)


def cols_out_kernel(places_ref, *refs):
    outs = refs[4:]
    sub = refs[0].shape[0]
    columns = refs[0].shape[1]
    part = (outs[0].shape[0] - 2 * sub) // 2
    for side in range(2):
        kept, taken = refs[2 * side : 2 * side + 2]
        for j in range(4):
            lanes = pl.ds(pl.multiple_of(places_ref[4 + j] * sub, sub), sub)
            total = kept[:, lanes].astype(jnp.float32) + taken[:, lanes].astype(jnp.float32)
            outs[j][side * sub : (side + 1) * sub, :] = total.astype(jnp.bfloat16)
            if part:
                rows = slice(j * part, (j + 1) * part)
                total = kept[rows, columns - sub :].astype(jnp.float32)
                total = total + taken[rows, columns - sub :].astype(jnp.float32)
                low = 2 * sub + side * part
                outs[j][low : low + part, :] = total.astype(jnp.bfloat16)


def mine_kernel(*refs):
    out_ref, at = refs[8], 0
    for group in (refs[0:4], refs[4:8]):
        total = group[0][...].astype(jnp.float32)
        for ref in group[1:]:
            total = total + ref[...].astype(jnp.float32)
        out_ref[at : at + total.shape[0], :] = total.astype(jnp.bfloat16)
        at += total.shape[0]


def finish_kernel(part_rows, places_ref, *refs):
    pieces, (fc2_ref, fc1_ref, proj_ref) = refs[:2], refs[2:]
    half, sub = fc1_ref.shape[0], pieces[0].shape[1]
    for s in range(4):
        piece, base = pieces[s // 2], (s % 2) * (pieces[0].shape[0] // 2)
        at = places_ref[s]
        rows = pl.ds(pl.multiple_of(at * sub, sub), sub)
        fc2_ref[rows, :] = piece[base : base + half, :].astype(jnp.float32).T
        fc1_ref[:, rows] = piece[base + half : base + 2 * half, :].astype(jnp.float32)
        rows = pl.ds(pl.multiple_of(at * part_rows, part_rows), part_rows)
        for i in range(2):
            low = base + 2 * half + i * part_rows
            proj_ref[rows, i * sub : (i + 1) * sub] = piece[low : low + part_rows, :].astype(jnp.float32)


def finish_qkv_kernel(places_ref, *refs):
    out_ref = refs[4]
    deep, width = refs[0].shape[0], out_ref.shape[2]
    for s in range(4):
        rows = pl.ds(pl.multiple_of(places_ref[s] * deep, deep), deep)
        for k in range(3):
            out_ref[k, rows, :] = refs[s][:, k * width : (k + 1) * width].astype(jnp.float32)


def finish(places, pieces, part_rows):
    rows, sub = pieces[0].shape
    half = (rows // 2 - 2 * part_rows) // 2
    vmem = pl.BlockSpec(memory_space=pltpu.VMEM)
    return pl.pallas_call(
        functools.partial(finish_kernel, part_rows),
        out_shape=(
            jax.ShapeDtypeStruct((4 * sub, half), jnp.float32),
            jax.ShapeDtypeStruct((half, 4 * sub), jnp.float32),
            jax.ShapeDtypeStruct((4 * part_rows, half), jnp.float32),
        ),
        in_specs=[pl.BlockSpec(memory_space=pltpu.SMEM)] + [vmem] * 2,
        out_specs=[vmem] * 3,
        cost_estimate=small_cost(100000000),
        name="finish",
    )(places, *pieces)


def finish_qkv(places, pieces):
    deep, width = pieces[0].shape
    vmem = pl.BlockSpec(memory_space=pltpu.VMEM)
    return pl.pallas_call(
        finish_qkv_kernel,
        out_shape=jax.ShapeDtypeStruct((3, 4 * deep, width // 3), jnp.float32),
        in_specs=[pl.BlockSpec(memory_space=pltpu.SMEM)] + [vmem] * 4,
        out_specs=vmem,
        cost_estimate=small_cost(100000000),
        name="finish_qkv",
    )(places, *pieces)


def tie(value, *others):
    return lax.optimization_barrier((value, *others))[0]


def add_up(own, taken):
    total = own.astype(jnp.float32)
    for piece in taken:
        total = total + piece.astype(jnp.float32)
    return total


def local_paired(
    states,
    ln1_gain,
    ln1_bias,
    w_qkv,
    q_bias,
    v_bias,
    w_proj,
    proj_bias,
    ln2_gain,
    ln2_bias,
    w_fc1,
    fc1_bias,
    w_fc2,
    fc2_bias,
    teacher,
    loss_mask,
    lengths,
):
    f32, bf16 = jnp.float32, jnp.bfloat16
    dp = lax.axis_index("dp")
    row = lax.axis_index("row")
    col = lax.axis_index("col")
    local_rows, width = states.shape
    half = width // 2
    head_width = w_qkv.shape[2]
    hidden_width = w_fc1.shape[1]
    sub = hidden_width // 4
    span = 4 * sub
    part_rows = head_width // 4
    clip = (dp * 2 + row) * 2 + col // 2
    second = col % 2

    def quarter(s):
        return dp ^ s

    def frame(values):
        return jnp.where(
            row == 0, values, jnp.concatenate([values[:, half:], values[:, :half]], axis=1)
        )

    places = jnp.stack([dp ^ s for s in range(4)] + [col ^ j for j in range(4)]).astype(jnp.int32)
    flip = row.reshape(1).astype(jnp.int32)
    states_other = over_col(states, 1)
    small = jnp.concatenate(
        [
            fc1_bias.reshape(4, sub),
            q_bias.reshape(1, sub),
            v_bias.reshape(1, sub),
            jnp.zeros((10, sub), bf16),
        ],
        axis=0,
    )
    slab = make_slab(places, w_fc1, w_fc2, w_proj, w_qkv.transpose(1, 0, 2), small)
    unit_rows_total = half + 2 * sub + 2 * part_rows + small.shape[0]
    small_at = unit_rows_total - small.shape[0]
    two = over_col(slab, 2)
    w_qkv2 = w_qkv.reshape(half, 3 * head_width)
    w_qkv2 = tie(w_qkv2, slab)
    qkv_near = jnp.concatenate([w_qkv2, over_row(w_qkv2)], axis=0)
    vectors = jnp.stack([ln1_gain, ln1_bias, proj_bias, ln2_gain, ln2_bias, fc2_bias])
    vectors, states, teacher, loss_mask = lax.optimization_barrier(
        (vectors, states, teacher, loss_mask, slab)
    )[:4]
    vectors = jnp.concatenate([vectors, over_row(vectors)], axis=1).astype(f32)
    fc1_other, fc2_other, proj_other = over_row(w_fc1), over_row(w_fc2), over_row(w_proj)
    two = tie(two, fc1_other, fc2_other, proj_other)
    two_x, two_y = over_dp(two, 1), over_dp(two, 2)
    states_other = tie(states_other, two)

    all_clips = lengths.shape[0]
    valid_all = (
        loss_mask.reshape(all_clips, L) * (jnp.arange(L)[None, :] < lengths[:, None])
    ).astype(f32)
    valid_total = jnp.maximum(jnp.sum(valid_all), 1.0)
    first_row = ((dp * 2 + row) * 4 + col) * local_rows
    valid = lax.dynamic_slice_in_dim(valid_all.reshape(all_clips * L), first_row, local_rows)
    my_length = lax.dynamic_slice_in_dim(lengths, clip, 1)
    spot = jnp.arange(L)
    position = jnp.where(
        spot < local_rows, second * local_rows + spot, (1 - second) * local_rows + spot - local_rows
    )
    key_bias = jnp.where(position < my_length, 0.0, MASKED).astype(f32)
    key_bias = jnp.broadcast_to(key_bias[:, None], (L, 128))

    norm_one = first_norm(flip, states, vectors)
    tokens_one = first_norm(flip, states_other, vectors, tie(norm_one, two))

    zero_bias = jnp.zeros((head_width,), f32)
    score_scale = HD**-0.5
    scale = jnp.where(jnp.arange(3 * head_width) < head_width, score_scale, 1.0).astype(bf16)
    split = local_rows // QT * QT
    later = L - split
    over = local_rows - split

    def project(matrix, q_add, v_add):
        projected = jnp.dot(tokens_one, matrix, preferred_element_type=f32)
        add = jnp.concatenate([q_add.astype(f32), zero_bias, v_add.astype(f32)])
        return (projected + add[None]).astype(bf16) * scale[None]

    table = jnp.stack(
        [(dp ^ s) * 4 + (col ^ j) for s in range(4) for j in range(4)]
        + [a * 4 + col for a in range(4)]
        + [dp ^ s for s in range(4)]
        + [col ^ b for b in range(4)]
        + [row]
    ).astype(jnp.int32)
    loss_scale = all_clips * L * width / 2.0
    factor = (loss_scale * 2.0 / (valid_total * width)).reshape(1)
    valid = valid[:, None]
    packed_near = tie(project(qkv_near, q_bias, v_bias), table, factor, valid)
    cut_at = two.shape[0] // 32 * 16
    two_x, two_y = tie(two_x, packed_near), tie(two_y, packed_near)
    two_low, two_high = over_dp(two_y[:cut_at], 1), over_dp(two_x[cut_at:], 2)
    one_give = jnp.concatenate([slab[:unit_rows_total], two[:unit_rows_total]], axis=0)
    one = over_col(tie(one_give, states_other), 1)
    turned = lax.optimization_barrier((tokens_one.T, packed_near))[0]
    near_late, near_late_lse = attend(
        tie(packed_near, two_x, two_y, one, turned), key_bias, split, later
    )
    two_low, two_high = tie(two_low, near_late), tie(two_high, near_late)
    two_all = jnp.concatenate([two, two_x, two_y, two_low, two_high], axis=0)
    two_theirs = over_row(two_all)
    near_other = over_col(near_late[over:], 1)
    one_x, one_y = over_dp(one, 1), over_dp(one, 2)
    one_other = over_row(tie(one, near_late))
    near_soon, near_soon_lse = attend(
        tie(packed_near, two_all, near_late, one), key_bias, 0, split
    )
    two_theirs = tie(two_theirs, near_soon, near_other)
    qkv_far = far_qkv(places, two_all, two_theirs, unit_rows_total, width)
    far_small = two_all[small_at : small_at + small.shape[0]]
    packed_far = project(qkv_far, far_small[4], far_small[5])
    packed_far = tie(packed_far, one, near_other)
    far_late, far_late_lse = attend(packed_far, key_bias, split, later)
    far_other = over_col(far_late[over:], 1)
    one_x, one_y = tie(one_x, far_late), tie(one_y, far_late)
    cut_at = one.shape[0] // 2
    one_low, one_high = over_dp(one_y[:cut_at], 1), over_dp(one_x[cut_at:], 2)
    one_theirs = [over_row(one_x), over_row(one_y)]
    far_soon, far_soon_lse = attend(
        tie(packed_far, one_x, one_y, far_late, one_other), key_bias, 0, split
    )
    one_low, one_high = tie(one_low, far_soon, far_other), tie(one_high, far_soon, far_other)
    one_mine = [one, one_x, one_y, one_low, one_high]
    one_theirs = [one_other, *one_theirs, over_row(one_low), over_row(one_high)]
    at = unit_rows_total + small_at
    smalls = jnp.stack(
        [small, one[small_at : small_at + 16], two_all[small_at : small_at + 16], one[at : at + 16]]
    ).astype(f32)
    (
        attended_rows,
        outputs,
        hidden,
        grad_pre,
        norm_two,
        grad_low,
        mid_low,
        grad_mid,
        up_own,
        up_give,
        hidden_sum,
        sums,
    ) = middle_block(
        table,
        factor,
        states,
        teacher,
        valid,
        vectors,
        smalls,
        (
            w_fc1,
            fc1_other,
            w_fc2,
            fc2_other,
            w_proj,
            proj_other,
            two_all,
            two_theirs,
            *one_mine,
            *one_theirs,
            near_soon,
            near_late,
            near_other,
            far_soon,
            far_late,
            far_other,
        ),
    )
    up_far = over_col(up_give, 1)

    def joined(kept, taken):
        return (kept.astype(f32) + taken.astype(f32)).astype(bf16)

    give_fc2 = over_row(dot_tn(grad_low[:, half:], hidden).astype(bf16))
    give_fc1 = over_row(dot_tn(norm_two[:, half:], grad_pre).astype(bf16))
    give_proj = over_row(dot_tn(attended_rows, mid_low[:, half:]).astype(bf16))
    kept_proj = dot_tn(attended_rows, mid_low[:, :half])

    def plane_first(wide):
        keep_x, give_x, keep_y, give_y = wide
        return (keep_x, keep_y), (give_x, give_y), (over_dp(give_x, 1), over_dp(give_y, 2))

    def plane_second(keep, taken):
        shape = ((keep[0].shape[0] // 2, keep[0].shape[1]), bf16)
        keep_x, give_x, keep_y, give_y = on_chip(
            plane_sum_kernel, [shape] * 4, "plane_sum", keep[0], taken[0], keep[1], taken[1]
        )
        return (keep_x, keep_y), (give_x, give_y), (over_dp(give_x, 2), over_dp(give_y, 1))

    def cols_out(keep, taken, rows):
        blocks = on_chip(
            cols_out_kernel,
            [((rows, sub), bf16)] * 4,
            "cols_out",
            *(places, keep[0], taken[0], keep[1], taken[1]),
            tables=1,
        )
        return blocks, [over_col(blocks[j], j) for j in (1, 2, 3)]

    def all_tied(values, *others):
        return [tie(v, *others) for v in values]

    wide = wide_grads(places, grad_low, hidden, give_fc2)
    fc2_keep, fc2_give, fc2_taken = plane_first(wide)
    wide = wide_grads(
        places, tie(norm_two, *fc2_give), grad_pre, give_fc1, (kept_proj, give_proj)
    )
    fc1_keep, fc1_give, fc1_taken = plane_first(wide)

    packed_near = tie(packed_near, *fc2_give, *fc1_give)
    part_near = attend_back(packed_near, key_bias, near_soon_lse, near_soon, up_own, None, 0, 0)
    fc2_keep, fc2_give, fc2_taken = plane_second(fc2_keep, all_tied(fc2_taken, part_near[0]))

    packed_far = tie(packed_far, *fc2_give, part_near[0])
    part_far = attend_back(
        packed_far, key_bias, far_soon_lse, far_soon, up_own, None, head_width, 0
    )
    fc2_blocks, fc2_cols = cols_out(fc2_keep, all_tied(fc2_taken, part_far[0]), 2 * sub)
    fc1_keep, fc1_give, fc1_taken = plane_second(fc1_keep, all_tied(fc1_taken, part_far[0]))

    packed_near = tie(packed_near, *fc2_blocks, *fc1_give)
    grad_near, near_sums = attend_back(
        packed_near, key_bias, near_late_lse, near_late, up_own, up_far, 0, split, part_near
    )
    fc2_cols = all_tied(fc2_cols, grad_near)
    fc1_blocks, fc1_cols = cols_out(
        fc1_keep, all_tied(fc1_taken, grad_near, *fc2_cols), 2 * sub + 2 * part_rows
    )
    near_tied = tie(grad_near, *fc1_blocks)
    near_row = over_row(dot_tn(tokens_one[:, half:], near_tied).astype(bf16))
    wide_near = joined(dot_tn(tokens_one[:, :half], near_tied), near_row)
    deep = half // 4
    near_give = jnp.concatenate([cut(wide_near, quarter(s), deep) for s in (1, 3)], axis=0)
    near_taken = over_dp(near_give, 1)

    packed_far = tie(packed_far, near_give, *fc1_blocks, *fc2_cols)
    grad_far, far_sums = attend_back(
        packed_far, key_bias, far_late_lse, far_late, up_own, up_far, head_width, split, part_far
    )

    norm_own, norm_give, norm_sums = token_back(
        flip, grad_near, grad_far, qkv_near, qkv_far, states, states_other
    )
    norm_taken = over_col(norm_give, 1)
    columns, slots = grad_far.shape[1], 2 * VECTORS
    vec_keep, row_give, kept = on_chip(
        far_grads_kernel,
        [((VECTORS, half), f32), ((half + slots, columns), bf16), ((half, columns), f32)],
        "far_grads",
        *(turned, tie(grad_far, norm_give, near_taken, *fc1_cols), sums, hidden_sum, norm_sums, near_sums, far_sums),
    )
    row_taken = over_row(row_give)
    near_own, far_own, vec_sum, *plane_give = on_chip(
        after_row_kernel,
        [((deep, columns), f32)] * 2
        + [((VECTORS, half), f32)]
        + [((deep + slots + (deep if s == 2 else 0), columns), bf16) for s in (1, 2, 3)],
        "after_row",
        *(places, kept, row_taken, vec_keep, wide_near, near_taken),
        tables=1,
    )
    plane_taken = [over_dp(plane_give[s - 1], s) for s in (1, 2, 3)]
    fc1_cols = all_tied(fc1_cols, *plane_give)
    mine_rows = fc2_blocks[0].shape[0] + fc1_blocks[0].shape[0]
    (mine,) = on_chip(
        mine_kernel,
        [((mine_rows, sub), bf16)],
        "mine",
        *(fc2_blocks[0], *fc2_cols, fc1_blocks[0], *fc1_cols),
    )
    mine_x = over_dp(mine, 1)
    plane_taken = all_tied(plane_taken, mine)
    near_own, vec_sum, col_give, vec_give = on_chip(
        after_plane_kernel,
        [
            ((deep, columns), f32),
            ((VECTORS, half), f32),
            ((deep + slots, columns), bf16),
            ((slots, half), bf16),
        ],
        "after_plane",
        *(near_own, far_own, vec_sum, *plane_taken),
    )
    mine_two = jnp.concatenate([mine, tie(mine_x, col_give)], axis=0)
    mine_y = over_dp(mine_two, 2)
    col_taken = [over_col(vec_give, 1), over_col(col_give, 2), over_col(vec_give, 3)]
    norm_taken = tie(norm_taken, col_give)
    grad_states = last_norm(flip, norm_own, norm_taken, states, grad_mid, vectors)

    qkv_mine, vec_total = on_chip(
        after_cols_kernel,
        [((deep, columns), bf16), ((VECTORS, half), f32)],
        "after_cols",
        *(near_own, vec_sum, *all_tied(col_taken, grad_states)),
    )
    qkv_back = [over_dp(qkv_mine, s) for s in (1, 2, 3)]
    fc2_grad, fc1_grad, proj_grad = finish(places, [mine_two, tie(mine_y, qkv_mine)], part_rows)
    qkv_grad = finish_qkv(places, [qkv_mine, *all_tied(qkv_back, fc2_grad)]).transpose(1, 0, 2)

    fc1_bias_grad = lax.dynamic_index_in_dim(vec_total[6:14].reshape(4, 4, sub), col, 1, False)
    loss_value = jnp.sum(vec_total[16]) / (valid_total * width)
    return (
        outputs,
        loss_value,
        grad_states,
        vec_total[4],
        vec_total[5],
        qkv_grad,
        vec_total[14, :head_width],
        vec_total[14, head_width:],
        proj_grad,
        vec_total[2],
        vec_total[0],
        vec_total[1],
        fc1_grad,
        fc1_bias_grad.reshape(span),
        fc2_grad,
        vec_total[3],
    )


def solution(mesh):
    sizes = (mesh.shape["dp"], mesh.shape["row"], mesh.shape["col"])
    body = local_paired if sizes == PAIRED_MESH else local_general
    in_specs = (
        P(("dp", "row", "col"), None),
        P("row"),
        P("row"),
        P("row", None, "col"),
        P("col"),
        P("col"),
        P("col", "row"),
        P("row"),
        P("row"),
        P("row"),
        P("row", "col"),
        P("col"),
        P("col", "row"),
        P("row"),
        P(("dp", "row", "col"), None),
        P(),
        P(),
    )
    out_specs = (
        P(("dp", "row", "col"), None),
        P(),
        P(("dp", "row", "col"), None),
        P("row"),
        P("row"),
        P("row", None, "col"),
        P("col"),
        P("col"),
        P("col", "row"),
        P("row"),
        P("row"),
        P("row"),
        P("row", "col"),
        P("col"),
        P("col", "row"),
        P("row"),
    )
    return jax.shard_map(body, mesh=mesh, in_specs=in_specs, out_specs=out_specs, check_vma=False)
```
